32 devices in a mesh: batch: 4 (over x, core), blk: 8 (over z, y).
Axes of the slice: x: 2, y: 2, z: 4, core: 2. Of those that a mesh axis runs over, the one named last changes fastest.
Arguments:
- inputs: bfloat16 [32, 1024, 768], P('batch', 'blk'), may hold values from -6 to 6
- cotangent: bfloat16 [32, 1024, 768], P('batch', 'blk'), may hold values from -6 to 6
- group_counts: int32 [4], replicated, may hold values from 1 to 8, as said below
- first_gain: float32 [768], replicated, may hold values from 0.5 to 1.5
- first_bias: float32 [768], replicated, may hold values from -1.25 to 1.25
- qkv_weight: bfloat16 [768, 2304], replicated, may hold values from -0.21875 to 0.21875
- qkv_bias: float32 [2304], replicated, may hold values from -1.25 to 1.25
- out_weight: bfloat16 [768, 768], replicated, may hold values from -1.75 to 1.75
- out_bias: float32 [768], replicated, may hold values from -1.25 to 1.25
- second_gain: float32 [768], replicated, may hold values from 0.5 to 1.5
- second_bias: float32 [768], replicated, may hold values from -1.25 to 1.25
- up_weight: bfloat16 [768, 3072], replicated, may hold values from -0.21875 to 0.21875
- up_bias: float32 [3072], replicated, may hold values from -1.25 to 1.25
- down_weight: bfloat16 [3072, 768], replicated, may hold values from -0.109375 to 0.109375
- down_bias: float32 [768], replicated, may hold values from -1.25 to 1.25
- compress: bfloat16 [256, 1024], P(None, 'blk'), may hold values from -0.1875 to 0.1875
Outputs:
- output: bfloat16 [32, 1024, 768], P('batch', 'blk')
- input_grad: bfloat16 [32, 1024, 768], P('batch', 'blk')
- first_gain_grad: float32 [768], P('blk')
- first_bias_grad: float32 [768], P('blk')
- qkv_weight_grad: float32 [768, 2304], P('blk')
- qkv_bias_grad: float32 [2304], P('blk')
- out_weight_grad: float32 [768, 768], P('blk')
- out_bias_grad: float32 [768], P('blk')
- second_gain_grad: float32 [768], P('blk')
- second_bias_grad: float32 [768], P('blk')
- up_weight_grad: float32 [768, 3072], P('blk')
- up_bias_grad: float32 [3072], P('blk')
- down_weight_grad: float32 [3072, 768], P('blk')
- down_bias_grad: float32 [768], P('blk')
- compress_grad: float32 [256, 1024], P(None, 'blk')
The draws below stay inside these ranges and needn't reach their ends.
Inputs may be any that keep to these rules, and one draw needn't show every extreme that they name: Group g holds sequences in its slots 0 to group_counts[g] - 1; the counts of all groups add up to exactly 20; in every draw some group uses all 8 slots and some group uses one.
All inputs are finite; a program needn't handle non-finite values.
Results may differ from the reference program's by a relative error of at most 0.02.
Values may be sent and summed in bfloat16 or wider, within the bound.
A program may use at most 192 MiB of HBM per device.

```python
import math
import jax
import jax.numpy as jnp
from jax import lax

D = 768
H = 12
HD = 64
FF = 3072
KP = 256
SLOTS = 8
LENGTH = 1024
SEQS = 32
N_BATCH = 4


def draw_group_counts(key, part):
    order_key, move_key = jax.random.split(key, 2)
    per_group = SLOTS // 2 + 1
    order = jax.random.permutation(order_key, N_BATCH)
    fullest = order[0]
    emptiest = order[1]
    adjusted = order[2]
    places = jnp.arange(N_BATCH, dtype=jnp.int32)
    counts = jnp.full((N_BATCH,), per_group, jnp.int32)
    counts = jnp.where(places == fullest, SLOTS, counts)
    counts = jnp.where(places == emptiest, 1, counts)
    counts = jnp.where(places == adjusted, counts + (2 * per_group - 1 - SLOTS), counts)

    def one_move(step, current):
        step_key = jax.random.fold_in(move_key, step)
        source_key, target_key = jax.random.split(step_key, 2)
        source = jax.random.randint(source_key, (), 0, N_BATCH)
        target = jax.random.randint(target_key, (), 0, N_BATCH)
        fixed_source = (source == fullest) | (source == emptiest)
        fixed_target = (target == fullest) | (target == emptiest)
        allowed = (source != target) & ~fixed_source & ~fixed_target
        allowed = allowed & (current[source] > 1) & (current[target] < SLOTS)
        change = jnp.where(allowed, 1, 0).astype(jnp.int32)
        current = current - jnp.where(places == source, change, 0)
        return current + jnp.where(places == target, change, 0)
    counts = lax.fori_loop(0, 4 * N_BATCH, one_move, counts)
    return counts.astype(jnp.int32)


def steps_of(rng, extent, cuts, low, top_value):
    factor_of = 1.0
    for dim, blocks in cuts:
        draws = jax.random.uniform(jax.random.fold_in(jax.random.fold_in(rng, 6), dim), (blocks,), jnp.float32, low / len(cuts), top_value / len(cuts))
        factor_of = factor_of * jnp.repeat(jnp.exp(draws), extent[dim] // blocks).reshape((-1,) + (1,) * (len(extent) - 1 - dim))
    return factor_of


def scatter_about(key, extent, deviation, reach, shards=(), kind=jnp.bfloat16):
    level = steps_of(key, extent, shards, -0.22, 0.18) if shards else 1.0
    drawn = jax.random.normal(key, extent, jnp.float32) * deviation * level
    return jnp.minimum(jnp.maximum(drawn, -reach), reach).astype(kind)


def setup_inputs(seed: int = 0) -> dict:
    key_list = jax.random.split(jax.random.key(seed), 17)
    return {
        "inputs": scatter_about(key_list[0], (SEQS, LENGTH, D), 1.0, 6.0, ((0, 4), (1, 8))),
        "cotangent": scatter_about(key_list[1], (SEQS, LENGTH, D), 1.0, 6.0, ((0, 4), (1, 8))),
        "group_counts": draw_group_counts(jax.random.fold_in(key_list[16], 71), 0),
        "first_gain": jnp.clip(1.0 + 0.1 * jax.random.normal(key_list[3], (D,), jnp.float32), 0.5, 1.5),
        "first_bias": scatter_about(key_list[4], (D,), 0.2, 1.25, (), jnp.float32),
        "qkv_weight": scatter_about(key_list[5], (D, 3 * D), D ** -0.5, 0.21875),
        "qkv_bias": scatter_about(key_list[6], (3 * D,), 0.2, 1.25, (), jnp.float32),
        "out_weight": scatter_about(key_list[7], (D, D), (max(D // 64, 4)) ** -0.5, 1.75),
        "out_bias": scatter_about(key_list[8], (D,), 0.2, 1.25, (), jnp.float32),
        "second_gain": jnp.clip(1.0 + 0.1 * jax.random.normal(key_list[9], (D,), jnp.float32), 0.5, 1.5),
        "second_bias": scatter_about(key_list[10], (D,), 0.2, 1.25, (), jnp.float32),
        "up_weight": scatter_about(key_list[11], (D, FF), D ** -0.5, 0.21875),
        "up_bias": scatter_about(key_list[12], (FF,), 0.2, 1.25, (), jnp.float32),
        "down_weight": scatter_about(key_list[13], (FF, D), FF ** -0.5, 0.109375),
        "down_bias": scatter_about(key_list[14], (D,), 0.2, 1.25, (), jnp.float32),
        "compress": scatter_about(key_list[15], (KP, LENGTH), LENGTH ** -0.5, 0.1875, ((1, 8),)),
    }


precise = lax.Precision.HIGHEST

@jax.custom_vjp
def low(v):
    return lax.optimization_barrier(v.astype(jnp.bfloat16)).astype(jnp.float32)

@jax.custom_vjp
def low_back(v):
    return v

def low_keep(v):
    return (low(v), None)

def low_pass(kept, grad):
    return (grad,)

def back_keep(v):
    return (v, None)

def back_low(kept, grad):
    return (low(grad),)
low.defvjp(low_keep, low_pass)
low_back.defvjp(back_keep, back_low)

def layer_norm(states, factor, offset):
    center = states - lax.optimization_barrier(jnp.mean(states, axis=-1, keepdims=True))
    spread = lax.optimization_barrier(jnp.mean(center * center, axis=-1, keepdims=True))
    return center * lax.rsqrt(spread + 1e-05) * factor + offset

def matmul(former, latter):
    return jnp.dot(former, latter, precision=precise)

def forward_layer(params, states):
    first_gain, first_bias, qkv_weight, qkv_bias, out_weight, out_bias, second_gain, second_bias, up_weight, up_bias, down_weight, down_bias, compress = params
    length = states.shape[0]
    normed = low(layer_norm(states, first_gain, first_bias))
    project = low_back(matmul(normed, qkv_weight) + qkv_bias)
    queries = low(project[:, :D]).reshape(length, H, HD)
    key_rows = low(project[:, D:2 * D])
    value_rows = low(project[:, 2 * D:])
    key_summary = low(low_back(matmul(compress, key_rows))).reshape(KP, H, HD)
    value_summary = low(low_back(matmul(compress, value_rows))).reshape(KP, H, HD)
    scores = low_back(jnp.einsum('thd,jhd->htj', queries, key_summary, precision=precise) * (1.0 / math.sqrt(HD)))
    weights = low(jax.nn.softmax(scores, axis=-1))
    mixed_heads = jnp.einsum('htj,jhd->thd', weights, value_summary, precision=precise).reshape(length, D)
    mixed_heads = low(low_back(mixed_heads))
    branch = low_back(matmul(mixed_heads, out_weight) + out_bias)
    middle = states + branch
    second_normed = low(layer_norm(middle, second_gain, second_bias))
    hidden = low_back(matmul(second_normed, up_weight) + up_bias)
    active = low(jax.nn.gelu(hidden, approximate=True))
    return middle + matmul(active, down_weight) + down_bias

def reference(inputs, cotangent, group_counts, first_gain, first_bias, qkv_weight, qkv_bias, out_weight, out_bias, second_gain, second_bias, up_weight, up_bias, down_weight, down_bias, compress):
    params = tuple((item.astype(jnp.float32) for item in (first_gain, first_bias, qkv_weight, qkv_bias, out_weight, out_bias, second_gain, second_bias, up_weight, up_bias, down_weight, down_bias, compress)))
    sequence_index = jnp.arange(N_BATCH * SLOTS, dtype=jnp.int32)
    alive = sequence_index % SLOTS < group_counts[sequence_index // SLOTS]

    def advance(totals, item):
        sequence, incoming, live_flag = item
        states = sequence.astype(jnp.float32)
        upstream = incoming.astype(jnp.float32)

        def compute(unused):
            result, backward = jax.vjp(forward_layer, params, states)
            param_grads, state_grad = backward(upstream)
            return (result, state_grad, param_grads)

        def vacant(unused):
            return (jnp.zeros_like(states), jnp.zeros_like(states), jax.tree.map(jnp.zeros_like, params))
        result, state_grad, param_grads = lax.cond(live_flag, compute, vacant, 0)
        totals = jax.tree.map(lambda accum, extra: accum + extra, totals, param_grads)
        return (totals, (result.astype(jnp.bfloat16), state_grad.astype(jnp.bfloat16)))
    start = jax.tree.map(jnp.zeros_like, params)
    totals, (output, input_grad) = lax.scan(advance, start, (inputs, cotangent, alive))
    return (output, input_grad) + tuple(totals)
```

```python
import functools
import math

import jax
import jax.numpy as jnp
from jax import lax
from jax.sharding import PartitionSpec as P

H = 12
HD = 64
F32 = jnp.float32
BF16 = jnp.bfloat16


def norm_stats(states):
    center = states - jnp.mean(states, axis=-1, keepdims=True)
    spread = jnp.mean(center * center, axis=-1, keepdims=True)
    rate = lax.rsqrt(spread + 1e-05)
    return center * rate, rate


def norm_back(hat, rate, upstream, gain):
    scaled = upstream * gain
    return rate * (
        scaled
        - jnp.mean(scaled, axis=-1, keepdims=True)
        - hat * jnp.mean(scaled * hat, axis=-1, keepdims=True)
    )


def dot(a, b):
    return jnp.dot(a, b, preferred_element_type=F32)


def dot_t(a, b):
    return lax.dot_general(a, b, (((1,), (1,)), ((), ())), preferred_element_type=F32)


def t_dot(a, b):
    return lax.dot_general(a, b, (((0,), (0,)), ((), ())), preferred_element_type=F32)


def swap(values, axis, size, bit):
    return lax.ppermute(values, axis, [(i, i ^ bit) for i in range(size)])


def halve(values, dim, axis, size, bit):
    mine = (lax.axis_index(axis) // bit) % 2
    send = lax.dynamic_index_in_dim(values, 1 - mine, dim, keepdims=False).astype(BF16)
    keep = lax.dynamic_index_in_dim(values, mine, dim, keepdims=False)
    return keep.astype(F32) + swap(send, axis, size, bit).astype(F32)


def scatter_sum(terms, bits, order, nb, nk):
    _, rows, cols = terms.shape
    values = halve(terms.reshape(-1, 2, rows // 2, cols), 1, "batch", nb, 1)
    left = list(bits)
    for bit in order:
        place = left.index(bit)
        values = values.reshape(1 << place, 2, -1, rows // 2, cols)
        values = halve(values, 1, "blk", nk, bit)
        left.remove(bit)
    values = values.reshape(rows // 2, cols)
    bit = 2
    while bit < nb:
        low = values.astype(BF16)
        values = low.astype(F32) + swap(low, "batch", nb, bit).astype(F32)
        bit *= 2
    mine = lax.axis_index("batch") % 2
    other = swap(values, "batch", nb, 1)
    first = jnp.where(mine == 0, values, other)
    second = jnp.where(mine == 0, other, values)
    return jnp.concatenate([first, second], axis=0)


def body(
    inputs,
    cotangent,
    group_counts,
    first_gain,
    first_bias,
    qkv_weight,
    qkv_bias,
    out_weight,
    out_bias,
    second_gain,
    second_bias,
    up_weight,
    up_bias,
    down_weight,
    down_bias,
    compress,
    *,
    nb,
    nk,
):
    slots, tokens, width = inputs.shape
    splits = nk // slots
    teams = [[t * slots + i for i in range(slots)] for t in range(splits)]
    across = [[t * slots + i for t in range(splits)] for i in range(slots)]
    rows = slots * tokens

    def gather_rows(values):
        return lax.all_to_all(values, "blk", 0, 0, axis_index_groups=teams, tiled=True).reshape(
            rows, width
        )

    def spread_rows(values):
        return lax.all_to_all(
            values.reshape(slots, tokens, width), "blk", 0, 0, axis_index_groups=teams, tiled=True
        )

    def over_splits(values):
        if splits == 1:
            return values
        return lax.psum(values, "blk", axis_index_groups=across)

    slot = lax.axis_index("blk") % slots
    alive = slot < group_counts[lax.axis_index("batch")]

    low_x = gather_rows(inputs)
    squeeze = lax.all_gather(compress, "blk", axis=1, tiled=True, axis_index_groups=teams)
    low_cot = gather_rows(cotangent)
    incoming = jnp.where(alive, low_cot, jnp.zeros_like(low_cot))

    states = low_x.astype(F32)
    hat_first, rate_first = norm_stats(states)
    normed = (hat_first * first_gain + first_bias).astype(BF16)
    query_weight, pair_weight = qkv_weight[:, :width], qkv_weight[:, width:]
    query_bias, pair_bias = qkv_bias[:width], qkv_bias[width:]
    query = (dot(normed, query_weight) + query_bias).astype(BF16)
    core = over_splits(dot(squeeze, normed)).astype(BF16)
    total = over_splits(jnp.sum(squeeze.astype(F32), axis=1))
    pair = (dot(core, pair_weight) + total[:, None] * pair_bias).astype(BF16)

    factor = 1.0 / math.sqrt(HD)
    query_heads = query.reshape(rows, H, HD)
    key_heads = pair[:, :width].reshape(-1, H, HD)
    value_heads = pair[:, width:].reshape(-1, H, HD)
    scores = (
        jnp.einsum("thd,jhd->htj", query_heads, key_heads, preferred_element_type=F32) * factor
    )
    expo = jnp.exp(scores - jnp.max(scores, axis=-1, keepdims=True))
    weights = expo / jnp.sum(expo, axis=-1, keepdims=True)
    weights_low = weights.astype(BF16)
    mixed = (
        jnp.einsum("htj,jhd->thd", weights_low, value_heads, preferred_element_type=F32)
        .reshape(rows, width)
        .astype(BF16)
    )
    middle = states + dot(mixed, out_weight) + out_bias
    hat_second, rate_second = norm_stats(middle)
    second = (hat_second * second_gain + second_bias).astype(BF16)
    hidden = dot(second, up_weight) + up_bias
    active, gelu_back = jax.vjp(functools.partial(jax.nn.gelu, approximate=True), hidden)
    active_low = active.astype(BF16)
    result = middle + dot(active_low, down_weight) + down_bias
    output = spread_rows(jnp.where(alive, result, 0.0).astype(BF16))

    incoming_full = incoming.astype(F32)
    down_grad = t_dot(active_low, incoming)
    down_bias_grad = jnp.sum(incoming_full, axis=0)
    hidden_low = gelu_back(dot_t(incoming, down_weight))[0].astype(BF16)
    up_grad = t_dot(second, hidden_low)
    up_bias_grad = jnp.sum(hidden_low.astype(F32), axis=0)
    second_up = dot_t(hidden_low, up_weight)
    second_gain_grad = jnp.sum(second_up * hat_second, axis=0)
    second_bias_grad = jnp.sum(second_up, axis=0)
    middle_grad = incoming_full + norm_back(hat_second, rate_second, second_up, second_gain)
    branch_low = middle_grad.astype(BF16)
    out_grad = t_dot(mixed, branch_low)
    out_bias_grad = jnp.sum(branch_low.astype(F32), axis=0)
    mixed_grad = dot_t(branch_low, out_weight).astype(BF16).reshape(rows, H, HD)

    weight_grad = jnp.einsum("thd,jhd->htj", mixed_grad, value_heads, preferred_element_type=F32)
    inner = jnp.sum(weights * weight_grad, axis=-1, keepdims=True)
    score_low = (weights * (weight_grad - inner)).astype(BF16)
    value_back = jnp.einsum("htj,thd->jhd", weights_low, mixed_grad, preferred_element_type=F32)
    key_back = (
        jnp.einsum("htj,thd->jhd", score_low, query_heads, preferred_element_type=F32) * factor
    )
    query_back = (
        jnp.einsum("htj,jhd->thd", score_low, key_heads, preferred_element_type=F32) * factor
    )
    pair_back = jnp.concatenate(
        [key_back.reshape(-1, width), value_back.reshape(-1, width)], axis=1
    )
    pair_back_low = pair_back.astype(BF16)
    query_back_low = query_back.reshape(rows, width).astype(BF16)
    core_back = over_splits(dot_t(pair_back_low, pair_weight)).astype(BF16)
    lift = over_splits(jnp.sum(pair_back * pair_bias, axis=1))
    query_weight_grad = t_dot(normed, query_back_low)
    pair_weight_grad = t_dot(core, pair_back_low)
    qkv_grad = jnp.concatenate([query_weight_grad, pair_weight_grad], axis=1)
    qkv_bias_grad = jnp.concatenate(
        [
            jnp.sum(query_back_low.astype(F32), axis=0),
            jnp.sum(total[:, None] * pair_back, axis=0),
        ]
    )
    first_up = dot_t(query_back_low, query_weight) + t_dot(squeeze, core_back)
    first_gain_grad = jnp.sum(first_up * hat_first, axis=0)
    first_bias_grad = jnp.sum(first_up, axis=0)
    input_grad = spread_rows(
        (middle_grad + norm_back(hat_first, rate_first, first_up, first_gain)).astype(BF16)
    )
    compress_terms = (
        jnp.einsum(
            "jc,btc->bjt",
            core_back,
            normed.reshape(slots, tokens, width),
            preferred_element_type=F32,
        )
        + lift[None, :, None]
    )

    low_first = [1 << i for i in range(nk.bit_length() - 1)]
    high_first = low_first[::-1]
    team_low = [1 << i for i in range(slots.bit_length() - 1)]

    def matrix(grad):
        blocks = grad.reshape(nk, grad.shape[0] // nk, grad.shape[1])
        return scatter_sum(blocks, high_first, low_first, nb, nk)

    down_rows = matrix(down_grad)
    up_rows = matrix(up_grad)
    out_rows = matrix(out_grad)
    qkv_rows = matrix(qkv_grad)
    compress_rows = scatter_sum(compress_terms, team_low[::-1], team_low, nb, nk)
    vectors = (
        first_gain_grad,
        first_bias_grad,
        qkv_bias_grad,
        out_bias_grad,
        second_gain_grad,
        second_bias_grad,
        up_bias_grad,
        down_bias_grad,
    )
    packed = jnp.concatenate([v.reshape(nk, -1) for v in vectors], axis=1)
    packed = lax.psum(packed, ("batch", "blk"))
    mine = lax.dynamic_index_in_dim(packed, lax.axis_index("blk"), 0, keepdims=False)
    pieces = []
    start = 0
    for v in vectors:
        size = v.shape[0] // nk
        pieces.append(mine[start : start + size])
        start += size
    (fg, fb, qb, ob, sg, sb, ub, db) = pieces
    return (
        output,
        input_grad,
        fg,
        fb,
        qkv_rows,
        qb,
        out_rows,
        ob,
        sg,
        sb,
        up_rows,
        ub,
        down_rows,
        db,
        compress_rows,
    )


def solution(mesh):
    rows = P("batch", "blk", None)
    placed = (rows, rows) + (P(),) * 13 + (P(None, "blk"),)
    vec, mat = P("blk"), P("blk", None)
    return jax.shard_map(
        functools.partial(body, nb=mesh.shape["batch"], nk=mesh.shape["blk"]),
        mesh=mesh,
        in_specs=placed,
        out_specs=(rows, rows, vec, vec, mat, vec, mat, vec, vec, vec, mat, vec, mat, vec, P(None, "blk")),
        check_vma=False,
    )
```

```python
import functools
import math

import jax
import jax.numpy as jnp
from jax import lax
from jax.experimental import pallas as pl
from jax.experimental.pallas import tpu as pltpu
from jax.sharding import PartitionSpec as P

F32 = jnp.float32
BF16 = jnp.bfloat16
HD = 64
LANES = 256
GELU_A = math.sqrt(2.0 / math.pi)
GELU_B = 0.044715


def norm_stats(states):
    center = states - jnp.mean(states, axis=-1, keepdims=True)
    spread = jnp.mean(center * center, axis=-1, keepdims=True)
    rate = lax.rsqrt(spread + 1e-05)
    return center * rate, rate


def norm_back(hat, rate, upstream, gain):
    scaled = upstream * gain
    return rate * (
        scaled
        - jnp.mean(scaled, axis=-1, keepdims=True)
        - hat * jnp.mean(scaled * hat, axis=-1, keepdims=True)
    )


def contract(a, b, dim_a, dim_b):
    return lax.dot_general(a, b, (((dim_a,), (dim_b,)), ((), ())), preferred_element_type=F32)


def whole(shape):
    return pl.BlockSpec(shape, lambda *_: (0,) * len(shape), pipeline_mode=pl.Buffered(1))


def columns(height, start, width=LANES):
    return pl.BlockSpec((height, width), lambda i: (0, start + i))


def below(width, start, height=LANES):
    return pl.BlockSpec((height, width), lambda i: (start + i, 0))


PARAMS = dict(vmem_limit_bytes=62 << 20, dimension_semantics=("arbitrary",))


def by_head(values):
    lane = lax.broadcasted_iota(jnp.int32, values.shape, 1) // HD
    zero = jnp.zeros_like(values)
    return jnp.concatenate([jnp.where(lane == h, values, zero) for h in range(LANES // HD)], axis=0)


def own_head(values):
    n = values.shape[0] // (LANES // HD)
    lane = lax.broadcasted_iota(jnp.int32, (n, LANES), 1) // HD
    picked = values[:n]
    for h in range(1, LANES // HD):
        picked = jnp.where(lane == h, values[h * n : (h + 1) * n], picked)
    return picked


def attend_kernel(tile, normed, core, total, wq, wk, wv, bq, bk, bv, query, key, value, weights, mixed):
    rows, n = normed.shape[0], core.shape[0]
    key[...] = (contract(core[...], wk[...], 1, 0) + total[...] * bk[...]).astype(BF16)
    value[...] = (contract(core[...], wv[...], 1, 0) + total[...] * bv[...]).astype(BF16)
    keys = by_head(key[...] * jnp.asarray(1.0 / math.sqrt(HD), BF16))
    values = by_head(value[...])

    for r in range(rows // tile):
        at = slice(r * tile, (r + 1) * tile)
        q = (contract(normed[at, :], wq[...], 1, 0) + bq[...]).astype(BF16)
        query[at, :] = q
        scores = contract(q, keys, 1, 1)
        heads = []
        for h in range(LANES // HD):
            s = scores[:, h * n : (h + 1) * n]
            e = jnp.exp(s - jnp.max(s, axis=-1, keepdims=True))
            heads.append((e * (1.0 / jnp.sum(e, axis=-1, keepdims=True))).astype(BF16))
        low = jnp.concatenate(heads, axis=1)
        weights[0, at, :] = low
        mixed[at, :] = contract(low, values, 1, 0).astype(BF16)


def attend(normed, core, total, qkv_weight, qkv_bias, tile=1024):
    rows, width = normed.shape
    n = core.shape[0]
    steps = width // LANES
    heads = LANES // HD
    return pl.pallas_call(
        functools.partial(attend_kernel, tile),
        grid=(steps,),
        in_specs=[whole((rows, width)), whole((n, width)), whole((n, 1))]
        + [columns(width, k * steps) for k in range(3)]
        + [columns(1, k * steps) for k in range(3)],
        out_specs=[
            columns(rows, 0),
            columns(n, 0),
            columns(n, 0),
            pl.BlockSpec((1, rows, heads * n), lambda i: (i, 0, 0)),
            columns(rows, 0),
        ],
        out_shape=[
            jax.ShapeDtypeStruct((rows, width), BF16),
            jax.ShapeDtypeStruct((n, width), BF16),
            jax.ShapeDtypeStruct((n, width), BF16),
            jax.ShapeDtypeStruct((steps, rows, heads * n), BF16),
            jax.ShapeDtypeStruct((rows, width), BF16),
        ],
        compiler_params=pltpu.CompilerParams(**PARAMS),
        name="attend",
    )(normed, core, total, qkv_weight, qkv_weight, qkv_weight, qkv_bias, qkv_bias, qkv_bias)


def forward_kernel(tile, alive, mixed, states, ow, ob, gain, bias, upw, upb, dnw, dnb,
                   middle, second, active, slope, output, total):
    f = pl.program_id(0)
    rows = mixed.shape[0]

    @pl.when(f == 0)
    def _():
        mid = states[...].astype(F32) + contract(mixed[...], ow[...], 1, 0) + ob[...]
        middle[...] = mid
        second[...] = (norm_stats(mid)[0] * gain[...] + bias[...]).astype(BF16)
        total[...] = mid + dnb[...]

    for r in range(rows // tile):
        at = slice(r * tile, (r + 1) * tile)
        v = contract(second[at, :], upw[...], 1, 0) + upb[...]
        square = v * v
        t = jnp.tanh(v * (GELU_A + (GELU_A * GELU_B) * square))
        half = 0.5 + 0.5 * t
        act = (v * half).astype(BF16)
        active[at, :] = act
        slope[at, :] = (
            half + (0.5 * v) * (1.0 - t * t) * (GELU_A + (3 * GELU_A * GELU_B) * square)
        ).astype(BF16)
        total[at, :] += contract(act, dnw[...], 1, 0)

    @pl.when(f == pl.num_programs(0) - 1)
    def _():
        output[...] = jnp.where(alive[0] > 0, total[...], 0.0).astype(BF16)


def forward(alive, mixed, states, ow, ob, gain, bias, upw, upb, dnw, dnb, block=512, tile=1024):
    rows, width = mixed.shape
    hidden = upw.shape[1]
    vec = whole((1, width))
    return pl.pallas_call(
        functools.partial(forward_kernel, tile),
        grid=(hidden // block,),
        in_specs=[
            pl.BlockSpec(memory_space=pltpu.SMEM),
            whole((rows, width)),
            whole((rows, width)),
            whole((width, width)),
            vec,
            vec,
            vec,
            columns(width, 0, block),
            columns(1, 0, block),
            below(width, 0, block),
            vec,
        ],
        out_specs=[
            whole((rows, width)),
            whole((rows, width)),
            columns(rows, 0, block),
            columns(rows, 0, block),
            whole((rows, width)),
        ],
        out_shape=[
            jax.ShapeDtypeStruct((rows, width), F32),
            jax.ShapeDtypeStruct((rows, width), BF16),
            jax.ShapeDtypeStruct((rows, hidden), BF16),
            jax.ShapeDtypeStruct((rows, hidden), BF16),
            jax.ShapeDtypeStruct((rows, width), BF16),
        ],
        scratch_shapes=[pltpu.VMEM((rows, width), F32)],
        compiler_params=pltpu.CompilerParams(**PARAMS),
        name="forward",
    )(alive, mixed, states, ow, ob, gain, bias, upw, upb, dnw, dnb)


def backward_kernel(alive, cot, active, slope, second, middle, mixed, upw, dnw, ow, gain,
                    up_grad, down_grad, up_bias_grad, middle_grad, mixed_grad, out_grad, sums,
                    incoming, total):
    f = pl.program_id(0)

    @pl.when(f == 0)
    def _():
        incoming[...] = jnp.where(alive[0] > 0, cot[...], jnp.zeros_like(cot))
        total[...] = jnp.zeros_like(total)

    d = contract(incoming[...], dnw[...], 1, 1)
    dh = (d * slope[...].astype(F32)).astype(BF16)
    up_bias_grad[...] = jnp.sum(dh.astype(F32), axis=0, keepdims=True)
    total[...] += contract(dh, upw[...], 1, 1)
    down_grad[...] = contract(active[...], incoming[...], 0, 0).astype(BF16)
    up_grad[...] = contract(second[...], dh, 0, 0).astype(BF16)

    @pl.when(f == pl.num_programs(0) - 1)
    def _():
        hat, rate = norm_stats(middle[...])
        up = total[...]
        inc = incoming[...].astype(F32)
        grad = inc + norm_back(hat, rate, up, gain[...])
        middle_grad[...] = grad
        branch = grad.astype(BF16)
        mixed_grad[...] = contract(branch, ow[...], 1, 1).astype(BF16)
        out_grad[...] = contract(mixed[...], branch, 0, 0).astype(BF16)
        sums[0:1, :] = jnp.sum(branch.astype(F32), axis=0, keepdims=True)
        sums[1:2, :] = jnp.sum(up * hat, axis=0, keepdims=True)
        sums[2:3, :] = jnp.sum(up, axis=0, keepdims=True)
        sums[3:4, :] = jnp.sum(inc, axis=0, keepdims=True)


def backward(alive, cot, active, slope, second, middle, mixed, upw, dnw, ow, gain, block=512):
    rows, width = mixed.shape
    hidden = upw.shape[1]
    return pl.pallas_call(
        backward_kernel,
        grid=(hidden // block,),
        in_specs=[
            pl.BlockSpec(memory_space=pltpu.SMEM),
            whole((rows, width)),
            columns(rows, 0, block),
            columns(rows, 0, block),
            whole((rows, width)),
            whole((rows, width)),
            whole((rows, width)),
            columns(width, 0, block),
            below(width, 0, block),
            whole((width, width)),
            whole((1, width)),
        ],
        out_specs=[
            columns(width, 0, block),
            below(width, 0, block),
            columns(1, 0, block),
            whole((rows, width)),
            whole((rows, width)),
            whole((width, width)),
            whole((4, width)),
        ],
        out_shape=[
            jax.ShapeDtypeStruct((width, hidden), BF16),
            jax.ShapeDtypeStruct((hidden, width), BF16),
            jax.ShapeDtypeStruct((1, hidden), F32),
            jax.ShapeDtypeStruct((rows, width), F32),
            jax.ShapeDtypeStruct((rows, width), BF16),
            jax.ShapeDtypeStruct((width, width), BF16),
            jax.ShapeDtypeStruct((4, width), F32),
        ],
        scratch_shapes=[pltpu.VMEM((rows, width), BF16), pltpu.VMEM((rows, width), F32)],
        compiler_params=pltpu.CompilerParams(**PARAMS),
        name="backward",
    )(alive, cot, active, slope, second, middle, mixed, upw, dnw, ow, gain)


def attend_back_kernel(mixed_grad, weights, query, key, value, normed, core, total, wq, wk, wv, bk, bv,
                       query_grad, key_grad, value_grad, qb, kb, vb, up, core_grad, lift):
    i = pl.program_id(0)
    n = core.shape[0]

    @pl.when(i == 0)
    def _():
        up[...] = jnp.zeros_like(up)
        core_grad[...] = jnp.zeros_like(core_grad)
        lift[...] = jnp.zeros_like(lift)

    keys = by_head(key[...] * jnp.asarray(1.0 / math.sqrt(HD), BF16))
    values = by_head(value[...])
    grads = mixed_grad[...]
    back = contract(grads, values, 1, 1)
    heads = []
    for h in range(LANES // HD):
        p = weights[0, :, h * n : (h + 1) * n].astype(F32)
        g = back[:, h * n : (h + 1) * n]
        heads.append((p * (g - jnp.sum(p * g, axis=-1, keepdims=True))).astype(BF16))
    score = jnp.concatenate(heads, axis=1)
    dv = own_head(contract(weights[0], grads, 0, 0))
    dk = own_head(contract(score, query[...], 0, 0)) * (1.0 / math.sqrt(HD))
    dq = contract(score, keys, 1, 0).astype(BF16)
    dk_low, dv_low = dk.astype(BF16), dv.astype(BF16)
    up[...] += contract(dq, wq[...], 1, 1)
    core_grad[...] += contract(dk_low, wk[...], 1, 1) + contract(dv_low, wv[...], 1, 1)
    lift[...] += jnp.sum(dk * bk[...] + dv * bv[...], axis=1, keepdims=True)
    query_grad[...] = contract(normed[...], dq, 0, 0).astype(BF16)
    key_grad[...] = contract(core[...], dk_low, 0, 0).astype(BF16)
    value_grad[...] = contract(core[...], dv_low, 0, 0).astype(BF16)
    qb[...] = jnp.sum(dq.astype(F32), axis=0, keepdims=True)
    kb[...] = jnp.sum(total[...] * dk, axis=0, keepdims=True)
    vb[...] = jnp.sum(total[...] * dv, axis=0, keepdims=True)


def attend_back(mixed_grad, weights, query, key, value, normed, core, total, qkv_weight, qkv_bias):
    rows, width = normed.shape
    n = core.shape[0]
    steps = width // LANES
    heads = LANES // HD
    return pl.pallas_call(
        attend_back_kernel,
        grid=(steps,),
        in_specs=[
            columns(rows, 0),
            pl.BlockSpec((1, rows, heads * n), lambda i: (i, 0, 0)),
            columns(rows, 0),
            columns(n, 0),
            columns(n, 0),
            whole((rows, width)),
            whole((n, width)),
            whole((n, 1)),
        ]
        + [columns(width, k * steps) for k in range(3)]
        + [columns(1, k * steps) for k in range(1, 3)],
        out_specs=[columns(width, 0)] * 3
        + [columns(1, 0)] * 3
        + [whole((rows, width)), whole((n, width)), whole((n, 1))],
        out_shape=[jax.ShapeDtypeStruct((width, width), BF16)] * 3
        + [jax.ShapeDtypeStruct((1, width), F32)] * 3
        + [
            jax.ShapeDtypeStruct((rows, width), F32),
            jax.ShapeDtypeStruct((n, width), F32),
            jax.ShapeDtypeStruct((n, 1), F32),
        ],
        compiler_params=pltpu.CompilerParams(**PARAMS),
        name="attend_back",
    )(mixed_grad, weights, query, key, value, normed, core, total, qkv_weight, qkv_weight, qkv_weight, qkv_bias, qkv_bias)


def swap(values, axis, size, bit):
    return lax.ppermute(values, axis, [(i, i ^ bit) for i in range(size)])


def halve(values, dim, axis, size, bit):
    mine = (lax.axis_index(axis) // bit) % 2
    send = lax.dynamic_index_in_dim(values, 1 - mine, dim, keepdims=False).astype(BF16)
    keep = lax.dynamic_index_in_dim(values, mine, dim, keepdims=False)
    return keep.astype(F32) + swap(send, axis, size, bit).astype(F32)


def join(values, dim, axis, size, bit):
    mine = (lax.axis_index(axis) // bit) % 2
    other = swap(values, axis, size, bit)
    first = jnp.where(mine == 0, values, other)
    second = jnp.where(mine == 0, other, values)
    return jnp.concatenate([first, second], axis=dim)


def scatter_sum(terms, bits, order, nb, nk, early):
    _, rows, cols = terms.shape
    values = halve(terms.reshape(-1, 2, rows // 2, cols), 1, "batch", nb, 1)
    chips = [1 << i for i in range(1, nb.bit_length() - 1)]
    if early:
        for bit in chips:
            cols //= 2
            values = halve(values.reshape(-1, rows // 2, 2, cols), 2, "batch", nb, bit)
    left = list(bits)
    for bit in order:
        place = left.index(bit)
        values = values.reshape(1 << place, 2, -1, rows // 2, cols)
        values = halve(values, 1, "blk", nk, bit)
        left.remove(bit)
    values = values.reshape(rows // 2, cols).astype(BF16)
    for bit in reversed(chips) if early else chips:
        if early:
            values = join(values, 1, "batch", nb, bit)
        else:
            values = (values.astype(F32) + swap(values, "batch", nb, bit).astype(F32)).astype(BF16)
    return join(values, 0, "batch", nb, 1).astype(F32)


def body(
    inputs,
    cotangent,
    group_counts,
    first_gain,
    first_bias,
    qkv_weight,
    qkv_bias,
    out_weight,
    out_bias,
    second_gain,
    second_bias,
    up_weight,
    up_bias,
    down_weight,
    down_bias,
    compress,
    *,
    nb,
    nk,
):
    slots, tokens, width = inputs.shape
    splits = nk // slots
    teams = [[t * slots + i for i in range(slots)] for t in range(splits)]
    across = [[t * slots + i for t in range(splits)] for i in range(slots)]
    rows = slots * tokens
    low_first = [1 << i for i in range(nk.bit_length() - 1)]
    high_first = low_first[::-1]
    team_low = [1 << i for i in range(slots.bit_length() - 1)]

    def gather_rows(values):
        return lax.all_to_all(values, "blk", 0, 0, axis_index_groups=teams, tiled=True).reshape(
            rows, width
        )

    def spread_rows(values):
        return lax.all_to_all(
            values.reshape(slots, tokens, width), "blk", 0, 0, axis_index_groups=teams, tiled=True
        )

    def over_splits(values):
        if splits == 1:
            return values
        return lax.psum(values, "blk", axis_index_groups=across)

    def line(vector):
        return vector.reshape(1, -1)

    slot = lax.axis_index("blk") % slots
    alive = (slot < group_counts[lax.axis_index("batch")]).astype(jnp.int32).reshape(1)

    gathered = compress[None]
    for bit in team_low[::-1]:
        gathered = join(gathered[:, None], 1, "blk", nk, bit)
        gathered = gathered.reshape((-1,) + compress.shape)
    squeeze = gathered.transpose(1, 0, 2).reshape(compress.shape[0], rows)

    low_x = gather_rows(inputs)
    low_cot = gather_rows(cotangent)

    states = low_x.astype(F32)
    hat_first, rate_first = norm_stats(states)
    normed = (hat_first * first_gain + first_bias).astype(BF16)
    core = over_splits(contract(squeeze, normed, 1, 0)).astype(BF16)
    total = over_splits(jnp.sum(squeeze.astype(F32), axis=1, keepdims=True))
    query, key, value, weights, mixed = attend(
        normed, core, total, qkv_weight, line(qkv_bias), tile=512
    )
    middle, second, active, slope, result = forward(
        alive,
        mixed,
        low_x,
        out_weight,
        line(out_bias),
        line(second_gain),
        line(second_bias),
        up_weight,
        line(up_bias),
        down_weight,
        line(down_bias),
    )
    output = spread_rows(result)
    up_grad, down_grad, up_bias_grad, middle_grad, mixed_grad, out_grad, sums = backward(
        alive,
        low_cot,
        active,
        slope,
        second,
        middle,
        mixed,
        up_weight,
        down_weight,
        out_weight,
        line(second_gain),
    )
    out_bias_grad, second_gain_grad, second_bias_grad, down_bias_grad = (sums[i] for i in range(4))
    (
        query_weight_grad,
        key_weight_grad,
        value_weight_grad,
        query_bias_grad,
        key_bias_grad,
        value_bias_grad,
        query_up,
        core_back,
        lift,
    ) = attend_back(
        mixed_grad, weights, query, key, value, normed, core, total, qkv_weight, line(qkv_bias)
    )
    core_back = over_splits(core_back).astype(BF16)
    lift = over_splits(lift)
    first_up = query_up + contract(squeeze, core_back, 0, 0)
    first_gain_grad = jnp.sum(first_up * hat_first, axis=0)
    first_bias_grad = jnp.sum(first_up, axis=0)
    input_grad = spread_rows(
        (middle_grad + norm_back(hat_first, rate_first, first_up, first_gain)).astype(BF16)
    )
    compress_terms = (
        jnp.einsum(
            "jc,btc->bjt",
            core_back,
            normed.reshape(slots, tokens, width),
            preferred_element_type=F32,
        )
        + lift[None]
    )

    def matrix(grad, early):
        blocks = grad.reshape(nk, grad.shape[0] // nk, grad.shape[1])
        return scatter_sum(blocks, high_first, low_first, nb, nk, early)

    down_rows = matrix(down_grad, False)
    up_rows = matrix(up_grad, True)
    qkv_out = jnp.concatenate(
        [query_weight_grad, key_weight_grad, value_weight_grad, out_grad], axis=1
    )
    qkv_out_rows = matrix(qkv_out, True)
    compress_rows = scatter_sum(compress_terms, team_low[::-1], team_low, nb, nk, False)
    vectors = (
        first_gain_grad,
        first_bias_grad,
        jnp.concatenate([query_bias_grad, key_bias_grad, value_bias_grad], axis=1),
        out_bias_grad,
        second_gain_grad,
        second_bias_grad,
        up_bias_grad,
        down_bias_grad,
    )
    sizes = [v.size // nk for v in vectors]
    packed = jnp.concatenate([v.reshape(nk, -1) for v in vectors], axis=1)
    tall = 32
    wide = -(-sum(sizes) // (tall * 128)) * 128
    packed = jnp.pad(packed, ((0, 0), (0, tall * wide - sum(sizes)))).reshape(nk, tall, wide)
    mine = scatter_sum(packed, high_first, low_first, nb, nk, False).reshape(-1)
    parts = []
    start = 0
    for size in sizes:
        parts.append(mine[start : start + size])
        start += size
    fg, fb, qb, ob, sg, sb, ub, db = parts
    third = qkv_weight.shape[1]
    return (
        output,
        input_grad,
        fg,
        fb,
        qkv_out_rows[:, :third],
        qb,
        qkv_out_rows[:, third:],
        ob,
        sg,
        sb,
        up_rows,
        ub,
        down_rows,
        db,
        compress_rows,
    )


def solution(mesh):
    rows = P("batch", "blk", None)
    placed = (rows, rows) + (P(),) * 13 + (P(None, "blk"),)
    vec, mat = P("blk"), P("blk", None)
    return jax.shard_map(
        functools.partial(body, nb=mesh.shape["batch"], nk=mesh.shape["blk"]),
        mesh=mesh,
        in_specs=placed,
        out_specs=(rows, rows, vec, vec, mat, vec, mat, vec, vec, vec, mat, vec, mat, vec)
        + (P(None, "blk"),),
        check_vma=False,
    )
```

```python
import functools
import math

import jax
import jax.numpy as jnp
from jax import lax
from jax.experimental import pallas as pl
from jax.experimental.pallas import tpu as pltpu
from jax.sharding import PartitionSpec as P

F32 = jnp.float32
BF16 = jnp.bfloat16
HD = 64
LANES = 256
GELU_A = math.sqrt(2.0 / math.pi)
GELU_B = 0.044715


def norm_stats(states):
    center = states - jnp.mean(states, axis=-1, keepdims=True)
    spread = jnp.mean(center * center, axis=-1, keepdims=True)
    rate = lax.rsqrt(spread + 1e-05)
    return center * rate, rate


def norm_back(hat, rate, upstream, gain):
    scaled = upstream * gain
    return rate * (
        scaled
        - jnp.mean(scaled, axis=-1, keepdims=True)
        - hat * jnp.mean(scaled * hat, axis=-1, keepdims=True)
    )


def contract(a, b, dim_a, dim_b):
    return lax.dot_general(a, b, (((dim_a,), (dim_b,)), ((), ())), preferred_element_type=F32)


def whole(shape):
    return pl.BlockSpec(shape, lambda *_: (0,) * len(shape), pipeline_mode=pl.Buffered(1))


def columns(height, start, width=LANES):
    return pl.BlockSpec((height, width), lambda i: (0, start + i))


def below(width, start, height=LANES):
    return pl.BlockSpec((height, width), lambda i: (start + i, 0))


PARAMS = dict(vmem_limit_bytes=62 << 20, dimension_semantics=("arbitrary",))


def by_head(values):
    lane = lax.broadcasted_iota(jnp.int32, values.shape, 1) // HD
    zero = jnp.zeros_like(values)
    return jnp.concatenate([jnp.where(lane == h, values, zero) for h in range(LANES // HD)], axis=0)


def own_head(values):
    n = values.shape[0] // (LANES // HD)
    lane = lax.broadcasted_iota(jnp.int32, (n, LANES), 1) // HD
    picked = values[:n]
    for h in range(1, LANES // HD):
        picked = jnp.where(lane == h, values[h * n : (h + 1) * n], picked)
    return picked


def attend_kernel(tile, normed, core, total, wq, wk, wv, bq, bk, bv, query, key, value, weights, mixed):
    rows, n = normed.shape[0], core.shape[0]
    key[...] = (contract(core[...], wk[...], 1, 0) + total[...] * bk[...]).astype(BF16)
    value[...] = (contract(core[...], wv[...], 1, 0) + total[...] * bv[...]).astype(BF16)
    keys = by_head(key[...] * jnp.asarray(1.0 / math.sqrt(HD), BF16))
    values = by_head(value[...])

    for r in range(rows // tile):
        at = slice(r * tile, (r + 1) * tile)
        q = (contract(normed[at, :], wq[...], 1, 0) + bq[...]).astype(BF16)
        query[at, :] = q
        scores = contract(q, keys, 1, 1)
        heads = []
        for h in range(LANES // HD):
            s = scores[:, h * n : (h + 1) * n]
            e = jnp.exp(s - jnp.max(s, axis=-1, keepdims=True))
            heads.append((e * (1.0 / jnp.sum(e, axis=-1, keepdims=True))).astype(BF16))
        low = jnp.concatenate(heads, axis=1)
        weights[0, at, :] = low
        mixed[at, :] = contract(low, values, 1, 0).astype(BF16)


def attend(normed, core, total, qkv_weight, qkv_bias, tile=1024):
    rows, width = normed.shape
    n = core.shape[0]
    steps = width // LANES
    heads = LANES // HD
    return pl.pallas_call(
        functools.partial(attend_kernel, tile),
        grid=(steps,),
        in_specs=[whole((rows, width)), whole((n, width)), whole((n, 1))]
        + [columns(width, k * steps) for k in range(3)]
        + [columns(1, k * steps) for k in range(3)],
        out_specs=[
            columns(rows, 0),
            columns(n, 0),
            columns(n, 0),
            pl.BlockSpec((1, rows, heads * n), lambda i: (i, 0, 0)),
            columns(rows, 0),
        ],
        out_shape=[
            jax.ShapeDtypeStruct((rows, width), BF16),
            jax.ShapeDtypeStruct((n, width), BF16),
            jax.ShapeDtypeStruct((n, width), BF16),
            jax.ShapeDtypeStruct((steps, rows, heads * n), BF16),
            jax.ShapeDtypeStruct((rows, width), BF16),
        ],
        compiler_params=pltpu.CompilerParams(**PARAMS),
        name="attend",
    )(normed, core, total, qkv_weight, qkv_weight, qkv_weight, qkv_bias, qkv_bias, qkv_bias)


def forward_kernel(tile, alive, mixed, states, ow, ob, gain, bias, upw, upb, dnw, dnb,
                   middle, second, active, slope, output, total):
    f = pl.program_id(0)
    rows = mixed.shape[0]

    @pl.when(f == 0)
    def _():
        mid = states[...].astype(F32) + contract(mixed[...], ow[...], 1, 0) + ob[...]
        middle[...] = mid
        second[...] = (norm_stats(mid)[0] * gain[...] + bias[...]).astype(BF16)
        total[...] = mid + dnb[...]

    for r in range(rows // tile):
        at = slice(r * tile, (r + 1) * tile)
        v = contract(second[at, :], upw[...], 1, 0) + upb[...]
        square = v * v
        t = jnp.tanh(v * (GELU_A + (GELU_A * GELU_B) * square))
        half = 0.5 + 0.5 * t
        act = (v * half).astype(BF16)
        active[at, :] = act
        slope[at, :] = (
            half + (0.5 * v) * (1.0 - t * t) * (GELU_A + (3 * GELU_A * GELU_B) * square)
        ).astype(BF16)
        total[at, :] += contract(act, dnw[...], 1, 0)

    @pl.when(f == pl.num_programs(0) - 1)
    def _():
        output[...] = jnp.where(alive[0] > 0, total[...], 0.0).astype(BF16)


def forward(alive, mixed, states, ow, ob, gain, bias, upw, upb, dnw, dnb, block=512, tile=1024):
    rows, width = mixed.shape
    hidden = upw.shape[1]
    vec = whole((1, width))
    return pl.pallas_call(
        functools.partial(forward_kernel, tile),
        grid=(hidden // block,),
        in_specs=[
            pl.BlockSpec(memory_space=pltpu.SMEM),
            whole((rows, width)),
            whole((rows, width)),
            whole((width, width)),
            vec,
            vec,
            vec,
            columns(width, 0, block),
            columns(1, 0, block),
            below(width, 0, block),
            vec,
        ],
        out_specs=[
            whole((rows, width)),
            whole((rows, width)),
            columns(rows, 0, block),
            columns(rows, 0, block),
            whole((rows, width)),
        ],
        out_shape=[
            jax.ShapeDtypeStruct((rows, width), F32),
            jax.ShapeDtypeStruct((rows, width), BF16),
            jax.ShapeDtypeStruct((rows, hidden), BF16),
            jax.ShapeDtypeStruct((rows, hidden), BF16),
            jax.ShapeDtypeStruct((rows, width), BF16),
        ],
        scratch_shapes=[pltpu.VMEM((rows, width), F32)],
        compiler_params=pltpu.CompilerParams(**PARAMS),
        name="forward",
    )(alive, mixed, states, ow, ob, gain, bias, upw, upb, dnw, dnb)


def backward_kernel(alive, cot, active, slope, second, middle, mixed, upw, dnw, ow, gain,
                    up_grad, down_grad, up_bias_grad, middle_grad, mixed_grad, out_grad, sums,
                    incoming, total):
    f = pl.program_id(0)

    @pl.when(f == 0)
    def _():
        incoming[...] = jnp.where(alive[0] > 0, cot[...], jnp.zeros_like(cot))
        total[...] = jnp.zeros_like(total)

    d = contract(incoming[...], dnw[...], 1, 1)
    dh = (d * slope[...].astype(F32)).astype(BF16)
    up_bias_grad[...] = jnp.sum(dh.astype(F32), axis=0, keepdims=True)
    total[...] += contract(dh, upw[...], 1, 1)
    down_grad[...] = contract(active[...], incoming[...], 0, 0).astype(BF16)
    up_grad[...] = contract(second[...], dh, 0, 0).astype(BF16)

    @pl.when(f == pl.num_programs(0) - 1)
    def _():
        hat, rate = norm_stats(middle[...])
        up = total[...]
        inc = incoming[...].astype(F32)
        grad = inc + norm_back(hat, rate, up, gain[...])
        middle_grad[...] = grad
        branch = grad.astype(BF16)
        mixed_grad[...] = contract(branch, ow[...], 1, 1).astype(BF16)
        out_grad[...] = contract(mixed[...], branch, 0, 0).astype(BF16)
        sums[0:1, :] = jnp.sum(branch.astype(F32), axis=0, keepdims=True)
        sums[1:2, :] = jnp.sum(up * hat, axis=0, keepdims=True)
        sums[2:3, :] = jnp.sum(up, axis=0, keepdims=True)
        sums[3:4, :] = jnp.sum(inc, axis=0, keepdims=True)


def backward(alive, cot, active, slope, second, middle, mixed, upw, dnw, ow, gain, block=512):
    rows, width = mixed.shape
    hidden = upw.shape[1]
    return pl.pallas_call(
        backward_kernel,
        grid=(hidden // block,),
        in_specs=[
            pl.BlockSpec(memory_space=pltpu.SMEM),
            whole((rows, width)),
            columns(rows, 0, block),
            columns(rows, 0, block),
            whole((rows, width)),
            whole((rows, width)),
            whole((rows, width)),
            columns(width, 0, block),
            below(width, 0, block),
            whole((width, width)),
            whole((1, width)),
        ],
        out_specs=[
            columns(width, 0, block),
            below(width, 0, block),
            columns(1, 0, block),
            whole((rows, width)),
            whole((rows, width)),
            whole((width, width)),
            whole((4, width)),
        ],
        out_shape=[
            jax.ShapeDtypeStruct((width, hidden), BF16),
            jax.ShapeDtypeStruct((hidden, width), BF16),
            jax.ShapeDtypeStruct((1, hidden), F32),
            jax.ShapeDtypeStruct((rows, width), F32),
            jax.ShapeDtypeStruct((rows, width), BF16),
            jax.ShapeDtypeStruct((width, width), BF16),
            jax.ShapeDtypeStruct((4, width), F32),
        ],
        scratch_shapes=[pltpu.VMEM((rows, width), BF16), pltpu.VMEM((rows, width), F32)],
        compiler_params=pltpu.CompilerParams(**PARAMS),
        name="backward",
    )(alive, cot, active, slope, second, middle, mixed, upw, dnw, ow, gain)


def attend_back_kernel(mixed_grad, weights, query, key, value, normed, core, total, wq, wk, wv, bk, bv,
                       query_grad, key_grad, value_grad, qb, kb, vb, up, core_grad, lift):
    i = pl.program_id(0)
    n = core.shape[0]

    @pl.when(i == 0)
    def _():
        up[...] = jnp.zeros_like(up)
        core_grad[...] = jnp.zeros_like(core_grad)
        lift[...] = jnp.zeros_like(lift)

    keys = by_head(key[...] * jnp.asarray(1.0 / math.sqrt(HD), BF16))
    values = by_head(value[...])
    grads = mixed_grad[...]
    back = contract(grads, values, 1, 1)
    heads = []
    for h in range(LANES // HD):
        p = weights[0, :, h * n : (h + 1) * n].astype(F32)
        g = back[:, h * n : (h + 1) * n]
        heads.append((p * (g - jnp.sum(p * g, axis=-1, keepdims=True))).astype(BF16))
    score = jnp.concatenate(heads, axis=1)
    dv = own_head(contract(weights[0], grads, 0, 0))
    dk = own_head(contract(score, query[...], 0, 0)) * (1.0 / math.sqrt(HD))
    dq = contract(score, keys, 1, 0).astype(BF16)
    dk_low, dv_low = dk.astype(BF16), dv.astype(BF16)
    up[...] += contract(dq, wq[...], 1, 1)
    core_grad[...] += contract(dk_low, wk[...], 1, 1) + contract(dv_low, wv[...], 1, 1)
    lift[...] += jnp.sum(dk * bk[...] + dv * bv[...], axis=1, keepdims=True)
    query_grad[...] = contract(normed[...], dq, 0, 0).astype(BF16)
    key_grad[...] = contract(core[...], dk_low, 0, 0).astype(BF16)
    value_grad[...] = contract(core[...], dv_low, 0, 0).astype(BF16)
    qb[...] = jnp.sum(dq.astype(F32), axis=0, keepdims=True)
    kb[...] = jnp.sum(total[...] * dk, axis=0, keepdims=True)
    vb[...] = jnp.sum(total[...] * dv, axis=0, keepdims=True)


def attend_back(mixed_grad, weights, query, key, value, normed, core, total, qkv_weight, qkv_bias):
    rows, width = normed.shape
    n = core.shape[0]
    steps = width // LANES
    heads = LANES // HD
    return pl.pallas_call(
        attend_back_kernel,
        grid=(steps,),
        in_specs=[
            columns(rows, 0),
            pl.BlockSpec((1, rows, heads * n), lambda i: (i, 0, 0)),
            columns(rows, 0),
            columns(n, 0),
            columns(n, 0),
            whole((rows, width)),
            whole((n, width)),
            whole((n, 1)),
        ]
        + [columns(width, k * steps) for k in range(3)]
        + [columns(1, k * steps) for k in range(1, 3)],
        out_specs=[columns(width, 0)] * 3
        + [columns(1, 0)] * 3
        + [whole((rows, width)), whole((n, width)), whole((n, 1))],
        out_shape=[jax.ShapeDtypeStruct((width, width), BF16)] * 3
        + [jax.ShapeDtypeStruct((1, width), F32)] * 3
        + [
            jax.ShapeDtypeStruct((rows, width), F32),
            jax.ShapeDtypeStruct((n, width), F32),
            jax.ShapeDtypeStruct((n, 1), F32),
        ],
        compiler_params=pltpu.CompilerParams(**PARAMS),
        name="attend_back",
    )(mixed_grad, weights, query, key, value, normed, core, total, qkv_weight, qkv_weight, qkv_weight, qkv_bias, qkv_bias)


MESH = pl.DeviceIdType.MESH


def at_batch(other):
    return {"batch": other}


def at_blk(other):
    return {"blk": other}


def remote(source, target, send, arrive, where):
    return pltpu.make_async_remote_copy(
        src_ref=source, dst_ref=target, send_sem=send, recv_sem=arrive, device_id=where, device_id_type=MESH
    )


def greet(places):
    barrier = pltpu.get_barrier_semaphore()
    for where in places:
        pl.semaphore_signal(barrier, inc=1, device_id=where, device_id_type=MESH)
    pl.semaphore_wait(barrier, len(places))


def spread_order(n):
    return sorted(range(1, n), key=lambda d: (-(d & (n // 2)), d))


def arrive_kernel(n, inputs, compress, gain, bias, low_x, normed, squeeze, core, total,
                  own, send_x, recv_x, send_e, recv_e):
    me = lax.axis_index("blk")
    greet([at_blk(me ^ d) for d in range(1, n)])
    for d in range(1, n):
        remote(compress, squeeze.at[me], send_e.at[d - 1], recv_e.at[d - 1], at_blk(me ^ d)).start()
    for d in spread_order(n):
        remote(inputs.at[me ^ d], low_x.at[me], send_x.at[d - 1], recv_x.at[d - 1], at_blk(me ^ d)).start()
    mine = pltpu.make_async_copy(inputs.at[me], low_x.at[me], own)
    mine.start()
    squeeze[me] = compress[...]
    core[...] = jnp.zeros_like(core)
    total[...] = jnp.zeros_like(total)
    for d in [0] + list(range(1, n)):
        slot = me ^ d
        if d == 0:
            mine.wait()
        else:
            remote(compress, squeeze.at[slot], send_e.at[d - 1], recv_e.at[d - 1], at_blk(slot)).wait_recv()
            remote(inputs.at[slot], low_x.at[slot], send_x.at[d - 1], recv_x.at[d - 1], at_blk(slot)).wait_recv()
        hat, _ = norm_stats(low_x[slot].astype(F32))
        low = (hat * gain[...] + bias[...]).astype(BF16)
        normed[slot] = low
        piece = squeeze[slot]
        core[...] += contract(piece, low, 1, 0)
        total[...] += jnp.sum(piece.astype(F32), axis=1, keepdims=True)
    for d in range(1, n):
        slot = me ^ d
        remote(compress, squeeze.at[me], send_e.at[d - 1], recv_e.at[d - 1], at_blk(slot)).wait_send()
        remote(inputs.at[slot], low_x.at[me], send_x.at[d - 1], recv_x.at[d - 1], at_blk(slot)).wait_send()


def arrive(inputs, compress, gain, bias):
    n, tokens, width = inputs.shape
    m = compress.shape[0]
    vmem = pl.BlockSpec(memory_space=pltpu.VMEM)
    sems = pltpu.SemaphoreType.DMA((n - 1,))
    return pl.pallas_call(
        functools.partial(arrive_kernel, n),
        in_specs=[pl.BlockSpec(memory_space=pl.ANY), vmem, vmem, vmem],
        out_specs=[vmem] * 5,
        out_shape=[
            jax.ShapeDtypeStruct((n, tokens, width), BF16),
            jax.ShapeDtypeStruct((n, tokens, width), BF16),
            jax.ShapeDtypeStruct((n, m, tokens), BF16),
            jax.ShapeDtypeStruct((m, width), F32),
            jax.ShapeDtypeStruct((m, 1), F32),
        ],
        scratch_shapes=[pltpu.SemaphoreType.DMA, sems, sems, sems, sems],
        compiler_params=pltpu.CompilerParams(collective_id=0, has_side_effects=True, vmem_limit_bytes=48 << 20),
        name="arrive",
    )(inputs, compress, gain, bias)


class Unit:
    def __init__(self, source, top, left, result, result_left, rows, cols, early):
        self.source, self.top, self.left = source, top, left
        self.result, self.result_left = result, result_left
        self.half, self.cols, self.early = rows // 2, cols, early

    def scratch(self):
        h, c = self.half, self.cols
        narrow = c // 2 if self.early else c
        shapes = [(2, 2, 2, h, c), (2, 2, 2, h, c)]
        if self.early:
            shapes.append((2, 2, 2, h, narrow))
        shapes += [(2, 2, h, narrow), (2, h, narrow), (h, narrow)]
        if not self.early:
            shapes.append((h, c))
        return [pltpu.VMEM(shape, BF16) for shape in shapes]


STAGES = 7
BUFFERS = 6


class Route:
    def __init__(self, unit, source, result, buffers, local, send, recv):
        self.unit, self.source, self.result = unit, source, result
        self.acc, self.got = buffers[0], buffers[1:]
        self.local, self.send, self.recv = local, send, recv
        batch, blk = lax.axis_index("batch"), lax.axis_index("blk")
        self.batch, self.blk = batch, blk
        self.core, self.x = batch % 2, batch // 2
        self.z2, self.z1, self.y = blk // 4, (blk // 2) % 2, blk % 2
        self.sent = []

    def rows_of(self, core):
        return pl.ds(pl.multiple_of(core * self.unit.half, 16), self.unit.half)

    def part(self, core):
        u = self.unit
        return self.source.at[
            :, :, :, pl.ds(pl.multiple_of(u.top + core * u.half, 16), u.half), pl.ds(u.left, u.cols)
        ]

    def lanes(self, x):
        u = self.unit
        if not u.early:
            return pl.ds(0, u.cols)
        return pl.ds(pl.multiple_of(x * (u.cols // 2), 128), u.cols // 2)

    def result_lanes(self, x):
        u = self.unit
        if not u.early:
            return pl.ds(u.result_left, u.cols)
        return pl.ds(pl.multiple_of(u.result_left + x * (u.cols // 2), 128), u.cols // 2)

    def result_rows(self, core):
        u = self.unit
        base = u.top if u.source == u.result else 0
        return pl.ds(pl.multiple_of(base + core * u.half, 16), u.half)

    def hops(self):
        if self.unit.early:
            return ["core", "x", "y", "z1", "z2", "join", "pair"]
        return ["core", "y", "z1", "z2", "late", "pair"]

    def copy(self, s):
        hop = self.hops()[s]
        u, acc, mine = self.unit, self.acc, self.lanes(self.x)
        y, z1, z2 = self.y, self.z1, self.z2
        every = slice(None)
        where = {
            "core": at_batch(self.batch ^ 1),
            "pair": at_batch(self.batch ^ 1),
            "x": at_batch(self.batch ^ 2),
            "late": at_batch(self.batch ^ 2),
            "join": at_batch(self.batch ^ 2),
            "y": at_blk(self.blk ^ 1),
            "z1": at_blk(self.blk ^ 2),
            "z2": at_blk(self.blk ^ 4),
        }[hop]
        if hop in ("join", "pair"):
            lanes = self.result_lanes(self.x) if hop == "join" else pl.ds(u.result_left, u.cols)
            source = target = self.result.at[self.result_rows(self.core), lanes]
        else:
            target = self.got[s]
            source = {
                "core": lambda: self.part(1 - self.core),
                "x": lambda: acc.at[:, :, :, :, self.lanes(1 - self.x)],
                "y": lambda: acc.at[:, :, 1 - y, :, mine],
                "z1": lambda: acc.at[:, 1 - z1, y, :, mine],
                "z2": lambda: acc.at[1 - z2, z1, y, :, mine],
                "late": lambda: acc.at[z2, z1, y, :, mine],
            }[hop]()
        return remote(source, target, self.send.at[s], self.recv.at[s], where)

    def start(self, s):
        if s == 0:
            pltpu.make_async_copy(self.part(self.core), self.acc, self.local).start()
        self.copy(s).start()

    def finish(self, s):
        hop = self.hops()[s]
        acc, got, mine = self.acc, self.got[s] if s < len(self.got) else None, self.lanes(self.x)
        if s == 0:
            pltpu.make_async_copy(self.part(self.core), acc, self.local).wait()
        self.copy(s).wait_recv()
        pairs = [(a, b) for a in range(2) for b in range(2)]

        def add(place, other):
            acc[place] = (acc[place].astype(F32) + got[other].astype(F32)).astype(BF16)

        if hop in ("core", "x"):
            for a, b in pairs:
                for c in range(2):
                    add((a, b, c, slice(None), mine if hop == "x" else slice(None)), (a, b, c))
        elif hop == "y":
            for a, b in pairs:
                add((a, b, self.y, slice(None), mine), (a, b))
        elif hop == "z1":
            for a in range(2):
                add((a, self.z1, self.y, slice(None), mine), (a,))
        if hop == "late" or (hop == "z2" and self.unit.early):
            value = acc[self.z2, self.z1, self.y, :, mine].astype(F32) + got[...].astype(F32)
            self.result[self.result_rows(self.core), self.result_lanes(self.x)] = value.astype(BF16)
        elif hop == "z2":
            add((self.z2, self.z1, self.y, slice(None), mine), slice(None))

    def close(self):
        for s in range(len(self.hops())):
            self.copy(s).wait_send()


def run_routes(routes, starts):
    last = max(starts[i] + len(r.hops()) for i, r in enumerate(routes))
    for t in range(last + 1):
        for i, route in enumerate(routes):
            s = t - starts[i]
            if 1 <= s <= len(route.hops()):
                route.finish(s - 1)
            if 0 <= s < len(route.hops()):
                route.start(s)


def depart_kernel(n, units, starts, n_in, n_out, *refs):
    sources, refs = refs[:n_in], refs[n_in:]
    results, refs = refs[:n_out], refs[n_out:]
    me = lax.axis_index("blk")
    own, send_d, recv_d, local, send, recv = refs[:6]
    refs = refs[6:]
    batch = lax.axis_index("batch")
    greet([at_batch(batch ^ 1), at_batch(batch ^ 2)] + [at_blk(me ^ d) for d in range(1, n)])

    def ship(d):
        return remote(
            sources[0].at[me ^ d], results[0].at[me], send_d.at[d - 1], recv_d.at[d - 1], at_blk(me ^ d)
        )

    for d in spread_order(n):
        ship(d).start()
    mine = pltpu.make_async_copy(sources[0].at[me], results[0].at[me], own)
    mine.start()
    routes = []
    for i, unit in enumerate(units):
        count = len(unit.scratch())
        buffers, refs = refs[:count], refs[count:]
        routes.append(
            Route(unit, sources[unit.source], results[unit.result], buffers, local.at[i], send.at[i], recv.at[i])
        )
    run_routes(routes, starts)
    for route in routes:
        route.close()
    mine.wait()
    for d in range(1, n):
        ship(d).wait()


def depart(rows_grad, arrays, units, starts, result_shapes):
    n = rows_grad.shape[0]
    anywhere = pl.BlockSpec(memory_space=pl.ANY)
    vmem = pl.BlockSpec(memory_space=pltpu.VMEM)
    dma = pltpu.SemaphoreType.DMA
    scratch = [dma, dma((n - 1,)), dma((n - 1,)), dma((len(units),)), dma((len(units), STAGES)), dma((len(units), STAGES))]
    for unit in units:
        scratch += unit.scratch()
    arrays = [a.reshape((2, 2, 2) + a.shape[1:]) for a in arrays]
    return pl.pallas_call(
        functools.partial(depart_kernel, n, units, starts, 1 + len(arrays), 1 + len(result_shapes)),
        in_specs=[anywhere] * (1 + len(arrays)),
        out_specs=[anywhere] + [vmem] * len(result_shapes),
        out_shape=[jax.ShapeDtypeStruct(rows_grad.shape, BF16)]
        + [jax.ShapeDtypeStruct(shape, BF16) for shape in result_shapes],
        scratch_shapes=scratch,
        compiler_params=pltpu.CompilerParams(collective_id=1, has_side_effects=True, vmem_limit_bytes=60 << 20),
        name="depart",
    )(rows_grad, *arrays)


def sum_all(rows_grad, arrays):
    down, up, small = arrays[0], arrays[1], arrays[-1]
    width = down.shape[2]
    tall = up.shape[1]
    downs = [Unit(1, tall * i, 0, 1, 0, tall, width, False) for i in range(down.shape[1] // tall)]
    ups = [Unit(2, 0, width * i, 2, width * i, tall, width, True) for i in range(up.shape[2] // width)]
    units = [unit for pair in zip(downs, ups) for unit in pair]
    units += [Unit(3 + i, 0, 0, 3, width * i, tall, width, i != 1) for i in range(3)]
    units += [Unit(6, 0, 0, 4, 0, tall, width, False)]
    units += [Unit(7, 0, 0, 5, 0, small.shape[1], small.shape[2], False)]
    starts = [i // 2 for i in range(len(units))]
    shapes = [down.shape[1:], up.shape[1:], (tall, 3 * width), (tall, width), small.shape[1:]]
    return depart(rows_grad, arrays, units, starts, shapes)


def swap(values, axis, size, bit):
    return lax.ppermute(values, axis, [(i, i ^ bit) for i in range(size)])


def halve(values, dim, axis, size, bit):
    mine = (lax.axis_index(axis) // bit) % 2
    send = lax.dynamic_index_in_dim(values, 1 - mine, dim, keepdims=False).astype(BF16)
    keep = lax.dynamic_index_in_dim(values, mine, dim, keepdims=False)
    return keep.astype(F32) + swap(send, axis, size, bit).astype(F32)


def join(values, dim, axis, size, bit):
    mine = (lax.axis_index(axis) // bit) % 2
    other = swap(values, axis, size, bit)
    first = jnp.where(mine == 0, values, other)
    second = jnp.where(mine == 0, other, values)
    return jnp.concatenate([first, second], axis=dim)


def scatter_sum(terms, bits, order, nb, nk, early):
    _, rows, cols = terms.shape
    values = halve(terms.reshape(-1, 2, rows // 2, cols), 1, "batch", nb, 1)
    chips = [1 << i for i in range(1, nb.bit_length() - 1)]
    if early:
        for bit in chips:
            cols //= 2
            values = halve(values.reshape(-1, rows // 2, 2, cols), 2, "batch", nb, bit)
    left = list(bits)
    for bit in order:
        place = left.index(bit)
        values = values.reshape(1 << place, 2, -1, rows // 2, cols)
        values = halve(values, 1, "blk", nk, bit)
        left.remove(bit)
    values = values.reshape(rows // 2, cols).astype(BF16)
    for bit in reversed(chips) if early else chips:
        if early:
            values = join(values, 1, "batch", nb, bit)
        else:
            values = (values.astype(F32) + swap(values, "batch", nb, bit).astype(F32)).astype(BF16)
    return join(values, 0, "batch", nb, 1).astype(F32)


def body(
    inputs,
    cotangent,
    group_counts,
    first_gain,
    first_bias,
    qkv_weight,
    qkv_bias,
    out_weight,
    out_bias,
    second_gain,
    second_bias,
    up_weight,
    up_bias,
    down_weight,
    down_bias,
    compress,
    *,
    nb,
    nk,
):
    slots, tokens, width = inputs.shape
    splits = nk // slots
    teams = [[t * slots + i for i in range(slots)] for t in range(splits)]
    across = [[t * slots + i for t in range(splits)] for i in range(slots)]
    rows = slots * tokens
    low_first = [1 << i for i in range(nk.bit_length() - 1)]
    high_first = low_first[::-1]
    team_low = [1 << i for i in range(slots.bit_length() - 1)]

    def gather_rows(values):
        return lax.all_to_all(values, "blk", 0, 0, axis_index_groups=teams, tiled=True).reshape(
            rows, width
        )

    def spread_rows(values):
        return lax.all_to_all(
            values.reshape(slots, tokens, width), "blk", 0, 0, axis_index_groups=teams, tiled=True
        )

    def over_splits(values):
        if splits == 1:
            return values
        return lax.psum(values, "blk", axis_index_groups=across)

    def line(vector):
        return vector.reshape(1, -1)

    slot = lax.axis_index("blk") % slots
    alive = (slot < group_counts[lax.axis_index("batch")]).astype(jnp.int32).reshape(1)

    compact = nb == 4 and nk == slots == 8
    if compact:
        low_x, normed, squeeze, core, total = arrive(
            inputs, compress, line(first_gain), line(first_bias)
        )
        low_x, normed = low_x.reshape(rows, width), normed.reshape(rows, width)
        cotangent, core = lax.optimization_barrier((cotangent, core))
        hat_first, rate_first = norm_stats(low_x.astype(F32))
    else:
        squeeze = compress[None]
        for bit in team_low[::-1]:
            squeeze = join(squeeze[:, None], 1, "blk", nk, bit)
            squeeze = squeeze.reshape((-1,) + compress.shape)
        low_x = gather_rows(inputs)
        hat_first, rate_first = norm_stats(low_x.astype(F32))
        normed = (hat_first * first_gain + first_bias).astype(BF16)
        core = jnp.einsum(
            "bjt,btc->jc",
            squeeze,
            normed.reshape(slots, tokens, width),
            preferred_element_type=F32,
        )
        total = jnp.sum(squeeze.astype(F32), axis=(0, 2))[:, None]
    low_cot = gather_rows(cotangent)
    core = over_splits(core).astype(BF16)
    total = over_splits(total)
    query, key, value, weights, mixed = attend(
        normed, core, total, qkv_weight, line(qkv_bias), tile=512
    )
    middle, second, active, slope, result = forward(
        alive,
        mixed,
        low_x,
        out_weight,
        line(out_bias),
        line(second_gain),
        line(second_bias),
        up_weight,
        line(up_bias),
        down_weight,
        line(down_bias),
    )
    output = spread_rows(result)
    up_grad, down_grad, up_bias_grad, middle_grad, mixed_grad, out_grad, sums = backward(
        alive,
        low_cot,
        active,
        slope,
        second,
        middle,
        mixed,
        up_weight,
        down_weight,
        out_weight,
        line(second_gain),
    )
    out_bias_grad, second_gain_grad, second_bias_grad, down_bias_grad = (sums[i] for i in range(4))
    (
        query_weight_grad,
        key_weight_grad,
        value_weight_grad,
        query_bias_grad,
        key_bias_grad,
        value_bias_grad,
        query_up,
        core_back,
        lift,
    ) = attend_back(
        mixed_grad, weights, query, key, value, normed, core, total, qkv_weight, line(qkv_bias)
    )
    core_back = over_splits(core_back).astype(BF16)
    lift = over_splits(lift)
    first_up = query_up + jnp.einsum(
        "bjt,jc->btc", squeeze, core_back, preferred_element_type=F32
    ).reshape(rows, width)
    first_gain_grad = jnp.sum(first_up * hat_first, axis=0)
    first_bias_grad = jnp.sum(first_up, axis=0)
    rows_grad = (
        middle_grad + norm_back(hat_first, rate_first, first_up, first_gain)
    ).astype(BF16)
    compress_terms = (
        jnp.einsum(
            "jc,btc->bjt",
            core_back,
            normed.reshape(slots, tokens, width),
            preferred_element_type=F32,
        )
        + lift[None]
    )

    vectors = (
        first_gain_grad,
        first_bias_grad,
        jnp.concatenate([query_bias_grad, key_bias_grad, value_bias_grad], axis=1),
        out_bias_grad,
        second_gain_grad,
        second_bias_grad,
        up_bias_grad,
        down_bias_grad,
    )
    sizes = [v.size // nk for v in vectors]
    packed = jnp.concatenate([v.reshape(nk, -1) for v in vectors], axis=1)
    tall = 32
    wide = -(-sum(sizes) // (tall * 128)) * 128
    packed = jnp.pad(packed, ((0, 0), (0, tall * wide - sum(sizes)))).reshape(nk, tall, wide)
    blocked = [
        grad.reshape(nk, grad.shape[0] // nk, grad.shape[1])
        for grad in (
            down_grad,
            up_grad,
            query_weight_grad,
            key_weight_grad,
            value_weight_grad,
            out_grad,
        )
    ]
    if compact:
        small = jnp.concatenate([compress_terms, packed], axis=1).astype(BF16)
        input_grad, *summed = sum_all(rows_grad.reshape(slots, tokens, width), blocked + [small])
        down_rows, up_rows, qkv_rows, out_rows, small = (v.astype(F32) for v in summed)
        compress_rows, mine = small[: compress.shape[0]], small[compress.shape[0] :].reshape(-1)
    else:
        input_grad = spread_rows(rows_grad)
        blocked = blocked[:2] + [jnp.concatenate(blocked[2:], axis=2)]
        down_rows, up_rows, joined = (
            scatter_sum(grad, high_first, low_first, nb, nk, i > 0)
            for i, grad in enumerate(blocked)
        )
        qkv_rows, out_rows = joined[:, : 3 * width], joined[:, 3 * width :]
        compress_rows = scatter_sum(compress_terms, team_low[::-1], team_low, nb, nk, False)
        mine = scatter_sum(packed, high_first, low_first, nb, nk, False).reshape(-1)
    parts = []
    start = 0
    for size in sizes:
        parts.append(mine[start : start + size])
        start += size
    fg, fb, qb, ob, sg, sb, ub, db = parts
    return (
        output,
        input_grad,
        fg,
        fb,
        qkv_rows,
        qb,
        out_rows,
        ob,
        sg,
        sb,
        up_rows,
        ub,
        down_rows,
        db,
        compress_rows,
    )


def solution(mesh):
    rows = P("batch", "blk", None)
    placed = (rows, rows) + (P(),) * 13 + (P(None, "blk"),)
    vec, mat = P("blk"), P("blk", None)
    return jax.shard_map(
        functools.partial(body, nb=mesh.shape["batch"], nk=mesh.shape["blk"]),
        mesh=mesh,
        in_specs=placed,
        out_specs=(rows, rows, vec, vec, mat, vec, mat, vec, vec, vec, mat, vec, mat, vec)
        + (P(None, "blk"),),
        check_vma=False,
    )
```

```python
import functools
import math

import jax
import jax.numpy as jnp
from jax import lax
from jax.experimental import pallas as pl
from jax.experimental.pallas import tpu as pltpu
from jax.sharding import PartitionSpec as P

F32 = jnp.float32
BF16 = jnp.bfloat16
HD = 64
LANES = 256
GELU_A = math.sqrt(2.0 / math.pi)
GELU_B = 0.044715


def norm_stats(states):
    center = states - jnp.mean(states, axis=-1, keepdims=True)
    spread = jnp.mean(center * center, axis=-1, keepdims=True)
    rate = lax.rsqrt(spread + 1e-05)
    return center * rate, rate


def norm_back(hat, rate, upstream, gain):
    scaled = upstream * gain
    return rate * (
        scaled
        - jnp.mean(scaled, axis=-1, keepdims=True)
        - hat * jnp.mean(scaled * hat, axis=-1, keepdims=True)
    )


def contract(a, b, dim_a, dim_b):
    return lax.dot_general(a, b, (((dim_a,), (dim_b,)), ((), ())), preferred_element_type=F32)


def whole(shape):
    return pl.BlockSpec(shape, lambda *_: (0,) * len(shape), pipeline_mode=pl.Buffered(1))


def columns(height, start, width=LANES):
    return pl.BlockSpec((height, width), lambda i: (0, start + i))


def below(width, start, height=LANES):
    return pl.BlockSpec((height, width), lambda i: (start + i, 0))


PARAMS = dict(vmem_limit_bytes=62 << 20, dimension_semantics=("arbitrary",))


def by_head(values):
    lane = lax.broadcasted_iota(jnp.int32, values.shape, 1) // HD
    zero = jnp.zeros_like(values)
    return jnp.concatenate([jnp.where(lane == h, values, zero) for h in range(LANES // HD)], axis=0)


def own_head(values):
    n = values.shape[0] // (LANES // HD)
    lane = lax.broadcasted_iota(jnp.int32, (n, LANES), 1) // HD
    picked = values[:n]
    for h in range(1, LANES // HD):
        picked = jnp.where(lane == h, values[h * n : (h + 1) * n], picked)
    return picked


def attend_kernel(tile, normed, core, total, wq, wk, wv, bq, bk, bv, query, key, value, weights, mixed):
    rows, n = normed.shape[0], core.shape[0]
    key[...] = (contract(core[...], wk[...], 1, 0) + total[...] * bk[...]).astype(BF16)
    value[...] = (contract(core[...], wv[...], 1, 0) + total[...] * bv[...]).astype(BF16)
    keys = by_head(key[...] * jnp.asarray(1.0 / math.sqrt(HD), BF16))
    values = by_head(value[...])

    for r in range(rows // tile):
        at = slice(r * tile, (r + 1) * tile)
        q = (contract(normed[at, :], wq[...], 1, 0) + bq[...]).astype(BF16)
        query[at, :] = q
        scores = contract(q, keys, 1, 1)
        heads = []
        for h in range(LANES // HD):
            s = scores[:, h * n : (h + 1) * n]
            e = jnp.exp(s - jnp.max(s, axis=-1, keepdims=True))
            heads.append((e * (1.0 / jnp.sum(e, axis=-1, keepdims=True))).astype(BF16))
        low = jnp.concatenate(heads, axis=1)
        weights[0, at, :] = low
        mixed[at, :] = contract(low, values, 1, 0).astype(BF16)


def attend(normed, core, total, qkv_weight, qkv_bias, tile=1024):
    rows, width = normed.shape
    n = core.shape[0]
    steps = width // LANES
    heads = LANES // HD
    return pl.pallas_call(
        functools.partial(attend_kernel, tile),
        grid=(steps,),
        in_specs=[whole((rows, width)), whole((n, width)), whole((n, 1))]
        + [columns(width, k * steps) for k in range(3)]
        + [columns(1, k * steps) for k in range(3)],
        out_specs=[
            columns(rows, 0),
            columns(n, 0),
            columns(n, 0),
            pl.BlockSpec((1, rows, heads * n), lambda i: (i, 0, 0)),
            columns(rows, 0),
        ],
        out_shape=[
            jax.ShapeDtypeStruct((rows, width), BF16),
            jax.ShapeDtypeStruct((n, width), BF16),
            jax.ShapeDtypeStruct((n, width), BF16),
            jax.ShapeDtypeStruct((steps, rows, heads * n), BF16),
            jax.ShapeDtypeStruct((rows, width), BF16),
        ],
        compiler_params=pltpu.CompilerParams(**PARAMS),
        name="attend",
    )(normed, core, total, qkv_weight, qkv_weight, qkv_weight, qkv_bias, qkv_bias, qkv_bias)


def forward_kernel(tile, alive, mixed, states, ow, ob, gain, bias, upw, upb, dnw, dnb,
                   middle, second, active, slope, output, total):
    f = pl.program_id(0)
    rows = mixed.shape[0]

    @pl.when(f == 0)
    def _():
        mid = states[...].astype(F32) + contract(mixed[...], ow[...], 1, 0) + ob[...]
        middle[...] = mid
        second[...] = (norm_stats(mid)[0] * gain[...] + bias[...]).astype(BF16)
        total[...] = mid + dnb[...]

    for r in range(rows // tile):
        at = slice(r * tile, (r + 1) * tile)
        v = contract(second[at, :], upw[...], 1, 0) + upb[...]
        square = v * v
        t = jnp.tanh(v * (GELU_A + (GELU_A * GELU_B) * square))
        half = 0.5 + 0.5 * t
        act = (v * half).astype(BF16)
        active[at, :] = act
        slope[at, :] = (
            half + (0.5 * v) * (1.0 - t * t) * (GELU_A + (3 * GELU_A * GELU_B) * square)
        ).astype(BF16)
        total[at, :] += contract(act, dnw[...], 1, 0)

    @pl.when(f == pl.num_programs(0) - 1)
    def _():
        output[...] = jnp.where(alive[0] > 0, total[...], 0.0).astype(BF16)


def forward(alive, mixed, states, ow, ob, gain, bias, upw, upb, dnw, dnb, block=512, tile=1024):
    rows, width = mixed.shape
    hidden = upw.shape[1]
    vec = whole((1, width))
    return pl.pallas_call(
        functools.partial(forward_kernel, tile),
        grid=(hidden // block,),
        in_specs=[
            pl.BlockSpec(memory_space=pltpu.SMEM),
            whole((rows, width)),
            whole((rows, width)),
            whole((width, width)),
            vec,
            vec,
            vec,
            columns(width, 0, block),
            columns(1, 0, block),
            below(width, 0, block),
            vec,
        ],
        out_specs=[
            whole((rows, width)),
            whole((rows, width)),
            columns(rows, 0, block),
            columns(rows, 0, block),
            whole((rows, width)),
        ],
        out_shape=[
            jax.ShapeDtypeStruct((rows, width), F32),
            jax.ShapeDtypeStruct((rows, width), BF16),
            jax.ShapeDtypeStruct((rows, hidden), BF16),
            jax.ShapeDtypeStruct((rows, hidden), BF16),
            jax.ShapeDtypeStruct((rows, width), BF16),
        ],
        scratch_shapes=[pltpu.VMEM((rows, width), F32)],
        compiler_params=pltpu.CompilerParams(**PARAMS),
        name="forward",
    )(alive, mixed, states, ow, ob, gain, bias, upw, upb, dnw, dnb)


def backward_kernel(alive, cot, active, slope, second, middle, mixed, upw, dnw, ow, gain,
                    up_grad, down_grad, up_bias_grad, middle_grad, mixed_grad, out_grad, sums,
                    incoming, total):
    f = pl.program_id(0)

    @pl.when(f == 0)
    def _():
        incoming[...] = jnp.where(alive[0] > 0, cot[...], jnp.zeros_like(cot))
        total[...] = jnp.zeros_like(total)

    d = contract(incoming[...], dnw[...], 1, 1)
    dh = (d * slope[...].astype(F32)).astype(BF16)
    up_bias_grad[...] = jnp.sum(dh.astype(F32), axis=0, keepdims=True)
    total[...] += contract(dh, upw[...], 1, 1)
    down_grad[...] = contract(active[...], incoming[...], 0, 0).astype(BF16)
    up_grad[...] = contract(second[...], dh, 0, 0).astype(BF16)

    @pl.when(f == pl.num_programs(0) - 1)
    def _():
        hat, rate = norm_stats(middle[...])
        up = total[...]
        inc = incoming[...].astype(F32)
        grad = inc + norm_back(hat, rate, up, gain[...])
        middle_grad[...] = grad
        branch = grad.astype(BF16)
        mixed_grad[...] = contract(branch, ow[...], 1, 1).astype(BF16)
        out_grad[...] = contract(mixed[...], branch, 0, 0).astype(BF16)
        sums[0:1, :] = jnp.sum(branch.astype(F32), axis=0, keepdims=True)
        sums[1:2, :] = jnp.sum(up * hat, axis=0, keepdims=True)
        sums[2:3, :] = jnp.sum(up, axis=0, keepdims=True)
        sums[3:4, :] = jnp.sum(inc, axis=0, keepdims=True)


def backward(alive, cot, active, slope, second, middle, mixed, upw, dnw, ow, gain, block=512):
    rows, width = mixed.shape
    hidden = upw.shape[1]
    return pl.pallas_call(
        backward_kernel,
        grid=(hidden // block,),
        in_specs=[
            pl.BlockSpec(memory_space=pltpu.SMEM),
            whole((rows, width)),
            columns(rows, 0, block),
            columns(rows, 0, block),
            whole((rows, width)),
            whole((rows, width)),
            whole((rows, width)),
            columns(width, 0, block),
            below(width, 0, block),
            whole((width, width)),
            whole((1, width)),
        ],
        out_specs=[
            columns(width, 0, block),
            below(width, 0, block),
            columns(1, 0, block),
            whole((rows, width)),
            whole((rows, width)),
            whole((width, width)),
            whole((4, width)),
        ],
        out_shape=[
            jax.ShapeDtypeStruct((width, hidden), BF16),
            jax.ShapeDtypeStruct((hidden, width), BF16),
            jax.ShapeDtypeStruct((1, hidden), F32),
            jax.ShapeDtypeStruct((rows, width), F32),
            jax.ShapeDtypeStruct((rows, width), BF16),
            jax.ShapeDtypeStruct((width, width), BF16),
            jax.ShapeDtypeStruct((4, width), F32),
        ],
        scratch_shapes=[pltpu.VMEM((rows, width), BF16), pltpu.VMEM((rows, width), F32)],
        compiler_params=pltpu.CompilerParams(**PARAMS),
        name="backward",
    )(alive, cot, active, slope, second, middle, mixed, upw, dnw, ow, gain)


def attend_back_kernel(mixed_grad, weights, query, key, value, normed, core, total, wq, wk, wv, bk, bv,
                       query_grad, key_grad, value_grad, qb, kb, vb, up, core_grad, lift):
    i = pl.program_id(0)
    n = core.shape[0]

    @pl.when(i == 0)
    def _():
        up[...] = jnp.zeros_like(up)
        core_grad[...] = jnp.zeros_like(core_grad)
        lift[...] = jnp.zeros_like(lift)

    keys = by_head(key[...] * jnp.asarray(1.0 / math.sqrt(HD), BF16))
    values = by_head(value[...])
    grads = mixed_grad[...]
    back = contract(grads, values, 1, 1)
    heads = []
    for h in range(LANES // HD):
        p = weights[0, :, h * n : (h + 1) * n].astype(F32)
        g = back[:, h * n : (h + 1) * n]
        heads.append((p * (g - jnp.sum(p * g, axis=-1, keepdims=True))).astype(BF16))
    score = jnp.concatenate(heads, axis=1)
    dv = own_head(contract(weights[0], grads, 0, 0))
    dk = own_head(contract(score, query[...], 0, 0)) * (1.0 / math.sqrt(HD))
    dq = contract(score, keys, 1, 0).astype(BF16)
    dk_low, dv_low = dk.astype(BF16), dv.astype(BF16)
    up[...] += contract(dq, wq[...], 1, 1)
    core_grad[...] += contract(dk_low, wk[...], 1, 1) + contract(dv_low, wv[...], 1, 1)
    lift[...] += jnp.sum(dk * bk[...] + dv * bv[...], axis=1, keepdims=True)
    query_grad[...] = contract(normed[...], dq, 0, 0).astype(BF16)
    key_grad[...] = contract(core[...], dk_low, 0, 0).astype(BF16)
    value_grad[...] = contract(core[...], dv_low, 0, 0).astype(BF16)
    qb[...] = jnp.sum(dq.astype(F32), axis=0, keepdims=True)
    kb[...] = jnp.sum(total[...] * dk, axis=0, keepdims=True)
    vb[...] = jnp.sum(total[...] * dv, axis=0, keepdims=True)


def attend_back(mixed_grad, weights, query, key, value, normed, core, total, qkv_weight, qkv_bias):
    rows, width = normed.shape
    n = core.shape[0]
    steps = width // LANES
    heads = LANES // HD
    return pl.pallas_call(
        attend_back_kernel,
        grid=(steps,),
        in_specs=[
            columns(rows, 0),
            pl.BlockSpec((1, rows, heads * n), lambda i: (i, 0, 0)),
            columns(rows, 0),
            columns(n, 0),
            columns(n, 0),
            whole((rows, width)),
            whole((n, width)),
            whole((n, 1)),
        ]
        + [columns(width, k * steps) for k in range(3)]
        + [columns(1, k * steps) for k in range(1, 3)],
        out_specs=[columns(width, 0)] * 3
        + [columns(1, 0)] * 3
        + [whole((rows, width)), whole((n, width)), whole((n, 1))],
        out_shape=[jax.ShapeDtypeStruct((width, width), BF16)] * 3
        + [jax.ShapeDtypeStruct((1, width), F32)] * 3
        + [
            jax.ShapeDtypeStruct((rows, width), F32),
            jax.ShapeDtypeStruct((n, width), F32),
            jax.ShapeDtypeStruct((n, 1), F32),
        ],
        compiler_params=pltpu.CompilerParams(**PARAMS),
        name="attend_back",
    )(mixed_grad, weights, query, key, value, normed, core, total, qkv_weight, qkv_weight, qkv_weight, qkv_bias, qkv_bias)


MESH = pl.DeviceIdType.MESH


def at_batch(other):
    return {"batch": other}


def at_blk(other):
    return {"blk": other}


def remote(source, target, send, arrive, where):
    return pltpu.make_async_remote_copy(
        src_ref=source, dst_ref=target, send_sem=send, recv_sem=arrive, device_id=where, device_id_type=MESH
    )


def greet(places):
    barrier = pltpu.get_barrier_semaphore()
    for where in places:
        pl.semaphore_signal(barrier, inc=1, device_id=where, device_id_type=MESH)
    pl.semaphore_wait(barrier, len(places))


def spread_order(n):
    return sorted(range(1, n), key=lambda d: (-(d & (n // 2)), d))


def arrive_kernel(n, inputs, compress, gain, bias, low_x, normed, squeeze, core, total,
                  own, send_x, recv_x, send_e, recv_e):
    me = lax.axis_index("blk")
    greet([at_blk(me ^ d) for d in range(1, n)])
    for d in range(1, n):
        remote(compress, squeeze.at[me], send_e.at[d - 1], recv_e.at[d - 1], at_blk(me ^ d)).start()
    for d in spread_order(n):
        remote(inputs.at[me ^ d], low_x.at[me], send_x.at[d - 1], recv_x.at[d - 1], at_blk(me ^ d)).start()
    mine = pltpu.make_async_copy(inputs.at[me], low_x.at[me], own)
    mine.start()
    squeeze[me] = compress[...]
    core[...] = jnp.zeros_like(core)
    total[...] = jnp.zeros_like(total)
    for d in [0] + list(range(1, n)):
        slot = me ^ d
        if d == 0:
            mine.wait()
        else:
            remote(compress, squeeze.at[slot], send_e.at[d - 1], recv_e.at[d - 1], at_blk(slot)).wait_recv()
            remote(inputs.at[slot], low_x.at[slot], send_x.at[d - 1], recv_x.at[d - 1], at_blk(slot)).wait_recv()
        hat, _ = norm_stats(low_x[slot].astype(F32))
        low = (hat * gain[...] + bias[...]).astype(BF16)
        normed[slot] = low
        piece = squeeze[slot]
        core[...] += contract(piece, low, 1, 0)
        total[...] += jnp.sum(piece.astype(F32), axis=1, keepdims=True)
    for d in range(1, n):
        slot = me ^ d
        remote(compress, squeeze.at[me], send_e.at[d - 1], recv_e.at[d - 1], at_blk(slot)).wait_send()
        remote(inputs.at[slot], low_x.at[me], send_x.at[d - 1], recv_x.at[d - 1], at_blk(slot)).wait_send()


def arrive(inputs, compress, gain, bias):
    n, tokens, width = inputs.shape
    m = compress.shape[0]
    vmem = pl.BlockSpec(memory_space=pltpu.VMEM)
    sems = pltpu.SemaphoreType.DMA((n - 1,))
    return pl.pallas_call(
        functools.partial(arrive_kernel, n),
        in_specs=[pl.BlockSpec(memory_space=pl.ANY), vmem, vmem, vmem],
        out_specs=[vmem] * 5,
        out_shape=[
            jax.ShapeDtypeStruct((n, tokens, width), BF16),
            jax.ShapeDtypeStruct((n, tokens, width), BF16),
            jax.ShapeDtypeStruct((n, m, tokens), BF16),
            jax.ShapeDtypeStruct((m, width), F32),
            jax.ShapeDtypeStruct((m, 1), F32),
        ],
        scratch_shapes=[pltpu.SemaphoreType.DMA, sems, sems, sems, sems],
        compiler_params=pltpu.CompilerParams(collective_id=0, has_side_effects=True, vmem_limit_bytes=48 << 20),
        name="arrive",
    )(inputs, compress, gain, bias)


class Unit:
    def __init__(self, top, left, result_top, result_left, rows, cols, early, inplace):
        self.top, self.left = top, left
        self.result_top, self.result_left = result_top, result_left
        self.half, self.cols = rows // 2, cols
        self.early, self.inplace = early, inplace

    def scratch(self):
        h, c = self.half, self.cols
        narrow = c // 2 if self.early else c
        shapes = [] if self.inplace else [(2, 2, 2, h, c)]
        shapes.append((2, 2, 2, h, c))
        if self.early:
            shapes.append((2, 2, 2, h, narrow))
        shapes += [(2, 2, h, narrow), (2, h, narrow), (h, narrow)]
        if not self.early:
            shapes.append((h, c))
        return [pltpu.VMEM(shape, BF16) for shape in shapes]


HOPS = 7


class Route:
    def __init__(self, unit, source, result, buffers, local, send, recv):
        self.unit, self.source, self.result = unit, source, result
        self.acc, self.got = (source, buffers) if unit.inplace else (buffers[0], buffers[1:])
        self.local, self.send, self.recv = local, send, recv
        self.batch, self.blk = lax.axis_index("batch"), lax.axis_index("blk")
        self.core, self.x = self.batch % 2, self.batch // 2
        self.z2, self.z1, self.y = self.blk // 4, (self.blk // 2) % 2, self.blk % 2
        self.hops = ["core", "x", "y", "z1", "z2", "join", "pair"]
        if not unit.early:
            self.hops = ["core", "y", "z1", "z2", "late", "pair"]

    def rows(self, top, core):
        return pl.ds(pl.multiple_of(top + core * self.unit.half, 16), self.unit.half)

    def lanes(self, left, x):
        u = self.unit
        if not u.early:
            return pl.ds(left, u.cols)
        return pl.ds(pl.multiple_of(left + x * (u.cols // 2), 128), u.cols // 2)

    def part(self, core):
        u = self.unit
        return self.source.at[:, :, :, self.rows(u.top, core), pl.ds(u.left, u.cols)]

    def inside(self, x):
        u = self.unit
        if u.inplace:
            return self.rows(u.top, self.core), self.lanes(u.left, x)
        return slice(None), self.lanes(0, x)

    def copy(self, s):
        hop = self.hops[s]
        u, acc, mine = self.unit, self.acc, self.inside(self.x)
        y, z1, z2 = self.y, self.z1, self.z2
        every = slice(None)
        where = {
            "core": at_batch(self.batch ^ 1),
            "pair": at_batch(self.batch ^ 1),
            "x": at_batch(self.batch ^ 2),
            "late": at_batch(self.batch ^ 2),
            "join": at_batch(self.batch ^ 2),
            "y": at_blk(self.blk ^ 1),
            "z1": at_blk(self.blk ^ 2),
            "z2": at_blk(self.blk ^ 4),
        }[hop]
        if hop in ("join", "pair"):
            lanes = pl.ds(u.result_left, u.cols)
            if hop == "join":
                lanes = self.lanes(u.result_left, self.x)
            source = target = self.result.at[self.rows(u.result_top, self.core), lanes]
        else:
            target = self.got[s]
            if hop == "core":
                source = self.part(1 - self.core)
            elif hop == "x":
                source = acc.at[(every, every, every) + self.inside(1 - self.x)]
            else:
                place = {
                    "y": (every, every, 1 - y),
                    "z1": (every, 1 - z1, y),
                    "z2": (1 - z2, z1, y),
                    "late": (z2, z1, y),
                }[hop]
                source = acc.at[place + mine]
        return remote(source, target, self.send.at[s], self.recv.at[s], where)

    def own(self):
        return pltpu.make_async_copy(self.part(self.core), self.acc, self.local)

    def start(self, s):
        if s == 0 and not self.unit.inplace:
            self.own().start()
        self.copy(s).start()

    def finish(self, s):
        hop = self.hops[s]
        acc, mine, every = self.acc, self.inside(self.x), (slice(None), slice(None))
        if s == 0 and not self.unit.inplace:
            self.own().wait()
        self.copy(s).wait_recv()
        pairs = [(a, b) for a in range(2) for b in range(2)]

        def add(place, other):
            acc[place] = (acc[place].astype(F32) + self.got[s][other].astype(F32)).astype(BF16)

        if hop in ("core", "x"):
            inside = mine
            if hop == "core" and self.unit.early:
                inside = (mine[0], pl.ds(self.unit.left if self.unit.inplace else 0, self.unit.cols))
            for a, b in pairs:
                for c in range(2):
                    add((a, b, c) + inside, (a, b, c) + every)
        elif hop == "y":
            for a, b in pairs:
                add((a, b, self.y) + mine, (a, b) + every)
        elif hop == "z1":
            for a in range(2):
                add((a, self.z1, self.y) + mine, (a,) + every)
        elif hop == "z2" and not self.unit.early:
            add((self.z2, self.z1, self.y) + mine, every)
        elif hop in ("z2", "late"):
            value = acc[(self.z2, self.z1, self.y) + mine].astype(F32) + self.got[s][...].astype(F32)
            u = self.unit
            self.result[self.rows(u.result_top, self.core), self.lanes(u.result_left, self.x)] = (
                value.astype(BF16)
            )

    def close(self):
        for s in range(len(self.hops)):
            self.copy(s).wait_send()


class Wave:
    def __init__(self, steps, got, send, recv):
        self.steps, self.got, self.send, self.recv = steps, got, send, recv
        batch, blk = lax.axis_index("batch"), lax.axis_index("blk")
        self.hops = [at_batch(batch ^ 1), at_batch(batch ^ 2), at_blk(blk ^ 1), at_blk(blk ^ 2), at_blk(blk ^ 4)]

    def copy(self, s):
        return remote(self.steps.at[s], self.got.at[s], self.send.at[s], self.recv.at[s], self.hops[s])

    def start(self, s):
        self.copy(s).start()

    def finish(self, s):
        self.copy(s).wait_recv()
        self.steps[s + 1] = self.steps[s] + self.got[s]

    def close(self):
        for s in range(len(self.hops)):
            self.copy(s).wait_send()


def run_round(routes, starts, t):
    for route, first in zip(routes, starts):
        s = t - first
        if 1 <= s <= len(route.hops):
            route.finish(s - 1)
        if 0 <= s < len(route.hops):
            route.start(s)


def rounds_of(routes, starts):
    return max(first + len(route.hops) for route, first in zip(routes, starts)) + 1


VECTORS = 16


def finish_kernel(n, tile, plan, *refs):
    (mixed_grad, weights, query, key, value, wq, wk, wv, bk, bv, normed, core, total, squeeze, low_x, middle_grad,
     gain, up_bias, sums, down_in, up_in, out_in) = refs[:22]
    home, *summed, vec_out = refs[22:29]
    (down_out, up_out, qkv_out, out_out, small_out, put, up, core_grad, lift, query_grad, key_grad, value_grad, small, ready, vectors, vec_got,
     own, send_d, recv_d, local, send, recv, vec_send, vec_recv) = refs[29:53]
    refs = refs[53:]
    units, early_starts, late_starts, early_rounds = plan
    i = pl.program_id(0)
    m, tokens = core.shape[0], low_x.shape[1]
    batch, me = lax.axis_index("batch"), lax.axis_index("blk")
    places = {
        "down": (down_in, down_out),
        "up": (up_in, up_out),
        "out": (out_in, out_out),
        "query": (query_grad, qkv_out),
        "key": (key_grad, qkv_out),
        "value": (value_grad, qkv_out),
        "small": (small, small_out),
    }
    routes = []
    for k, (name, unit) in enumerate(units):
        count = len(unit.scratch())
        buffers, refs = refs[:count], refs[count:]
        routes.append(Route(unit, *places[name], buffers, local.at[k], send.at[k], recv.at[k]))
    first, second = routes[: len(early_starts)], routes[len(early_starts) :]
    wave = Wave(vectors, vec_got, vec_send, vec_recv)

    @pl.when(i == 0)
    def _():
        greet([at_batch(batch ^ 1), at_batch(batch ^ 2)] + [at_blk(me ^ d) for d in range(1, n)])
        up[...] = jnp.zeros_like(up)
        core_grad[...] = jnp.zeros_like(core_grad)
        lift[...] = jnp.zeros_like(lift)
        vectors[0] = jnp.zeros(vectors.shape[1:], F32)

    done = 0
    for step, number in enumerate(early_rounds):
        @pl.when(i == step)
        def _(begin=done, number=number):
            for t in range(begin, begin + number):
                run_round(first, early_starts, t)
        done += number

    scale = 1.0 / math.sqrt(HD)
    keys = by_head(key[...] * jnp.asarray(scale, BF16))
    values = by_head(value[...])
    rows = mixed_grad.shape[0]
    dv = dk = None
    grads_q = []
    for r in range(rows // tile):
        at = slice(r * tile, (r + 1) * tile)
        grads = mixed_grad[at, :]
        back = contract(grads, values, 1, 1)
        low = weights[0, at, :]
        heads = []
        for h in range(LANES // HD):
            p = low[:, h * m : (h + 1) * m].astype(F32)
            g = back[:, h * m : (h + 1) * m]
            heads.append((p * (g - jnp.sum(p * g, axis=-1, keepdims=True))).astype(BF16))
        score = jnp.concatenate(heads, axis=1)
        part_v = own_head(contract(low, grads, 0, 0))
        part_k = own_head(contract(score, query[at, :], 0, 0))
        dv = part_v if dv is None else dv + part_v
        dk = part_k if dk is None else dk + part_k
        grads_q.append(contract(score, keys, 1, 0).astype(BF16))
    dq = jnp.concatenate(grads_q, axis=0)
    dk = dk * scale
    dk_low, dv_low = dk.astype(BF16), dv.astype(BF16)
    up[...] += contract(dq, wq[...], 1, 1)
    core_grad[...] += contract(dk_low, wk[...], 1, 1) + contract(dv_low, wv[...], 1, 1)
    lift[...] += jnp.sum(dk * bk[...] + dv * bv[...], axis=1, keepdims=True)
    lanes = pl.ds(pl.multiple_of(i * LANES, LANES), LANES)
    for target, grad in (
        (query_grad, contract(normed[...], dq, 0, 0)),
        (key_grad, contract(core[...], dk_low, 0, 0)),
        (value_grad, contract(core[...], dv_low, 0, 0)),
    ):
        block = grad.shape[0] // n
        for b in range(n):
            target[b // 4, (b // 2) % 2, b % 2, :, lanes] = grad[b * block : (b + 1) * block].astype(BF16)
    vectors[0, 2:3, lanes] = jnp.sum(dq.astype(F32), axis=0, keepdims=True)
    vectors[0, 3:4, lanes] = jnp.sum(total[...] * dk, axis=0, keepdims=True)
    vectors[0, 4:5, lanes] = jnp.sum(total[...] * dv, axis=0, keepdims=True)

    @pl.when(i == pl.num_programs(0) - 1)
    def _():
        width = low_x.shape[2]

        def ship(d):
            return remote(
                ready.at[me ^ d], home.at[me], send_d.at[d - 1], recv_d.at[d - 1], at_blk(me ^ d)
            )

        low_core = core_grad[...].astype(BF16)
        gain_sum = bias_sum = jnp.zeros((1, width), F32)
        mine = pltpu.make_async_copy(ready.at[me], home.at[me], own)
        for d in spread_order(n) + [0]:
            b = me ^ d
            at = pl.ds(pl.multiple_of(b * tokens, tokens), tokens)
            rise = up[at, :] + contract(squeeze[b], low_core, 0, 0)
            hat, rate = norm_stats(low_x[b].astype(F32))
            gain_sum += jnp.sum(rise * hat, axis=0, keepdims=True)
            bias_sum += jnp.sum(rise, axis=0, keepdims=True)
            ready[b] = (middle_grad[at, :] + norm_back(hat, rate, rise, gain[...])).astype(BF16)
            if d:
                ship(d).start()
            else:
                mine.start()
            terms = contract(low_core, normed[at, :], 1, 1) + lift[...]
            small[b // 4, (b // 2) % 2, b % 2] = terms.astype(BF16)
        vectors[0, 0:1, :] = gain_sum
        vectors[0, 1:2, :] = bias_sum
        vectors[0, 5:6, :] = sums[0:1, :]
        vectors[0, 6:7, :] = sums[1:2, :]
        vectors[0, 7:8, :] = sums[2:3, :]
        for k in range(up_bias.shape[1] // width):
            vectors[0, 8 + k : 9 + k, :] = up_bias[:, k * width : (k + 1) * width]
        vectors[0, 12:13, :] = sums[3:4, :]
        everyone = first + second + [wave]
        begins = [s - done for s in early_starts] + list(late_starts)
        for t in range(rounds_of(everyone, begins)):
            run_round(everyone, begins, t)
        puts = [
            pltpu.make_async_copy(source, target, put.at[k])
            for k, (source, target) in enumerate(
                zip((down_out, up_out, qkv_out, out_out, small_out), summed)
            )
        ]
        for copy in puts:
            copy.start()
        vec_out[...] = vectors[len(wave.hops)]
        for route in everyone:
            route.close()
        mine.wait()
        for d in range(1, n):
            ship(d).wait()
        for copy in puts:
            copy.wait()


def finish(mixed_grad, weights, query, key, value, normed, core, total, squeeze, low_x, middle_grad, gain,
           qkv_weight, qkv_bias, up_bias, sums, down, up, out, tile=512):
    n, m, tokens = squeeze.shape
    rows, width = normed.shape
    steps, heads = width // LANES, LANES // HD
    tall, hidden = width // n, up.shape[1]
    down = down.reshape(2, 2, 2, -1, width)
    up = up.reshape(2, 2, 2, tall, hidden)
    out = out.reshape(2, 2, 2, tall, width)
    downs = [("down", Unit(tall * k, 0, tall * k, 0, tall, width, False, False)) for k in range(hidden // width)]
    ups = [("up", Unit(0, width * k, 0, width * k, tall, width, True, False)) for k in range(hidden // width)]
    units = [unit for pair in zip(downs, ups) for unit in pair]
    units.append(("out", Unit(0, 0, 0, 0, tall, width, False, False)))
    early_starts = [k // 2 for k in range(len(units))]
    for k, name in enumerate(("query", "key", "value")):
        units.append((name, Unit(0, 0, 0, width * k, tall, width, k != 1, True)))
    units.append(("small", Unit(0, 0, 0, 0, m, tokens, False, True)))
    late_starts = [0, 0, 1, 1, 0]
    plan = (units, early_starts, late_starts, EARLY_ROUNDS)
    anywhere = pl.BlockSpec(memory_space=pl.ANY)
    vmem = pl.BlockSpec(memory_space=pltpu.VMEM)
    dma = pltpu.SemaphoreType.DMA
    blocks = (2, 2, 2, tall, width)
    results = [(hidden // n, width), (tall, hidden), (tall, 3 * width), (tall, width), (m, tokens)]
    scratch = [pltpu.VMEM(shape, BF16) for shape in results] + [
        dma((len(results),)),
        pltpu.VMEM((rows, width), F32),
        pltpu.VMEM((m, width), F32),
        pltpu.VMEM((m, 1), F32),
        pltpu.VMEM(blocks, BF16),
        pltpu.VMEM(blocks, BF16),
        pltpu.VMEM(blocks, BF16),
        pltpu.VMEM((2, 2, 2, m, tokens), BF16),
        pltpu.VMEM((n, tokens, width), BF16),
        pltpu.VMEM((6, VECTORS, width), F32),
        pltpu.VMEM((5, VECTORS, width), F32),
        dma,
        dma((n - 1,)),
        dma((n - 1,)),
        dma((len(units),)),
        dma((len(units), HOPS)),
        dma((len(units), HOPS)),
        dma((5,)),
        dma((5,)),
    ]
    for _, unit in units:
        scratch += unit.scratch()
    return pl.pallas_call(
        functools.partial(finish_kernel, n, tile, plan),
        grid=(steps,),
        in_specs=[
            columns(rows, 0),
            pl.BlockSpec((1, rows, heads * m), lambda i: (i, 0, 0)),
            columns(rows, 0),
            columns(m, 0),
            columns(m, 0),
        ]
        + [columns(width, k * steps) for k in range(3)]
        + [columns(1, k * steps) for k in range(1, 3)]
        + [
            whole((rows, width)),
            whole((m, width)),
            whole((m, 1)),
            whole((n, m, tokens)),
            whole((n, tokens, width)),
            whole((rows, width)),
            whole((1, width)),
            whole((1, hidden)),
            whole((4, width)),
            anywhere,
            anywhere,
            anywhere,
        ],
        out_specs=[anywhere] * (1 + len(results)) + [whole((VECTORS, width))],
        out_shape=[jax.ShapeDtypeStruct((n, tokens, width), BF16)]
        + [jax.ShapeDtypeStruct(shape, BF16) for shape in results]
        + [jax.ShapeDtypeStruct((VECTORS, width), F32)],
        scratch_shapes=scratch,
        compiler_params=pltpu.CompilerParams(
            collective_id=1, has_side_effects=True, vmem_limit_bytes=67043328, dimension_semantics=("arbitrary",)
        ),
        name="finish",
    )(mixed_grad, weights, query, key, value, qkv_weight, qkv_weight, qkv_weight, qkv_bias, qkv_bias, normed, core,
      total, squeeze, low_x, middle_grad, gain, up_bias, sums, down, up, out)


EARLY_ROUNDS = (1, 1, 1)


def swap(values, axis, size, bit):
    return lax.ppermute(values, axis, [(i, i ^ bit) for i in range(size)])


def halve(values, dim, axis, size, bit):
    mine = (lax.axis_index(axis) // bit) % 2
    send = lax.dynamic_index_in_dim(values, 1 - mine, dim, keepdims=False).astype(BF16)
    keep = lax.dynamic_index_in_dim(values, mine, dim, keepdims=False)
    return keep.astype(F32) + swap(send, axis, size, bit).astype(F32)


def join(values, dim, axis, size, bit):
    mine = (lax.axis_index(axis) // bit) % 2
    other = swap(values, axis, size, bit)
    first = jnp.where(mine == 0, values, other)
    second = jnp.where(mine == 0, other, values)
    return jnp.concatenate([first, second], axis=dim)


def scatter_sum(terms, bits, order, nb, nk, early):
    _, rows, cols = terms.shape
    values = halve(terms.reshape(-1, 2, rows // 2, cols), 1, "batch", nb, 1)
    chips = [1 << i for i in range(1, nb.bit_length() - 1)]
    if early:
        for bit in chips:
            cols //= 2
            values = halve(values.reshape(-1, rows // 2, 2, cols), 2, "batch", nb, bit)
    left = list(bits)
    for bit in order:
        place = left.index(bit)
        values = values.reshape(1 << place, 2, -1, rows // 2, cols)
        values = halve(values, 1, "blk", nk, bit)
        left.remove(bit)
    values = values.reshape(rows // 2, cols).astype(BF16)
    for bit in reversed(chips) if early else chips:
        if early:
            values = join(values, 1, "batch", nb, bit)
        else:
            values = (values.astype(F32) + swap(values, "batch", nb, bit).astype(F32)).astype(BF16)
    return join(values, 0, "batch", nb, 1).astype(F32)


def body(
    inputs,
    cotangent,
    group_counts,
    first_gain,
    first_bias,
    qkv_weight,
    qkv_bias,
    out_weight,
    out_bias,
    second_gain,
    second_bias,
    up_weight,
    up_bias,
    down_weight,
    down_bias,
    compress,
    *,
    nb,
    nk,
):
    slots, tokens, width = inputs.shape
    splits = nk // slots
    teams = [[t * slots + i for i in range(slots)] for t in range(splits)]
    across = [[t * slots + i for t in range(splits)] for i in range(slots)]
    rows = slots * tokens
    low_first = [1 << i for i in range(nk.bit_length() - 1)]
    high_first = low_first[::-1]
    team_low = [1 << i for i in range(slots.bit_length() - 1)]

    def gather_rows(values):
        return lax.all_to_all(values, "blk", 0, 0, axis_index_groups=teams, tiled=True).reshape(
            rows, width
        )

    def spread_rows(values):
        return lax.all_to_all(
            values.reshape(slots, tokens, width), "blk", 0, 0, axis_index_groups=teams, tiled=True
        )

    def over_splits(values):
        if splits == 1:
            return values
        return lax.psum(values, "blk", axis_index_groups=across)

    def line(vector):
        return vector.reshape(1, -1)

    slot = lax.axis_index("blk") % slots
    alive = (slot < group_counts[lax.axis_index("batch")]).astype(jnp.int32).reshape(1)

    compact = nb == 4 and nk == slots == 8
    if compact:
        low_x, normed, squeeze, core, total = arrive(
            inputs, compress, line(first_gain), line(first_bias)
        )
        low_x, normed = low_x.reshape(rows, width), normed.reshape(rows, width)
        cotangent, core = lax.optimization_barrier((cotangent, core))
        hat_first, rate_first = norm_stats(low_x.astype(F32))
    else:
        squeeze = compress[None]
        for bit in team_low[::-1]:
            squeeze = join(squeeze[:, None], 1, "blk", nk, bit)
            squeeze = squeeze.reshape((-1,) + compress.shape)
        low_x = gather_rows(inputs)
        hat_first, rate_first = norm_stats(low_x.astype(F32))
        normed = (hat_first * first_gain + first_bias).astype(BF16)
        core = jnp.einsum(
            "bjt,btc->jc",
            squeeze,
            normed.reshape(slots, tokens, width),
            preferred_element_type=F32,
        )
        total = jnp.sum(squeeze.astype(F32), axis=(0, 2))[:, None]
    low_cot = gather_rows(cotangent)
    core = over_splits(core).astype(BF16)
    total = over_splits(total)
    query, key, value, weights, mixed = attend(
        normed, core, total, qkv_weight, line(qkv_bias), tile=512
    )
    middle, second, active, slope, result = forward(
        alive,
        mixed,
        low_x,
        out_weight,
        line(out_bias),
        line(second_gain),
        line(second_bias),
        up_weight,
        line(up_bias),
        down_weight,
        line(down_bias),
    )
    output = spread_rows(result)
    up_grad, down_grad, up_bias_grad, middle_grad, mixed_grad, out_grad, sums = backward(
        alive,
        low_cot,
        active,
        slope,
        second,
        middle,
        mixed,
        up_weight,
        down_weight,
        out_weight,
        line(second_gain),
    )
    out_bias_grad, second_gain_grad, second_bias_grad, down_bias_grad = (sums[i] for i in range(4))
    if compact:
        input_grad, *summed = finish(
            mixed_grad,
            weights,
            query,
            key,
            value,
            normed,
            core,
            total,
            squeeze,
            low_x.reshape(slots, tokens, width),
            middle_grad,
            line(first_gain),
            qkv_weight,
            line(qkv_bias),
            up_bias_grad,
            sums,
            down_grad,
            up_grad,
            out_grad,
        )
        down_rows, up_rows, qkv_rows, out_rows, compress_rows, flat = (
            v.astype(F32) for v in summed
        )
        stretches = [(0, 1), (1, 1), (2, 3), (5, 1), (6, 1), (7, 1), (8, 4), (12, 1)]
        sizes = [count * width // nk for _, count in stretches]
        packed = jnp.concatenate(
            [flat[at : at + count].reshape(nk, -1) for at, count in stretches], axis=1
        )
        mine = lax.dynamic_index_in_dim(packed, lax.axis_index("blk"), 0, keepdims=False)
    else:
        (
            query_weight_grad,
            key_weight_grad,
            value_weight_grad,
            query_bias_grad,
            key_bias_grad,
            value_bias_grad,
            query_up,
            core_back,
            lift,
        ) = attend_back(
            mixed_grad, weights, query, key, value, normed, core, total, qkv_weight, line(qkv_bias)
        )
        core_back = over_splits(core_back).astype(BF16)
        lift = over_splits(lift)
        first_up = query_up + jnp.einsum(
            "bjt,jc->btc", squeeze, core_back, preferred_element_type=F32
        ).reshape(rows, width)
        first_gain_grad = jnp.sum(first_up * hat_first, axis=0)
        first_bias_grad = jnp.sum(first_up, axis=0)
        rows_grad = (
            middle_grad + norm_back(hat_first, rate_first, first_up, first_gain)
        ).astype(BF16)
        compress_terms = (
            jnp.einsum(
                "jc,btc->bjt",
                core_back,
                normed.reshape(slots, tokens, width),
                preferred_element_type=F32,
            )
            + lift[None]
        )

        vectors = (
            first_gain_grad,
            first_bias_grad,
            jnp.concatenate([query_bias_grad, key_bias_grad, value_bias_grad], axis=1),
            out_bias_grad,
            second_gain_grad,
            second_bias_grad,
            up_bias_grad,
            down_bias_grad,
        )
        sizes = [v.size // nk for v in vectors]
        packed = jnp.concatenate([v.reshape(nk, -1) for v in vectors], axis=1)
        tall = 32
        wide = -(-sum(sizes) // (tall * 128)) * 128
        packed = jnp.pad(packed, ((0, 0), (0, tall * wide - sum(sizes)))).reshape(nk, tall, wide)
        blocked = [
            grad.reshape(nk, grad.shape[0] // nk, grad.shape[1])
            for grad in (
                down_grad,
                up_grad,
                query_weight_grad,
                key_weight_grad,
                value_weight_grad,
                out_grad,
            )
        ]
        input_grad = spread_rows(rows_grad)
        blocked = blocked[:2] + [jnp.concatenate(blocked[2:], axis=2)]
        down_rows, up_rows, joined = (
            scatter_sum(grad, high_first, low_first, nb, nk, i > 0)
            for i, grad in enumerate(blocked)
        )
        qkv_rows, out_rows = joined[:, : 3 * width], joined[:, 3 * width :]
        compress_rows = scatter_sum(compress_terms, team_low[::-1], team_low, nb, nk, False)
        mine = scatter_sum(packed, high_first, low_first, nb, nk, False).reshape(-1)
    parts = []
    start = 0
    for size in sizes:
        parts.append(mine[start : start + size])
        start += size
    fg, fb, qb, ob, sg, sb, ub, db = parts
    return (
        output,
        input_grad,
        fg,
        fb,
        qkv_rows,
        qb,
        out_rows,
        ob,
        sg,
        sb,
        up_rows,
        ub,
        down_rows,
        db,
        compress_rows,
    )


def solution(mesh):
    rows = P("batch", "blk", None)
    placed = (rows, rows) + (P(),) * 13 + (P(None, "blk"),)
    vec, mat = P("blk"), P("blk", None)
    return jax.shard_map(
        functools.partial(body, nb=mesh.shape["batch"], nk=mesh.shape["blk"]),
        mesh=mesh,
        in_specs=placed,
        out_specs=(rows, rows, vec, vec, mat, vec, mat, vec, vec, vec, mat, vec, mat, vec)
        + (P(None, "blk"),),
        check_vma=False,
    )
```

```python
import functools
import math

import jax
import jax.numpy as jnp
from jax import lax
from jax.experimental import pallas as pl
from jax.experimental.pallas import tpu as pltpu
from jax.sharding import PartitionSpec as P

F32 = jnp.float32
BF16 = jnp.bfloat16
HD = 64
LANES = 256
GELU_A = math.sqrt(2.0 / math.pi)
GELU_B = 0.044715


def norm_stats(states):
    center = states - jnp.mean(states, axis=-1, keepdims=True)
    spread = jnp.mean(center * center, axis=-1, keepdims=True)
    rate = lax.rsqrt(spread + 1e-05)
    return center * rate, rate


def norm_back(hat, rate, upstream, gain):
    scaled = upstream * gain
    return rate * (
        scaled
        - jnp.mean(scaled, axis=-1, keepdims=True)
        - hat * jnp.mean(scaled * hat, axis=-1, keepdims=True)
    )


def contract(a, b, dim_a, dim_b):
    return lax.dot_general(a, b, (((dim_a,), (dim_b,)), ((), ())), preferred_element_type=F32)


def whole(shape):
    return pl.BlockSpec(shape, lambda *_: (0,) * len(shape), pipeline_mode=pl.Buffered(1))


def columns(height, start, width=LANES):
    return pl.BlockSpec((height, width), lambda i: (0, start + i))


def below(width, start, height=LANES):
    return pl.BlockSpec((height, width), lambda i: (start + i, 0))


PARAMS = dict(vmem_limit_bytes=62 << 20, dimension_semantics=("arbitrary",))


def by_head(values):
    lane = lax.broadcasted_iota(jnp.int32, values.shape, 1) // HD
    zero = jnp.zeros_like(values)
    return jnp.concatenate([jnp.where(lane == h, values, zero) for h in range(LANES // HD)], axis=0)


def own_head(values):
    n = values.shape[0] // (LANES // HD)
    lane = lax.broadcasted_iota(jnp.int32, (n, LANES), 1) // HD
    picked = values[:n]
    for h in range(1, LANES // HD):
        picked = jnp.where(lane == h, values[h * n : (h + 1) * n], picked)
    return picked


def attend_kernel(tile, normed, core, total, wq, wk, wv, bq, bk, bv, query, key, value, weights, mixed):
    rows, n = normed.shape[0], core.shape[0]
    key[...] = (contract(core[...], wk[...], 1, 0) + total[...] * bk[...]).astype(BF16)
    value[...] = (contract(core[...], wv[...], 1, 0) + total[...] * bv[...]).astype(BF16)
    keys = by_head(key[...] * jnp.asarray(1.0 / math.sqrt(HD), BF16))
    values = by_head(value[...])

    for r in range(rows // tile):
        at = slice(r * tile, (r + 1) * tile)
        q = (contract(normed[at, :], wq[...], 1, 0) + bq[...]).astype(BF16)
        query[at, :] = q
        scores = contract(q, keys, 1, 1)
        heads = []
        for h in range(LANES // HD):
            s = scores[:, h * n : (h + 1) * n]
            e = jnp.exp(s - jnp.max(s, axis=-1, keepdims=True))
            heads.append((e * (1.0 / jnp.sum(e, axis=-1, keepdims=True))).astype(BF16))
        low = jnp.concatenate(heads, axis=1)
        weights[0, at, :] = low
        mixed[at, :] = contract(low, values, 1, 0).astype(BF16)


def attend(normed, core, total, qkv_weight, qkv_bias, tile=1024):
    rows, width = normed.shape
    n = core.shape[0]
    steps = width // LANES
    heads = LANES // HD
    return pl.pallas_call(
        functools.partial(attend_kernel, tile),
        grid=(steps,),
        in_specs=[whole((rows, width)), whole((n, width)), whole((n, 1))]
        + [columns(width, k * steps) for k in range(3)]
        + [columns(1, k * steps) for k in range(3)],
        out_specs=[
            columns(rows, 0),
            columns(n, 0),
            columns(n, 0),
            pl.BlockSpec((1, rows, heads * n), lambda i: (i, 0, 0)),
            columns(rows, 0),
        ],
        out_shape=[
            jax.ShapeDtypeStruct((rows, width), BF16),
            jax.ShapeDtypeStruct((n, width), BF16),
            jax.ShapeDtypeStruct((n, width), BF16),
            jax.ShapeDtypeStruct((steps, rows, heads * n), BF16),
            jax.ShapeDtypeStruct((rows, width), BF16),
        ],
        compiler_params=pltpu.CompilerParams(**PARAMS),
        name="attend",
    )(normed, core, total, qkv_weight, qkv_weight, qkv_weight, qkv_bias, qkv_bias, qkv_bias)


def forward_kernel(tile, alive, mixed, states, ow, ob, gain, bias, upw, upb, dnw, dnb,
                   middle, second, active, slope, output, total):
    f = pl.program_id(0)
    rows = mixed.shape[0]

    @pl.when(f == 0)
    def _():
        mid = states[...].astype(F32) + contract(mixed[...], ow[...], 1, 0) + ob[...]
        middle[...] = mid
        second[...] = (norm_stats(mid)[0] * gain[...] + bias[...]).astype(BF16)
        total[...] = mid + dnb[...]

    for r in range(rows // tile):
        at = slice(r * tile, (r + 1) * tile)
        v = contract(second[at, :], upw[...], 1, 0) + upb[...]
        square = v * v
        t = jnp.tanh(v * (GELU_A + (GELU_A * GELU_B) * square))
        half = 0.5 + 0.5 * t
        act = (v * half).astype(BF16)
        active[at, :] = act
        slope[at, :] = (
            half + (0.5 * v) * (1.0 - t * t) * (GELU_A + (3 * GELU_A * GELU_B) * square)
        ).astype(BF16)
        total[at, :] += contract(act, dnw[...], 1, 0)

    @pl.when(f == pl.num_programs(0) - 1)
    def _():
        output[...] = jnp.where(alive[0] > 0, total[...], 0.0).astype(BF16)


def forward(alive, mixed, states, ow, ob, gain, bias, upw, upb, dnw, dnb, block=512, tile=1024):
    rows, width = mixed.shape
    hidden = upw.shape[1]
    vec = whole((1, width))
    return pl.pallas_call(
        functools.partial(forward_kernel, tile),
        grid=(hidden // block,),
        in_specs=[
            pl.BlockSpec(memory_space=pltpu.SMEM),
            whole((rows, width)),
            whole((rows, width)),
            whole((width, width)),
            vec,
            vec,
            vec,
            columns(width, 0, block),
            columns(1, 0, block),
            below(width, 0, block),
            vec,
        ],
        out_specs=[
            whole((rows, width)),
            whole((rows, width)),
            columns(rows, 0, block),
            columns(rows, 0, block),
            whole((rows, width)),
        ],
        out_shape=[
            jax.ShapeDtypeStruct((rows, width), F32),
            jax.ShapeDtypeStruct((rows, width), BF16),
            jax.ShapeDtypeStruct((rows, hidden), BF16),
            jax.ShapeDtypeStruct((rows, hidden), BF16),
            jax.ShapeDtypeStruct((rows, width), BF16),
        ],
        scratch_shapes=[pltpu.VMEM((rows, width), F32)],
        compiler_params=pltpu.CompilerParams(**PARAMS),
        name="forward",
    )(alive, mixed, states, ow, ob, gain, bias, upw, upb, dnw, dnb)


def backward_kernel(alive, cot, active, slope, second, middle, mixed, upw, dnw, ow, gain,
                    up_grad, down_grad, up_bias_grad, middle_grad, mixed_grad, out_grad, sums,
                    incoming, total):
    f = pl.program_id(0)

    @pl.when(f == 0)
    def _():
        incoming[...] = jnp.where(alive[0] > 0, cot[...], jnp.zeros_like(cot))
        total[...] = jnp.zeros_like(total)

    d = contract(incoming[...], dnw[...], 1, 1)
    dh = (d * slope[...].astype(F32)).astype(BF16)
    up_bias_grad[...] = jnp.sum(dh.astype(F32), axis=0, keepdims=True)
    total[...] += contract(dh, upw[...], 1, 1)
    down_grad[...] = contract(active[...], incoming[...], 0, 0).astype(BF16)
    up_grad[...] = contract(second[...], dh, 0, 0).astype(BF16)

    @pl.when(f == pl.num_programs(0) - 1)
    def _():
        hat, rate = norm_stats(middle[...])
        up = total[...]
        inc = incoming[...].astype(F32)
        grad = inc + norm_back(hat, rate, up, gain[...])
        middle_grad[...] = grad
        branch = grad.astype(BF16)
        mixed_grad[...] = contract(branch, ow[...], 1, 1).astype(BF16)
        out_grad[...] = contract(mixed[...], branch, 0, 0).astype(BF16)
        sums[0:1, :] = jnp.sum(branch.astype(F32), axis=0, keepdims=True)
        sums[1:2, :] = jnp.sum(up * hat, axis=0, keepdims=True)
        sums[2:3, :] = jnp.sum(up, axis=0, keepdims=True)
        sums[3:4, :] = jnp.sum(inc, axis=0, keepdims=True)


def backward(alive, cot, active, slope, second, middle, mixed, upw, dnw, ow, gain, block=512):
    rows, width = mixed.shape
    hidden = upw.shape[1]
    return pl.pallas_call(
        backward_kernel,
        grid=(hidden // block,),
        in_specs=[
            pl.BlockSpec(memory_space=pltpu.SMEM),
            whole((rows, width)),
            columns(rows, 0, block),
            columns(rows, 0, block),
            whole((rows, width)),
            whole((rows, width)),
            whole((rows, width)),
            columns(width, 0, block),
            below(width, 0, block),
            whole((width, width)),
            whole((1, width)),
        ],
        out_specs=[
            columns(width, 0, block),
            below(width, 0, block),
            columns(1, 0, block),
            whole((rows, width)),
            whole((rows, width)),
            whole((width, width)),
            whole((4, width)),
        ],
        out_shape=[
            jax.ShapeDtypeStruct((width, hidden), BF16),
            jax.ShapeDtypeStruct((hidden, width), BF16),
            jax.ShapeDtypeStruct((1, hidden), F32),
            jax.ShapeDtypeStruct((rows, width), F32),
            jax.ShapeDtypeStruct((rows, width), BF16),
            jax.ShapeDtypeStruct((width, width), BF16),
            jax.ShapeDtypeStruct((4, width), F32),
        ],
        scratch_shapes=[pltpu.VMEM((rows, width), BF16), pltpu.VMEM((rows, width), F32)],
        compiler_params=pltpu.CompilerParams(**PARAMS),
        name="backward",
    )(alive, cot, active, slope, second, middle, mixed, upw, dnw, ow, gain)


def attend_back_kernel(mixed_grad, weights, query, key, value, normed, core, total, wq, wk, wv, bk, bv,
                       query_grad, key_grad, value_grad, qb, kb, vb, up, core_grad, lift):
    i = pl.program_id(0)
    n = core.shape[0]

    @pl.when(i == 0)
    def _():
        up[...] = jnp.zeros_like(up)
        core_grad[...] = jnp.zeros_like(core_grad)
        lift[...] = jnp.zeros_like(lift)

    keys = by_head(key[...] * jnp.asarray(1.0 / math.sqrt(HD), BF16))
    values = by_head(value[...])
    grads = mixed_grad[...]
    back = contract(grads, values, 1, 1)
    heads = []
    for h in range(LANES // HD):
        p = weights[0, :, h * n : (h + 1) * n].astype(F32)
        g = back[:, h * n : (h + 1) * n]
        heads.append((p * (g - jnp.sum(p * g, axis=-1, keepdims=True))).astype(BF16))
    score = jnp.concatenate(heads, axis=1)
    dv = own_head(contract(weights[0], grads, 0, 0))
    dk = own_head(contract(score, query[...], 0, 0)) * (1.0 / math.sqrt(HD))
    dq = contract(score, keys, 1, 0).astype(BF16)
    dk_low, dv_low = dk.astype(BF16), dv.astype(BF16)
    up[...] += contract(dq, wq[...], 1, 1)
    core_grad[...] += contract(dk_low, wk[...], 1, 1) + contract(dv_low, wv[...], 1, 1)
    lift[...] += jnp.sum(dk * bk[...] + dv * bv[...], axis=1, keepdims=True)
    query_grad[...] = contract(normed[...], dq, 0, 0).astype(BF16)
    key_grad[...] = contract(core[...], dk_low, 0, 0).astype(BF16)
    value_grad[...] = contract(core[...], dv_low, 0, 0).astype(BF16)
    qb[...] = jnp.sum(dq.astype(F32), axis=0, keepdims=True)
    kb[...] = jnp.sum(total[...] * dk, axis=0, keepdims=True)
    vb[...] = jnp.sum(total[...] * dv, axis=0, keepdims=True)


def attend_back(mixed_grad, weights, query, key, value, normed, core, total, qkv_weight, qkv_bias):
    rows, width = normed.shape
    n = core.shape[0]
    steps = width // LANES
    heads = LANES // HD
    return pl.pallas_call(
        attend_back_kernel,
        grid=(steps,),
        in_specs=[
            columns(rows, 0),
            pl.BlockSpec((1, rows, heads * n), lambda i: (i, 0, 0)),
            columns(rows, 0),
            columns(n, 0),
            columns(n, 0),
            whole((rows, width)),
            whole((n, width)),
            whole((n, 1)),
        ]
        + [columns(width, k * steps) for k in range(3)]
        + [columns(1, k * steps) for k in range(1, 3)],
        out_specs=[columns(width, 0)] * 3
        + [columns(1, 0)] * 3
        + [whole((rows, width)), whole((n, width)), whole((n, 1))],
        out_shape=[jax.ShapeDtypeStruct((width, width), BF16)] * 3
        + [jax.ShapeDtypeStruct((1, width), F32)] * 3
        + [
            jax.ShapeDtypeStruct((rows, width), F32),
            jax.ShapeDtypeStruct((n, width), F32),
            jax.ShapeDtypeStruct((n, 1), F32),
        ],
        compiler_params=pltpu.CompilerParams(**PARAMS),
        name="attend_back",
    )(mixed_grad, weights, query, key, value, normed, core, total, qkv_weight, qkv_weight, qkv_weight, qkv_bias, qkv_bias)


MESH = pl.DeviceIdType.MESH


def at_batch(other):
    return {"batch": other}


def at_blk(other):
    return {"blk": other}


def remote(source, target, send, arrive, where):
    return pltpu.make_async_remote_copy(
        src_ref=source, dst_ref=target, send_sem=send, recv_sem=arrive, device_id=where, device_id_type=MESH
    )


def greet(places):
    barrier = pltpu.get_barrier_semaphore()
    for where in places:
        pl.semaphore_signal(barrier, inc=1, device_id=where, device_id_type=MESH)
    pl.semaphore_wait(barrier, len(places))


def spread_order(n):
    return sorted(range(1, n), key=lambda d: (-(d & (n // 2)), d))


class Unit:
    def __init__(self, top, left, result_top, result_left, rows, cols, early, inplace, lead=0):
        self.lead = lead
        self.top, self.left = top, left
        self.result_top, self.result_left = result_top, result_left
        self.half, self.cols = rows // 2, cols
        self.early, self.inplace = early, inplace

    def scratch(self):
        h, c = self.half, self.cols
        narrow = c // 2 if self.early else c
        shapes = [] if self.inplace else [(2, 2, 2, h, c)]
        shapes.append((2, 2, 2, h, c))
        if self.early:
            shapes.append((2, 2, 2, h, narrow))
        shapes += [(2, 2, h, narrow), (2, h, narrow), (h, narrow)]
        if not self.early:
            shapes.append((h, c))
        return [pltpu.VMEM(shape, BF16) for shape in shapes]


HOPS = 7


class Route:
    def __init__(self, unit, source, result, buffers, local, send, recv):
        self.unit, self.source, self.result = unit, source, result
        self.acc, self.got = (source, buffers) if unit.inplace else (buffers[0], buffers[1:])
        self.local, self.send, self.recv = local, send, recv
        self.batch, self.blk = lax.axis_index("batch"), lax.axis_index("blk")
        self.core, self.x = self.batch % 2, self.batch // 2
        self.z2, self.z1, self.y = self.blk // 4, (self.blk // 2) % 2, self.blk % 2
        self.hops = ["core", "x", "y", "z1", "z2", "join", "pair"]
        if not unit.early:
            self.hops = ["core", "y", "z1", "z2", "late", "pair"]

    def rows(self, top, core):
        return pl.ds(pl.multiple_of(top + core * self.unit.half, 16), self.unit.half)

    def lanes(self, left, x):
        u = self.unit
        if not u.early:
            return pl.ds(left, u.cols)
        return pl.ds(pl.multiple_of(left + x * (u.cols // 2), 128), u.cols // 2)

    def part(self, core):
        u = self.unit
        return self.source.at[:, :, :, self.rows(u.top, core), pl.ds(u.left, u.cols)]

    def inside(self, x):
        u = self.unit
        if u.inplace:
            return self.rows(u.top, self.core), self.lanes(u.left, x)
        return slice(None), self.lanes(0, x)

    def copy(self, s):
        hop = self.hops[s]
        u, acc, mine = self.unit, self.acc, self.inside(self.x)
        y, z1, z2 = self.y, self.z1, self.z2
        every = slice(None)
        where = {
            "core": at_batch(self.batch ^ 1),
            "pair": at_batch(self.batch ^ 1),
            "x": at_batch(self.batch ^ 2),
            "late": at_batch(self.batch ^ 2),
            "join": at_batch(self.batch ^ 2),
            "y": at_blk(self.blk ^ 1),
            "z1": at_blk(self.blk ^ 2),
            "z2": at_blk(self.blk ^ 4),
        }[hop]
        if hop in ("join", "pair"):
            lanes = pl.ds(u.result_left, u.cols)
            if hop == "join":
                lanes = self.lanes(u.result_left, self.x)
            source = target = self.result.at[self.rows(u.result_top, self.core), lanes]
        else:
            target = self.got[s]
            if hop == "core":
                source = self.part(1 - self.core)
            elif hop == "x":
                source = acc.at[(every, every, every) + self.inside(1 - self.x)]
            else:
                place = {
                    "y": (every, every, 1 - y),
                    "z1": (every, 1 - z1, y),
                    "z2": (1 - z2, z1, y),
                    "late": (z2, z1, y),
                }[hop]
                source = acc.at[place + mine]
        return remote(source, target, self.send.at[s], self.recv.at[s], where)

    def own(self):
        return pltpu.make_async_copy(self.part(self.core), self.acc, self.local)

    def start(self, s):
        if s == 0 and not self.unit.inplace:
            self.own().start()
        self.copy(s).start()

    def finish(self, s):
        hop = self.hops[s]
        acc, mine, every = self.acc, self.inside(self.x), (slice(None), slice(None))
        if s == 0 and not self.unit.inplace:
            self.own().wait()
        self.copy(s).wait_recv()
        pairs = [(a, b) for a in range(2) for b in range(2)]

        def add(place, other):
            acc[place] = (acc[place].astype(F32) + self.got[s][other].astype(F32)).astype(BF16)

        if hop in ("core", "x"):
            inside = mine
            if hop == "core" and self.unit.early:
                inside = (mine[0], pl.ds(self.unit.left if self.unit.inplace else 0, self.unit.cols))
            for a, b in pairs:
                for c in range(2):
                    add((a, b, c) + inside, (a, b, c) + every)
        elif hop == "y":
            for a, b in pairs:
                add((a, b, self.y) + mine, (a, b) + every)
        elif hop == "z1":
            for a in range(2):
                add((a, self.z1, self.y) + mine, (a,) + every)
        elif hop == "z2" and not self.unit.early:
            add((self.z2, self.z1, self.y) + mine, every)
        elif hop in ("z2", "late"):
            value = acc[(self.z2, self.z1, self.y) + mine].astype(F32) + self.got[s][...].astype(F32)
            u = self.unit
            self.result[self.rows(u.result_top, self.core), self.lanes(u.result_left, self.x)] = (
                value.astype(BF16)
            )

    def close(self):
        for s in range(len(self.hops)):
            self.copy(s).wait_send()


class Wave:
    def __init__(self, steps, got, send, recv):
        self.steps, self.got, self.send, self.recv = steps, got, send, recv
        batch, blk = lax.axis_index("batch"), lax.axis_index("blk")
        self.hops = [at_batch(batch ^ 1), at_batch(batch ^ 2), at_blk(blk ^ 1), at_blk(blk ^ 2), at_blk(blk ^ 4)]

    def copy(self, s):
        return remote(self.steps.at[s], self.got.at[s], self.send.at[s], self.recv.at[s], self.hops[s])

    def start(self, s):
        self.copy(s).start()

    def finish(self, s):
        self.copy(s).wait_recv()
        self.steps[s + 1] = self.steps[s] + self.got[s]

    def close(self):
        for s in range(len(self.hops)):
            self.copy(s).wait_send()


def run_round(routes, starts, t):
    for route, first in zip(routes, starts):
        s = t - first
        if 1 <= s <= len(route.hops):
            route.finish(s - 1)
        if 0 <= s < len(route.hops):
            route.start(s)


def rounds_of(routes, starts):
    return max(first + len(route.hops) for route, first in zip(routes, starts)) + 1


VECTORS = 16


def finish_kernel(n, tile, plan, *refs):
    (mixed_grad, weights, query, key, value, wq, wk, wv, bk, bv, normed, core, total, squeeze, low_x, middle_grad,
     gain, up_bias, sums, down_in, up_in, out_in) = refs[:22]
    home, *summed, vec_out = refs[22:29]
    (down_out, up_out, qkv_out, out_out, small_out, put, up, core_grad, lift, query_grad, key_grad, value_grad, small, ready, vectors, vec_got,
     own, send_d, recv_d, local, send, recv, vec_send, vec_recv) = refs[29:53]
    refs = refs[53:]
    units, early_starts, late_starts, early_rounds = plan
    i = pl.program_id(0)
    m, tokens = core.shape[0], low_x.shape[1]
    batch, me = lax.axis_index("batch"), lax.axis_index("blk")
    places = {
        "out": (out_in, out_out),
        "query": (query_grad, qkv_out),
        "key": (key_grad, qkv_out),
        "value": (value_grad, qkv_out),
        "small": (small, small_out),
    }
    routes = []
    for k, (name, unit) in enumerate(units):
        count = len(unit.scratch())
        buffers, refs = refs[:count], refs[count:]
        if name == "down" or name == "up":
            source, result = (down_in, down_out) if name == "down" else (up_in, up_out)
            source = source.at[unit.lead]
        else:
            source, result = places[name]
        routes.append(Route(unit, source, result, buffers, local.at[k], send.at[k], recv.at[k]))
    first, second = routes[: len(early_starts)], routes[len(early_starts) :]
    wave = Wave(vectors, vec_got, vec_send, vec_recv)

    @pl.when(i == 0)
    def _():
        greet([at_batch(batch ^ 1), at_batch(batch ^ 2)] + [at_blk(me ^ d) for d in range(1, n)])
        up[...] = jnp.zeros_like(up)
        core_grad[...] = jnp.zeros_like(core_grad)
        lift[...] = jnp.zeros_like(lift)
        vectors[0] = jnp.zeros(vectors.shape[1:], F32)

    done = 0
    for step, number in enumerate(early_rounds):
        @pl.when(i == step)
        def _(begin=done, number=number):
            for t in range(begin, begin + number):
                run_round(first, early_starts, t)
        done += number

    scale = 1.0 / math.sqrt(HD)
    keys = by_head(key[...] * jnp.asarray(scale, BF16))
    values = by_head(value[...])
    rows = mixed_grad.shape[0]
    dv = dk = None
    grads_q = []
    for r in range(rows // tile):
        at = slice(r * tile, (r + 1) * tile)
        grads = mixed_grad[at, :]
        back = contract(grads, values, 1, 1)
        low = weights[0, at, :]
        heads = []
        for h in range(LANES // HD):
            p = low[:, h * m : (h + 1) * m].astype(F32)
            g = back[:, h * m : (h + 1) * m]
            heads.append((p * (g - jnp.sum(p * g, axis=-1, keepdims=True))).astype(BF16))
        score = jnp.concatenate(heads, axis=1)
        part_v = own_head(contract(low, grads, 0, 0))
        part_k = own_head(contract(score, query[at, :], 0, 0))
        dv = part_v if dv is None else dv + part_v
        dk = part_k if dk is None else dk + part_k
        grads_q.append(contract(score, keys, 1, 0).astype(BF16))
    dq = jnp.concatenate(grads_q, axis=0)
    dk = dk * scale
    dk_low, dv_low = dk.astype(BF16), dv.astype(BF16)
    up[...] += contract(dq, wq[...], 1, 1)
    core_grad[...] += contract(dk_low, wk[...], 1, 1) + contract(dv_low, wv[...], 1, 1)
    lift[...] += jnp.sum(dk * bk[...] + dv * bv[...], axis=1, keepdims=True)
    lanes = pl.ds(pl.multiple_of(i * LANES, LANES), LANES)
    for target, grad in (
        (query_grad, contract(normed[...], dq, 0, 0)),
        (key_grad, contract(core[...], dk_low, 0, 0)),
        (value_grad, contract(core[...], dv_low, 0, 0)),
    ):
        block = grad.shape[0] // n
        for b in range(n):
            target[b // 4, (b // 2) % 2, b % 2, :, lanes] = grad[b * block : (b + 1) * block].astype(BF16)
    vectors[0, 2:3, lanes] = jnp.sum(dq.astype(F32), axis=0, keepdims=True)
    vectors[0, 3:4, lanes] = jnp.sum(total[...] * dk, axis=0, keepdims=True)
    vectors[0, 4:5, lanes] = jnp.sum(total[...] * dv, axis=0, keepdims=True)

    @pl.when(i == pl.num_programs(0) - 1)
    def _():
        width = low_x.shape[2]

        def ship(d):
            return remote(
                ready.at[me ^ d], home.at[me], send_d.at[d - 1], recv_d.at[d - 1], at_blk(me ^ d)
            )

        low_core = core_grad[...].astype(BF16)
        gain_sum = bias_sum = jnp.zeros((1, width), F32)
        mine = pltpu.make_async_copy(ready.at[me], home.at[me], own)
        for d in spread_order(n) + [0]:
            b = me ^ d
            at = pl.ds(pl.multiple_of(b * tokens, tokens), tokens)
            rise = up[at, :] + contract(squeeze[b], low_core, 0, 0)
            hat, rate = norm_stats(low_x[b].astype(F32))
            gain_sum += jnp.sum(rise * hat, axis=0, keepdims=True)
            bias_sum += jnp.sum(rise, axis=0, keepdims=True)
            ready[b] = (middle_grad[at, :] + norm_back(hat, rate, rise, gain[...])).astype(BF16)
            if d:
                ship(d).start()
            else:
                mine.start()
            terms = contract(low_core, normed[at, :], 1, 1) + lift[...]
            small[b // 4, (b // 2) % 2, b % 2] = terms.astype(BF16)
        vectors[0, 0:1, :] = gain_sum
        vectors[0, 1:2, :] = bias_sum
        vectors[0, 5:6, :] = sums[0:1, :]
        vectors[0, 6:7, :] = sums[1:2, :]
        vectors[0, 7:8, :] = sums[2:3, :]
        for k in range(up_bias.shape[1] // width):
            vectors[0, 8 + k : 9 + k, :] = up_bias[:, k * width : (k + 1) * width]
        vectors[0, 12:13, :] = sums[3:4, :]
        everyone = first + second + [wave]
        begins = [s - done for s in early_starts] + list(late_starts)
        for t in range(rounds_of(everyone, begins)):
            run_round(everyone, begins, t)
        puts = [
            pltpu.make_async_copy(source, target, put.at[k])
            for k, (source, target) in enumerate(
                zip((down_out, up_out, qkv_out, out_out, small_out), summed)
            )
        ]
        for copy in puts:
            copy.start()
        vec_out[...] = vectors[len(wave.hops)]
        for route in everyone:
            route.close()
        mine.wait()
        for d in range(1, n):
            ship(d).wait()
        for copy in puts:
            copy.wait()


def finish(mixed_grad, weights, query, key, value, normed, core, total, squeeze, low_x, middle_grad, gain,
           qkv_weight, qkv_bias, up_bias, sums, down, up, out, tile=512):
    n, m, tokens = squeeze.shape
    rows, width = normed.shape
    steps, heads = width // LANES, LANES // HD
    tall = width // n
    feeds, block = up.shape[0], up.shape[2]
    hidden = feeds * block
    down = down.reshape(feeds, 2, 2, 2, -1, width)
    deep = down.shape[4]
    up = up.reshape(feeds, 2, 2, 2, tall, block)
    out = out.reshape(2, 2, 2, tall, width)
    downs = [("down", Unit(0, 0, deep * k, 0, deep, width, False, False, k)) for k in range(feeds)]
    ups = [("up", Unit(0, 0, 0, block * k, tall, block, True, False, k)) for k in range(feeds)]
    units = [unit for pair in zip(downs, ups) for unit in pair]
    units.append(("out", Unit(0, 0, 0, 0, tall, width, False, False)))
    early_starts = [k // 2 for k in range(len(units))]
    for k, name in enumerate(("query", "key", "value")):
        units.append((name, Unit(0, 0, 0, width * k, tall, width, k != 1, True)))
    units.append(("small", Unit(0, 0, 0, 0, m, tokens, False, True)))
    late_starts = [0, 0, 1, 1, 0]
    plan = (units, early_starts, late_starts, EARLY_ROUNDS)
    anywhere = pl.BlockSpec(memory_space=pl.ANY)
    vmem = pl.BlockSpec(memory_space=pltpu.VMEM)
    dma = pltpu.SemaphoreType.DMA
    blocks = (2, 2, 2, tall, width)
    results = [(hidden // n, width), (tall, hidden), (tall, 3 * width), (tall, width), (m, tokens)]
    scratch = [pltpu.VMEM(shape, BF16) for shape in results] + [
        dma((len(results),)),
        pltpu.VMEM((rows, width), F32),
        pltpu.VMEM((m, width), F32),
        pltpu.VMEM((m, 1), F32),
        pltpu.VMEM(blocks, BF16),
        pltpu.VMEM(blocks, BF16),
        pltpu.VMEM(blocks, BF16),
        pltpu.VMEM((2, 2, 2, m, tokens), BF16),
        pltpu.VMEM((n, tokens, width), BF16),
        pltpu.VMEM((6, VECTORS, width), F32),
        pltpu.VMEM((5, VECTORS, width), F32),
        dma,
        dma((n - 1,)),
        dma((n - 1,)),
        dma((len(units),)),
        dma((len(units), HOPS)),
        dma((len(units), HOPS)),
        dma((5,)),
        dma((5,)),
    ]
    for _, unit in units:
        scratch += unit.scratch()
    return pl.pallas_call(
        functools.partial(finish_kernel, n, tile, plan),
        grid=(steps,),
        in_specs=[
            columns(rows, 0),
            pl.BlockSpec((1, rows, heads * m), lambda i: (i, 0, 0)),
            columns(rows, 0),
            columns(m, 0),
            columns(m, 0),
        ]
        + [columns(width, k * steps) for k in range(3)]
        + [columns(1, k * steps) for k in range(1, 3)]
        + [
            whole((rows, width)),
            whole((m, width)),
            whole((m, 1)),
            whole((n, m, tokens)),
            whole((n, tokens, width)),
            whole((rows, width)),
            whole((1, width)),
            whole((1, hidden)),
            whole((4, width)),
            anywhere,
            anywhere,
            anywhere,
        ],
        out_specs=[anywhere] * (1 + len(results)) + [whole((VECTORS, width))],
        out_shape=[jax.ShapeDtypeStruct((n, tokens, width), BF16)]
        + [jax.ShapeDtypeStruct(shape, BF16) for shape in results]
        + [jax.ShapeDtypeStruct((VECTORS, width), F32)],
        scratch_shapes=scratch,
        compiler_params=pltpu.CompilerParams(
            collective_id=1, has_side_effects=True, vmem_limit_bytes=67043328, dimension_semantics=("arbitrary",)
        ),
        name="finish",
    )(mixed_grad, weights, query, key, value, qkv_weight, qkv_weight, qkv_weight, qkv_bias, qkv_bias, normed, core,
      total, squeeze, low_x, middle_grad, gain, up_bias, sums, down, up, out)


EARLY_ROUNDS = (1, 1, 1)


class Exchange:
    def __init__(self, source, target, own, send, recv):
        self.source, self.target = source, target
        self.own, self.send, self.recv = own, send, recv
        self.n = source.shape[0]
        self.me = lax.axis_index("blk")

    def copy(self, d):
        return remote(
            self.source.at[self.me ^ d],
            self.target.at[self.me],
            self.send.at[d - 1],
            self.recv.at[d - 1],
            at_blk(self.me ^ d),
        )

    def mine(self):
        return pltpu.make_async_copy(self.source.at[self.me], self.target.at[self.me], self.own)

    def start(self):
        for d in spread_order(self.n):
            self.copy(d).start()
        self.mine().start()

    def wait(self):
        self.mine().wait()
        for d in range(1, self.n):
            self.copy(d).wait()


def exchange_scratch(n):
    dma = pltpu.SemaphoreType.DMA
    return [dma, dma((n - 1,)), dma((n - 1,))]


def alive_here(counts):
    return lax.axis_index("blk") < counts[lax.axis_index("batch")]


def side_by_side(refs, axis):
    return jnp.concatenate([ref[...] for ref in refs], axis=axis)


def open_kernel(n, attends, tile, counts, inputs, cotangent, compress, gain, bias, *refs):
    (wq, wk, wv, bq, bk, bv, ow, ob, gain2, bias2), refs = refs[:10], refs[10:]
    upw, upb, dnw, dnb, refs = refs[:n], refs[n : 2 * n], refs[2 * n : 3 * n], refs[3 * n], refs[3 * n + 1 :]
    (low_x, normed, squeeze, low_cot, core_out, total_out, query, key, value, weights, mixed,
     middle, second, active, slope, output) = refs[:16]
    (x_here, n_here, e_here, core_sum, total, acc, core, keep, send_e, recv_e) = refs[16:26]
    x_sems, cot_sems = refs[26:29], refs[29:32]
    i = pl.program_id(0)
    me = lax.axis_index("blk")
    tokens = inputs.shape[1]
    rows, m = n * tokens, compress.shape[0]
    xs = Exchange(inputs, x_here, *x_sems)
    cots = Exchange(cotangent, low_cot, *cot_sems)

    def piece(d):
        return remote(compress, e_here.at[me], send_e.at[d - 1], recv_e.at[d - 1], at_blk(me ^ d))

    keeps = [
        pltpu.make_async_copy(source, target, keep.at[k])
        for k, (source, target) in enumerate(((x_here, low_x), (n_here, normed), (e_here, squeeze)))
    ]

    @pl.when(i == 0)
    def _():
        greet([at_blk(me ^ d) for d in range(1, n)])
        for d in range(1, n):
            piece(d).start()
        xs.start()
        cots.start()
        e_here[me] = compress[...]
        core_sum[...] = jnp.zeros_like(core_sum)
        total[...] = jnp.zeros_like(total)
        for d in range(n):
            slot = me ^ d
            if d == 0:
                xs.mine().wait()
            else:
                piece(d).wait_recv()
                xs.copy(d).wait_recv()
            low = (norm_stats(x_here[slot].astype(F32))[0] * gain[...] + bias[...]).astype(BF16)
            n_here[slot] = low
            part = e_here[slot]
            core_sum[...] += contract(part, low, 1, 0)
            total[...] += jnp.sum(part.astype(F32), axis=1, keepdims=True)
        core[...] = core_sum[...].astype(BF16)
        core_out[...] = core[...]
        total_out[...] = total[...]
        for copy in keeps:
            copy.start()

    @pl.when(i < attends)
    def _():
        key[...] = (contract(core[...], wk[...], 1, 0) + total[...] * bk[...]).astype(BF16)
        value[...] = (contract(core[...], wv[...], 1, 0) + total[...] * bv[...]).astype(BF16)
        keys = by_head(key[...] * jnp.asarray(1.0 / math.sqrt(HD), BF16))
        values = by_head(value[...])
        lanes = pl.ds(pl.multiple_of(i * LANES, LANES), LANES)
        for r in range(rows // tile):
            at = slice(r * tile, (r + 1) * tile)
            blocks = slice(r * tile // tokens, (r + 1) * tile // tokens)
            low_n = n_here[blocks].reshape(tile, -1)
            q = (contract(low_n, wq[...], 1, 0) + bq[...]).astype(BF16)
            query[at, :] = q
            scores = contract(q, keys, 1, 1)
            heads = []
            for h in range(LANES // HD):
                s = scores[:, h * m : (h + 1) * m]
                e = jnp.exp(s - jnp.max(s, axis=-1, keepdims=True))
                heads.append((e * (1.0 / jnp.sum(e, axis=-1, keepdims=True))).astype(BF16))
            low = jnp.concatenate(heads, axis=1)
            weights[0, at, :] = low
            mixed[at, lanes] = contract(low, values, 1, 0).astype(BF16)

    @pl.when(i == attends)
    def _():
        mid = x_here[...].reshape(rows, -1).astype(F32) + contract(mixed[...], ow[...], 1, 0) + ob[...]
        middle[...] = mid
        second[...] = (norm_stats(mid)[0] * gain2[...] + bias2[...]).astype(BF16)
        acc[...] = mid + dnb[...]

    @pl.when(i >= attends)
    def _():
        v = contract(second[...], side_by_side(upw, 1), 1, 0) + side_by_side(upb, 1)
        square = v * v
        t = jnp.tanh(v * (GELU_A + (GELU_A * GELU_B) * square))
        half = 0.5 + 0.5 * t
        act = (v * half).astype(BF16)
        active[...] = act
        slope[...] = (
            half + (0.5 * v) * (1.0 - t * t) * (GELU_A + (3 * GELU_A * GELU_B) * square)
        ).astype(BF16)
        acc[...] += contract(act, side_by_side(dnw, 0), 1, 0)

    @pl.when(i == pl.num_programs(0) - 1)
    def _():
        output[...] = jnp.where(alive_here(counts), acc[...], 0.0).astype(BF16).reshape(output.shape)
        for copy in keeps:
            copy.wait()
        for d in range(1, n):
            piece(d).wait_send()
            xs.copy(d).wait_send()
        cots.wait()


def open_all(counts, inputs, cotangent, compress, gain, bias, qkv_weight, qkv_bias, ow, ob, gain2, bias2,
             upw, upb, dnw, dnb, tile=512):
    n, tokens, width = inputs.shape
    rows, m, hidden = n * tokens, compress.shape[0], upw.shape[1]
    attends, heads = width // LANES, LANES // HD
    feeds = hidden // n // 128
    block = n * 128
    anywhere = pl.BlockSpec(memory_space=pl.ANY)
    vec = whole((1, width))

    def early(i):
        return jnp.minimum(i, attends - 1)

    def late(i):
        return jnp.maximum(i - attends, 0)

    def wide(height, start):
        return pl.BlockSpec((height, LANES), lambda i: (0, start + early(i)))

    def chunk(shape, dim, b):
        if dim:
            return pl.BlockSpec(shape, lambda i: (0, b * feeds + late(i)))
        return pl.BlockSpec(shape, lambda i: (b * feeds + late(i), 0))

    struct = jax.ShapeDtypeStruct
    dma = pltpu.SemaphoreType.DMA
    return pl.pallas_call(
        functools.partial(open_kernel, n, attends, tile),
        grid=(attends + feeds,),
        in_specs=[pl.BlockSpec(memory_space=pltpu.SMEM), anywhere, anywhere, whole((m, tokens)), vec, vec]
        + [wide(width, k * attends) for k in range(3)]
        + [wide(1, k * attends) for k in range(3)]
        + [whole((width, width)), vec, vec, vec]
        + [chunk((width, 128), 1, b) for b in range(n)]
        + [chunk((1, 128), 1, b) for b in range(n)]
        + [chunk((128, width), 0, b) for b in range(n)]
        + [vec],
        out_specs=[anywhere] * 4
        + [whole((m, width)), whole((m, 1)), wide(rows, 0), wide(m, 0), wide(m, 0)]
        + [pl.BlockSpec((1, rows, heads * m), lambda i: (early(i), 0, 0))]
        + [whole((rows, width))] * 3
        + [pl.BlockSpec((rows, block), lambda i: (0, late(i)))] * 2
        + [whole((n, tokens, width))],
        out_shape=[
            struct((n, tokens, width), BF16),
            struct((n, tokens, width), BF16),
            struct((n, m, tokens), BF16),
            struct((n, tokens, width), BF16),
            struct((m, width), BF16),
            struct((m, 1), F32),
            struct((rows, width), BF16),
            struct((m, width), BF16),
            struct((m, width), BF16),
            struct((attends, rows, heads * m), BF16),
            struct((rows, width), BF16),
            struct((rows, width), F32),
            struct((rows, width), BF16),
            struct((rows, hidden), BF16),
            struct((rows, hidden), BF16),
            struct((n, tokens, width), BF16),
        ],
        scratch_shapes=[
            pltpu.VMEM((n, tokens, width), BF16),
            pltpu.VMEM((n, tokens, width), BF16),
            pltpu.VMEM((n, m, tokens), BF16),
            pltpu.VMEM((m, width), F32),
            pltpu.VMEM((m, 1), F32),
            pltpu.VMEM((rows, width), F32),
            pltpu.VMEM((m, width), BF16),
            dma((3,)),
            dma((n - 1,)),
            dma((n - 1,)),
        ]
        + exchange_scratch(n)
        + exchange_scratch(n),
        compiler_params=pltpu.CompilerParams(
            collective_id=0, has_side_effects=True, vmem_limit_bytes=67043328, dimension_semantics=("arbitrary",)
        ),
        name="open",
    )(counts, inputs, cotangent, compress, gain, bias, qkv_weight, qkv_weight, qkv_weight, qkv_bias, qkv_bias, qkv_bias,
      ow, ob, gain2, bias2, *[upw] * n, *[upb] * n, *[dnw] * n, dnb)


def back_kernel(n, counts, cot, result, active, slope, second, middle, mixed, *refs):
    upw, dnw, (ow, gain), refs = refs[:n], refs[n : 2 * n], refs[2 * n : 2 * n + 2], refs[2 * n + 2 :]
    (home, up_grad, down_grad, up_bias_grad, middle_grad, mixed_grad, out_grad, sums, incoming, total) = refs[:10]
    outs = Exchange(result, home, *refs[10:13])
    f = pl.program_id(0)
    me = lax.axis_index("blk")

    @pl.when(f == 0)
    def _():
        greet([at_blk(me ^ d) for d in range(1, n)])
        outs.start()
        incoming[...] = jnp.where(alive_here(counts), cot[...], jnp.zeros_like(cot)).reshape(incoming.shape)
        total[...] = jnp.zeros_like(total)

    d = contract(incoming[...], side_by_side(dnw, 0), 1, 1)
    dh = (d * slope[...].astype(F32)).astype(BF16)
    up_bias_grad[...] = jnp.sum(dh.astype(F32), axis=0, keepdims=True)
    total[...] += contract(dh, side_by_side(upw, 1), 1, 1)
    down_grad[0] = contract(active[...], incoming[...], 0, 0).astype(BF16)
    up_grad[0] = contract(second[...], dh, 0, 0).astype(BF16)

    @pl.when(f == pl.num_programs(0) - 1)
    def _():
        hat, rate = norm_stats(middle[...])
        up = total[...]
        inc = incoming[...].astype(F32)
        grad = inc + norm_back(hat, rate, up, gain[...])
        middle_grad[...] = grad
        branch = grad.astype(BF16)
        mixed_grad[...] = contract(branch, ow[...], 1, 1).astype(BF16)
        out_grad[...] = contract(mixed[...], branch, 0, 0).astype(BF16)
        sums[0:1, :] = jnp.sum(branch.astype(F32), axis=0, keepdims=True)
        sums[1:2, :] = jnp.sum(up * hat, axis=0, keepdims=True)
        sums[2:3, :] = jnp.sum(up, axis=0, keepdims=True)
        sums[3:4, :] = jnp.sum(inc, axis=0, keepdims=True)
        outs.wait()


def back_all(counts, cot, result, active, slope, second, middle, mixed, upw, dnw, ow, gain):
    n, tokens, width = cot.shape
    rows, hidden = active.shape
    feeds, block = hidden // n // 128, n * 128
    anywhere = pl.BlockSpec(memory_space=pl.ANY)

    def chunk(shape, dim, b):
        if dim:
            return pl.BlockSpec(shape, lambda i: (0, b * feeds + i))
        return pl.BlockSpec(shape, lambda i: (b * feeds + i, 0))

    struct = jax.ShapeDtypeStruct
    return pl.pallas_call(
        functools.partial(back_kernel, n),
        grid=(feeds,),
        in_specs=[
            pl.BlockSpec(memory_space=pltpu.SMEM),
            whole((n, tokens, width)),
            anywhere,
            columns(rows, 0, block),
            columns(rows, 0, block),
            whole((rows, width)),
            whole((rows, width)),
            whole((rows, width)),
        ]
        + [chunk((width, 128), 1, b) for b in range(n)]
        + [chunk((128, width), 0, b) for b in range(n)]
        + [whole((width, width)), whole((1, width))],
        out_specs=[
            anywhere,
            pl.BlockSpec((1, width, block), lambda i: (i, 0, 0)),
            pl.BlockSpec((1, block, width), lambda i: (i, 0, 0)),
            columns(1, 0, block),
            whole((rows, width)),
            whole((rows, width)),
            whole((width, width)),
            whole((4, width)),
        ],
        out_shape=[
            struct((n, tokens, width), BF16),
            struct((feeds, width, block), BF16),
            struct((feeds, block, width), BF16),
            struct((1, hidden), F32),
            struct((rows, width), F32),
            struct((rows, width), BF16),
            struct((width, width), BF16),
            struct((4, width), F32),
        ],
        scratch_shapes=[pltpu.VMEM((rows, width), BF16), pltpu.VMEM((rows, width), F32)] + exchange_scratch(n),
        compiler_params=pltpu.CompilerParams(
            collective_id=2, has_side_effects=True, vmem_limit_bytes=67043328, dimension_semantics=("arbitrary",)
        ),
        name="back",
    )(counts, cot, result, active, slope, second, middle, mixed, *[upw] * n, *[dnw] * n, ow, gain)


def settle_kernel(output, home, down, up, qkv, out, small, *refs):
    output_to, home_to, down_to, up_to, qkv_to, out_to, small_to = refs
    output_to[...] = output[...]
    home_to[...] = home[...]
    for source, target in ((down, down_to), (qkv, qkv_to), (out, out_to), (small, small_to)):
        target[...] = source[...].astype(F32)
    feeds = up.shape[1] // 128 // output.shape[0]
    for u in range(feeds):
        for b in range(output.shape[0]):
            start, end = (u * output.shape[0] + b) * 128, (b * feeds + u) * 128
            up_to[:, end : end + 128] = up[:, start : start + 128].astype(F32)


def settle(output, home, *summed):
    vmem = pl.BlockSpec(memory_space=pltpu.VMEM)
    struct = jax.ShapeDtypeStruct
    return pl.pallas_call(
        settle_kernel,
        in_specs=[vmem] * 7,
        out_specs=[vmem] * 7,
        out_shape=[struct(output.shape, BF16), struct(home.shape, BF16)] + [struct(v.shape, F32) for v in summed],
        compiler_params=pltpu.CompilerParams(vmem_limit_bytes=48 << 20),
        name="settle",
    )(output, home, *summed)


def swap(values, axis, size, bit):
    return lax.ppermute(values, axis, [(i, i ^ bit) for i in range(size)])


def halve(values, dim, axis, size, bit):
    mine = (lax.axis_index(axis) // bit) % 2
    send = lax.dynamic_index_in_dim(values, 1 - mine, dim, keepdims=False).astype(BF16)
    keep = lax.dynamic_index_in_dim(values, mine, dim, keepdims=False)
    return keep.astype(F32) + swap(send, axis, size, bit).astype(F32)


def join(values, dim, axis, size, bit):
    mine = (lax.axis_index(axis) // bit) % 2
    other = swap(values, axis, size, bit)
    first = jnp.where(mine == 0, values, other)
    second = jnp.where(mine == 0, other, values)
    return jnp.concatenate([first, second], axis=dim)


def scatter_sum(terms, bits, order, nb, nk, early):
    _, rows, cols = terms.shape
    values = halve(terms.reshape(-1, 2, rows // 2, cols), 1, "batch", nb, 1)
    chips = [1 << i for i in range(1, nb.bit_length() - 1)]
    if early:
        for bit in chips:
            cols //= 2
            values = halve(values.reshape(-1, rows // 2, 2, cols), 2, "batch", nb, bit)
    left = list(bits)
    for bit in order:
        place = left.index(bit)
        values = values.reshape(1 << place, 2, -1, rows // 2, cols)
        values = halve(values, 1, "blk", nk, bit)
        left.remove(bit)
    values = values.reshape(rows // 2, cols).astype(BF16)
    for bit in reversed(chips) if early else chips:
        if early:
            values = join(values, 1, "batch", nb, bit)
        else:
            values = (values.astype(F32) + swap(values, "batch", nb, bit).astype(F32)).astype(BF16)
    return join(values, 0, "batch", nb, 1).astype(F32)


def body(
    inputs,
    cotangent,
    group_counts,
    first_gain,
    first_bias,
    qkv_weight,
    qkv_bias,
    out_weight,
    out_bias,
    second_gain,
    second_bias,
    up_weight,
    up_bias,
    down_weight,
    down_bias,
    compress,
    *,
    nb,
    nk,
):
    slots, tokens, width = inputs.shape
    splits = nk // slots
    teams = [[t * slots + i for i in range(slots)] for t in range(splits)]
    across = [[t * slots + i for t in range(splits)] for i in range(slots)]
    rows = slots * tokens
    low_first = [1 << i for i in range(nk.bit_length() - 1)]
    high_first = low_first[::-1]
    team_low = [1 << i for i in range(slots.bit_length() - 1)]

    def gather_rows(values):
        return lax.all_to_all(values, "blk", 0, 0, axis_index_groups=teams, tiled=True).reshape(
            rows, width
        )

    def spread_rows(values):
        return lax.all_to_all(
            values.reshape(slots, tokens, width), "blk", 0, 0, axis_index_groups=teams, tiled=True
        )

    def over_splits(values):
        if splits == 1:
            return values
        return lax.psum(values, "blk", axis_index_groups=across)

    def line(vector):
        return vector.reshape(1, -1)

    if nb == 4 and nk == slots == 8:
        (
            low_x,
            normed,
            squeeze,
            low_cot,
            core,
            total,
            query,
            key,
            value,
            weights,
            mixed,
            middle,
            second,
            active,
            slope,
            result,
        ) = open_all(
            group_counts,
            inputs,
            cotangent,
            compress,
            line(first_gain),
            line(first_bias),
            qkv_weight,
            line(qkv_bias),
            out_weight,
            line(out_bias),
            line(second_gain),
            line(second_bias),
            up_weight,
            line(up_bias),
            down_weight,
            line(down_bias),
        )
        output, up_grad, down_grad, up_bias_grad, middle_grad, mixed_grad, out_grad, sums = back_all(
            group_counts,
            low_cot,
            result,
            active,
            slope,
            second,
            middle,
            mixed,
            up_weight,
            down_weight,
            out_weight,
            line(second_gain),
        )
        input_grad, *summed, flat = finish(
            mixed_grad,
            weights,
            query,
            key,
            value,
            normed.reshape(rows, width),
            core,
            total,
            squeeze,
            low_x,
            middle_grad,
            line(first_gain),
            qkv_weight,
            line(qkv_bias),
            up_bias_grad,
            sums,
            down_grad,
            up_grad,
            out_grad,
        )
        output, input_grad, down_rows, up_rows, qkv_rows, out_rows, compress_rows = settle(
            output, input_grad, *summed
        )
        stretches = [(0, 1), (1, 1), (2, 3), (5, 1), (6, 1), (7, 1), (8, 4), (12, 1)]
        sizes = [count * width // nk for _, count in stretches]
        feeds = up_grad.shape[0]
        vectors = [flat[at : at + count] for at, count in stretches]
        vectors[6] = vectors[6].reshape(feeds, nk, -1).transpose(1, 0, 2)
        packed = jnp.concatenate([v.reshape(nk, -1) for v in vectors], axis=1)
        mine = lax.dynamic_index_in_dim(packed, lax.axis_index("blk"), 0, keepdims=False)
    else:
        slot = lax.axis_index("blk") % slots
        alive = (slot < group_counts[lax.axis_index("batch")]).astype(jnp.int32).reshape(1)

        squeeze = compress[None]
        for bit in team_low[::-1]:
            squeeze = join(squeeze[:, None], 1, "blk", nk, bit)
            squeeze = squeeze.reshape((-1,) + compress.shape)
        low_x = gather_rows(inputs)
        hat_first, rate_first = norm_stats(low_x.astype(F32))
        normed = (hat_first * first_gain + first_bias).astype(BF16)
        core = jnp.einsum(
            "bjt,btc->jc",
            squeeze,
            normed.reshape(slots, tokens, width),
            preferred_element_type=F32,
        )
        total = jnp.sum(squeeze.astype(F32), axis=(0, 2))[:, None]
        low_cot = gather_rows(cotangent)
        core = over_splits(core).astype(BF16)
        total = over_splits(total)
        query, key, value, weights, mixed = attend(
            normed, core, total, qkv_weight, line(qkv_bias), tile=512
        )
        middle, second, active, slope, result = forward(
            alive,
            mixed,
            low_x,
            out_weight,
            line(out_bias),
            line(second_gain),
            line(second_bias),
            up_weight,
            line(up_bias),
            down_weight,
            line(down_bias),
        )
        output = spread_rows(result)
        up_grad, down_grad, up_bias_grad, middle_grad, mixed_grad, out_grad, sums = backward(
            alive,
            low_cot,
            active,
            slope,
            second,
            middle,
            mixed,
            up_weight,
            down_weight,
            out_weight,
            line(second_gain),
        )
        out_bias_grad, second_gain_grad, second_bias_grad, down_bias_grad = (sums[i] for i in range(4))
        (
            query_weight_grad,
            key_weight_grad,
            value_weight_grad,
            query_bias_grad,
            key_bias_grad,
            value_bias_grad,
            query_up,
            core_back,
            lift,
        ) = attend_back(
            mixed_grad, weights, query, key, value, normed, core, total, qkv_weight, line(qkv_bias)
        )
        core_back = over_splits(core_back).astype(BF16)
        lift = over_splits(lift)
        first_up = query_up + jnp.einsum(
            "bjt,jc->btc", squeeze, core_back, preferred_element_type=F32
        ).reshape(rows, width)
        first_gain_grad = jnp.sum(first_up * hat_first, axis=0)
        first_bias_grad = jnp.sum(first_up, axis=0)
        rows_grad = (
            middle_grad + norm_back(hat_first, rate_first, first_up, first_gain)
        ).astype(BF16)
        compress_terms = (
            jnp.einsum(
                "jc,btc->bjt",
                core_back,
                normed.reshape(slots, tokens, width),
                preferred_element_type=F32,
            )
            + lift[None]
        )

        vectors = (
            first_gain_grad,
            first_bias_grad,
            jnp.concatenate([query_bias_grad, key_bias_grad, value_bias_grad], axis=1),
            out_bias_grad,
            second_gain_grad,
            second_bias_grad,
            up_bias_grad,
            down_bias_grad,
        )
        sizes = [v.size // nk for v in vectors]
        packed = jnp.concatenate([v.reshape(nk, -1) for v in vectors], axis=1)
        tall = 32
        wide = -(-sum(sizes) // (tall * 128)) * 128
        packed = jnp.pad(packed, ((0, 0), (0, tall * wide - sum(sizes)))).reshape(nk, tall, wide)
        blocked = [
            grad.reshape(nk, grad.shape[0] // nk, grad.shape[1])
            for grad in (
                down_grad,
                up_grad,
                query_weight_grad,
                key_weight_grad,
                value_weight_grad,
                out_grad,
            )
        ]
        input_grad = spread_rows(rows_grad)
        blocked = blocked[:2] + [jnp.concatenate(blocked[2:], axis=2)]
        down_rows, up_rows, joined = (
            scatter_sum(grad, high_first, low_first, nb, nk, i > 0)
            for i, grad in enumerate(blocked)
        )
        qkv_rows, out_rows = joined[:, : 3 * width], joined[:, 3 * width :]
        compress_rows = scatter_sum(compress_terms, team_low[::-1], team_low, nb, nk, False)
        mine = scatter_sum(packed, high_first, low_first, nb, nk, False).reshape(-1)
    parts = []
    start = 0
    for size in sizes:
        parts.append(mine[start : start + size])
        start += size
    fg, fb, qb, ob, sg, sb, ub, db = parts
    return (
        output,
        input_grad,
        fg,
        fb,
        qkv_rows,
        qb,
        out_rows,
        ob,
        sg,
        sb,
        up_rows,
        ub,
        down_rows,
        db,
        compress_rows,
    )


def solution(mesh):
    rows = P("batch", "blk", None)
    placed = (rows, rows) + (P(),) * 13 + (P(None, "blk"),)
    vec, mat = P("blk"), P("blk", None)
    return jax.shard_map(
        functools.partial(body, nb=mesh.shape["batch"], nk=mesh.shape["blk"]),
        mesh=mesh,
        in_specs=placed,
        out_specs=(rows, rows, vec, vec, mat, vec, mat, vec, vec, vec, mat, vec, mat, vec)
        + (P(None, "blk"),),
        check_vma=False,
    )
```

```python
import functools
import math

import jax
import jax.numpy as jnp
from jax import lax
from jax.experimental import pallas as pl
from jax.experimental.pallas import tpu as pltpu
from jax.sharding import PartitionSpec as P

F32 = jnp.float32
BF16 = jnp.bfloat16
HD = 64
LANES = 256
GELU_A = math.sqrt(2.0 / math.pi)
GELU_B = 0.044715


def norm_stats(states):
    center = states - jnp.mean(states, axis=-1, keepdims=True)
    spread = jnp.mean(center * center, axis=-1, keepdims=True)
    rate = lax.rsqrt(spread + 1e-05)
    return center * rate, rate


def norm_back(hat, rate, upstream, gain):
    scaled = upstream * gain
    return rate * (
        scaled
        - jnp.mean(scaled, axis=-1, keepdims=True)
        - hat * jnp.mean(scaled * hat, axis=-1, keepdims=True)
    )


def contract(a, b, dim_a, dim_b):
    return lax.dot_general(a, b, (((dim_a,), (dim_b,)), ((), ())), preferred_element_type=F32)


def whole(shape):
    return pl.BlockSpec(shape, lambda *_: (0,) * len(shape), pipeline_mode=pl.Buffered(1))


def columns(height, start, width=LANES):
    return pl.BlockSpec((height, width), lambda i: (0, start + i))


def below(width, start, height=LANES):
    return pl.BlockSpec((height, width), lambda i: (start + i, 0))


PARAMS = dict(vmem_limit_bytes=62 << 20, dimension_semantics=("arbitrary",))


def by_head(values):
    lane = lax.broadcasted_iota(jnp.int32, values.shape, 1) // HD
    zero = jnp.zeros_like(values)
    return jnp.concatenate([jnp.where(lane == h, values, zero) for h in range(LANES // HD)], axis=0)


def own_head(values):
    n = values.shape[0] // (LANES // HD)
    lane = lax.broadcasted_iota(jnp.int32, (n, LANES), 1) // HD
    picked = values[:n]
    for h in range(1, LANES // HD):
        picked = jnp.where(lane == h, values[h * n : (h + 1) * n], picked)
    return picked


def attend_kernel(tile, normed, core, total, wq, wk, wv, bq, bk, bv, query, key, value, weights, mixed):
    rows, n = normed.shape[0], core.shape[0]
    key[...] = (contract(core[...], wk[...], 1, 0) + total[...] * bk[...]).astype(BF16)
    value[...] = (contract(core[...], wv[...], 1, 0) + total[...] * bv[...]).astype(BF16)
    keys = by_head(key[...] * jnp.asarray(1.0 / math.sqrt(HD), BF16))
    values = by_head(value[...])

    for r in range(rows // tile):
        at = slice(r * tile, (r + 1) * tile)
        q = (contract(normed[at, :], wq[...], 1, 0) + bq[...]).astype(BF16)
        query[at, :] = q
        scores = contract(q, keys, 1, 1)
        heads = []
        for h in range(LANES // HD):
            s = scores[:, h * n : (h + 1) * n]
            e = jnp.exp(s - jnp.max(s, axis=-1, keepdims=True))
            heads.append((e * (1.0 / jnp.sum(e, axis=-1, keepdims=True))).astype(BF16))
        low = jnp.concatenate(heads, axis=1)
        weights[0, at, :] = low
        mixed[at, :] = contract(low, values, 1, 0).astype(BF16)


def attend(normed, core, total, qkv_weight, qkv_bias, tile=1024):
    rows, width = normed.shape
    n = core.shape[0]
    steps = width // LANES
    heads = LANES // HD
    return pl.pallas_call(
        functools.partial(attend_kernel, tile),
        grid=(steps,),
        in_specs=[whole((rows, width)), whole((n, width)), whole((n, 1))]
        + [columns(width, k * steps) for k in range(3)]
        + [columns(1, k * steps) for k in range(3)],
        out_specs=[
            columns(rows, 0),
            columns(n, 0),
            columns(n, 0),
            pl.BlockSpec((1, rows, heads * n), lambda i: (i, 0, 0)),
            columns(rows, 0),
        ],
        out_shape=[
            jax.ShapeDtypeStruct((rows, width), BF16),
            jax.ShapeDtypeStruct((n, width), BF16),
            jax.ShapeDtypeStruct((n, width), BF16),
            jax.ShapeDtypeStruct((steps, rows, heads * n), BF16),
            jax.ShapeDtypeStruct((rows, width), BF16),
        ],
        compiler_params=pltpu.CompilerParams(**PARAMS),
        name="attend",
    )(normed, core, total, qkv_weight, qkv_weight, qkv_weight, qkv_bias, qkv_bias, qkv_bias)


def forward_kernel(tile, alive, mixed, states, ow, ob, gain, bias, upw, upb, dnw, dnb,
                   middle, second, active, slope, output, total):
    f = pl.program_id(0)
    rows = mixed.shape[0]

    @pl.when(f == 0)
    def _():
        mid = states[...].astype(F32) + contract(mixed[...], ow[...], 1, 0) + ob[...]
        middle[...] = mid
        second[...] = (norm_stats(mid)[0] * gain[...] + bias[...]).astype(BF16)
        total[...] = mid + dnb[...]

    for r in range(rows // tile):
        at = slice(r * tile, (r + 1) * tile)
        v = contract(second[at, :], upw[...], 1, 0) + upb[...]
        square = v * v
        t = jnp.tanh(v * (GELU_A + (GELU_A * GELU_B) * square))
        half = 0.5 + 0.5 * t
        act = (v * half).astype(BF16)
        active[at, :] = act
        slope[at, :] = (
            half + (0.5 * v) * (1.0 - t * t) * (GELU_A + (3 * GELU_A * GELU_B) * square)
        ).astype(BF16)
        total[at, :] += contract(act, dnw[...], 1, 0)

    @pl.when(f == pl.num_programs(0) - 1)
    def _():
        output[...] = jnp.where(alive[0] > 0, total[...], 0.0).astype(BF16)


def forward(alive, mixed, states, ow, ob, gain, bias, upw, upb, dnw, dnb, block=512, tile=1024):
    rows, width = mixed.shape
    hidden = upw.shape[1]
    vec = whole((1, width))
    return pl.pallas_call(
        functools.partial(forward_kernel, tile),
        grid=(hidden // block,),
        in_specs=[
            pl.BlockSpec(memory_space=pltpu.SMEM),
            whole((rows, width)),
            whole((rows, width)),
            whole((width, width)),
            vec,
            vec,
            vec,
            columns(width, 0, block),
            columns(1, 0, block),
            below(width, 0, block),
            vec,
        ],
        out_specs=[
            whole((rows, width)),
            whole((rows, width)),
            columns(rows, 0, block),
            columns(rows, 0, block),
            whole((rows, width)),
        ],
        out_shape=[
            jax.ShapeDtypeStruct((rows, width), F32),
            jax.ShapeDtypeStruct((rows, width), BF16),
            jax.ShapeDtypeStruct((rows, hidden), BF16),
            jax.ShapeDtypeStruct((rows, hidden), BF16),
            jax.ShapeDtypeStruct((rows, width), BF16),
        ],
        scratch_shapes=[pltpu.VMEM((rows, width), F32)],
        compiler_params=pltpu.CompilerParams(**PARAMS),
        name="forward",
    )(alive, mixed, states, ow, ob, gain, bias, upw, upb, dnw, dnb)


def backward_kernel(alive, cot, active, slope, second, middle, mixed, upw, dnw, ow, gain,
                    up_grad, down_grad, up_bias_grad, middle_grad, mixed_grad, out_grad, sums,
                    incoming, total):
    f = pl.program_id(0)

    @pl.when(f == 0)
    def _():
        incoming[...] = jnp.where(alive[0] > 0, cot[...], jnp.zeros_like(cot))
        total[...] = jnp.zeros_like(total)

    d = contract(incoming[...], dnw[...], 1, 1)
    dh = (d * slope[...].astype(F32)).astype(BF16)
    up_bias_grad[...] = jnp.sum(dh.astype(F32), axis=0, keepdims=True)
    total[...] += contract(dh, upw[...], 1, 1)
    down_grad[...] = contract(active[...], incoming[...], 0, 0).astype(BF16)
    up_grad[...] = contract(second[...], dh, 0, 0).astype(BF16)

    @pl.when(f == pl.num_programs(0) - 1)
    def _():
        hat, rate = norm_stats(middle[...])
        up = total[...]
        inc = incoming[...].astype(F32)
        grad = inc + norm_back(hat, rate, up, gain[...])
        middle_grad[...] = grad
        branch = grad.astype(BF16)
        mixed_grad[...] = contract(branch, ow[...], 1, 1).astype(BF16)
        out_grad[...] = contract(mixed[...], branch, 0, 0).astype(BF16)
        sums[0:1, :] = jnp.sum(branch.astype(F32), axis=0, keepdims=True)
        sums[1:2, :] = jnp.sum(up * hat, axis=0, keepdims=True)
        sums[2:3, :] = jnp.sum(up, axis=0, keepdims=True)
        sums[3:4, :] = jnp.sum(inc, axis=0, keepdims=True)


def backward(alive, cot, active, slope, second, middle, mixed, upw, dnw, ow, gain, block=512):
    rows, width = mixed.shape
    hidden = upw.shape[1]
    return pl.pallas_call(
        backward_kernel,
        grid=(hidden // block,),
        in_specs=[
            pl.BlockSpec(memory_space=pltpu.SMEM),
            whole((rows, width)),
            columns(rows, 0, block),
            columns(rows, 0, block),
            whole((rows, width)),
            whole((rows, width)),
            whole((rows, width)),
            columns(width, 0, block),
            below(width, 0, block),
            whole((width, width)),
            whole((1, width)),
        ],
        out_specs=[
            columns(width, 0, block),
            below(width, 0, block),
            columns(1, 0, block),
            whole((rows, width)),
            whole((rows, width)),
            whole((width, width)),
            whole((4, width)),
        ],
        out_shape=[
            jax.ShapeDtypeStruct((width, hidden), BF16),
            jax.ShapeDtypeStruct((hidden, width), BF16),
            jax.ShapeDtypeStruct((1, hidden), F32),
            jax.ShapeDtypeStruct((rows, width), F32),
            jax.ShapeDtypeStruct((rows, width), BF16),
            jax.ShapeDtypeStruct((width, width), BF16),
            jax.ShapeDtypeStruct((4, width), F32),
        ],
        scratch_shapes=[pltpu.VMEM((rows, width), BF16), pltpu.VMEM((rows, width), F32)],
        compiler_params=pltpu.CompilerParams(**PARAMS),
        name="backward",
    )(alive, cot, active, slope, second, middle, mixed, upw, dnw, ow, gain)


def attend_back_kernel(mixed_grad, weights, query, key, value, normed, core, total, wq, wk, wv, bk, bv,
                       query_grad, key_grad, value_grad, qb, kb, vb, up, core_grad, lift):
    i = pl.program_id(0)
    n = core.shape[0]

    @pl.when(i == 0)
    def _():
        up[...] = jnp.zeros_like(up)
        core_grad[...] = jnp.zeros_like(core_grad)
        lift[...] = jnp.zeros_like(lift)

    keys = by_head(key[...] * jnp.asarray(1.0 / math.sqrt(HD), BF16))
    values = by_head(value[...])
    grads = mixed_grad[...]
    back = contract(grads, values, 1, 1)
    heads = []
    for h in range(LANES // HD):
        p = weights[0, :, h * n : (h + 1) * n].astype(F32)
        g = back[:, h * n : (h + 1) * n]
        heads.append((p * (g - jnp.sum(p * g, axis=-1, keepdims=True))).astype(BF16))
    score = jnp.concatenate(heads, axis=1)
    dv = own_head(contract(weights[0], grads, 0, 0))
    dk = own_head(contract(score, query[...], 0, 0)) * (1.0 / math.sqrt(HD))
    dq = contract(score, keys, 1, 0).astype(BF16)
    dk_low, dv_low = dk.astype(BF16), dv.astype(BF16)
    up[...] += contract(dq, wq[...], 1, 1)
    core_grad[...] += contract(dk_low, wk[...], 1, 1) + contract(dv_low, wv[...], 1, 1)
    lift[...] += jnp.sum(dk * bk[...] + dv * bv[...], axis=1, keepdims=True)
    query_grad[...] = contract(normed[...], dq, 0, 0).astype(BF16)
    key_grad[...] = contract(core[...], dk_low, 0, 0).astype(BF16)
    value_grad[...] = contract(core[...], dv_low, 0, 0).astype(BF16)
    qb[...] = jnp.sum(dq.astype(F32), axis=0, keepdims=True)
    kb[...] = jnp.sum(total[...] * dk, axis=0, keepdims=True)
    vb[...] = jnp.sum(total[...] * dv, axis=0, keepdims=True)


def attend_back(mixed_grad, weights, query, key, value, normed, core, total, qkv_weight, qkv_bias):
    rows, width = normed.shape
    n = core.shape[0]
    steps = width // LANES
    heads = LANES // HD
    return pl.pallas_call(
        attend_back_kernel,
        grid=(steps,),
        in_specs=[
            columns(rows, 0),
            pl.BlockSpec((1, rows, heads * n), lambda i: (i, 0, 0)),
            columns(rows, 0),
            columns(n, 0),
            columns(n, 0),
            whole((rows, width)),
            whole((n, width)),
            whole((n, 1)),
        ]
        + [columns(width, k * steps) for k in range(3)]
        + [columns(1, k * steps) for k in range(1, 3)],
        out_specs=[columns(width, 0)] * 3
        + [columns(1, 0)] * 3
        + [whole((rows, width)), whole((n, width)), whole((n, 1))],
        out_shape=[jax.ShapeDtypeStruct((width, width), BF16)] * 3
        + [jax.ShapeDtypeStruct((1, width), F32)] * 3
        + [
            jax.ShapeDtypeStruct((rows, width), F32),
            jax.ShapeDtypeStruct((n, width), F32),
            jax.ShapeDtypeStruct((n, 1), F32),
        ],
        compiler_params=pltpu.CompilerParams(**PARAMS),
        name="attend_back",
    )(mixed_grad, weights, query, key, value, normed, core, total, qkv_weight, qkv_weight, qkv_weight, qkv_bias, qkv_bias)


MESH = pl.DeviceIdType.MESH


def at_batch(other):
    return {"batch": other}


def at_blk(other):
    return {"blk": other}


def remote(source, target, send, arrive, where):
    return pltpu.make_async_remote_copy(
        src_ref=source, dst_ref=target, send_sem=send, recv_sem=arrive, device_id=where, device_id_type=MESH
    )


def greet(places):
    barrier = pltpu.get_barrier_semaphore()
    for where in places:
        pl.semaphore_signal(barrier, inc=1, device_id=where, device_id_type=MESH)
    pl.semaphore_wait(barrier, len(places))


def spread_order(n):
    return sorted(range(1, n), key=lambda d: (-(d & (n // 2)), d))


class Unit:
    def __init__(self, rows, cols, early, result_top=0, result_left=0, kept="all", hops=None, lead=0):
        self.half, self.cols, self.early = rows // 2, cols, early
        self.result_top, self.result_left = result_top, result_left
        self.kept, self.lead = kept, lead
        every = ["core", "x", "y", "z1", "z2", "join", "pair"]
        if not early:
            every = ["core", "y", "z1", "z2", "late", "pair"]
        begin = {"all": 0, "core": 1, "first": 2}[kept]
        self.hops = every[begin : None if hops is None else begin + hops]

    def shape_after(self, hop):
        h, c = self.half, self.cols
        narrow = c // 2 if self.early else c
        return {
            "core": (2, 2, 2, h, c),
            "x": (2, 2, 2, h, narrow),
            "y": (2, 2, h, narrow),
            "z1": (2, h, narrow),
            "z2": (h, narrow),
            "late": (h, c),
        }.get(hop)

    def kept_shape(self):
        if self.kept == "core":
            return self.shape_after("core")
        return self.shape_after("x" if self.early else "y")

    def scratch(self):
        shapes = [] if self.kept == "all" else [self.kept_shape()]
        shapes += [self.shape_after(hop) for hop in self.hops if self.shape_after(hop)]
        return [pltpu.VMEM(shape, BF16) for shape in shapes]


HOPS = 7


class Route:
    def __init__(self, unit, source, result, buffers, local, send, recv):
        self.unit, self.source, self.result = unit, source, result
        self.hops = unit.hops
        self.moved = unit.kept != "all"
        self.acc, self.got = (buffers[0], buffers[1:]) if self.moved else (source, buffers)
        self.local, self.send, self.recv = local, send, recv
        self.batch, self.blk = lax.axis_index("batch"), lax.axis_index("blk")
        self.core, self.x = self.batch % 2, self.batch // 2
        self.z2, self.z1, self.y = self.blk // 4, (self.blk // 2) % 2, self.blk % 2

    def rows(self, top, core):
        return pl.ds(pl.multiple_of(top + core * self.unit.half, 16), self.unit.half)

    def lanes(self, left, x):
        u = self.unit
        if not u.early:
            return pl.ds(left, u.cols)
        return pl.ds(pl.multiple_of(left + x * (u.cols // 2), 128), u.cols // 2)

    def inside(self, x):
        rows = slice(None) if self.moved else self.rows(0, self.core)
        if self.unit.kept == "first":
            return rows, slice(None)
        return rows, self.lanes(0, x)

    def blocks(self, *place):
        if self.unit.kept == "first" and not self.unit.early:
            return place[:2]
        return place

    def copy(self, s):
        hop = self.hops[s]
        u, acc, mine = self.unit, self.acc, self.inside(self.x)
        y, z1, z2 = self.y, self.z1, self.z2
        every = slice(None)
        where = {
            "core": at_batch(self.batch ^ 1),
            "pair": at_batch(self.batch ^ 1),
            "x": at_batch(self.batch ^ 2),
            "late": at_batch(self.batch ^ 2),
            "join": at_batch(self.batch ^ 2),
            "y": at_blk(self.blk ^ 1),
            "z1": at_blk(self.blk ^ 2),
            "z2": at_blk(self.blk ^ 4),
        }[hop]
        if hop in ("join", "pair"):
            lanes = pl.ds(u.result_left, u.cols)
            if hop == "join":
                lanes = self.lanes(u.result_left, self.x)
            source = target = self.result.at[self.rows(u.result_top, self.core), lanes]
        else:
            target = self.got[s]
            if hop == "core":
                source = self.source.at[:, :, :, self.rows(0, 1 - self.core)]
            elif hop == "x":
                source = acc.at[(every, every, every) + self.inside(1 - self.x)]
            else:
                place = {
                    "y": (every, every, 1 - y),
                    "z1": (every, 1 - z1, y),
                    "z2": (1 - z2, z1, y),
                    "late": (z2, z1, y),
                }[hop]
                source = acc.at[self.blocks(*place) + mine]
        return remote(source, target, self.send.at[s], self.recv.at[s], where)

    def fetch(self):
        return pltpu.make_async_copy(self.source, self.acc, self.local)

    def left_over(self, target):
        every = slice(None)
        rows = self.rows(0, self.core)
        if len(self.hops) == 1:
            source = self.acc.at[:, :, :, rows]
        elif self.unit.early:
            source = self.acc.at[:, :, :, rows, self.lanes(0, self.x)]
        else:
            source = self.acc.at[:, :, self.y, rows]
        return pltpu.make_async_copy(source, target, self.local)

    def start(self, s):
        if s == 0 and self.moved:
            self.fetch().wait()
        self.copy(s).start()

    def finish(self, s):
        hop = self.hops[s]
        acc, mine, every = self.acc, self.inside(self.x), (slice(None), slice(None))
        self.copy(s).wait_recv()
        pairs = [(a, b) for a in range(2) for b in range(2)]

        def add(place, other):
            acc[place] = acc[place] + self.got[s][other]

        if hop in ("core", "x"):
            inside = (mine[0], slice(None)) if hop == "core" else mine
            for a, b in pairs:
                for c in range(2):
                    add((a, b, c) + inside, (a, b, c) + every)
        elif hop == "y":
            for a, b in pairs:
                add((a, b, self.y) + mine, (a, b) + every)
        elif hop == "z1":
            for a in range(2):
                add(self.blocks(a, self.z1, self.y) + mine, (a,) + every)
        elif hop == "z2" and not self.unit.early:
            add(self.blocks(self.z2, self.z1, self.y) + mine, every)
        elif hop in ("z2", "late"):
            place = self.blocks(self.z2, self.z1, self.y) + mine
            u = self.unit
            self.result[self.rows(u.result_top, self.core), self.lanes(u.result_left, self.x)] = (
                acc[place] + self.got[s][...]
            )

    def close(self):
        for s in range(len(self.hops)):
            self.copy(s).wait_send()


class Wave:
    def __init__(self, steps, got, send, recv):
        self.steps, self.got, self.send, self.recv = steps, got, send, recv
        batch, blk = lax.axis_index("batch"), lax.axis_index("blk")
        self.hops = [at_batch(batch ^ 1), at_batch(batch ^ 2), at_blk(blk ^ 1), at_blk(blk ^ 2), at_blk(blk ^ 4)]

    def copy(self, s):
        return remote(self.steps.at[s], self.got.at[s], self.send.at[s], self.recv.at[s], self.hops[s])

    def start(self, s):
        self.copy(s).start()

    def finish(self, s):
        self.copy(s).wait_recv()
        self.steps[s + 1] = self.steps[s] + self.got[s]

    def close(self):
        for s in range(len(self.hops)):
            self.copy(s).wait_send()


DELAY = {"core": 1.5, "x": 2.2, "y": 2.2, "z1": 2.2, "z2": 3.0}
RATE = {"core": (260e3, 260e3), "x": (45e3, 45e3), "y": (45e3, 30e3), "z1": (45e3, 18e3), "z2": (22e3, 9e3)}
LINK = {"pair": "core", "late": "x", "join": "x"}


def hop_bytes(unit, hop):
    shape = unit.shape_after(hop)
    if shape is None:
        shape = (unit.half, unit.cols // 2 if hop == "join" else unit.cols)
    return 2 * math.prod(shape)


def plan_hops(jobs, marks, busy_from):
    free = {link: 0.0 for link in RATE}
    due = {}
    result = []

    def begin(job, number, now):
        hop, size = jobs[job][1][number]
        link = LINK.get(hop, hop)
        start = max(now, free[link])
        free[link] = start + size / RATE[link][now >= busy_from]
        due[job] = (free[link] + DELAY[link], number)

    for k, mark in enumerate(marks):
        now, last, events = mark, k == len(marks) - 1, []
        for job, (ready, _) in enumerate(jobs):
            if ready == k:
                events.append((job, 0, False))
                begin(job, 0, now)
        while due:
            job = min(due, key=lambda j: due[j][0])
            when, number = due[job]
            if when > now:
                if not last:
                    break
                now = when
            now += 0.2 if last else 0.0
            del due[job]
            events.append((job, number, True))
            if number + 1 < len(jobs[job][1]):
                begin(job, number + 1, now)
        result.append(events)
    return result


def follow(routes, events):
    for job, number, ends in events:
        route = routes[job]
        if ends:
            route.finish(number)
            number += 1
        if number < len(route.hops):
            route.start(number)


VECTORS = 16


def finish_kernel(n, tile, plan, *refs):
    (mixed_grad, weights, query, key, value, wq, wk, wv, normed, core, total, squeeze, low_x, middle_grad,
     params, up_bias, sums, down_in, up_in, down_last, up_last, out_in) = refs[:22]
    home, *summed, vec_out = refs[22:29]
    (down_out, up_out, qkv_out, out_out, small_out, put, out_here, out_sem, up, core_grad, lift, qkv_grad, small, ready, vectors, vec_got,
     own, send_d, recv_d, local, send, recv, vec_send, vec_recv) = refs[29:53]
    refs = refs[53:]
    units, plan = plan
    i = pl.program_id(0)
    m, tokens = core.shape[0], low_x.shape[1]
    batch, me = lax.axis_index("batch"), lax.axis_index("blk")
    places = {
        "up": (up_in, up_out),
        "up_last": (up_last, up_out),
        "down": (down_in, down_out),
        "down_last": (down_last, down_out),
        "out": (out_here, out_out),
        "qkv": (qkv_grad, qkv_out),
        "small": (small, small_out),
    }
    routes = []
    for k, (name, unit) in enumerate(units):
        count = len(unit.scratch())
        buffers, refs = refs[:count], refs[count:]
        source, result = places[name]
        if unit.kept == "first" or name == "qkv":
            source = source.at[unit.lead]
        routes.append(Route(unit, source, result, buffers, local.at[k], send.at[k], recv.at[k]))
    take_out = pltpu.make_async_copy(out_in, out_here, out_sem)
    wave = Wave(vectors, vec_got, vec_send, vec_recv)
    everyone = routes + [wave]

    def look(step, mark):
        @pl.when(i == step)
        def _():
            follow(everyone, plan[mark])

    @pl.when(i == 0)
    def _():
        for route in routes:
            if route.moved:
                route.fetch().start()
        take_out.start()
        greet([at_batch(batch ^ 1), at_batch(batch ^ 2)] + [at_blk(me ^ d) for d in range(1, n)])
        take_out.wait()
        up[...] = jnp.zeros_like(up)
        core_grad[...] = jnp.zeros_like(core_grad)
        lift[...] = jnp.zeros_like(lift)
        vectors[0] = jnp.zeros(vectors.shape[1:], F32)

    look(0, 0)
    steps = qkv_grad.shape[0]
    scale = 1.0 / math.sqrt(HD)
    keys = by_head(key[...] * jnp.asarray(scale, BF16))
    values = by_head(value[...])
    rows = mixed_grad.shape[0]
    dv = dk = None
    grads_q = []
    for r in range(rows // tile):
        at = slice(r * tile, (r + 1) * tile)
        grads = mixed_grad[at, :]
        back = contract(grads, values, 1, 1)
        low = weights[0, at, :]
        heads = []
        for h in range(LANES // HD):
            p = low[:, h * m : (h + 1) * m].astype(F32)
            g = back[:, h * m : (h + 1) * m]
            heads.append((p * (g - jnp.sum(p * g, axis=-1, keepdims=True))).astype(BF16))
        score = jnp.concatenate(heads, axis=1)
        part_v = own_head(contract(low, grads, 0, 0))
        part_k = own_head(contract(score, query[at, :], 0, 0))
        dv = part_v if dv is None else dv + part_v
        dk = part_k if dk is None else dk + part_k
        grads_q.append(contract(score, keys, 1, 0).astype(BF16))
        if r == 0:
            for step in range(steps):
                look(step, 2 * step + 1)
    dq = jnp.concatenate(grads_q, axis=0)
    dk = dk * scale
    dk_low, dv_low = dk.astype(BF16), dv.astype(BF16)
    up[...] += contract(dq, wq[...], 1, 1)
    core_grad[...] += contract(dk_low, wk[...], 1, 1) + contract(dv_low, wv[...], 1, 1)
    lanes = pl.ds(pl.multiple_of(i * LANES, LANES), LANES)
    lift[...] += jnp.sum(dk * params[3:4, lanes] + dv * params[4:5, lanes], axis=1, keepdims=True)
    for k, grad in enumerate(
        (
            contract(normed[...], dq, 0, 0),
            contract(core[...], dk_low, 0, 0),
            contract(core[...], dv_low, 0, 0),
        )
    ):
        block = grad.shape[0] // n
        for b in range(n):
            qkv_grad[i, b // 4, (b // 2) % 2, b % 2, :, k * LANES : (k + 1) * LANES] = grad[
                b * block : (b + 1) * block
            ].astype(BF16)
    vectors[0, 2:3, lanes] = jnp.sum(dq.astype(F32), axis=0, keepdims=True)
    vectors[0, 3:4, lanes] = jnp.sum(total[...] * dk, axis=0, keepdims=True)
    vectors[0, 4:5, lanes] = jnp.sum(total[...] * dv, axis=0, keepdims=True)

    for step in range(steps):
        look(step, 2 * step + 2)

    @pl.when(i == steps - 1)
    def _():
        width = low_x.shape[2]

        def ship(d):
            return remote(
                ready.at[me ^ d], home.at[me], send_d.at[d - 1], recv_d.at[d - 1], at_blk(me ^ d)
            )

        low_core = core_grad[...].astype(BF16)
        gain_sum = bias_sum = jnp.zeros((1, width), F32)
        mine = pltpu.make_async_copy(ready.at[me], home.at[me], own)
        for turn, d in enumerate(spread_order(n) + [0]):
            b = me ^ d
            at = pl.ds(pl.multiple_of(b * tokens, tokens), tokens)
            rise = up[at, :] + contract(squeeze[b], low_core, 0, 0)
            hat, rate = norm_stats(low_x[b].astype(F32))
            gain_sum += jnp.sum(rise * hat, axis=0, keepdims=True)
            bias_sum += jnp.sum(rise, axis=0, keepdims=True)
            ready[b] = (middle_grad[at, :] + norm_back(hat, rate, rise, params[0:1, :])).astype(BF16)
            if d:
                ship(d).start()
            else:
                mine.start()
            if turn == n // 2 - 1:
                follow(everyone, plan[2 * steps + 1])
        follow(everyone, plan[2 * steps + 2])
        for b in range(n):
            terms = contract(low_core, normed[b * tokens : (b + 1) * tokens, :], 1, 1) + lift[...]
            small[b // 4, (b // 2) % 2, b % 2] = terms.astype(BF16)
        vectors[0, 0:1, :] = gain_sum
        vectors[0, 1:2, :] = bias_sum
        vectors[0, 5:6, :] = sums[0:1, :]
        vectors[0, 6:7, :] = sums[1:2, :]
        vectors[0, 7:8, :] = sums[2:3, :]
        for k in range(up_bias.shape[1] // width):
            vectors[0, 8 + k : 9 + k, :] = up_bias[:, k * width : (k + 1) * width]
        vectors[0, 12:13, :] = sums[3:4, :]
        follow(everyone, plan[2 * steps + 3])
        puts = [
            pltpu.make_async_copy(source, target, put.at[k])
            for k, (source, target) in enumerate(
                zip((down_out, up_out, qkv_out, out_out, small_out), summed)
            )
        ]
        for copy in puts:
            copy.start()
        vec_out[...] = vectors[len(wave.hops)]
        for route in everyone:
            route.close()
        mine.wait()
        for d in range(1, n):
            ship(d).wait()
        for copy in puts:
            copy.wait()


def finish(mixed_grad, weights, query, key, value, normed, core, total, squeeze, low_x, middle_grad, params,
           qkv_weight, up_bias, sums, down, up, down_last, up_last, out, tile=512):
    n, m, tokens = squeeze.shape
    rows, width = normed.shape
    steps, heads = width // LANES, LANES // HD
    tall = width // n
    feeds, block = up.shape[0] + 1, up.shape[-1] * 2
    hidden = feeds * block
    deep = down.shape[-2] * 2
    out = out.reshape(2, 2, 2, tall, width)
    units = []
    for k in range(feeds):
        kept = "core" if k == feeds - 1 else "first"
        tail = "_last" if k == feeds - 1 else ""
        units.append(("up" + tail, Unit(tall, block, True, 0, block * k, kept, None, k)))
        units.append(("down" + tail, Unit(deep, width, False, deep * k, 0, kept, None, k)))
    units.append(("out", Unit(tall, width, False)))
    for k in range(steps):
        units.append(("qkv", Unit(tall, 3 * LANES, k % 2 == 0, 0, 3 * LANES * k, lead=k)))
    units.append(("small", Unit(m, tokens, False)))
    end = 2 * steps + 3
    jobs = []
    for name, unit in units:
        begin = {"qkv": 2 * unit.lead + 2, "small": end}.get(name, 0)
        jobs.append((begin, [(hop, hop_bytes(unit, hop)) for hop in unit.hops]))
    jobs.append((end, [(hop, 4 * VECTORS * width) for hop in ("core", "x", "y", "z1", "z2")]))
    plan = (units, plan_hops(jobs, MARKS, MARKS[2 * steps]))
    anywhere = pl.BlockSpec(memory_space=pl.ANY)
    vmem = pl.BlockSpec(memory_space=pltpu.VMEM)
    dma = pltpu.SemaphoreType.DMA
    blocks = (2, 2, 2, tall, width)
    results = [(hidden // n, width), (tall, hidden), (tall, 3 * width), (tall, width), (m, tokens)]
    scratch = [pltpu.VMEM(shape, BF16) for shape in results] + [
        dma((len(results),)),
        pltpu.VMEM(blocks, BF16),
        dma,
        pltpu.VMEM((rows, width), F32),
        pltpu.VMEM((m, width), F32),
        pltpu.VMEM((m, 1), F32),
        pltpu.VMEM((steps,) + blocks, BF16),
        pltpu.VMEM((2, 2, 2, m, tokens), BF16),
        pltpu.VMEM((n, tokens, width), BF16),
        pltpu.VMEM((6, VECTORS, width), F32),
        pltpu.VMEM((5, VECTORS, width), F32),
        dma,
        dma((n - 1,)),
        dma((n - 1,)),
        dma((len(units),)),
        dma((len(units), HOPS)),
        dma((len(units), HOPS)),
        dma((5,)),
        dma((5,)),
    ]
    for _, unit in units:
        scratch += unit.scratch()
    return pl.pallas_call(
        functools.partial(finish_kernel, n, tile, plan),
        grid=(steps,),
        in_specs=[
            columns(rows, 0),
            pl.BlockSpec((1, rows, heads * m), lambda i: (i, 0, 0)),
            columns(rows, 0),
            columns(m, 0),
            columns(m, 0),
        ]
        + [columns(width, k * steps) for k in range(3)]
        + [
            whole((rows, width)),
            whole((m, width)),
            whole((m, 1)),
            whole((n, m, tokens)),
            whole((n, tokens, width)),
            whole((rows, width)),
            whole(params.shape),
            whole((1, hidden)),
            whole((4, width)),
            anywhere,
            anywhere,
            anywhere,
            anywhere,
            anywhere,
        ],
        out_specs=[anywhere] * (1 + len(results)) + [whole((VECTORS, width))],
        out_shape=[jax.ShapeDtypeStruct((n, tokens, width), BF16)]
        + [jax.ShapeDtypeStruct(shape, BF16) for shape in results]
        + [jax.ShapeDtypeStruct((VECTORS, width), F32)],
        scratch_shapes=scratch,
        compiler_params=pltpu.CompilerParams(
            collective_id=1, has_side_effects=True, vmem_limit_bytes=67043328, dimension_semantics=("arbitrary",)
        ),
        name="finish",
    )(mixed_grad, weights, query, key, value, qkv_weight, qkv_weight, qkv_weight, normed, core,
      total, squeeze, low_x, middle_grad, params, up_bias, sums, down, up, down_last, up_last, out)


MARKS = (1.0, 4.5, 8.0, 11.5, 15.0, 18.5, 22.0, 26.0, 30.0, 33.0)


class Exchange:
    def __init__(self, source, target, own, send, recv):
        self.source, self.target = source, target
        self.own, self.send, self.recv = own, send, recv
        self.n = source.shape[0]
        self.me = lax.axis_index("blk")

    def copy(self, d):
        return remote(
            self.source.at[self.me ^ d],
            self.target.at[self.me],
            self.send.at[d - 1],
            self.recv.at[d - 1],
            at_blk(self.me ^ d),
        )

    def mine(self):
        return pltpu.make_async_copy(self.source.at[self.me], self.target.at[self.me], self.own)

    def start(self):
        for d in spread_order(self.n):
            self.copy(d).start()
        self.mine().start()

    def wait(self):
        self.mine().wait()
        for d in range(1, self.n):
            self.copy(d).wait()


def exchange_scratch(n):
    dma = pltpu.SemaphoreType.DMA
    return [dma, dma((n - 1,)), dma((n - 1,))]


def alive_here(counts):
    return lax.axis_index("blk") < counts[lax.axis_index("batch")]


def side_by_side(refs, axis):
    return jnp.concatenate([ref[...] for ref in refs], axis=axis)


COTS_FIRST = False
COTS_AFTER = 6
ARRIVAL = (1, 2, 3, 4, 5, 6, 7)


def open_kernel(n, nb, attends, feeds, tile, counts, inputs, cotangent, compress, *refs):
    given, refs = refs[:8], refs[8:]
    (wq, wk, wv, ow), refs = refs[:4], refs[4:]
    upw, dnw, refs = refs[:n], refs[n : 2 * n], refs[2 * n :]
    (low_x, normed, squeeze, low_cot, core_out, total_out, query, key, value, weights, mixed,
     middle, second, active, slope, output, vectors) = refs[:17]
    (x_here, n_here, e_part, e_here, core_sum, total, acc, core) = refs[17:25]
    (keep, send_e, recv_e, send_q, recv_q, own_q) = refs[25:31]
    x_sems, cot_sems = refs[31:34], refs[34:37]
    i = pl.program_id(0)
    me, batch = lax.axis_index("blk"), lax.axis_index("batch")
    tokens = inputs.shape[1]
    rows, m, width = n * tokens, compress.shape[0], inputs.shape[2]
    share = m // nb

    def vector(k):
        return vectors[k : k + 1, :]

    def quarter(q):
        return pl.ds(pl.multiple_of(q * share, share), share)

    xs = Exchange(inputs, x_here, *x_sems)
    cots = Exchange(cotangent, low_cot, *cot_sems)

    def piece(d):
        return remote(
            compress.at[quarter(batch)], e_part.at[me], send_e.at[d - 1], recv_e.at[d - 1], at_blk(me ^ d)
        )

    def pass_on(c):
        return remote(
            e_part, e_here.at[:, quarter(batch)], send_q.at[c - 1], recv_q.at[c - 1], at_batch(batch ^ c)
        )

    keep_part = pltpu.make_async_copy(e_part, e_here.at[:, quarter(batch)], own_q)

    keeps = [
        pltpu.make_async_copy(source, target, keep.at[k])
        for k, (source, target) in enumerate(((x_here, low_x), (n_here, normed), (e_here, squeeze)))
    ]

    @pl.when(i == 0)
    def _():
        greet([at_blk(me ^ d) for d in range(1, n)] + [at_batch(batch ^ c) for c in range(1, nb)])
        for d in range(1, n):
            piece(d).start()
        xs.start()
        if COTS_FIRST:
            cots.start()
        e_part[me] = compress[quarter(batch), :]
        row = 0
        for ref in given:
            for k in range(ref.shape[0] // width):
                vectors[row : row + 1, :] = ref[k * width : (k + 1) * width].reshape(1, width)
                row += 1
        core_sum[...] = jnp.zeros_like(core_sum)
        total[...] = jnp.zeros_like(total)
        for d in range(1, n):
            piece(d).wait_recv()
        for c in range(1, nb):
            pass_on(c).start()
        keep_part.start()

        def arrived(slot):
            low = (norm_stats(x_here[slot].astype(F32))[0] * vector(0) + vector(1)).astype(BF16)
            n_here[slot] = low

        def gather(slot):
            part = e_here[slot]
            core_sum[...] += contract(part, n_here[slot], 1, 0)
            total[...] += jnp.sum(part.astype(F32), axis=1, keepdims=True)

        xs.mine().wait()
        arrived(me)
        keep_part.wait()
        for c in range(1, nb):
            pass_on(c).wait_recv()
        gather(me)
        for d in ARRIVAL:
            xs.copy(d).wait_recv()
            if not COTS_FIRST and d == ARRIVAL[COTS_AFTER]:
                cots.start()
            arrived(me ^ d)
            gather(me ^ d)
        core[...] = core_sum[...].astype(BF16)
        core_out[...] = core[...]
        total_out[...] = total[...]
        for copy in keeps:
            copy.start()

    @pl.when(i < attends)
    def _():
        lanes = pl.ds(pl.multiple_of(i * LANES, LANES), LANES)
        bq, bk, bv = (vectors[k : k + 1, lanes] for k in (2, 3, 4))
        key[...] = (contract(core[...], wk[...], 1, 0) + total[...] * bk).astype(BF16)
        value[...] = (contract(core[...], wv[...], 1, 0) + total[...] * bv).astype(BF16)
        keys = by_head(key[...] * jnp.asarray(1.0 / math.sqrt(HD), BF16))
        values = by_head(value[...])
        for r in range(rows // tile):
            at = slice(r * tile, (r + 1) * tile)
            blocks = slice(r * tile // tokens, (r + 1) * tile // tokens)
            low_n = n_here[blocks].reshape(tile, -1)
            q = (contract(low_n, wq[...], 1, 0) + bq).astype(BF16)
            query[at, :] = q
            scores = contract(q, keys, 1, 1)
            heads = []
            for h in range(LANES // HD):
                s = scores[:, h * m : (h + 1) * m]
                e = jnp.exp(s - jnp.max(s, axis=-1, keepdims=True))
                heads.append((e * (1.0 / jnp.sum(e, axis=-1, keepdims=True))).astype(BF16))
            low = jnp.concatenate(heads, axis=1)
            weights[0, at, :] = low
            mixed[at, lanes] = contract(low, values, 1, 0).astype(BF16)

    @pl.when(i == attends)
    def _():
        mid = x_here[...].reshape(rows, -1).astype(F32) + contract(mixed[...], ow[...], 1, 0) + vector(5)
        middle[...] = mid
        second[...] = (norm_stats(mid)[0] * vector(6) + vector(7)).astype(BF16)
        acc[...] = mid + vector(12)

    @pl.when(i >= attends)
    def _():
        pieces = []
        for b in range(n):
            chosen = None
            for u in range(feeds):
                row, lane = divmod((b * feeds + u) * 128, width)
                here = vectors[8 + row : 9 + row, lane : lane + 128]
                chosen = here if u == 0 else jnp.where(i == attends + u, here, chosen)
            pieces.append(chosen)
        v = contract(second[...], side_by_side(upw, 1), 1, 0) + jnp.concatenate(pieces, axis=1)
        square = v * v
        t = jnp.tanh(v * (GELU_A + (GELU_A * GELU_B) * square))
        half = 0.5 + 0.5 * t
        act = (v * half).astype(BF16)
        active[...] = act
        slope[...] = (
            half + (0.5 * v) * (1.0 - t * t) * (GELU_A + (3 * GELU_A * GELU_B) * square)
        ).astype(BF16)
        acc[...] += contract(act, side_by_side(dnw, 0), 1, 0)

    @pl.when(i == pl.num_programs(0) - 1)
    def _():
        output[...] = jnp.where(alive_here(counts), acc[...], 0.0).astype(BF16).reshape(output.shape)
        for copy in keeps:
            copy.wait()
        for d in range(1, n):
            piece(d).wait_send()
            xs.copy(d).wait_send()
        for c in range(1, nb):
            pass_on(c).wait_send()
        cots.wait()


def open_all(nb, counts, inputs, cotangent, compress, given, qkv_weight, ow, upw, dnw, tile=512):
    n, tokens, width = inputs.shape
    rows, m, hidden = n * tokens, compress.shape[0], upw.shape[1]
    attends, heads = width // LANES, LANES // HD
    feeds = hidden // n // 128
    block = n * 128
    anywhere = pl.BlockSpec(memory_space=pl.ANY)

    def early(i):
        return jnp.minimum(i, attends - 1)

    def late(i):
        return jnp.maximum(i - attends, 0)

    def wide(height, start):
        return pl.BlockSpec((height, LANES), lambda i: (0, start + early(i)))

    def chunk(shape, dim, b):
        if dim:
            return pl.BlockSpec(shape, lambda i: (0, b * feeds + late(i)))
        return pl.BlockSpec(shape, lambda i: (b * feeds + late(i), 0))

    struct = jax.ShapeDtypeStruct
    dma = pltpu.SemaphoreType.DMA
    return pl.pallas_call(
        functools.partial(open_kernel, n, nb, attends, feeds, tile),
        grid=(attends + feeds,),
        in_specs=[pl.BlockSpec(memory_space=pltpu.SMEM), anywhere, anywhere, whole((m, tokens))]
        + [whole(v.shape) for v in given]
        + [wide(width, k * attends) for k in range(3)]
        + [whole((width, width))]
        + [chunk((width, 128), 1, b) for b in range(n)]
        + [chunk((128, width), 0, b) for b in range(n)],
        out_specs=[anywhere] * 4
        + [whole((m, width)), whole((m, 1)), wide(rows, 0), wide(m, 0), wide(m, 0)]
        + [pl.BlockSpec((1, rows, heads * m), lambda i: (early(i), 0, 0))]
        + [whole((rows, width))] * 3
        + [pl.BlockSpec((rows, block), lambda i: (0, late(i)))] * 2
        + [whole((n, tokens, width)), whole((VECTORS, width))],
        out_shape=[
            struct((n, tokens, width), BF16),
            struct((n, tokens, width), BF16),
            struct((n, m, tokens), BF16),
            struct((n, tokens, width), BF16),
            struct((m, width), BF16),
            struct((m, 1), F32),
            struct((rows, width), BF16),
            struct((m, width), BF16),
            struct((m, width), BF16),
            struct((attends, rows, heads * m), BF16),
            struct((rows, width), BF16),
            struct((rows, width), F32),
            struct((rows, width), BF16),
            struct((rows, hidden), BF16),
            struct((rows, hidden), BF16),
            struct((n, tokens, width), BF16),
            struct((VECTORS, width), F32),
        ],
        scratch_shapes=[
            pltpu.VMEM((n, tokens, width), BF16),
            pltpu.VMEM((n, tokens, width), BF16),
            pltpu.VMEM((n, m // nb, tokens), BF16),
            pltpu.VMEM((n, m, tokens), BF16),
            pltpu.VMEM((m, width), F32),
            pltpu.VMEM((m, 1), F32),
            pltpu.VMEM((rows, width), F32),
            pltpu.VMEM((m, width), BF16),
            dma((3,)),
            dma((n - 1,)),
            dma((n - 1,)),
            dma((nb - 1,)),
            dma((nb - 1,)),
            dma,
        ]
        + exchange_scratch(n)
        + exchange_scratch(n),
        compiler_params=pltpu.CompilerParams(
            collective_id=0, has_side_effects=True, vmem_limit_bytes=67043328, dimension_semantics=("arbitrary",)
        ),
        name="open",
    )(counts, inputs, cotangent, compress, *given, qkv_weight, qkv_weight, qkv_weight, ow, *[upw] * n, *[dnw] * n)


def back_kernel(n, units, counts, cot, result, active, slope, second, middle, mixed, *refs):
    upw, dnw, (ow, vectors), refs = refs[:n], refs[n : 2 * n], refs[2 * n : 2 * n + 2], refs[2 * n + 2 :]
    (home, up_part, down_part, up_last, down_last, up_bias_grad, middle_grad, mixed_grad, out_grad, sums) = refs[:10]
    (incoming, total, up_grad, down_grad, take, local, send, recv) = refs[10:18]
    outs = Exchange(result, home, *refs[18:21])
    refs = refs[21:]
    f = pl.program_id(0)
    batch, me = lax.axis_index("batch"), lax.axis_index("blk")
    feeds = len(units) // 2
    routes = []
    for k, unit in enumerate(units):
        count = len(unit.scratch())
        buffers, refs = refs[:count], refs[count:]
        source = (down_grad if k % 2 else up_grad).at[unit.lead]
        routes.append(Route(unit, source, None, buffers, local.at[k], send.at[k], recv.at[k]))
    pairs = [routes[2 * k : 2 * k + 2] for k in range(feeds)]

    def put(k):
        last = k == feeds - 1
        targets = (up_last, down_last) if last else (up_part.at[k], down_part.at[k])
        return [route.left_over(target) for route, target in zip(pairs[k], targets)]

    def advance(k, s):
        for route in pairs[k]:
            route.finish(s)
            if s + 1 < len(route.hops):
                route.start(s + 1)
        if s + 1 == len(pairs[k][0].hops):
            for copy in put(k):
                copy.start()

    @pl.when(f == 0)
    def _():
        fetch = pltpu.make_async_copy(cot, incoming, take)
        fetch.start()
        greet([at_batch(batch ^ 1), at_batch(batch ^ 2)] + [at_blk(me ^ d) for d in range(1, n)])
        outs.start()
        total[...] = jnp.zeros_like(total)
        fetch.wait()
        incoming[...] = jnp.where(alive_here(counts), incoming[...], jnp.zeros_like(incoming))

    low = incoming[...].reshape(total.shape)
    d = contract(low, side_by_side(dnw, 0), 1, 1)
    dh = (d * slope[...].astype(F32)).astype(BF16)
    up_bias_grad[...] = jnp.sum(dh.astype(F32), axis=0, keepdims=True)
    total[...] += contract(dh, side_by_side(upw, 1), 1, 1)

    for k in range(1, feeds):
        @pl.when(f == k)
        def _(k=k):
            if k > 1:
                advance(k - 2, 1)
            advance(k - 1, 0)

    grad = contract(active[...], low, 0, 0)
    for b in range(n):
        at = slice(b * 128, (b + 1) * 128)
        down_grad[f, b // 4, (b // 2) % 2, b % 2] = grad[at].astype(BF16)
    grad = contract(second[...], dh, 0, 0)
    tall = grad.shape[0] // n
    for b in range(n):
        at = slice(b * tall, (b + 1) * tall)
        up_grad[f, b // 4, (b // 2) % 2, b % 2] = grad[at].astype(BF16)

    for k in range(feeds):
        @pl.when(f == k)
        def _(k=k):
            for route in pairs[k]:
                route.start(0)

    @pl.when(f == feeds - 1)
    def _():
        hat, rate = norm_stats(middle[...])
        up = total[...]
        inc = low.astype(F32)
        grad = inc + norm_back(hat, rate, up, vectors[6:7, :])
        middle_grad[...] = grad
        branch = grad.astype(BF16)
        mixed_grad[...] = contract(branch, ow[...], 1, 1).astype(BF16)
        out_grad[...] = contract(mixed[...], branch, 0, 0).astype(BF16)
        sums[0:1, :] = jnp.sum(branch.astype(F32), axis=0, keepdims=True)
        sums[1:2, :] = jnp.sum(up * hat, axis=0, keepdims=True)
        sums[2:3, :] = jnp.sum(up, axis=0, keepdims=True)
        sums[3:4, :] = jnp.sum(inc, axis=0, keepdims=True)
        advance(feeds - 2, 1)
        advance(feeds - 1, 0)
        for k in range(feeds):
            for copy in put(k):
                copy.wait()
        for route in routes:
            route.close()
        outs.wait()


def back_all(counts, cot, result, active, slope, second, middle, mixed, upw, dnw, ow, vectors):
    n, tokens, width = cot.shape
    rows, hidden = active.shape
    feeds, block, tall = hidden // n // 128, n * 128, width // n
    anywhere = pl.BlockSpec(memory_space=pl.ANY)

    def chunk(shape, dim, b):
        if dim:
            return pl.BlockSpec(shape, lambda i: (0, b * feeds + i))
        return pl.BlockSpec(shape, lambda i: (b * feeds + i, 0))

    units = []
    for k in range(feeds):
        hops = 1 if k == feeds - 1 else 2
        units.append(Unit(tall, block, True, hops=hops, lead=k))
        units.append(Unit(128, width, False, hops=hops, lead=k))
    struct = jax.ShapeDtypeStruct
    dma = pltpu.SemaphoreType.DMA
    scratch = [
        pltpu.VMEM((n, tokens, width), BF16),
        pltpu.VMEM((rows, width), F32),
        pltpu.VMEM((feeds, 2, 2, 2, tall, block), BF16),
        pltpu.VMEM((feeds, 2, 2, 2, 128, width), BF16),
        dma,
        dma((len(units),)),
        dma((len(units), 2)),
        dma((len(units), 2)),
    ] + exchange_scratch(n)
    for unit in units:
        scratch += unit.scratch()
    return pl.pallas_call(
        functools.partial(back_kernel, n, units),
        grid=(feeds,),
        in_specs=[
            pl.BlockSpec(memory_space=pltpu.SMEM),
            anywhere,
            anywhere,
            columns(rows, 0, block),
            columns(rows, 0, block),
            whole((rows, width)),
            whole((rows, width)),
            whole((rows, width)),
        ]
        + [chunk((width, 128), 1, b) for b in range(n)]
        + [chunk((128, width), 0, b) for b in range(n)]
        + [whole((width, width)), whole(vectors.shape)],
        out_specs=[
            anywhere,
            anywhere,
            anywhere,
            anywhere,
            anywhere,
            columns(1, 0, block),
            whole((rows, width)),
            whole((rows, width)),
            whole((width, width)),
            whole((4, width)),
        ],
        out_shape=[
            struct((n, tokens, width), BF16),
            struct((feeds - 1, 2, 2, 2, tall // 2, block // 2), BF16),
            struct((feeds - 1, 2, 2, 64, width), BF16),
            struct((2, 2, 2, tall // 2, block), BF16),
            struct((2, 2, 2, 64, width), BF16),
            struct((1, hidden), F32),
            struct((rows, width), F32),
            struct((rows, width), BF16),
            struct((width, width), BF16),
            struct((4, width), F32),
        ],
        scratch_shapes=scratch,
        compiler_params=pltpu.CompilerParams(
            collective_id=2, has_side_effects=True, vmem_limit_bytes=67043328, dimension_semantics=("arbitrary",)
        ),
        name="back",
    )(counts, cot, result, active, slope, second, middle, mixed, *[upw] * n, *[dnw] * n, ow, vectors)


def settle_kernel(n, *refs):
    sources, targets, refs = refs[:8], refs[8:23], refs[23:]
    held, wide, take, put = refs[:8], refs[8:13], refs[13], refs[14]
    blk = lax.axis_index("blk")
    takes = [pltpu.make_async_copy(a, b, take.at[k]) for k, (a, b) in enumerate(zip(sources, held))]
    ready = list(held[:2]) + list(wide)
    puts = [pltpu.make_async_copy(a, b, put.at[k]) for k, (a, b) in enumerate(zip(ready, targets[:7]))]
    order = (3, 2, 4, 5, 6, 0, 1)
    for k in order + (7,):
        takes[k].start()
    for k in order:
        takes[k].wait()
        if k == 3:
            feeds = held[k].shape[1] // 128 // n
            for u in range(feeds):
                for b in range(n):
                    start, end = (u * n + b) * 128, (b * feeds + u) * 128
                    wide[1][:, end : end + 128] = held[k][:, start : start + 128].astype(F32)
        elif k == 4:
            steps = held[k].shape[1] // (3 * LANES)
            for i in range(steps):
                for j in range(3):
                    start, end = (i * 3 + j) * LANES, (j * steps + i) * LANES
                    wide[2][:, end : end + LANES] = held[k][:, start : start + LANES].astype(F32)
        elif k > 1:
            wide[k - 2][...] = held[k][...].astype(F32)
        puts[k].start()
    takes[7].wait()
    sums = held[7]
    width = sums.shape[1]
    small = width // n

    def cut(rows, size):
        line = rows[0] if len(rows) == 1 else jnp.concatenate(rows, axis=1)
        return pltpu.roll(line, line.shape[1] - blk * size, 1)[:, :size]

    row = [sums[k : k + 1, :] for k in range(13)]
    feeds = 4 * width // n // 128
    hidden = jnp.concatenate(row[8:12], axis=1)
    ups = [cut([hidden[:, u * n * 128 : (u + 1) * n * 128]], 128) for u in range(feeds)]
    lines = [
        cut([row[0]], small),
        cut([row[1]], small),
        cut(row[2:5], 3 * small),
        cut([row[5]], small),
        cut([row[6]], small),
        cut([row[7]], small),
        jnp.concatenate(ups, axis=1),
        cut([row[12]], small),
    ]
    for target, line in zip(targets[7:], lines):
        target[...] = line.reshape(target.shape)
    for copy in puts:
        copy.wait()


def settle(output, home, summed, sums):
    anywhere = pl.BlockSpec(memory_space=pl.ANY)
    vmem = pl.BlockSpec(memory_space=pltpu.VMEM)
    struct = jax.ShapeDtypeStruct
    dma = pltpu.SemaphoreType.DMA
    n, width = output.shape[0], output.shape[2]
    sizes = [width // n * k for k in (1, 1, 3, 1, 1, 1, 4, 1)]
    arrays = [output, home] + list(summed)
    return pl.pallas_call(
        functools.partial(settle_kernel, n),
        in_specs=[anywhere] * 8,
        out_specs=[anywhere] * 7 + [vmem] * 8,
        out_shape=[struct(output.shape, BF16), struct(home.shape, BF16)]
        + [struct(v.shape, F32) for v in summed]
        + [struct((size,), F32) for size in sizes],
        scratch_shapes=[pltpu.VMEM(v.shape, v.dtype) for v in arrays + [sums]]
        + [pltpu.VMEM(v.shape, F32) for v in summed]
        + [dma((8,)), dma((7,))],
        compiler_params=pltpu.CompilerParams(vmem_limit_bytes=60 << 20),
        name="settle",
    )(*arrays, sums)


def swap(values, axis, size, bit):
    return lax.ppermute(values, axis, [(i, i ^ bit) for i in range(size)])


def halve(values, dim, axis, size, bit):
    mine = (lax.axis_index(axis) // bit) % 2
    send = lax.dynamic_index_in_dim(values, 1 - mine, dim, keepdims=False).astype(BF16)
    keep = lax.dynamic_index_in_dim(values, mine, dim, keepdims=False)
    return keep.astype(F32) + swap(send, axis, size, bit).astype(F32)


def join(values, dim, axis, size, bit):
    mine = (lax.axis_index(axis) // bit) % 2
    other = swap(values, axis, size, bit)
    first = jnp.where(mine == 0, values, other)
    second = jnp.where(mine == 0, other, values)
    return jnp.concatenate([first, second], axis=dim)


def scatter_sum(terms, bits, order, nb, nk, early):
    _, rows, cols = terms.shape
    values = halve(terms.reshape(-1, 2, rows // 2, cols), 1, "batch", nb, 1)
    chips = [1 << i for i in range(1, nb.bit_length() - 1)]
    if early:
        for bit in chips:
            cols //= 2
            values = halve(values.reshape(-1, rows // 2, 2, cols), 2, "batch", nb, bit)
    left = list(bits)
    for bit in order:
        place = left.index(bit)
        values = values.reshape(1 << place, 2, -1, rows // 2, cols)
        values = halve(values, 1, "blk", nk, bit)
        left.remove(bit)
    values = values.reshape(rows // 2, cols).astype(BF16)
    for bit in reversed(chips) if early else chips:
        if early:
            values = join(values, 1, "batch", nb, bit)
        else:
            values = (values.astype(F32) + swap(values, "batch", nb, bit).astype(F32)).astype(BF16)
    return join(values, 0, "batch", nb, 1).astype(F32)


def body(
    inputs,
    cotangent,
    group_counts,
    first_gain,
    first_bias,
    qkv_weight,
    qkv_bias,
    out_weight,
    out_bias,
    second_gain,
    second_bias,
    up_weight,
    up_bias,
    down_weight,
    down_bias,
    compress,
    *,
    nb,
    nk,
):
    slots, tokens, width = inputs.shape
    splits = nk // slots
    teams = [[t * slots + i for i in range(slots)] for t in range(splits)]
    across = [[t * slots + i for t in range(splits)] for i in range(slots)]
    rows = slots * tokens
    low_first = [1 << i for i in range(nk.bit_length() - 1)]
    high_first = low_first[::-1]
    team_low = [1 << i for i in range(slots.bit_length() - 1)]

    def gather_rows(values):
        return lax.all_to_all(values, "blk", 0, 0, axis_index_groups=teams, tiled=True).reshape(
            rows, width
        )

    def spread_rows(values):
        return lax.all_to_all(
            values.reshape(slots, tokens, width), "blk", 0, 0, axis_index_groups=teams, tiled=True
        )

    def over_splits(values):
        if splits == 1:
            return values
        return lax.psum(values, "blk", axis_index_groups=across)

    def line(vector):
        return vector.reshape(1, -1)

    if nb == 4 and nk == slots == 8:
        lines = (
            first_gain,
            first_bias,
            qkv_bias,
            out_bias,
            second_gain,
            second_bias,
            up_bias,
            down_bias,
        )
        (
            low_x,
            normed,
            squeeze,
            low_cot,
            core,
            total,
            query,
            key,
            value,
            weights,
            mixed,
            middle,
            second,
            active,
            slope,
            result,
            vectors,
        ) = open_all(
            nb, group_counts, inputs, cotangent, compress, lines, qkv_weight, out_weight, up_weight, down_weight
        )
        (
            output,
            up_grad,
            down_grad,
            up_last,
            down_last,
            up_bias_grad,
            middle_grad,
            mixed_grad,
            out_grad,
            sums,
        ) = back_all(
            group_counts,
            low_cot,
            result,
            active,
            slope,
            second,
            middle,
            mixed,
            up_weight,
            down_weight,
            out_weight,
            vectors,
        )
        input_grad, *summed, flat = finish(
            mixed_grad,
            weights,
            query,
            key,
            value,
            normed.reshape(rows, width),
            core,
            total,
            squeeze,
            low_x,
            middle_grad,
            vectors,
            qkv_weight,
            up_bias_grad,
            sums,
            down_grad,
            up_grad,
            down_last,
            up_last,
            out_grad,
        )
        (
            output,
            input_grad,
            down_rows,
            up_rows,
            qkv_rows,
            out_rows,
            compress_rows,
            fg,
            fb,
            qb,
            ob,
            sg,
            sb,
            ub,
            db,
        ) = settle(output, input_grad, summed, flat)
    else:
        slot = lax.axis_index("blk") % slots
        alive = (slot < group_counts[lax.axis_index("batch")]).astype(jnp.int32).reshape(1)

        squeeze = compress[None]
        for bit in team_low[::-1]:
            squeeze = join(squeeze[:, None], 1, "blk", nk, bit)
            squeeze = squeeze.reshape((-1,) + compress.shape)
        low_x = gather_rows(inputs)
        hat_first, rate_first = norm_stats(low_x.astype(F32))
        normed = (hat_first * first_gain + first_bias).astype(BF16)
        core = jnp.einsum(
            "bjt,btc->jc",
            squeeze,
            normed.reshape(slots, tokens, width),
            preferred_element_type=F32,
        )
        total = jnp.sum(squeeze.astype(F32), axis=(0, 2))[:, None]
        low_cot = gather_rows(cotangent)
        core = over_splits(core).astype(BF16)
        total = over_splits(total)
        query, key, value, weights, mixed = attend(
            normed, core, total, qkv_weight, line(qkv_bias), tile=512
        )
        middle, second, active, slope, result = forward(
            alive,
            mixed,
            low_x,
            out_weight,
            line(out_bias),
            line(second_gain),
            line(second_bias),
            up_weight,
            line(up_bias),
            down_weight,
            line(down_bias),
        )
        output = spread_rows(result)
        up_grad, down_grad, up_bias_grad, middle_grad, mixed_grad, out_grad, sums = backward(
            alive,
            low_cot,
            active,
            slope,
            second,
            middle,
            mixed,
            up_weight,
            down_weight,
            out_weight,
            line(second_gain),
        )
        out_bias_grad, second_gain_grad, second_bias_grad, down_bias_grad = (sums[i] for i in range(4))
        (
            query_weight_grad,
            key_weight_grad,
            value_weight_grad,
            query_bias_grad,
            key_bias_grad,
            value_bias_grad,
            query_up,
            core_back,
            lift,
        ) = attend_back(
            mixed_grad, weights, query, key, value, normed, core, total, qkv_weight, line(qkv_bias)
        )
        core_back = over_splits(core_back).astype(BF16)
        lift = over_splits(lift)
        first_up = query_up + jnp.einsum(
            "bjt,jc->btc", squeeze, core_back, preferred_element_type=F32
        ).reshape(rows, width)
        first_gain_grad = jnp.sum(first_up * hat_first, axis=0)
        first_bias_grad = jnp.sum(first_up, axis=0)
        rows_grad = (
            middle_grad + norm_back(hat_first, rate_first, first_up, first_gain)
        ).astype(BF16)
        compress_terms = (
            jnp.einsum(
                "jc,btc->bjt",
                core_back,
                normed.reshape(slots, tokens, width),
                preferred_element_type=F32,
            )
            + lift[None]
        )

        vectors = (
            first_gain_grad,
            first_bias_grad,
            jnp.concatenate([query_bias_grad, key_bias_grad, value_bias_grad], axis=1),
            out_bias_grad,
            second_gain_grad,
            second_bias_grad,
            up_bias_grad,
            down_bias_grad,
        )
        sizes = [v.size // nk for v in vectors]
        packed = jnp.concatenate([v.reshape(nk, -1) for v in vectors], axis=1)
        tall = 32
        wide = -(-sum(sizes) // (tall * 128)) * 128
        packed = jnp.pad(packed, ((0, 0), (0, tall * wide - sum(sizes)))).reshape(nk, tall, wide)
        blocked = [
            grad.reshape(nk, grad.shape[0] // nk, grad.shape[1])
            for grad in (
                down_grad,
                up_grad,
                query_weight_grad,
                key_weight_grad,
                value_weight_grad,
                out_grad,
            )
        ]
        input_grad = spread_rows(rows_grad)
        blocked = blocked[:2] + [jnp.concatenate(blocked[2:], axis=2)]
        down_rows, up_rows, joined = (
            scatter_sum(grad, high_first, low_first, nb, nk, i > 0)
            for i, grad in enumerate(blocked)
        )
        qkv_rows, out_rows = joined[:, : 3 * width], joined[:, 3 * width :]
        compress_rows = scatter_sum(compress_terms, team_low[::-1], team_low, nb, nk, False)
        mine = scatter_sum(packed, high_first, low_first, nb, nk, False).reshape(-1)
        parts = []
        start = 0
        for size in sizes:
            parts.append(mine[start : start + size])
            start += size
        fg, fb, qb, ob, sg, sb, ub, db = parts
    return (
        output,
        input_grad,
        fg,
        fb,
        qkv_rows,
        qb,
        out_rows,
        ob,
        sg,
        sb,
        up_rows,
        ub,
        down_rows,
        db,
        compress_rows,
    )


def solution(mesh):
    rows = P("batch", "blk", None)
    placed = (rows, rows) + (P(),) * 13 + (P(None, "blk"),)
    vec, mat = P("blk"), P("blk", None)
    return jax.shard_map(
        functools.partial(body, nb=mesh.shape["batch"], nk=mesh.shape["blk"]),
        mesh=mesh,
        in_specs=placed,
        out_specs=(rows, rows, vec, vec, mat, vec, mat, vec, vec, vec, mat, vec, mat, vec)
        + (P(None, "blk"),),
        check_vma=False,
    )
```

```python
import functools
import math

import jax
import jax.numpy as jnp
from jax import lax
from jax.experimental import pallas as pl
from jax.experimental.pallas import tpu as pltpu
from jax.sharding import PartitionSpec as P

F32 = jnp.float32
BF16 = jnp.bfloat16
HD = 64
LANES = 256
GELU_A = math.sqrt(2.0 / math.pi)
GELU_B = 0.044715


def norm_stats(states):
    center = states - jnp.mean(states, axis=-1, keepdims=True)
    spread = jnp.mean(center * center, axis=-1, keepdims=True)
    rate = lax.rsqrt(spread + 1e-05)
    return center * rate, rate


def norm_back(hat, rate, upstream, gain):
    scaled = upstream * gain
    return rate * (
        scaled
        - jnp.mean(scaled, axis=-1, keepdims=True)
        - hat * jnp.mean(scaled * hat, axis=-1, keepdims=True)
    )


def contract(a, b, dim_a, dim_b):
    return lax.dot_general(a, b, (((dim_a,), (dim_b,)), ((), ())), preferred_element_type=F32)


def whole(shape):
    return pl.BlockSpec(shape, lambda *_: (0,) * len(shape), pipeline_mode=pl.Buffered(1))


def columns(height, start, width=LANES):
    return pl.BlockSpec((height, width), lambda i: (0, start + i))


def below(width, start, height=LANES):
    return pl.BlockSpec((height, width), lambda i: (start + i, 0))


PARAMS = dict(vmem_limit_bytes=62 << 20, dimension_semantics=("arbitrary",))


def by_head(values):
    lane = lax.broadcasted_iota(jnp.int32, values.shape, 1) // HD
    zero = jnp.zeros_like(values)
    return jnp.concatenate([jnp.where(lane == h, values, zero) for h in range(LANES // HD)], axis=0)


def own_head(values):
    n = values.shape[0] // (LANES // HD)
    lane = lax.broadcasted_iota(jnp.int32, (n, LANES), 1) // HD
    picked = values[:n]
    for h in range(1, LANES // HD):
        picked = jnp.where(lane == h, values[h * n : (h + 1) * n], picked)
    return picked


def attend_kernel(tile, normed, core, total, wq, wk, wv, bq, bk, bv, query, key, value, weights, mixed):
    rows, n = normed.shape[0], core.shape[0]
    key[...] = (contract(core[...], wk[...], 1, 0) + total[...] * bk[...]).astype(BF16)
    value[...] = (contract(core[...], wv[...], 1, 0) + total[...] * bv[...]).astype(BF16)
    keys = by_head(key[...] * jnp.asarray(1.0 / math.sqrt(HD), BF16))
    values = by_head(value[...])

    for r in range(rows // tile):
        at = slice(r * tile, (r + 1) * tile)
        q = (contract(normed[at, :], wq[...], 1, 0) + bq[...]).astype(BF16)
        query[at, :] = q
        scores = contract(q, keys, 1, 1)
        heads = []
        for h in range(LANES // HD):
            s = scores[:, h * n : (h + 1) * n]
            e = jnp.exp(s - jnp.max(s, axis=-1, keepdims=True))
            heads.append((e * (1.0 / jnp.sum(e, axis=-1, keepdims=True))).astype(BF16))
        low = jnp.concatenate(heads, axis=1)
        weights[0, at, :] = low
        mixed[at, :] = contract(low, values, 1, 0).astype(BF16)


def attend(normed, core, total, qkv_weight, qkv_bias, tile=1024):
    rows, width = normed.shape
    n = core.shape[0]
    steps = width // LANES
    heads = LANES // HD
    return pl.pallas_call(
        functools.partial(attend_kernel, tile),
        grid=(steps,),
        in_specs=[whole((rows, width)), whole((n, width)), whole((n, 1))]
        + [columns(width, k * steps) for k in range(3)]
        + [columns(1, k * steps) for k in range(3)],
        out_specs=[
            columns(rows, 0),
            columns(n, 0),
            columns(n, 0),
            pl.BlockSpec((1, rows, heads * n), lambda i: (i, 0, 0)),
            columns(rows, 0),
        ],
        out_shape=[
            jax.ShapeDtypeStruct((rows, width), BF16),
            jax.ShapeDtypeStruct((n, width), BF16),
            jax.ShapeDtypeStruct((n, width), BF16),
            jax.ShapeDtypeStruct((steps, rows, heads * n), BF16),
            jax.ShapeDtypeStruct((rows, width), BF16),
        ],
        compiler_params=pltpu.CompilerParams(**PARAMS),
        name="attend",
    )(normed, core, total, qkv_weight, qkv_weight, qkv_weight, qkv_bias, qkv_bias, qkv_bias)


def forward_kernel(tile, alive, mixed, states, ow, ob, gain, bias, upw, upb, dnw, dnb,
                   middle, second, active, slope, output, total):
    f = pl.program_id(0)
    rows = mixed.shape[0]

    @pl.when(f == 0)
    def _():
        mid = states[...].astype(F32) + contract(mixed[...], ow[...], 1, 0) + ob[...]
        middle[...] = mid
        second[...] = (norm_stats(mid)[0] * gain[...] + bias[...]).astype(BF16)
        total[...] = mid + dnb[...]

    for r in range(rows // tile):
        at = slice(r * tile, (r + 1) * tile)
        v = contract(second[at, :], upw[...], 1, 0) + upb[...]
        square = v * v
        t = jnp.tanh(v * (GELU_A + (GELU_A * GELU_B) * square))
        half = 0.5 + 0.5 * t
        act = (v * half).astype(BF16)
        active[at, :] = act
        slope[at, :] = (
            half + (0.5 * v) * (1.0 - t * t) * (GELU_A + (3 * GELU_A * GELU_B) * square)
        ).astype(BF16)
        total[at, :] += contract(act, dnw[...], 1, 0)

    @pl.when(f == pl.num_programs(0) - 1)
    def _():
        output[...] = jnp.where(alive[0] > 0, total[...], 0.0).astype(BF16)


def forward(alive, mixed, states, ow, ob, gain, bias, upw, upb, dnw, dnb, block=512, tile=1024):
    rows, width = mixed.shape
    hidden = upw.shape[1]
    vec = whole((1, width))
    return pl.pallas_call(
        functools.partial(forward_kernel, tile),
        grid=(hidden // block,),
        in_specs=[
            pl.BlockSpec(memory_space=pltpu.SMEM),
            whole((rows, width)),
            whole((rows, width)),
            whole((width, width)),
            vec,
            vec,
            vec,
            columns(width, 0, block),
            columns(1, 0, block),
            below(width, 0, block),
            vec,
        ],
        out_specs=[
            whole((rows, width)),
            whole((rows, width)),
            columns(rows, 0, block),
            columns(rows, 0, block),
            whole((rows, width)),
        ],
        out_shape=[
            jax.ShapeDtypeStruct((rows, width), F32),
            jax.ShapeDtypeStruct((rows, width), BF16),
            jax.ShapeDtypeStruct((rows, hidden), BF16),
            jax.ShapeDtypeStruct((rows, hidden), BF16),
            jax.ShapeDtypeStruct((rows, width), BF16),
        ],
        scratch_shapes=[pltpu.VMEM((rows, width), F32)],
        compiler_params=pltpu.CompilerParams(**PARAMS),
        name="forward",
    )(alive, mixed, states, ow, ob, gain, bias, upw, upb, dnw, dnb)


def backward_kernel(alive, cot, active, slope, second, middle, mixed, upw, dnw, ow, gain,
                    up_grad, down_grad, up_bias_grad, middle_grad, mixed_grad, out_grad, sums,
                    incoming, total):
    f = pl.program_id(0)

    @pl.when(f == 0)
    def _():
        incoming[...] = jnp.where(alive[0] > 0, cot[...], jnp.zeros_like(cot))
        total[...] = jnp.zeros_like(total)

    d = contract(incoming[...], dnw[...], 1, 1)
    dh = (d * slope[...].astype(F32)).astype(BF16)
    up_bias_grad[...] = jnp.sum(dh.astype(F32), axis=0, keepdims=True)
    total[...] += contract(dh, upw[...], 1, 1)
    down_grad[...] = contract(active[...], incoming[...], 0, 0).astype(BF16)
    up_grad[...] = contract(second[...], dh, 0, 0).astype(BF16)

    @pl.when(f == pl.num_programs(0) - 1)
    def _():
        hat, rate = norm_stats(middle[...])
        up = total[...]
        inc = incoming[...].astype(F32)
        grad = inc + norm_back(hat, rate, up, gain[...])
        middle_grad[...] = grad
        branch = grad.astype(BF16)
        mixed_grad[...] = contract(branch, ow[...], 1, 1).astype(BF16)
        out_grad[...] = contract(mixed[...], branch, 0, 0).astype(BF16)
        sums[0:1, :] = jnp.sum(branch.astype(F32), axis=0, keepdims=True)
        sums[1:2, :] = jnp.sum(up * hat, axis=0, keepdims=True)
        sums[2:3, :] = jnp.sum(up, axis=0, keepdims=True)
        sums[3:4, :] = jnp.sum(inc, axis=0, keepdims=True)


def backward(alive, cot, active, slope, second, middle, mixed, upw, dnw, ow, gain, block=512):
    rows, width = mixed.shape
    hidden = upw.shape[1]
    return pl.pallas_call(
        backward_kernel,
        grid=(hidden // block,),
        in_specs=[
            pl.BlockSpec(memory_space=pltpu.SMEM),
            whole((rows, width)),
            columns(rows, 0, block),
            columns(rows, 0, block),
            whole((rows, width)),
            whole((rows, width)),
            whole((rows, width)),
            columns(width, 0, block),
            below(width, 0, block),
            whole((width, width)),
            whole((1, width)),
        ],
        out_specs=[
            columns(width, 0, block),
            below(width, 0, block),
            columns(1, 0, block),
            whole((rows, width)),
            whole((rows, width)),
            whole((width, width)),
            whole((4, width)),
        ],
        out_shape=[
            jax.ShapeDtypeStruct((width, hidden), BF16),
            jax.ShapeDtypeStruct((hidden, width), BF16),
            jax.ShapeDtypeStruct((1, hidden), F32),
            jax.ShapeDtypeStruct((rows, width), F32),
            jax.ShapeDtypeStruct((rows, width), BF16),
            jax.ShapeDtypeStruct((width, width), BF16),
            jax.ShapeDtypeStruct((4, width), F32),
        ],
        scratch_shapes=[pltpu.VMEM((rows, width), BF16), pltpu.VMEM((rows, width), F32)],
        compiler_params=pltpu.CompilerParams(**PARAMS),
        name="backward",
    )(alive, cot, active, slope, second, middle, mixed, upw, dnw, ow, gain)


def attend_back_kernel(mixed_grad, weights, query, key, value, normed, core, total, wq, wk, wv, bk, bv,
                       query_grad, key_grad, value_grad, qb, kb, vb, up, core_grad, lift):
    i = pl.program_id(0)
    n = core.shape[0]

    @pl.when(i == 0)
    def _():
        up[...] = jnp.zeros_like(up)
        core_grad[...] = jnp.zeros_like(core_grad)
        lift[...] = jnp.zeros_like(lift)

    keys = by_head(key[...] * jnp.asarray(1.0 / math.sqrt(HD), BF16))
    values = by_head(value[...])
    grads = mixed_grad[...]
    back = contract(grads, values, 1, 1)
    heads = []
    for h in range(LANES // HD):
        p = weights[0, :, h * n : (h + 1) * n].astype(F32)
        g = back[:, h * n : (h + 1) * n]
        heads.append((p * (g - jnp.sum(p * g, axis=-1, keepdims=True))).astype(BF16))
    score = jnp.concatenate(heads, axis=1)
    dv = own_head(contract(weights[0], grads, 0, 0))
    dk = own_head(contract(score, query[...], 0, 0)) * (1.0 / math.sqrt(HD))
    dq = contract(score, keys, 1, 0).astype(BF16)
    dk_low, dv_low = dk.astype(BF16), dv.astype(BF16)
    up[...] += contract(dq, wq[...], 1, 1)
    core_grad[...] += contract(dk_low, wk[...], 1, 1) + contract(dv_low, wv[...], 1, 1)
    lift[...] += jnp.sum(dk * bk[...] + dv * bv[...], axis=1, keepdims=True)
    query_grad[...] = contract(normed[...], dq, 0, 0).astype(BF16)
    key_grad[...] = contract(core[...], dk_low, 0, 0).astype(BF16)
    value_grad[...] = contract(core[...], dv_low, 0, 0).astype(BF16)
    qb[...] = jnp.sum(dq.astype(F32), axis=0, keepdims=True)
    kb[...] = jnp.sum(total[...] * dk, axis=0, keepdims=True)
    vb[...] = jnp.sum(total[...] * dv, axis=0, keepdims=True)


def attend_back(mixed_grad, weights, query, key, value, normed, core, total, qkv_weight, qkv_bias):
    rows, width = normed.shape
    n = core.shape[0]
    steps = width // LANES
    heads = LANES // HD
    return pl.pallas_call(
        attend_back_kernel,
        grid=(steps,),
        in_specs=[
            columns(rows, 0),
            pl.BlockSpec((1, rows, heads * n), lambda i: (i, 0, 0)),
            columns(rows, 0),
            columns(n, 0),
            columns(n, 0),
            whole((rows, width)),
            whole((n, width)),
            whole((n, 1)),
        ]
        + [columns(width, k * steps) for k in range(3)]
        + [columns(1, k * steps) for k in range(1, 3)],
        out_specs=[columns(width, 0)] * 3
        + [columns(1, 0)] * 3
        + [whole((rows, width)), whole((n, width)), whole((n, 1))],
        out_shape=[jax.ShapeDtypeStruct((width, width), BF16)] * 3
        + [jax.ShapeDtypeStruct((1, width), F32)] * 3
        + [
            jax.ShapeDtypeStruct((rows, width), F32),
            jax.ShapeDtypeStruct((n, width), F32),
            jax.ShapeDtypeStruct((n, 1), F32),
        ],
        compiler_params=pltpu.CompilerParams(**PARAMS),
        name="attend_back",
    )(mixed_grad, weights, query, key, value, normed, core, total, qkv_weight, qkv_weight, qkv_weight, qkv_bias, qkv_bias)


MESH = pl.DeviceIdType.MESH


def at_batch(other):
    return {"batch": other}


def at_blk(other):
    return {"blk": other}


def remote(source, target, send, arrive, where):
    return pltpu.make_async_remote_copy(
        src_ref=source, dst_ref=target, send_sem=send, recv_sem=arrive, device_id=where, device_id_type=MESH
    )


def greet(places):
    barrier = pltpu.get_barrier_semaphore()
    for where in places:
        pl.semaphore_signal(barrier, inc=1, device_id=where, device_id_type=MESH)
    pl.semaphore_wait(barrier, len(places))


def spread_order(n, far_first=True):
    return sorted(range(1, n), key=lambda d: ((d & (n // 2)) * (-1 if far_first else 1), d))


class Unit:
    def __init__(self, rows, cols, early, result_top=0, result_left=0, kept="all", hops=None, lead=0):
        self.half, self.cols, self.early = rows // 2, cols, early
        self.result_top, self.result_left = result_top, result_left
        self.kept, self.lead = kept, lead
        every = ["core", "x", "y", "z1", "z2", "join", "pair"]
        if not early:
            every = ["core", "y", "z1", "z2", "late", "pair"]
        begin = {"all": 0, "core": 1, "first": 2}[kept]
        self.hops = every[begin : None if hops is None else begin + hops]

    def shape_after(self, hop):
        h, c = self.half, self.cols
        narrow = c // 2 if self.early else c
        return {
            "core": (2, 2, 2, h, c),
            "x": (2, 2, 2, h, narrow),
            "y": (2, 2, h, narrow),
            "z1": (2, h, narrow),
            "z2": (h, narrow),
            "late": (h, c),
        }.get(hop)

    def kept_shape(self):
        if self.kept == "core":
            return self.shape_after("core")
        return self.shape_after("x" if self.early else "y")

    def scratch(self):
        shapes = [] if self.kept == "all" else [self.kept_shape()]
        shapes += [self.shape_after(hop) for hop in self.hops if self.shape_after(hop)]
        return [pltpu.VMEM(shape, BF16) for shape in shapes]


HOPS = 7


class Route:
    def __init__(self, unit, source, result, buffers, local, send, recv):
        self.unit, self.source, self.result = unit, source, result
        self.hops = unit.hops
        self.moved = unit.kept != "all"
        self.acc, self.got = (buffers[0], buffers[1:]) if self.moved else (source, buffers)
        self.local, self.send, self.recv = local, send, recv
        self.batch, self.blk = lax.axis_index("batch"), lax.axis_index("blk")
        self.core, self.x = self.batch % 2, self.batch // 2
        self.z2, self.z1, self.y = self.blk // 4, (self.blk // 2) % 2, self.blk % 2

    def rows(self, top, core):
        return pl.ds(pl.multiple_of(top + core * self.unit.half, 16), self.unit.half)

    def lanes(self, left, x):
        u = self.unit
        if not u.early:
            return pl.ds(left, u.cols)
        return pl.ds(pl.multiple_of(left + x * (u.cols // 2), 128), u.cols // 2)

    def inside(self, x):
        rows = slice(None) if self.moved else self.rows(0, self.core)
        if self.unit.kept == "first":
            return rows, slice(None)
        return rows, self.lanes(0, x)

    def blocks(self, *place):
        if self.unit.kept == "first" and not self.unit.early:
            return place[:2]
        return place

    def copy(self, s):
        hop = self.hops[s]
        u, acc, mine = self.unit, self.acc, self.inside(self.x)
        y, z1, z2 = self.y, self.z1, self.z2
        every = slice(None)
        where = {
            "core": at_batch(self.batch ^ 1),
            "pair": at_batch(self.batch ^ 1),
            "x": at_batch(self.batch ^ 2),
            "late": at_batch(self.batch ^ 2),
            "join": at_batch(self.batch ^ 2),
            "y": at_blk(self.blk ^ 1),
            "z1": at_blk(self.blk ^ 2),
            "z2": at_blk(self.blk ^ 4),
        }[hop]
        if hop in ("join", "pair"):
            lanes = pl.ds(u.result_left, u.cols)
            if hop == "join":
                lanes = self.lanes(u.result_left, self.x)
            source = target = self.result.at[self.rows(u.result_top, self.core), lanes]
        else:
            target = self.got[s]
            if hop == "core":
                source = self.source.at[:, :, :, self.rows(0, 1 - self.core)]
            elif hop == "x":
                source = acc.at[(every, every, every) + self.inside(1 - self.x)]
            else:
                place = {
                    "y": (every, every, 1 - y),
                    "z1": (every, 1 - z1, y),
                    "z2": (1 - z2, z1, y),
                    "late": (z2, z1, y),
                }[hop]
                source = acc.at[self.blocks(*place) + mine]
        return remote(source, target, self.send.at[s], self.recv.at[s], where)

    def fetch(self):
        return pltpu.make_async_copy(self.source, self.acc, self.local)

    def left_over(self, target):
        every = slice(None)
        rows = self.rows(0, self.core)
        if len(self.hops) == 1:
            source = self.acc.at[:, :, :, rows]
        elif self.unit.early:
            source = self.acc.at[:, :, :, rows, self.lanes(0, self.x)]
        else:
            source = self.acc.at[:, :, self.y, rows]
        return pltpu.make_async_copy(source, target, self.local)

    def start(self, s):
        if s == 0 and self.moved:
            self.fetch().wait()
        self.copy(s).start()

    def finish(self, s):
        hop = self.hops[s]
        acc, mine, every = self.acc, self.inside(self.x), (slice(None), slice(None))
        self.copy(s).wait_recv()
        pairs = [(a, b) for a in range(2) for b in range(2)]

        def add(place, other):
            acc[place] = acc[place] + self.got[s][other]

        if hop in ("core", "x"):
            inside = (mine[0], slice(None)) if hop == "core" else mine
            for a, b in pairs:
                for c in range(2):
                    add((a, b, c) + inside, (a, b, c) + every)
        elif hop == "y":
            for a, b in pairs:
                add((a, b, self.y) + mine, (a, b) + every)
        elif hop == "z1":
            for a in range(2):
                add(self.blocks(a, self.z1, self.y) + mine, (a,) + every)
        elif hop == "z2" and not self.unit.early:
            add(self.blocks(self.z2, self.z1, self.y) + mine, every)
        elif hop in ("z2", "late"):
            place = self.blocks(self.z2, self.z1, self.y) + mine
            u = self.unit
            self.result[self.rows(u.result_top, self.core), self.lanes(u.result_left, self.x)] = (
                acc[place] + self.got[s][...]
            )

    def close(self):
        for s in range(len(self.hops)):
            self.copy(s).wait_send()


class Wave:
    def __init__(self, steps, got, send, recv):
        self.steps, self.got, self.send, self.recv = steps, got, send, recv
        batch, blk = lax.axis_index("batch"), lax.axis_index("blk")
        self.hops = [at_batch(batch ^ 1), at_batch(batch ^ 2), at_blk(blk ^ 1), at_blk(blk ^ 2), at_blk(blk ^ 4)]

    def copy(self, s):
        return remote(self.steps.at[s], self.got.at[s], self.send.at[s], self.recv.at[s], self.hops[s])

    def start(self, s):
        self.copy(s).start()

    def finish(self, s):
        self.copy(s).wait_recv()
        self.steps[s + 1] = self.steps[s] + self.got[s]

    def close(self):
        for s in range(len(self.hops)):
            self.copy(s).wait_send()


DELAY = {k: a * 1.2 for k, a in {"core": 1.5, "x": 2.2, "y": 2.2, "z1": 2.2, "z2": 3.0}.items()}
RATE = {k: (a * 0.8, b * 0.8) for k, (a, b) in {"core": (260e3, 260e3), "x": (45e3, 45e3), "y": (45e3, 30e3), "z1": (45e3, 18e3), "z2": (22e3, 9e3)}.items()}
LINK = {"pair": "core", "late": "x", "join": "x"}


def hop_bytes(unit, hop):
    shape = unit.shape_after(hop)
    if shape is None:
        shape = (unit.half, unit.cols // 2 if hop == "join" else unit.cols)
    return 2 * math.prod(shape)


def plan_hops(jobs, marks, busy_from):
    free = {link: 0.0 for link in RATE}
    due = {}
    result = []

    def begin(job, number, now):
        hop, size = jobs[job][1][number]
        link = LINK.get(hop, hop)
        start = max(now, free[link])
        free[link] = start + size / RATE[link][now >= busy_from]
        due[job] = (free[link] + DELAY[link], number)

    for k, mark in enumerate(marks):
        now, last, events = mark, k == len(marks) - 1, []
        for job, (ready, _) in enumerate(jobs):
            if ready == k:
                events.append((job, 0, False))
                begin(job, 0, now)
        while due:
            job = min(due, key=lambda j: due[j][0])
            when, number = due[job]
            if when > now:
                if not last:
                    break
                now = when
            now += 0.2 if last else 0.0
            del due[job]
            events.append((job, number, True))
            if number + 1 < len(jobs[job][1]):
                begin(job, number + 1, now)
        result.append(events)
    return result


def follow(routes, events):
    for job, number, ends in events:
        route = routes[job]
        if ends:
            route.finish(number)
            number += 1
        if number < len(route.hops):
            route.start(number)


VECTORS = 16


def finish_kernel(n, tile, plan, *refs):
    (mixed_grad, weights, query, key, value, wq, wk, wv, normed, core, total, squeeze, low_x, middle_grad,
     params, up_bias, sums, down_in, up_in, down_last, up_last, out_in) = refs[:22]
    home, *summed, vec_out = refs[22:29]
    (down_out, up_out, qkv_out, out_out, small_out, put, out_here, out_sem, up, core_grad, lift, qkv_grad, small, ready, vectors, vec_got,
     own, send_d, recv_d, local, send, recv, vec_send, vec_recv) = refs[29:53]
    refs = refs[53:]
    units, plan = plan
    i = pl.program_id(0)
    m, tokens = core.shape[0], low_x.shape[1]
    batch, me = lax.axis_index("batch"), lax.axis_index("blk")
    places = {
        "up": (up_in, up_out),
        "up_last": (up_last, up_out),
        "down": (down_in, down_out),
        "down_last": (down_last, down_out),
        "out": (out_here, out_out),
        "qkv": (qkv_grad, qkv_out),
        "small": (small, small_out),
    }
    routes = []
    for k, (name, unit) in enumerate(units):
        count = len(unit.scratch())
        buffers, refs = refs[:count], refs[count:]
        source, result = places[name]
        if unit.kept == "first" or name == "qkv":
            source = source.at[unit.lead]
        routes.append(Route(unit, source, result, buffers, local.at[k], send.at[k], recv.at[k]))
    take_out = pltpu.make_async_copy(out_in, out_here, out_sem)
    wave = Wave(vectors, vec_got, vec_send, vec_recv)
    everyone = routes + [wave]

    def look(step, mark):
        @pl.when(i == step)
        def _():
            follow(everyone, plan[mark])

    @pl.when(i == 0)
    def _():
        for route in routes:
            if route.moved:
                route.fetch().start()
        take_out.start()
        greet([at_batch(batch ^ 1), at_batch(batch ^ 2)] + [at_blk(me ^ d) for d in range(1, n)])
        take_out.wait()
        up[...] = jnp.zeros_like(up)
        core_grad[...] = jnp.zeros_like(core_grad)
        lift[...] = jnp.zeros_like(lift)
        vectors[0] = jnp.zeros(vectors.shape[1:], F32)

    look(0, 0)
    steps = qkv_grad.shape[0]
    scale = 1.0 / math.sqrt(HD)
    keys = by_head(key[...] * jnp.asarray(scale, BF16))
    values = by_head(value[...])
    rows = mixed_grad.shape[0]
    dv = dk = None
    grads_q = []
    for r in range(rows // tile):
        at = slice(r * tile, (r + 1) * tile)
        grads = mixed_grad[at, :]
        back = contract(grads, values, 1, 1)
        low = weights[0, at, :]
        heads = []
        for h in range(LANES // HD):
            p = low[:, h * m : (h + 1) * m].astype(F32)
            g = back[:, h * m : (h + 1) * m]
            heads.append((p * (g - jnp.sum(p * g, axis=-1, keepdims=True))).astype(BF16))
        score = jnp.concatenate(heads, axis=1)
        part_v = own_head(contract(low, grads, 0, 0))
        part_k = own_head(contract(score, query[at, :], 0, 0))
        dv = part_v if dv is None else dv + part_v
        dk = part_k if dk is None else dk + part_k
        grads_q.append(contract(score, keys, 1, 0).astype(BF16))
        if r == 0:
            for step in range(steps):
                look(step, 2 * step + 1)
    dq = jnp.concatenate(grads_q, axis=0)
    dk = dk * scale
    dk_low, dv_low = dk.astype(BF16), dv.astype(BF16)
    up[...] += contract(dq, wq[...], 1, 1)
    core_grad[...] += contract(dk_low, wk[...], 1, 1) + contract(dv_low, wv[...], 1, 1)
    lanes = pl.ds(pl.multiple_of(i * LANES, LANES), LANES)
    lift[...] += jnp.sum(dk * params[3:4, lanes] + dv * params[4:5, lanes], axis=1, keepdims=True)
    for k, grad in enumerate(
        (
            contract(normed[...], dq, 0, 0),
            contract(core[...], dk_low, 0, 0),
            contract(core[...], dv_low, 0, 0),
        )
    ):
        block = grad.shape[0] // n
        for b in range(n):
            qkv_grad[i, b // 4, (b // 2) % 2, b % 2, :, k * LANES : (k + 1) * LANES] = grad[
                b * block : (b + 1) * block
            ].astype(BF16)
    vectors[0, 2:3, lanes] = jnp.sum(dq.astype(F32), axis=0, keepdims=True)
    vectors[0, 3:4, lanes] = jnp.sum(total[...] * dk, axis=0, keepdims=True)
    vectors[0, 4:5, lanes] = jnp.sum(total[...] * dv, axis=0, keepdims=True)

    for step in range(steps):
        look(step, 2 * step + 2)

    @pl.when(i == steps - 1)
    def _():
        width = low_x.shape[2]

        def ship(d):
            return remote(
                ready.at[me ^ d], home.at[me], send_d.at[d - 1], recv_d.at[d - 1], at_blk(me ^ d)
            )

        low_core = core_grad[...].astype(BF16)
        gain_sum = bias_sum = jnp.zeros((1, width), F32)
        mine = pltpu.make_async_copy(ready.at[me], home.at[me], own)
        for turn, d in enumerate(spread_order(n) + [0]):
            b = me ^ d
            at = pl.ds(pl.multiple_of(b * tokens, tokens), tokens)
            rise = up[at, :] + contract(squeeze[b], low_core, 0, 0)
            hat, rate = norm_stats(low_x[b].astype(F32))
            gain_sum += jnp.sum(rise * hat, axis=0, keepdims=True)
            bias_sum += jnp.sum(rise, axis=0, keepdims=True)
            ready[b] = (middle_grad[at, :] + norm_back(hat, rate, rise, params[0:1, :])).astype(BF16)
            if d:
                ship(d).start()
            else:
                mine.start()
            if turn == n // 2 - 1:
                follow(everyone, plan[2 * steps + 1])
        follow(everyone, plan[2 * steps + 2])
        for b in range(n):
            terms = contract(low_core, normed[b * tokens : (b + 1) * tokens, :], 1, 1) + lift[...]
            small[b // 4, (b // 2) % 2, b % 2] = terms.astype(BF16)
        vectors[0, 0:1, :] = gain_sum
        vectors[0, 1:2, :] = bias_sum
        vectors[0, 5:6, :] = sums[0:1, :]
        vectors[0, 6:7, :] = sums[1:2, :]
        vectors[0, 7:8, :] = sums[2:3, :]
        for k in range(up_bias.shape[1] // width):
            vectors[0, 8 + k : 9 + k, :] = up_bias[:, k * width : (k + 1) * width]
        vectors[0, 12:13, :] = sums[3:4, :]
        follow(everyone, plan[2 * steps + 3])
        puts = [
            pltpu.make_async_copy(source, target, put.at[k])
            for k, (source, target) in enumerate(
                zip((down_out, up_out, qkv_out, out_out, small_out), summed)
            )
        ]
        for copy in puts:
            copy.start()
        vec_out[...] = vectors[len(wave.hops)]
        for route in everyone:
            route.close()
        mine.wait()
        for d in range(1, n):
            ship(d).wait()
        for copy in puts:
            copy.wait()


def finish(mixed_grad, weights, query, key, value, normed, core, total, squeeze, low_x, middle_grad, params,
           qkv_weight, up_bias, sums, down, up, down_last, up_last, out, tile=512):
    n, m, tokens = squeeze.shape
    rows, width = normed.shape
    steps, heads = width // LANES, LANES // HD
    tall = width // n
    feeds, block = up.shape[0] + 1, up.shape[-1] * 2
    hidden = feeds * block
    deep = down.shape[-2] * 2
    out = out.reshape(2, 2, 2, tall, width)
    units = []
    for k in range(feeds):
        kept = "core" if k == feeds - 1 else "first"
        tail = "_last" if k == feeds - 1 else ""
        units.append(("up" + tail, Unit(tall, block, True, 0, block * k, kept, None, k)))
        units.append(("down" + tail, Unit(deep, width, k == feeds - 1, deep * k, 0, kept, None, k)))
    units.append(("out", Unit(tall, width, True)))
    for k in range(steps):
        units.append(("qkv", Unit(tall, 3 * LANES, True, 0, 3 * LANES * k, lead=k)))
    units.append(("small", Unit(m, tokens, False)))
    end = 2 * steps + 3
    jobs = []
    for name, unit in units:
        begin = {"qkv": 2 * unit.lead + 2, "small": end}.get(name, 0)
        jobs.append((begin, [(hop, hop_bytes(unit, hop)) for hop in unit.hops]))
    jobs.append((end, [(hop, 4 * VECTORS * width) for hop in ("core", "x", "y", "z1", "z2")]))
    plan = (units, plan_hops(jobs, MARKS, MARKS[2 * steps]))
    anywhere = pl.BlockSpec(memory_space=pl.ANY)
    vmem = pl.BlockSpec(memory_space=pltpu.VMEM)
    dma = pltpu.SemaphoreType.DMA
    blocks = (2, 2, 2, tall, width)
    results = [(hidden // n, width), (tall, hidden), (tall, 3 * width), (tall, width), (m, tokens)]
    scratch = [pltpu.VMEM(shape, BF16) for shape in results] + [
        dma((len(results),)),
        pltpu.VMEM(blocks, BF16),
        dma,
        pltpu.VMEM((rows, width), F32),
        pltpu.VMEM((m, width), F32),
        pltpu.VMEM((m, 1), F32),
        pltpu.VMEM((steps,) + blocks, BF16),
        pltpu.VMEM((2, 2, 2, m, tokens), BF16),
        pltpu.VMEM((n, tokens, width), BF16),
        pltpu.VMEM((6, VECTORS, width), F32),
        pltpu.VMEM((5, VECTORS, width), F32),
        dma,
        dma((n - 1,)),
        dma((n - 1,)),
        dma((len(units),)),
        dma((len(units), HOPS)),
        dma((len(units), HOPS)),
        dma((5,)),
        dma((5,)),
    ]
    for _, unit in units:
        scratch += unit.scratch()
    return pl.pallas_call(
        functools.partial(finish_kernel, n, tile, plan),
        grid=(steps,),
        in_specs=[
            columns(rows, 0),
            pl.BlockSpec((1, rows, heads * m), lambda i: (i, 0, 0)),
            columns(rows, 0),
            columns(m, 0),
            columns(m, 0),
        ]
        + [columns(width, k * steps) for k in range(3)]
        + [
            whole((rows, width)),
            whole((m, width)),
            whole((m, 1)),
            whole((n, m, tokens)),
            whole((n, tokens, width)),
            whole((rows, width)),
            whole(params.shape),
            whole((1, hidden)),
            whole((4, width)),
            anywhere,
            anywhere,
            anywhere,
            anywhere,
            anywhere,
        ],
        out_specs=[anywhere] * (1 + len(results)) + [whole((VECTORS, width))],
        out_shape=[jax.ShapeDtypeStruct((n, tokens, width), BF16)]
        + [jax.ShapeDtypeStruct(shape, BF16) for shape in results]
        + [jax.ShapeDtypeStruct((VECTORS, width), F32)],
        scratch_shapes=scratch,
        compiler_params=pltpu.CompilerParams(
            collective_id=1, has_side_effects=True, vmem_limit_bytes=67043328, dimension_semantics=("arbitrary",)
        ),
        name="finish",
    )(mixed_grad, weights, query, key, value, qkv_weight, qkv_weight, qkv_weight, normed, core,
      total, squeeze, low_x, middle_grad, params, up_bias, sums, down, up, down_last, up_last, out)


MARKS = (1, 5.2, 9.5, 13.8, 18, 22.5, 27, 31, 35, 38)


class Exchange:
    def __init__(self, source, target, own, send, recv):
        self.source, self.target = source, target
        self.own, self.send, self.recv = own, send, recv
        self.n = source.shape[0]
        self.me = lax.axis_index("blk")

    def copy(self, d):
        return remote(
            self.source.at[self.me ^ d],
            self.target.at[self.me],
            self.send.at[d - 1],
            self.recv.at[d - 1],
            at_blk(self.me ^ d),
        )

    def mine(self):
        return pltpu.make_async_copy(self.source.at[self.me], self.target.at[self.me], self.own)

    def start(self, far_first=True):
        for d in spread_order(self.n, far_first):
            self.copy(d).start()
        self.mine().start()

    def wait(self):
        self.mine().wait()
        for d in range(1, self.n):
            self.copy(d).wait()


def exchange_scratch(n):
    dma = pltpu.SemaphoreType.DMA
    return [dma, dma((n - 1,)), dma((n - 1,))]


def alive_here(counts):
    return lax.axis_index("blk") < counts[lax.axis_index("batch")]


def side_by_side(refs, axis):
    return jnp.concatenate([ref[...] for ref in refs], axis=axis)


COTS_FIRST = False
COTS_AFTER = 6
ARRIVAL = (1, 2, 3, 4, 5, 6, 7)


def open_kernel(n, nb, attends, feeds, tile, counts, inputs, cotangent, compress, *refs):
    given, refs = refs[:8], refs[8:]
    (wq, wk, wv, ow), refs = refs[:4], refs[4:]
    upw, dnw, refs = refs[:n], refs[n : 2 * n], refs[2 * n :]
    (low_x, normed, squeeze, low_cot, core_out, total_out, query, key, value, weights, mixed,
     middle, second, active, slope, output, vectors) = refs[:17]
    (x_here, n_here, e_part, e_here, core_sum, total, acc, core) = refs[17:25]
    (keep, send_e, recv_e, send_q, recv_q, own_q) = refs[25:31]
    x_sems, cot_sems = refs[31:34], refs[34:37]
    i = pl.program_id(0)
    me, batch = lax.axis_index("blk"), lax.axis_index("batch")
    tokens = inputs.shape[1]
    rows, m, width = n * tokens, compress.shape[0], inputs.shape[2]
    share = m // nb

    def vector(k):
        return vectors[k : k + 1, :]

    def quarter(q):
        return pl.ds(pl.multiple_of(q * share, share), share)

    xs = Exchange(inputs, x_here, *x_sems)
    cots = Exchange(cotangent, low_cot, *cot_sems)

    def piece(d):
        return remote(
            compress.at[quarter(batch)], e_part.at[me], send_e.at[d - 1], recv_e.at[d - 1], at_blk(me ^ d)
        )

    def pass_on(c):
        return remote(
            e_part, e_here.at[:, quarter(batch)], send_q.at[c - 1], recv_q.at[c - 1], at_batch(batch ^ c)
        )

    keep_part = pltpu.make_async_copy(e_part, e_here.at[:, quarter(batch)], own_q)

    keeps = [
        pltpu.make_async_copy(source, target, keep.at[k])
        for k, (source, target) in enumerate(((x_here, low_x), (n_here, normed), (e_here, squeeze)))
    ]

    @pl.when(i == 0)
    def _():
        greet([at_blk(me ^ d) for d in range(1, n)] + [at_batch(batch ^ c) for c in range(1, nb)])
        for d in range(1, n):
            piece(d).start()
        xs.start(False)
        if COTS_FIRST:
            cots.start()
        e_part[me] = compress[quarter(batch), :]
        row = 0
        for ref in given:
            for k in range(ref.shape[0] // width):
                vectors[row : row + 1, :] = ref[k * width : (k + 1) * width].reshape(1, width)
                row += 1
        core_sum[...] = jnp.zeros_like(core_sum)
        total[...] = jnp.zeros_like(total)
        for d in range(1, n):
            piece(d).wait_recv()
        for c in range(1, nb):
            pass_on(c).start()
        keep_part.start()

        def arrived(slot):
            low = (norm_stats(x_here[slot].astype(F32))[0] * vector(0) + vector(1)).astype(BF16)
            n_here[slot] = low

        def gather(slot):
            part = e_here[slot]
            core_sum[...] += contract(part, n_here[slot], 1, 0)
            total[...] += jnp.sum(part.astype(F32), axis=1, keepdims=True)

        xs.mine().wait()
        arrived(me)
        keep_part.wait()
        for c in range(1, nb):
            pass_on(c).wait_recv()
        gather(me)
        for d in ARRIVAL:
            xs.copy(d).wait_recv()
            if not COTS_FIRST and d == ARRIVAL[COTS_AFTER]:
                cots.start(False)
            arrived(me ^ d)
            gather(me ^ d)
        core[...] = core_sum[...].astype(BF16)
        core_out[...] = core[...]
        total_out[...] = total[...]
        for copy in keeps:
            copy.start()

    @pl.when(i < attends)
    def _():
        lanes = pl.ds(pl.multiple_of(i * LANES, LANES), LANES)
        bq, bk, bv = (vectors[k : k + 1, lanes] for k in (2, 3, 4))
        key[...] = (contract(core[...], wk[...], 1, 0) + total[...] * bk).astype(BF16)
        value[...] = (contract(core[...], wv[...], 1, 0) + total[...] * bv).astype(BF16)
        keys = by_head(key[...] * jnp.asarray(1.0 / math.sqrt(HD), BF16))
        values = by_head(value[...])
        for r in range(rows // tile):
            at = slice(r * tile, (r + 1) * tile)
            blocks = slice(r * tile // tokens, (r + 1) * tile // tokens)
            low_n = n_here[blocks].reshape(tile, -1)
            q = (contract(low_n, wq[...], 1, 0) + bq).astype(BF16)
            query[at, :] = q
            scores = contract(q, keys, 1, 1)
            heads = []
            for h in range(LANES // HD):
                s = scores[:, h * m : (h + 1) * m]
                e = jnp.exp(s - jnp.max(s, axis=-1, keepdims=True))
                heads.append((e * (1.0 / jnp.sum(e, axis=-1, keepdims=True))).astype(BF16))
            low = jnp.concatenate(heads, axis=1)
            weights[0, at, :] = low
            mixed[at, lanes] = contract(low, values, 1, 0).astype(BF16)

    @pl.when(i == attends)
    def _():
        mid = x_here[...].reshape(rows, -1).astype(F32) + contract(mixed[...], ow[...], 1, 0) + vector(5)
        middle[...] = mid
        second[...] = (norm_stats(mid)[0] * vector(6) + vector(7)).astype(BF16)
        acc[...] = mid + vector(12)

    @pl.when(i >= attends)
    def _():
        pieces = []
        for b in range(n):
            chosen = None
            for u in range(feeds):
                row, lane = divmod((b * feeds + u) * 128, width)
                here = vectors[8 + row : 9 + row, lane : lane + 128]
                chosen = here if u == 0 else jnp.where(i == attends + u, here, chosen)
            pieces.append(chosen)
        v = contract(second[...], side_by_side(upw, 1), 1, 0) + jnp.concatenate(pieces, axis=1)
        square = v * v
        t = jnp.tanh(v * (GELU_A + (GELU_A * GELU_B) * square))
        half = 0.5 + 0.5 * t
        act = (v * half).astype(BF16)
        active[...] = act
        slope[...] = (
            half + (0.5 * v) * (1.0 - t * t) * (GELU_A + (3 * GELU_A * GELU_B) * square)
        ).astype(BF16)
        acc[...] += contract(act, side_by_side(dnw, 0), 1, 0)

    @pl.when(i == pl.num_programs(0) - 1)
    def _():
        output[...] = jnp.where(alive_here(counts), acc[...], 0.0).astype(BF16).reshape(output.shape)
        for copy in keeps:
            copy.wait()
        for d in range(1, n):
            piece(d).wait_send()
            xs.copy(d).wait_send()
        for c in range(1, nb):
            pass_on(c).wait_send()
        cots.wait()


def open_all(nb, counts, inputs, cotangent, compress, given, qkv_weight, ow, upw, dnw, tile=512):
    n, tokens, width = inputs.shape
    rows, m, hidden = n * tokens, compress.shape[0], upw.shape[1]
    attends, heads = width // LANES, LANES // HD
    feeds = hidden // n // 128
    block = n * 128
    anywhere = pl.BlockSpec(memory_space=pl.ANY)

    def early(i):
        return jnp.minimum(i, attends - 1)

    def late(i):
        return jnp.maximum(i - attends, 0)

    def wide(height, start):
        return pl.BlockSpec((height, LANES), lambda i: (0, start + early(i)))

    def chunk(shape, dim, b):
        if dim:
            return pl.BlockSpec(shape, lambda i: (0, b * feeds + late(i)))
        return pl.BlockSpec(shape, lambda i: (b * feeds + late(i), 0))

    struct = jax.ShapeDtypeStruct
    dma = pltpu.SemaphoreType.DMA
    return pl.pallas_call(
        functools.partial(open_kernel, n, nb, attends, feeds, tile),
        grid=(attends + feeds,),
        in_specs=[pl.BlockSpec(memory_space=pltpu.SMEM), anywhere, anywhere, whole((m, tokens))]
        + [whole(v.shape) for v in given]
        + [wide(width, k * attends) for k in range(3)]
        + [whole((width, width))]
        + [chunk((width, 128), 1, b) for b in range(n)]
        + [chunk((128, width), 0, b) for b in range(n)],
        out_specs=[anywhere] * 4
        + [whole((m, width)), whole((m, 1)), wide(rows, 0), wide(m, 0), wide(m, 0)]
        + [pl.BlockSpec((1, rows, heads * m), lambda i: (early(i), 0, 0))]
        + [whole((rows, width))] * 3
        + [pl.BlockSpec((rows, block), lambda i: (0, late(i)))] * 2
        + [whole((n, tokens, width)), whole((VECTORS, width))],
        out_shape=[
            struct((n, tokens, width), BF16),
            struct((n, tokens, width), BF16),
            struct((n, m, tokens), BF16),
            struct((n, tokens, width), BF16),
            struct((m, width), BF16),
            struct((m, 1), F32),
            struct((rows, width), BF16),
            struct((m, width), BF16),
            struct((m, width), BF16),
            struct((attends, rows, heads * m), BF16),
            struct((rows, width), BF16),
            struct((rows, width), F32),
            struct((rows, width), BF16),
            struct((rows, hidden), BF16),
            struct((rows, hidden), BF16),
            struct((n, tokens, width), BF16),
            struct((VECTORS, width), F32),
        ],
        scratch_shapes=[
            pltpu.VMEM((n, tokens, width), BF16),
            pltpu.VMEM((n, tokens, width), BF16),
            pltpu.VMEM((n, m // nb, tokens), BF16),
            pltpu.VMEM((n, m, tokens), BF16),
            pltpu.VMEM((m, width), F32),
            pltpu.VMEM((m, 1), F32),
            pltpu.VMEM((rows, width), F32),
            pltpu.VMEM((m, width), BF16),
            dma((3,)),
            dma((n - 1,)),
            dma((n - 1,)),
            dma((nb - 1,)),
            dma((nb - 1,)),
            dma,
        ]
        + exchange_scratch(n)
        + exchange_scratch(n),
        compiler_params=pltpu.CompilerParams(
            collective_id=0, has_side_effects=True, vmem_limit_bytes=67043328, dimension_semantics=("arbitrary",)
        ),
        name="open",
    )(counts, inputs, cotangent, compress, *given, qkv_weight, qkv_weight, qkv_weight, ow, *[upw] * n, *[dnw] * n)


def back_kernel(n, units, counts, cot, result, active, slope, second, middle, mixed, *refs):
    upw, dnw, (ow, vectors), refs = refs[:n], refs[n : 2 * n], refs[2 * n : 2 * n + 2], refs[2 * n + 2 :]
    (home, up_part, down_part, up_last, down_last, up_bias_grad, middle_grad, mixed_grad, out_grad, sums) = refs[:10]
    (incoming, total, up_grad, down_grad, take, local, send, recv) = refs[10:18]
    outs = Exchange(result, home, *refs[18:21])
    refs = refs[21:]
    f = pl.program_id(0)
    batch, me = lax.axis_index("batch"), lax.axis_index("blk")
    feeds = len(units) // 2
    routes = []
    for k, unit in enumerate(units):
        count = len(unit.scratch())
        buffers, refs = refs[:count], refs[count:]
        source = (down_grad if k % 2 else up_grad).at[unit.lead]
        routes.append(Route(unit, source, None, buffers, local.at[k], send.at[k], recv.at[k]))
    pairs = [routes[2 * k : 2 * k + 2] for k in range(feeds)]

    def put(k):
        last = k == feeds - 1
        targets = (up_last, down_last) if last else (up_part.at[k], down_part.at[k])
        return [route.left_over(target) for route, target in zip(pairs[k], targets)]

    def advance(k, s):
        for route in pairs[k]:
            route.finish(s)
            if s + 1 < len(route.hops):
                route.start(s + 1)
        if s + 1 == len(pairs[k][0].hops):
            for copy in put(k):
                copy.start()

    @pl.when(f == 0)
    def _():
        fetch = pltpu.make_async_copy(cot, incoming, take)
        fetch.start()
        greet([at_batch(batch ^ 1), at_batch(batch ^ 2)] + [at_blk(me ^ d) for d in range(1, n)])
        outs.start()
        total[...] = jnp.zeros_like(total)
        fetch.wait()
        incoming[...] = jnp.where(alive_here(counts), incoming[...], jnp.zeros_like(incoming))

    low = incoming[...].reshape(total.shape)
    d = contract(low, side_by_side(dnw, 0), 1, 1)
    dh = (d * slope[...].astype(F32)).astype(BF16)
    up_bias_grad[...] = jnp.sum(dh.astype(F32), axis=0, keepdims=True)
    total[...] += contract(dh, side_by_side(upw, 1), 1, 1)

    for k in range(1, feeds):
        @pl.when(f == k)
        def _(k=k):
            if k > 1:
                advance(k - 2, 1)
            advance(k - 1, 0)

    grad = contract(active[...], low, 0, 0)
    for b in range(n):
        at = slice(b * 128, (b + 1) * 128)
        down_grad[f, b // 4, (b // 2) % 2, b % 2] = grad[at].astype(BF16)
    grad = contract(second[...], dh, 0, 0)
    tall = grad.shape[0] // n
    for b in range(n):
        at = slice(b * tall, (b + 1) * tall)
        up_grad[f, b // 4, (b // 2) % 2, b % 2] = grad[at].astype(BF16)

    for k in range(feeds):
        @pl.when(f == k)
        def _(k=k):
            for route in pairs[k]:
                route.start(0)

    @pl.when(f == feeds - 1)
    def _():
        hat, rate = norm_stats(middle[...])
        up = total[...]
        inc = low.astype(F32)
        grad = inc + norm_back(hat, rate, up, vectors[6:7, :])
        middle_grad[...] = grad
        branch = grad.astype(BF16)
        mixed_grad[...] = contract(branch, ow[...], 1, 1).astype(BF16)
        out_grad[...] = contract(mixed[...], branch, 0, 0).astype(BF16)
        sums[0:1, :] = jnp.sum(branch.astype(F32), axis=0, keepdims=True)
        sums[1:2, :] = jnp.sum(up * hat, axis=0, keepdims=True)
        sums[2:3, :] = jnp.sum(up, axis=0, keepdims=True)
        sums[3:4, :] = jnp.sum(inc, axis=0, keepdims=True)
        advance(feeds - 2, 1)
        advance(feeds - 1, 0)
        for k in range(feeds):
            for copy in put(k):
                copy.wait()
        for route in routes:
            route.close()
        outs.wait()


def back_all(counts, cot, result, active, slope, second, middle, mixed, upw, dnw, ow, vectors):
    n, tokens, width = cot.shape
    rows, hidden = active.shape
    feeds, block, tall = hidden // n // 128, n * 128, width // n
    anywhere = pl.BlockSpec(memory_space=pl.ANY)

    def chunk(shape, dim, b):
        if dim:
            return pl.BlockSpec(shape, lambda i: (0, b * feeds + i))
        return pl.BlockSpec(shape, lambda i: (b * feeds + i, 0))

    units = []
    for k in range(feeds):
        hops = 1 if k == feeds - 1 else 2
        units.append(Unit(tall, block, True, hops=hops, lead=k))
        units.append(Unit(128, width, k == feeds - 1, hops=hops, lead=k))
    struct = jax.ShapeDtypeStruct
    dma = pltpu.SemaphoreType.DMA
    scratch = [
        pltpu.VMEM((n, tokens, width), BF16),
        pltpu.VMEM((rows, width), F32),
        pltpu.VMEM((feeds, 2, 2, 2, tall, block), BF16),
        pltpu.VMEM((feeds, 2, 2, 2, 128, width), BF16),
        dma,
        dma((len(units),)),
        dma((len(units), 2)),
        dma((len(units), 2)),
    ] + exchange_scratch(n)
    for unit in units:
        scratch += unit.scratch()
    return pl.pallas_call(
        functools.partial(back_kernel, n, units),
        grid=(feeds,),
        in_specs=[
            pl.BlockSpec(memory_space=pltpu.SMEM),
            anywhere,
            anywhere,
            columns(rows, 0, block),
            columns(rows, 0, block),
            whole((rows, width)),
            whole((rows, width)),
            whole((rows, width)),
        ]
        + [chunk((width, 128), 1, b) for b in range(n)]
        + [chunk((128, width), 0, b) for b in range(n)]
        + [whole((width, width)), whole(vectors.shape)],
        out_specs=[
            anywhere,
            anywhere,
            anywhere,
            anywhere,
            anywhere,
            columns(1, 0, block),
            whole((rows, width)),
            whole((rows, width)),
            whole((width, width)),
            whole((4, width)),
        ],
        out_shape=[
            struct((n, tokens, width), BF16),
            struct((feeds - 1, 2, 2, 2, tall // 2, block // 2), BF16),
            struct((feeds - 1, 2, 2, 64, width), BF16),
            struct((2, 2, 2, tall // 2, block), BF16),
            struct((2, 2, 2, 64, width), BF16),
            struct((1, hidden), F32),
            struct((rows, width), F32),
            struct((rows, width), BF16),
            struct((width, width), BF16),
            struct((4, width), F32),
        ],
        scratch_shapes=scratch,
        compiler_params=pltpu.CompilerParams(
            collective_id=2, has_side_effects=True, vmem_limit_bytes=67043328, dimension_semantics=("arbitrary",)
        ),
        name="back",
    )(counts, cot, result, active, slope, second, middle, mixed, *[upw] * n, *[dnw] * n, ow, vectors)


def settle_kernel(n, *refs):
    sources, targets, refs = refs[:8], refs[8:23], refs[23:]
    held, wide, take, put = refs[:8], refs[8:13], refs[13], refs[14]
    blk = lax.axis_index("blk")
    takes = [pltpu.make_async_copy(a, b, take.at[k]) for k, (a, b) in enumerate(zip(sources, held))]
    ready = list(held[:2]) + list(wide)
    puts = [pltpu.make_async_copy(a, b, put.at[k]) for k, (a, b) in enumerate(zip(ready, targets[:7]))]
    order = (3, 2, 4, 5, 6, 0, 1)
    for k in order + (7,):
        takes[k].start()
    for k in order:
        takes[k].wait()
        if k == 3:
            feeds = held[k].shape[1] // 128 // n
            for u in range(feeds):
                for b in range(n):
                    start, end = (u * n + b) * 128, (b * feeds + u) * 128
                    wide[1][:, end : end + 128] = held[k][:, start : start + 128].astype(F32)
        elif k == 4:
            steps = held[k].shape[1] // (3 * LANES)
            for i in range(steps):
                for j in range(3):
                    start, end = (i * 3 + j) * LANES, (j * steps + i) * LANES
                    wide[2][:, end : end + LANES] = held[k][:, start : start + LANES].astype(F32)
        elif k > 1:
            wide[k - 2][...] = held[k][...].astype(F32)
        puts[k].start()
    takes[7].wait()
    sums = held[7]
    width = sums.shape[1]
    small = width // n

    def cut(rows, size):
        line = rows[0] if len(rows) == 1 else jnp.concatenate(rows, axis=1)
        return pltpu.roll(line, line.shape[1] - blk * size, 1)[:, :size]

    row = [sums[k : k + 1, :] for k in range(13)]
    feeds = 4 * width // n // 128
    hidden = jnp.concatenate(row[8:12], axis=1)
    ups = [cut([hidden[:, u * n * 128 : (u + 1) * n * 128]], 128) for u in range(feeds)]
    lines = [
        cut([row[0]], small),
        cut([row[1]], small),
        cut(row[2:5], 3 * small),
        cut([row[5]], small),
        cut([row[6]], small),
        cut([row[7]], small),
        jnp.concatenate(ups, axis=1),
        cut([row[12]], small),
    ]
    for target, line in zip(targets[7:], lines):
        target[...] = line.reshape(target.shape)
    for copy in puts:
        copy.wait()


def settle(output, home, summed, sums):
    anywhere = pl.BlockSpec(memory_space=pl.ANY)
    vmem = pl.BlockSpec(memory_space=pltpu.VMEM)
    struct = jax.ShapeDtypeStruct
    dma = pltpu.SemaphoreType.DMA
    n, width = output.shape[0], output.shape[2]
    sizes = [width // n * k for k in (1, 1, 3, 1, 1, 1, 4, 1)]
    arrays = [output, home] + list(summed)
    return pl.pallas_call(
        functools.partial(settle_kernel, n),
        in_specs=[anywhere] * 8,
        out_specs=[anywhere] * 7 + [vmem] * 8,
        out_shape=[struct(output.shape, BF16), struct(home.shape, BF16)]
        + [struct(v.shape, F32) for v in summed]
        + [struct((size,), F32) for size in sizes],
        scratch_shapes=[pltpu.VMEM(v.shape, v.dtype) for v in arrays + [sums]]
        + [pltpu.VMEM(v.shape, F32) for v in summed]
        + [dma((8,)), dma((7,))],
        compiler_params=pltpu.CompilerParams(vmem_limit_bytes=60 << 20),
        name="settle",
    )(*arrays, sums)


def swap(values, axis, size, bit):
    return lax.ppermute(values, axis, [(i, i ^ bit) for i in range(size)])


def halve(values, dim, axis, size, bit):
    mine = (lax.axis_index(axis) // bit) % 2
    send = lax.dynamic_index_in_dim(values, 1 - mine, dim, keepdims=False).astype(BF16)
    keep = lax.dynamic_index_in_dim(values, mine, dim, keepdims=False)
    return keep.astype(F32) + swap(send, axis, size, bit).astype(F32)


def join(values, dim, axis, size, bit):
    mine = (lax.axis_index(axis) // bit) % 2
    other = swap(values, axis, size, bit)
    first = jnp.where(mine == 0, values, other)
    second = jnp.where(mine == 0, other, values)
    return jnp.concatenate([first, second], axis=dim)


def scatter_sum(terms, bits, order, nb, nk, early):
    _, rows, cols = terms.shape
    values = halve(terms.reshape(-1, 2, rows // 2, cols), 1, "batch", nb, 1)
    chips = [1 << i for i in range(1, nb.bit_length() - 1)]
    if early:
        for bit in chips:
            cols //= 2
            values = halve(values.reshape(-1, rows // 2, 2, cols), 2, "batch", nb, bit)
    left = list(bits)
    for bit in order:
        place = left.index(bit)
        values = values.reshape(1 << place, 2, -1, rows // 2, cols)
        values = halve(values, 1, "blk", nk, bit)
        left.remove(bit)
    values = values.reshape(rows // 2, cols).astype(BF16)
    for bit in reversed(chips) if early else chips:
        if early:
            values = join(values, 1, "batch", nb, bit)
        else:
            values = (values.astype(F32) + swap(values, "batch", nb, bit).astype(F32)).astype(BF16)
    return join(values, 0, "batch", nb, 1).astype(F32)


def body(
    inputs,
    cotangent,
    group_counts,
    first_gain,
    first_bias,
    qkv_weight,
    qkv_bias,
    out_weight,
    out_bias,
    second_gain,
    second_bias,
    up_weight,
    up_bias,
    down_weight,
    down_bias,
    compress,
    *,
    nb,
    nk,
):
    slots, tokens, width = inputs.shape
    splits = nk // slots
    teams = [[t * slots + i for i in range(slots)] for t in range(splits)]
    across = [[t * slots + i for t in range(splits)] for i in range(slots)]
    rows = slots * tokens
    low_first = [1 << i for i in range(nk.bit_length() - 1)]
    high_first = low_first[::-1]
    team_low = [1 << i for i in range(slots.bit_length() - 1)]

    def gather_rows(values):
        return lax.all_to_all(values, "blk", 0, 0, axis_index_groups=teams, tiled=True).reshape(
            rows, width
        )

    def spread_rows(values):
        return lax.all_to_all(
            values.reshape(slots, tokens, width), "blk", 0, 0, axis_index_groups=teams, tiled=True
        )

    def over_splits(values):
        if splits == 1:
            return values
        return lax.psum(values, "blk", axis_index_groups=across)

    def line(vector):
        return vector.reshape(1, -1)

    if nb == 4 and nk == slots == 8:
        lines = (
            first_gain,
            first_bias,
            qkv_bias,
            out_bias,
            second_gain,
            second_bias,
            up_bias,
            down_bias,
        )
        (
            low_x,
            normed,
            squeeze,
            low_cot,
            core,
            total,
            query,
            key,
            value,
            weights,
            mixed,
            middle,
            second,
            active,
            slope,
            result,
            vectors,
        ) = open_all(
            nb, group_counts, inputs, cotangent, compress, lines, qkv_weight, out_weight, up_weight, down_weight
        )
        (
            output,
            up_grad,
            down_grad,
            up_last,
            down_last,
            up_bias_grad,
            middle_grad,
            mixed_grad,
            out_grad,
            sums,
        ) = back_all(
            group_counts,
            low_cot,
            result,
            active,
            slope,
            second,
            middle,
            mixed,
            up_weight,
            down_weight,
            out_weight,
            vectors,
        )
        input_grad, *summed, flat = finish(
            mixed_grad,
            weights,
            query,
            key,
            value,
            normed.reshape(rows, width),
            core,
            total,
            squeeze,
            low_x,
            middle_grad,
            vectors,
            qkv_weight,
            up_bias_grad,
            sums,
            down_grad,
            up_grad,
            down_last,
            up_last,
            out_grad,
        )
        (
            output,
            input_grad,
            down_rows,
            up_rows,
            qkv_rows,
            out_rows,
            compress_rows,
            fg,
            fb,
            qb,
            ob,
            sg,
            sb,
            ub,
            db,
        ) = settle(output, input_grad, summed, flat)
    else:
        slot = lax.axis_index("blk") % slots
        alive = (slot < group_counts[lax.axis_index("batch")]).astype(jnp.int32).reshape(1)

        squeeze = compress[None]
        for bit in team_low[::-1]:
            squeeze = join(squeeze[:, None], 1, "blk", nk, bit)
            squeeze = squeeze.reshape((-1,) + compress.shape)
        low_x = gather_rows(inputs)
        hat_first, rate_first = norm_stats(low_x.astype(F32))
        normed = (hat_first * first_gain + first_bias).astype(BF16)
        core = jnp.einsum(
            "bjt,btc->jc",
            squeeze,
            normed.reshape(slots, tokens, width),
            preferred_element_type=F32,
        )
        total = jnp.sum(squeeze.astype(F32), axis=(0, 2))[:, None]
        low_cot = gather_rows(cotangent)
        core = over_splits(core).astype(BF16)
        total = over_splits(total)
        query, key, value, weights, mixed = attend(
            normed, core, total, qkv_weight, line(qkv_bias), tile=512
        )
        middle, second, active, slope, result = forward(
            alive,
            mixed,
            low_x,
            out_weight,
            line(out_bias),
            line(second_gain),
            line(second_bias),
            up_weight,
            line(up_bias),
            down_weight,
            line(down_bias),
        )
        output = spread_rows(result)
        up_grad, down_grad, up_bias_grad, middle_grad, mixed_grad, out_grad, sums = backward(
            alive,
            low_cot,
            active,
            slope,
            second,
            middle,
            mixed,
            up_weight,
            down_weight,
            out_weight,
            line(second_gain),
        )
        out_bias_grad, second_gain_grad, second_bias_grad, down_bias_grad = (sums[i] for i in range(4))
        (
            query_weight_grad,
            key_weight_grad,
            value_weight_grad,
            query_bias_grad,
            key_bias_grad,
            value_bias_grad,
            query_up,
            core_back,
            lift,
        ) = attend_back(
            mixed_grad, weights, query, key, value, normed, core, total, qkv_weight, line(qkv_bias)
        )
        core_back = over_splits(core_back).astype(BF16)
        lift = over_splits(lift)
        first_up = query_up + jnp.einsum(
            "bjt,jc->btc", squeeze, core_back, preferred_element_type=F32
        ).reshape(rows, width)
        first_gain_grad = jnp.sum(first_up * hat_first, axis=0)
        first_bias_grad = jnp.sum(first_up, axis=0)
        rows_grad = (
            middle_grad + norm_back(hat_first, rate_first, first_up, first_gain)
        ).astype(BF16)
        compress_terms = (
            jnp.einsum(
                "jc,btc->bjt",
                core_back,
                normed.reshape(slots, tokens, width),
                preferred_element_type=F32,
            )
            + lift[None]
        )

        vectors = (
            first_gain_grad,
            first_bias_grad,
            jnp.concatenate([query_bias_grad, key_bias_grad, value_bias_grad], axis=1),
            out_bias_grad,
            second_gain_grad,
            second_bias_grad,
            up_bias_grad,
            down_bias_grad,
        )
        sizes = [v.size // nk for v in vectors]
        packed = jnp.concatenate([v.reshape(nk, -1) for v in vectors], axis=1)
        tall = 32
        wide = -(-sum(sizes) // (tall * 128)) * 128
        packed = jnp.pad(packed, ((0, 0), (0, tall * wide - sum(sizes)))).reshape(nk, tall, wide)
        blocked = [
            grad.reshape(nk, grad.shape[0] // nk, grad.shape[1])
            for grad in (
                down_grad,
                up_grad,
                query_weight_grad,
                key_weight_grad,
                value_weight_grad,
                out_grad,
            )
        ]
        input_grad = spread_rows(rows_grad)
        blocked = blocked[:2] + [jnp.concatenate(blocked[2:], axis=2)]
        down_rows, up_rows, joined = (
            scatter_sum(grad, high_first, low_first, nb, nk, i > 0)
            for i, grad in enumerate(blocked)
        )
        qkv_rows, out_rows = joined[:, : 3 * width], joined[:, 3 * width :]
        compress_rows = scatter_sum(compress_terms, team_low[::-1], team_low, nb, nk, False)
        mine = scatter_sum(packed, high_first, low_first, nb, nk, False).reshape(-1)
        parts = []
        start = 0
        for size in sizes:
            parts.append(mine[start : start + size])
            start += size
        fg, fb, qb, ob, sg, sb, ub, db = parts
    return (
        output,
        input_grad,
        fg,
        fb,
        qkv_rows,
        qb,
        out_rows,
        ob,
        sg,
        sb,
        up_rows,
        ub,
        down_rows,
        db,
        compress_rows,
    )


def solution(mesh):
    rows = P("batch", "blk", None)
    placed = (rows, rows) + (P(),) * 13 + (P(None, "blk"),)
    vec, mat = P("blk"), P("blk", None)
    return jax.shard_map(
        functools.partial(body, nb=mesh.shape["batch"], nk=mesh.shape["blk"]),
        mesh=mesh,
        in_specs=placed,
        out_specs=(rows, rows, vec, vec, mat, vec, mat, vec, vec, vec, mat, vec, mat, vec)
        + (P(None, "blk"),),
        check_vma=False,
    )
```

```python
import functools
import math

import jax
import jax.numpy as jnp
from jax import lax
from jax.experimental import pallas as pl
from jax.experimental.pallas import tpu as pltpu
from jax.sharding import PartitionSpec as P

F32 = jnp.float32
BF16 = jnp.bfloat16
HD = 64
LANES = 256
GELU_A = math.sqrt(2.0 / math.pi)
GELU_B = 0.044715


def norm_stats(states):
    center = states - jnp.mean(states, axis=-1, keepdims=True)
    spread = jnp.mean(center * center, axis=-1, keepdims=True)
    rate = lax.rsqrt(spread + 1e-05)
    return center * rate, rate


def norm_back(hat, rate, upstream, gain):
    scaled = upstream * gain
    return rate * (
        scaled
        - jnp.mean(scaled, axis=-1, keepdims=True)
        - hat * jnp.mean(scaled * hat, axis=-1, keepdims=True)
    )


def contract(a, b, dim_a, dim_b):
    return lax.dot_general(a, b, (((dim_a,), (dim_b,)), ((), ())), preferred_element_type=F32)


def whole(shape):
    return pl.BlockSpec(shape, lambda *_: (0,) * len(shape), pipeline_mode=pl.Buffered(1))


def columns(height, start, width=LANES):
    return pl.BlockSpec((height, width), lambda i: (0, start + i))


def below(width, start, height=LANES):
    return pl.BlockSpec((height, width), lambda i: (start + i, 0))


PARAMS = dict(vmem_limit_bytes=62 << 20, dimension_semantics=("arbitrary",))


def by_head(values):
    lane = lax.broadcasted_iota(jnp.int32, values.shape, 1) // HD
    zero = jnp.zeros_like(values)
    return jnp.concatenate([jnp.where(lane == h, values, zero) for h in range(LANES // HD)], axis=0)


def own_head(values):
    n = values.shape[0] // (LANES // HD)
    lane = lax.broadcasted_iota(jnp.int32, (n, LANES), 1) // HD
    picked = values[:n]
    for h in range(1, LANES // HD):
        picked = jnp.where(lane == h, values[h * n : (h + 1) * n], picked)
    return picked


def attend_kernel(tile, normed, core, total, wq, wk, wv, bq, bk, bv, query, key, value, weights, mixed):
    rows, n = normed.shape[0], core.shape[0]
    key[...] = (contract(core[...], wk[...], 1, 0) + total[...] * bk[...]).astype(BF16)
    value[...] = (contract(core[...], wv[...], 1, 0) + total[...] * bv[...]).astype(BF16)
    keys = by_head(key[...] * jnp.asarray(1.0 / math.sqrt(HD), BF16))
    values = by_head(value[...])

    for r in range(rows // tile):
        at = slice(r * tile, (r + 1) * tile)
        q = (contract(normed[at, :], wq[...], 1, 0) + bq[...]).astype(BF16)
        query[at, :] = q
        scores = contract(q, keys, 1, 1)
        heads = []
        for h in range(LANES // HD):
            s = scores[:, h * n : (h + 1) * n]
            e = jnp.exp(s - jnp.max(s, axis=-1, keepdims=True))
            heads.append((e * (1.0 / jnp.sum(e, axis=-1, keepdims=True))).astype(BF16))
        low = jnp.concatenate(heads, axis=1)
        weights[0, at, :] = low
        mixed[at, :] = contract(low, values, 1, 0).astype(BF16)


def attend(normed, core, total, qkv_weight, qkv_bias, tile=1024):
    rows, width = normed.shape
    n = core.shape[0]
    steps = width // LANES
    heads = LANES // HD
    return pl.pallas_call(
        functools.partial(attend_kernel, tile),
        grid=(steps,),
        in_specs=[whole((rows, width)), whole((n, width)), whole((n, 1))]
        + [columns(width, k * steps) for k in range(3)]
        + [columns(1, k * steps) for k in range(3)],
        out_specs=[
            columns(rows, 0),
            columns(n, 0),
            columns(n, 0),
            pl.BlockSpec((1, rows, heads * n), lambda i: (i, 0, 0)),
            columns(rows, 0),
        ],
        out_shape=[
            jax.ShapeDtypeStruct((rows, width), BF16),
            jax.ShapeDtypeStruct((n, width), BF16),
            jax.ShapeDtypeStruct((n, width), BF16),
            jax.ShapeDtypeStruct((steps, rows, heads * n), BF16),
            jax.ShapeDtypeStruct((rows, width), BF16),
        ],
        compiler_params=pltpu.CompilerParams(**PARAMS),
        name="attend",
    )(normed, core, total, qkv_weight, qkv_weight, qkv_weight, qkv_bias, qkv_bias, qkv_bias)


def forward_kernel(tile, alive, mixed, states, ow, ob, gain, bias, upw, upb, dnw, dnb,
                   middle, second, active, slope, output, total):
    f = pl.program_id(0)
    rows = mixed.shape[0]

    @pl.when(f == 0)
    def _():
        mid = states[...].astype(F32) + contract(mixed[...], ow[...], 1, 0) + ob[...]
        middle[...] = mid
        second[...] = (norm_stats(mid)[0] * gain[...] + bias[...]).astype(BF16)
        total[...] = mid + dnb[...]

    for r in range(rows // tile):
        at = slice(r * tile, (r + 1) * tile)
        v = contract(second[at, :], upw[...], 1, 0) + upb[...]
        square = v * v
        t = jnp.tanh(v * (GELU_A + (GELU_A * GELU_B) * square))
        half = 0.5 + 0.5 * t
        act = (v * half).astype(BF16)
        active[at, :] = act
        slope[at, :] = (
            half + (0.5 * v) * (1.0 - t * t) * (GELU_A + (3 * GELU_A * GELU_B) * square)
        ).astype(BF16)
        total[at, :] += contract(act, dnw[...], 1, 0)

    @pl.when(f == pl.num_programs(0) - 1)
    def _():
        output[...] = jnp.where(alive[0] > 0, total[...], 0.0).astype(BF16)


def forward(alive, mixed, states, ow, ob, gain, bias, upw, upb, dnw, dnb, block=512, tile=1024):
    rows, width = mixed.shape
    hidden = upw.shape[1]
    vec = whole((1, width))
    return pl.pallas_call(
        functools.partial(forward_kernel, tile),
        grid=(hidden // block,),
        in_specs=[
            pl.BlockSpec(memory_space=pltpu.SMEM),
            whole((rows, width)),
            whole((rows, width)),
            whole((width, width)),
            vec,
            vec,
            vec,
            columns(width, 0, block),
            columns(1, 0, block),
            below(width, 0, block),
            vec,
        ],
        out_specs=[
            whole((rows, width)),
            whole((rows, width)),
            columns(rows, 0, block),
            columns(rows, 0, block),
            whole((rows, width)),
        ],
        out_shape=[
            jax.ShapeDtypeStruct((rows, width), F32),
            jax.ShapeDtypeStruct((rows, width), BF16),
            jax.ShapeDtypeStruct((rows, hidden), BF16),
            jax.ShapeDtypeStruct((rows, hidden), BF16),
            jax.ShapeDtypeStruct((rows, width), BF16),
        ],
        scratch_shapes=[pltpu.VMEM((rows, width), F32)],
        compiler_params=pltpu.CompilerParams(**PARAMS),
        name="forward",
    )(alive, mixed, states, ow, ob, gain, bias, upw, upb, dnw, dnb)


def backward_kernel(alive, cot, active, slope, second, middle, mixed, upw, dnw, ow, gain,
                    up_grad, down_grad, up_bias_grad, middle_grad, mixed_grad, out_grad, sums,
                    incoming, total):
    f = pl.program_id(0)

    @pl.when(f == 0)
    def _():
        incoming[...] = jnp.where(alive[0] > 0, cot[...], jnp.zeros_like(cot))
        total[...] = jnp.zeros_like(total)

    d = contract(incoming[...], dnw[...], 1, 1)
    dh = (d * slope[...].astype(F32)).astype(BF16)
    up_bias_grad[...] = jnp.sum(dh.astype(F32), axis=0, keepdims=True)
    total[...] += contract(dh, upw[...], 1, 1)
    down_grad[...] = contract(active[...], incoming[...], 0, 0).astype(BF16)
    up_grad[...] = contract(second[...], dh, 0, 0).astype(BF16)

    @pl.when(f == pl.num_programs(0) - 1)
    def _():
        hat, rate = norm_stats(middle[...])
        up = total[...]
        inc = incoming[...].astype(F32)
        grad = inc + norm_back(hat, rate, up, gain[...])
        middle_grad[...] = grad
        branch = grad.astype(BF16)
        mixed_grad[...] = contract(branch, ow[...], 1, 1).astype(BF16)
        out_grad[...] = contract(mixed[...], branch, 0, 0).astype(BF16)
        sums[0:1, :] = jnp.sum(branch.astype(F32), axis=0, keepdims=True)
        sums[1:2, :] = jnp.sum(up * hat, axis=0, keepdims=True)
        sums[2:3, :] = jnp.sum(up, axis=0, keepdims=True)
        sums[3:4, :] = jnp.sum(inc, axis=0, keepdims=True)


def backward(alive, cot, active, slope, second, middle, mixed, upw, dnw, ow, gain, block=512):
    rows, width = mixed.shape
    hidden = upw.shape[1]
    return pl.pallas_call(
        backward_kernel,
        grid=(hidden // block,),
        in_specs=[
            pl.BlockSpec(memory_space=pltpu.SMEM),
            whole((rows, width)),
            columns(rows, 0, block),
            columns(rows, 0, block),
            whole((rows, width)),
            whole((rows, width)),
            whole((rows, width)),
            columns(width, 0, block),
            below(width, 0, block),
            whole((width, width)),
            whole((1, width)),
        ],
        out_specs=[
            columns(width, 0, block),
            below(width, 0, block),
            columns(1, 0, block),
            whole((rows, width)),
            whole((rows, width)),
            whole((width, width)),
            whole((4, width)),
        ],
        out_shape=[
            jax.ShapeDtypeStruct((width, hidden), BF16),
            jax.ShapeDtypeStruct((hidden, width), BF16),
            jax.ShapeDtypeStruct((1, hidden), F32),
            jax.ShapeDtypeStruct((rows, width), F32),
            jax.ShapeDtypeStruct((rows, width), BF16),
            jax.ShapeDtypeStruct((width, width), BF16),
            jax.ShapeDtypeStruct((4, width), F32),
        ],
        scratch_shapes=[pltpu.VMEM((rows, width), BF16), pltpu.VMEM((rows, width), F32)],
        compiler_params=pltpu.CompilerParams(**PARAMS),
        name="backward",
    )(alive, cot, active, slope, second, middle, mixed, upw, dnw, ow, gain)


def attend_back_kernel(mixed_grad, weights, query, key, value, normed, core, total, wq, wk, wv, bk, bv,
                       query_grad, key_grad, value_grad, qb, kb, vb, up, core_grad, lift):
    i = pl.program_id(0)
    n = core.shape[0]

    @pl.when(i == 0)
    def _():
        up[...] = jnp.zeros_like(up)
        core_grad[...] = jnp.zeros_like(core_grad)
        lift[...] = jnp.zeros_like(lift)

    keys = by_head(key[...] * jnp.asarray(1.0 / math.sqrt(HD), BF16))
    values = by_head(value[...])
    grads = mixed_grad[...]
    back = contract(grads, values, 1, 1)
    heads = []
    for h in range(LANES // HD):
        p = weights[0, :, h * n : (h + 1) * n].astype(F32)
        g = back[:, h * n : (h + 1) * n]
        heads.append((p * (g - jnp.sum(p * g, axis=-1, keepdims=True))).astype(BF16))
    score = jnp.concatenate(heads, axis=1)
    dv = own_head(contract(weights[0], grads, 0, 0))
    dk = own_head(contract(score, query[...], 0, 0)) * (1.0 / math.sqrt(HD))
    dq = contract(score, keys, 1, 0).astype(BF16)
    dk_low, dv_low = dk.astype(BF16), dv.astype(BF16)
    up[...] += contract(dq, wq[...], 1, 1)
    core_grad[...] += contract(dk_low, wk[...], 1, 1) + contract(dv_low, wv[...], 1, 1)
    lift[...] += jnp.sum(dk * bk[...] + dv * bv[...], axis=1, keepdims=True)
    query_grad[...] = contract(normed[...], dq, 0, 0).astype(BF16)
    key_grad[...] = contract(core[...], dk_low, 0, 0).astype(BF16)
    value_grad[...] = contract(core[...], dv_low, 0, 0).astype(BF16)
    qb[...] = jnp.sum(dq.astype(F32), axis=0, keepdims=True)
    kb[...] = jnp.sum(total[...] * dk, axis=0, keepdims=True)
    vb[...] = jnp.sum(total[...] * dv, axis=0, keepdims=True)


def attend_back(mixed_grad, weights, query, key, value, normed, core, total, qkv_weight, qkv_bias):
    rows, width = normed.shape
    n = core.shape[0]
    steps = width // LANES
    heads = LANES // HD
    return pl.pallas_call(
        attend_back_kernel,
        grid=(steps,),
        in_specs=[
            columns(rows, 0),
            pl.BlockSpec((1, rows, heads * n), lambda i: (i, 0, 0)),
            columns(rows, 0),
            columns(n, 0),
            columns(n, 0),
            whole((rows, width)),
            whole((n, width)),
            whole((n, 1)),
        ]
        + [columns(width, k * steps) for k in range(3)]
        + [columns(1, k * steps) for k in range(1, 3)],
        out_specs=[columns(width, 0)] * 3
        + [columns(1, 0)] * 3
        + [whole((rows, width)), whole((n, width)), whole((n, 1))],
        out_shape=[jax.ShapeDtypeStruct((width, width), BF16)] * 3
        + [jax.ShapeDtypeStruct((1, width), F32)] * 3
        + [
            jax.ShapeDtypeStruct((rows, width), F32),
            jax.ShapeDtypeStruct((n, width), F32),
            jax.ShapeDtypeStruct((n, 1), F32),
        ],
        compiler_params=pltpu.CompilerParams(**PARAMS),
        name="attend_back",
    )(mixed_grad, weights, query, key, value, normed, core, total, qkv_weight, qkv_weight, qkv_weight, qkv_bias, qkv_bias)


MESH = pl.DeviceIdType.MESH


def at_batch(other):
    return {"batch": other}


def at_blk(other):
    return {"blk": other}


def remote(source, target, send, arrive, where):
    return pltpu.make_async_remote_copy(
        src_ref=source, dst_ref=target, send_sem=send, recv_sem=arrive, device_id=where, device_id_type=MESH
    )


def greet(places):
    barrier = pltpu.get_barrier_semaphore()
    for where in places:
        pl.semaphore_signal(barrier, inc=1, device_id=where, device_id_type=MESH)
    pl.semaphore_wait(barrier, len(places))


def spread_order(n, far_first=True):
    return sorted(range(1, n), key=lambda d: ((d & (n // 2)) * (-1 if far_first else 1), d))


class Unit:
    def __init__(self, rows, cols, early, result_top=0, result_left=0, kept="all", hops=None, lead=0):
        self.half, self.cols, self.early = rows // 2, cols, early
        self.result_top, self.result_left = result_top, result_left
        self.kept, self.lead = kept, lead
        every = ["core", "x", "y", "z1", "z2", "join", "pair"]
        if not early:
            every = ["core", "y", "z1", "z2", "late", "pair"]
        begin = {"all": 0, "core": 1, "first": 2}[kept]
        self.hops = every[begin : None if hops is None else begin + hops]

    def shape_after(self, hop):
        h, c = self.half, self.cols
        narrow = c // 2 if self.early else c
        return {
            "core": (2, 2, 2, h, c),
            "x": (2, 2, 2, h, narrow),
            "y": (2, 2, h, narrow),
            "z1": (2, h, narrow),
            "z2": (h, narrow),
            "late": (h, c),
        }.get(hop)

    def kept_shape(self):
        if self.kept == "core":
            return self.shape_after("core")
        return self.shape_after("x" if self.early else "y")

    def scratch(self):
        shapes = [] if self.kept == "all" else [self.kept_shape()]
        shapes += [self.shape_after(hop) for hop in self.hops if self.shape_after(hop)]
        return [pltpu.VMEM(shape, BF16) for shape in shapes]


HOPS = 7


class Route:
    def __init__(self, unit, source, result, buffers, local, send, recv):
        self.unit, self.source, self.result = unit, source, result
        self.hops = unit.hops
        self.moved = unit.kept != "all"
        self.acc, self.got = (buffers[0], buffers[1:]) if self.moved else (source, buffers)
        self.local, self.send, self.recv = local, send, recv
        self.batch, self.blk = lax.axis_index("batch"), lax.axis_index("blk")
        self.core, self.x = self.batch % 2, self.batch // 2
        self.z2, self.z1, self.y = self.blk // 4, (self.blk // 2) % 2, self.blk % 2

    def rows(self, top, core):
        return pl.ds(pl.multiple_of(top + core * self.unit.half, 16), self.unit.half)

    def lanes(self, left, x):
        u = self.unit
        if not u.early:
            return pl.ds(left, u.cols)
        return pl.ds(pl.multiple_of(left + x * (u.cols // 2), 128), u.cols // 2)

    def inside(self, x):
        rows = slice(None) if self.moved else self.rows(0, self.core)
        if self.unit.kept == "first":
            return rows, slice(None)
        return rows, self.lanes(0, x)

    def blocks(self, *place):
        if self.unit.kept == "first" and not self.unit.early:
            return place[:2]
        return place

    def copy(self, s):
        hop = self.hops[s]
        u, acc, mine = self.unit, self.acc, self.inside(self.x)
        y, z1, z2 = self.y, self.z1, self.z2
        every = slice(None)
        where = {
            "core": at_batch(self.batch ^ 1),
            "pair": at_batch(self.batch ^ 1),
            "x": at_batch(self.batch ^ 2),
            "late": at_batch(self.batch ^ 2),
            "join": at_batch(self.batch ^ 2),
            "y": at_blk(self.blk ^ 1),
            "z1": at_blk(self.blk ^ 2),
            "z2": at_blk(self.blk ^ 4),
        }[hop]
        if hop in ("join", "pair"):
            lanes = pl.ds(u.result_left, u.cols)
            if hop == "join":
                lanes = self.lanes(u.result_left, self.x)
            source = target = self.result.at[self.rows(u.result_top, self.core), lanes]
        else:
            target = self.got[s]
            if hop == "core":
                source = self.source.at[:, :, :, self.rows(0, 1 - self.core)]
            elif hop == "x":
                source = acc.at[(every, every, every) + self.inside(1 - self.x)]
            else:
                place = {
                    "y": (every, every, 1 - y),
                    "z1": (every, 1 - z1, y),
                    "z2": (1 - z2, z1, y),
                    "late": (z2, z1, y),
                }[hop]
                source = acc.at[self.blocks(*place) + mine]
        return remote(source, target, self.send.at[s], self.recv.at[s], where)

    def fetch(self):
        return pltpu.make_async_copy(self.source, self.acc, self.local)

    def left_over(self, target):
        every = slice(None)
        rows = self.rows(0, self.core)
        if len(self.hops) == 1:
            source = self.acc.at[:, :, :, rows]
        elif self.unit.early:
            source = self.acc.at[:, :, :, rows, self.lanes(0, self.x)]
        else:
            source = self.acc.at[:, :, self.y, rows]
        return pltpu.make_async_copy(source, target, self.local)

    def start(self, s):
        if s == 0 and self.moved:
            self.fetch().wait()
        self.copy(s).start()

    def finish(self, s):
        hop = self.hops[s]
        acc, mine, every = self.acc, self.inside(self.x), (slice(None), slice(None))
        self.copy(s).wait_recv()
        pairs = [(a, b) for a in range(2) for b in range(2)]

        def add(place, other):
            acc[place] = acc[place] + self.got[s][other]

        if hop in ("core", "x"):
            inside = (mine[0], slice(None)) if hop == "core" else mine
            for a, b in pairs:
                for c in range(2):
                    add((a, b, c) + inside, (a, b, c) + every)
        elif hop == "y":
            for a, b in pairs:
                add((a, b, self.y) + mine, (a, b) + every)
        elif hop == "z1":
            for a in range(2):
                add(self.blocks(a, self.z1, self.y) + mine, (a,) + every)
        elif hop == "z2" and not self.unit.early:
            add(self.blocks(self.z2, self.z1, self.y) + mine, every)
        elif hop in ("z2", "late"):
            place = self.blocks(self.z2, self.z1, self.y) + mine
            u = self.unit
            self.result[self.rows(u.result_top, self.core), self.lanes(u.result_left, self.x)] = (
                acc[place] + self.got[s][...]
            )

    def close(self):
        for s in range(len(self.hops)):
            self.copy(s).wait_send()


class Stream:
    def __init__(self, copies):
        self.hops = copies

    def start(self, s):
        self.hops[s].start()

    def finish(self, s):
        self.hops[s].wait_send()

    def close(self):
        pass


STREAMS = (((4, "z2"), (6, "z2")), ((5, "z2"), (7, "z2")), ((2, "z1"), (3, "z1")), ((1, "y"),))


class Wave:
    def __init__(self, steps, got, send, recv):
        self.steps, self.got, self.send, self.recv = steps, got, send, recv
        batch, blk = lax.axis_index("batch"), lax.axis_index("blk")
        self.hops = [at_batch(batch ^ 1), at_batch(batch ^ 2), at_blk(blk ^ 1), at_blk(blk ^ 2), at_blk(blk ^ 4)]

    def copy(self, s):
        return remote(self.steps.at[s], self.got.at[s], self.send.at[s], self.recv.at[s], self.hops[s])

    def start(self, s):
        self.copy(s).start()

    def finish(self, s):
        self.copy(s).wait_recv()
        self.steps[s + 1] = self.steps[s] + self.got[s]

    def close(self):
        for s in range(len(self.hops)):
            self.copy(s).wait_send()


DELAY = {"core": 1.8, "x": 2.6, "y": 2.6, "z1": 2.6, "z2": 3.6}
RATE = {"core": 210e3, "x": 36e3, "y": 36e3, "z1": 36e3, "z2": 22e3}
SAME = {"pair": "core", "late": "x", "join": "x"}
LINK = {"z1": "z", "z2": "z"}


def hop_bytes(unit, hop):
    shape = unit.shape_after(hop)
    if shape is None:
        shape = (unit.half, unit.cols // 2 if hop == "join" else unit.cols)
    return 2 * math.prod(shape)


def plan_hops(jobs, marks):
    free = {LINK.get(kind, kind): 0.0 for kind in RATE}
    due = {}
    result = []

    def begin(job, number, now):
        hop, size = jobs[job][1][number]
        kind = SAME.get(hop, hop)
        link = LINK.get(kind, kind)
        free[link] = max(now, free[link]) + size / RATE[kind]
        due[job] = (free[link] + DELAY[kind], number)

    for k, mark in enumerate(marks):
        now, last, events = mark, k == len(marks) - 1, []
        for job, (ready, _) in enumerate(jobs):
            if ready == k:
                events.append((job, 0, False))
                begin(job, 0, now)
        while due:
            job = min(due, key=lambda j: due[j][0])
            when, number = due[job]
            if when > now:
                if not last:
                    break
                now = when
            now += 0.2 if last else 0.0
            del due[job]
            events.append((job, number, True))
            if number + 1 < len(jobs[job][1]):
                begin(job, number + 1, now)
        result.append(events)
    return result


def follow(routes, events):
    for job, number, ends in events:
        route = routes[job]
        if ends:
            route.finish(number)
            number += 1
        if number < len(route.hops):
            route.start(number)


VECTORS = 16


def finish_kernel(n, tile, plan, *refs):
    (mixed_grad, weights, query, key, value, wq, wk, wv, normed, core, total, squeeze, low_x, middle_grad,
     params, up_bias, sums, down_in, up_in, down_last, up_last, out_in) = refs[:22]
    home, *summed, vec_out = refs[22:29]
    (down_out, up_out, qkv_out, out_out, small_out, put, out_here, out_sem, up, core_grad, lift, qkv_grad, small, ready, vectors, vec_got,
     own, send_d, recv_d, local, send, recv, vec_send, vec_recv) = refs[29:53]
    refs = refs[53:]
    units, plan = plan
    i = pl.program_id(0)
    m, tokens = core.shape[0], low_x.shape[1]
    batch, me = lax.axis_index("batch"), lax.axis_index("blk")
    places = {
        "up": (up_in, up_out),
        "up_last": (up_last, up_out),
        "down": (down_in, down_out),
        "down_last": (down_last, down_out),
        "out": (out_here, out_out),
        "qkv": (qkv_grad, qkv_out),
        "small": (small, small_out),
    }
    routes = []
    for k, (name, unit) in enumerate(units):
        count = len(unit.scratch())
        buffers, refs = refs[:count], refs[count:]
        source, result = places[name]
        if unit.kept == "first" or name == "qkv":
            source = source.at[unit.lead]
        routes.append(Route(unit, source, result, buffers, local.at[k], send.at[k], recv.at[k]))
    take_out = pltpu.make_async_copy(out_in, out_here, out_sem)
    wave = Wave(vectors, vec_got, vec_send, vec_recv)

    def ship(d):
        return remote(ready.at[me ^ d], home.at[me], send_d.at[d - 1], recv_d.at[d - 1], at_blk(me ^ d))

    streams = [Stream([ship(d) for d, _ in stream]) for stream in STREAMS]
    everyone = routes + [wave] + streams

    def look(step, mark):
        @pl.when(i == step)
        def _():
            follow(everyone, plan[mark])

    @pl.when(i == 0)
    def _():
        for route in routes:
            if route.moved:
                route.fetch().start()
        take_out.start()
        greet([at_batch(batch ^ 1), at_batch(batch ^ 2)] + [at_blk(me ^ d) for d in range(1, n)])
        take_out.wait()
        up[...] = jnp.zeros_like(up)
        core_grad[...] = jnp.zeros_like(core_grad)
        lift[...] = jnp.zeros_like(lift)
        vectors[0] = jnp.zeros(vectors.shape[1:], F32)

    look(0, 0)
    steps = qkv_grad.shape[0]
    scale = 1.0 / math.sqrt(HD)
    keys = by_head(key[...] * jnp.asarray(scale, BF16))
    values = by_head(value[...])
    rows = mixed_grad.shape[0]
    dv = dk = None
    grads_q = []
    for r in range(rows // tile):
        at = slice(r * tile, (r + 1) * tile)
        grads = mixed_grad[at, :]
        back = contract(grads, values, 1, 1)
        low = weights[0, at, :]
        heads = []
        for h in range(LANES // HD):
            p = low[:, h * m : (h + 1) * m].astype(F32)
            g = back[:, h * m : (h + 1) * m]
            heads.append((p * (g - jnp.sum(p * g, axis=-1, keepdims=True))).astype(BF16))
        score = jnp.concatenate(heads, axis=1)
        part_v = own_head(contract(low, grads, 0, 0))
        part_k = own_head(contract(score, query[at, :], 0, 0))
        dv = part_v if dv is None else dv + part_v
        dk = part_k if dk is None else dk + part_k
        grads_q.append(contract(score, keys, 1, 0).astype(BF16))
        if r < rows // tile - 1:
            for step in range(steps):
                look(step, step * (rows // tile) + r + 1)
    dq = jnp.concatenate(grads_q, axis=0)
    dk = dk * scale
    dk_low, dv_low = dk.astype(BF16), dv.astype(BF16)
    up[...] += contract(dq, wq[...], 1, 1)
    core_grad[...] += contract(dk_low, wk[...], 1, 1) + contract(dv_low, wv[...], 1, 1)
    lanes = pl.ds(pl.multiple_of(i * LANES, LANES), LANES)
    lift[...] += jnp.sum(dk * params[3:4, lanes] + dv * params[4:5, lanes], axis=1, keepdims=True)
    for k, grad in enumerate(
        (
            contract(normed[...], dq, 0, 0),
            contract(core[...], dk_low, 0, 0),
            contract(core[...], dv_low, 0, 0),
        )
    ):
        block = grad.shape[0] // n
        for b in range(n):
            qkv_grad[i, b // 4, (b // 2) % 2, b % 2, :, k * LANES : (k + 1) * LANES] = grad[
                b * block : (b + 1) * block
            ].astype(BF16)
    vectors[0, 2:3, lanes] = jnp.sum(dq.astype(F32), axis=0, keepdims=True)
    vectors[0, 3:4, lanes] = jnp.sum(total[...] * dk, axis=0, keepdims=True)
    vectors[0, 4:5, lanes] = jnp.sum(total[...] * dv, axis=0, keepdims=True)

    looks = rows // tile
    for step in range(steps):
        look(step, (step + 1) * looks)

    @pl.when(i == steps - 1)
    def _():
        width = low_x.shape[2]

        low_core = core_grad[...].astype(BF16)
        gain_sum = bias_sum = jnp.zeros((1, width), F32)
        mine = pltpu.make_async_copy(ready.at[me], home.at[me], own)
        for turn, d in enumerate(spread_order(n) + [0]):
            b = me ^ d
            at = pl.ds(pl.multiple_of(b * tokens, tokens), tokens)
            rise = up[at, :] + contract(squeeze[b], low_core, 0, 0)
            hat, rate = norm_stats(low_x[b].astype(F32))
            gain_sum += jnp.sum(rise * hat, axis=0, keepdims=True)
            bias_sum += jnp.sum(rise, axis=0, keepdims=True)
            ready[b] = (middle_grad[at, :] + norm_back(hat, rate, rise, params[0:1, :])).astype(BF16)
            if d == 0:
                mine.start()
            if turn == TURN:
                follow(everyone, plan[steps * looks + 1])
        follow(everyone, plan[steps * looks + 2])
        for b in range(n):
            terms = contract(low_core, normed[b * tokens : (b + 1) * tokens, :], 1, 1) + lift[...]
            small[b // 4, (b // 2) % 2, b % 2] = terms.astype(BF16)
        vectors[0, 0:1, :] = gain_sum
        vectors[0, 1:2, :] = bias_sum
        vectors[0, 5:6, :] = sums[0:1, :]
        vectors[0, 6:7, :] = sums[1:2, :]
        vectors[0, 7:8, :] = sums[2:3, :]
        for k in range(up_bias.shape[1] // width):
            vectors[0, 8 + k : 9 + k, :] = up_bias[:, k * width : (k + 1) * width]
        vectors[0, 12:13, :] = sums[3:4, :]
        follow(everyone, plan[steps * looks + 3])
        puts = [
            pltpu.make_async_copy(source, target, put.at[k])
            for k, (source, target) in enumerate(
                zip((down_out, up_out, qkv_out, out_out, small_out), summed)
            )
        ]
        for copy in puts:
            copy.start()
        vec_out[...] = vectors[len(wave.hops)]
        for route in everyone:
            route.close()
        mine.wait()
        for d in range(1, n):
            ship(d).wait_recv()
        for copy in puts:
            copy.wait()


def finish(mixed_grad, weights, query, key, value, normed, core, total, squeeze, low_x, middle_grad, params,
           qkv_weight, up_bias, sums, down, up, down_last, up_last, out, tile=512):
    n, m, tokens = squeeze.shape
    rows, width = normed.shape
    steps, heads = width // LANES, LANES // HD
    tall = width // n
    feeds, block = up.shape[0] + 1, up.shape[-1] * 2
    hidden = feeds * block
    deep = down.shape[-2] * 2
    out = out.reshape(2, 2, 2, tall, width)
    units = []
    for k in range(feeds):
        kept = "core" if k == feeds - 1 else "first"
        tail = "_last" if k == feeds - 1 else ""
        units.append(("up" + tail, Unit(tall, block, True, 0, block * k, kept, None, k)))
        units.append(("down" + tail, Unit(deep, width, k == feeds - 1, deep * k, 0, kept, None, k)))
    units.append(("out", Unit(tall, width, True)))
    for k in range(steps):
        units.append(("qkv", Unit(tall, 3 * LANES, True, 0, 3 * LANES * k, lead=k)))
    units.append(("small", Unit(m, tokens, False)))
    looks = rows // tile
    end = steps * looks + 3
    begun = MARKS[0]
    marks = [begun] + [begun + MARKS[1] * (k + 1) / looks for k in range(steps * looks)]
    marks += [marks[-1] + late for late in MARKS[2:]]
    jobs = []
    for name, unit in units:
        begin = {"qkv": (unit.lead + 1) * looks, "small": end}.get(name, 0)
        jobs.append((begin, [(hop, hop_bytes(unit, hop)) for hop in unit.hops]))
    jobs.append((end, [(hop, 4 * VECTORS * width) for hop in ("core", "x", "y", "z1", "z2")]))
    for k, stream in enumerate(STREAMS):
        jobs.append((end - 2 + (k > 1), [(hop, 2 * tokens * width) for _, hop in stream]))
    plan = (units, plan_hops(jobs, marks))
    anywhere = pl.BlockSpec(memory_space=pl.ANY)
    vmem = pl.BlockSpec(memory_space=pltpu.VMEM)
    dma = pltpu.SemaphoreType.DMA
    blocks = (2, 2, 2, tall, width)
    results = [(hidden // n, width), (tall, hidden), (tall, 3 * width), (tall, width), (m, tokens)]
    scratch = [pltpu.VMEM(shape, BF16) for shape in results] + [
        dma((len(results),)),
        pltpu.VMEM(blocks, BF16),
        dma,
        pltpu.VMEM((rows, width), F32),
        pltpu.VMEM((m, width), F32),
        pltpu.VMEM((m, 1), F32),
        pltpu.VMEM((steps,) + blocks, BF16),
        pltpu.VMEM((2, 2, 2, m, tokens), BF16),
        pltpu.VMEM((n, tokens, width), BF16),
        pltpu.VMEM((6, VECTORS, width), F32),
        pltpu.VMEM((5, VECTORS, width), F32),
        dma,
        dma((n - 1,)),
        dma((n - 1,)),
        dma((len(units),)),
        dma((len(units), HOPS)),
        dma((len(units), HOPS)),
        dma((5,)),
        dma((5,)),
    ]
    for _, unit in units:
        scratch += unit.scratch()
    return pl.pallas_call(
        functools.partial(finish_kernel, n, tile, plan),
        grid=(steps,),
        in_specs=[
            columns(rows, 0),
            pl.BlockSpec((1, rows, heads * m), lambda i: (i, 0, 0)),
            columns(rows, 0),
            columns(m, 0),
            columns(m, 0),
        ]
        + [columns(width, k * steps) for k in range(3)]
        + [
            whole((rows, width)),
            whole((m, width)),
            whole((m, 1)),
            whole((n, m, tokens)),
            whole((n, tokens, width)),
            whole((rows, width)),
            whole(params.shape),
            whole((1, hidden)),
            whole((4, width)),
            anywhere,
            anywhere,
            anywhere,
            anywhere,
            anywhere,
        ],
        out_specs=[anywhere] * (1 + len(results)) + [whole((VECTORS, width))],
        out_shape=[jax.ShapeDtypeStruct((n, tokens, width), BF16)]
        + [jax.ShapeDtypeStruct(shape, BF16) for shape in results]
        + [jax.ShapeDtypeStruct((VECTORS, width), F32)],
        scratch_shapes=scratch,
        compiler_params=pltpu.CompilerParams(
            collective_id=1, has_side_effects=True, vmem_limit_bytes=67043328, dimension_semantics=("arbitrary",)
        ),
        name="finish",
    )(mixed_grad, weights, query, key, value, qkv_weight, qkv_weight, qkv_weight, normed, core,
      total, squeeze, low_x, middle_grad, params, up_bias, sums, down, up, down_last, up_last, out)


MARKS = (1.0, 8.7, 3.0, 8.0, 11.0)
TURN = 3


class Exchange:
    def __init__(self, source, target, own, send, recv):
        self.source, self.target = source, target
        self.own, self.send, self.recv = own, send, recv
        self.n = source.shape[0]
        self.me = lax.axis_index("blk")

    def copy(self, d):
        return remote(
            self.source.at[self.me ^ d],
            self.target.at[self.me],
            self.send.at[d - 1],
            self.recv.at[d - 1],
            at_blk(self.me ^ d),
        )

    def mine(self):
        return pltpu.make_async_copy(self.source.at[self.me], self.target.at[self.me], self.own)

    def start(self, far_first=True):
        for d in spread_order(self.n, far_first):
            self.copy(d).start()
        self.mine().start()

    def wait(self):
        self.mine().wait()
        for d in range(1, self.n):
            self.copy(d).wait()


def exchange_scratch(n):
    dma = pltpu.SemaphoreType.DMA
    return [dma, dma((n - 1,)), dma((n - 1,))]


def alive_here(counts):
    return lax.axis_index("blk") < counts[lax.axis_index("batch")]


def side_by_side(refs, axis):
    return jnp.concatenate([ref[...] for ref in refs], axis=axis)


COTS_FIRST = False
COTS_AFTER = 6
ARRIVAL = (1, 2, 3, 4, 5, 6, 7)


def open_kernel(n, nb, attends, feeds, tile, counts, inputs, cotangent, compress, *refs):
    given, refs = refs[:8], refs[8:]
    (wq, wk, wv, ow), refs = refs[:4], refs[4:]
    upw, dnw, refs = refs[:n], refs[n : 2 * n], refs[2 * n :]
    (low_x, normed, squeeze, low_cot, core_out, total_out, query, key, value, weights, mixed,
     middle, second, active, slope, output, vectors) = refs[:17]
    (x_here, n_here, e_part, e_here, core_sum, total, acc, core) = refs[17:25]
    (keep, send_e, recv_e, send_q, recv_q, own_q) = refs[25:31]
    x_sems, cot_sems = refs[31:34], refs[34:37]
    i = pl.program_id(0)
    me, batch = lax.axis_index("blk"), lax.axis_index("batch")
    tokens = inputs.shape[1]
    rows, m, width = n * tokens, compress.shape[0], inputs.shape[2]
    share = m // nb

    def vector(k):
        return vectors[k : k + 1, :]

    def quarter(q):
        return pl.ds(pl.multiple_of(q * share, share), share)

    xs = Exchange(inputs, x_here, *x_sems)
    cots = Exchange(cotangent, low_cot, *cot_sems)

    def piece(d):
        return remote(
            compress.at[quarter(batch)], e_part.at[me], send_e.at[d - 1], recv_e.at[d - 1], at_blk(me ^ d)
        )

    def pass_on(c):
        return remote(
            e_part, e_here.at[:, quarter(batch)], send_q.at[c - 1], recv_q.at[c - 1], at_batch(batch ^ c)
        )

    keep_part = pltpu.make_async_copy(e_part, e_here.at[:, quarter(batch)], own_q)

    keeps = [
        pltpu.make_async_copy(source, target, keep.at[k])
        for k, (source, target) in enumerate(((x_here, low_x), (n_here, normed), (e_here, squeeze)))
    ]

    @pl.when(i == 0)
    def _():
        greet([at_blk(me ^ d) for d in range(1, n)] + [at_batch(batch ^ c) for c in range(1, nb)])
        for d in range(1, n):
            piece(d).start()
        for e in (7, 1, 6, 2, 5, 3, 4):
            xs.copy(e).start()
        xs.mine().start()
        if COTS_FIRST:
            cots.start()
        e_part[me] = compress[quarter(batch), :]
        row = 0
        for ref in given:
            for k in range(ref.shape[0] // width):
                vectors[row : row + 1, :] = ref[k * width : (k + 1) * width].reshape(1, width)
                row += 1
        core_sum[...] = jnp.zeros_like(core_sum)
        total[...] = jnp.zeros_like(total)
        for d in range(1, n):
            piece(d).wait_recv()
        for c in range(1, nb):
            pass_on(c).start()
        keep_part.start()

        def arrived(slot):
            low = (norm_stats(x_here[slot].astype(F32))[0] * vector(0) + vector(1)).astype(BF16)
            n_here[slot] = low

        def gather(slot):
            part = e_here[slot]
            core_sum[...] += contract(part, n_here[slot], 1, 0)
            total[...] += jnp.sum(part.astype(F32), axis=1, keepdims=True)

        xs.mine().wait()
        arrived(me)
        keep_part.wait()
        for c in range(1, nb):
            pass_on(c).wait_recv()
        gather(me)
        for d in ARRIVAL:
            xs.copy(d).wait_recv()
            if not COTS_FIRST and d == ARRIVAL[COTS_AFTER]:
                cots.start(False)
            arrived(me ^ d)
            gather(me ^ d)
        core[...] = core_sum[...].astype(BF16)
        core_out[...] = core[...]
        total_out[...] = total[...]
        for copy in keeps:
            copy.start()

    @pl.when(i < attends)
    def _():
        lanes = pl.ds(pl.multiple_of(i * LANES, LANES), LANES)
        bq, bk, bv = (vectors[k : k + 1, lanes] for k in (2, 3, 4))
        key[...] = (contract(core[...], wk[...], 1, 0) + total[...] * bk).astype(BF16)
        value[...] = (contract(core[...], wv[...], 1, 0) + total[...] * bv).astype(BF16)
        keys = by_head(key[...] * jnp.asarray(1.0 / math.sqrt(HD), BF16))
        values = by_head(value[...])
        for r in range(rows // tile):
            at = slice(r * tile, (r + 1) * tile)
            blocks = slice(r * tile // tokens, (r + 1) * tile // tokens)
            low_n = n_here[blocks].reshape(tile, -1)
            q = (contract(low_n, wq[...], 1, 0) + bq).astype(BF16)
            query[at, :] = q
            scores = contract(q, keys, 1, 1)
            heads = []
            for h in range(LANES // HD):
                s = scores[:, h * m : (h + 1) * m]
                e = jnp.exp(s - jnp.max(s, axis=-1, keepdims=True))
                heads.append((e * (1.0 / jnp.sum(e, axis=-1, keepdims=True))).astype(BF16))
            low = jnp.concatenate(heads, axis=1)
            weights[0, at, :] = low
            mixed[at, lanes] = contract(low, values, 1, 0).astype(BF16)

    @pl.when(i == attends)
    def _():
        mid = x_here[...].reshape(rows, -1).astype(F32) + contract(mixed[...], ow[...], 1, 0) + vector(5)
        middle[...] = mid
        second[...] = (norm_stats(mid)[0] * vector(6) + vector(7)).astype(BF16)
        acc[...] = mid + vector(12)

    @pl.when(i >= attends)
    def _():
        pieces = []
        for b in range(n):
            chosen = None
            for u in range(feeds):
                row, lane = divmod((b * feeds + u) * 128, width)
                here = vectors[8 + row : 9 + row, lane : lane + 128]
                chosen = here if u == 0 else jnp.where(i == attends + u, here, chosen)
            pieces.append(chosen)
        v = contract(second[...], side_by_side(upw, 1), 1, 0) + jnp.concatenate(pieces, axis=1)
        square = v * v
        t = jnp.tanh(v * (GELU_A + (GELU_A * GELU_B) * square))
        half = 0.5 + 0.5 * t
        act = (v * half).astype(BF16)
        active[...] = act
        slope[...] = (
            half + (0.5 * v) * (1.0 - t * t) * (GELU_A + (3 * GELU_A * GELU_B) * square)
        ).astype(BF16)
        acc[...] += contract(act, side_by_side(dnw, 0), 1, 0)

    @pl.when(i == pl.num_programs(0) - 1)
    def _():
        output[...] = jnp.where(alive_here(counts), acc[...], 0.0).astype(BF16).reshape(output.shape)
        for copy in keeps:
            copy.wait()
        for d in range(1, n):
            piece(d).wait_send()
            xs.copy(d).wait_send()
        for c in range(1, nb):
            pass_on(c).wait_send()
        cots.wait()


def open_all(nb, counts, inputs, cotangent, compress, given, qkv_weight, ow, upw, dnw, tile=512):
    n, tokens, width = inputs.shape
    rows, m, hidden = n * tokens, compress.shape[0], upw.shape[1]
    attends, heads = width // LANES, LANES // HD
    feeds = hidden // n // 128
    block = n * 128
    anywhere = pl.BlockSpec(memory_space=pl.ANY)

    def early(i):
        return jnp.minimum(i, attends - 1)

    def late(i):
        return jnp.maximum(i - attends, 0)

    def wide(height, start):
        return pl.BlockSpec((height, LANES), lambda i: (0, start + early(i)))

    def chunk(shape, dim, b):
        if dim:
            return pl.BlockSpec(shape, lambda i: (0, b * feeds + late(i)))
        return pl.BlockSpec(shape, lambda i: (b * feeds + late(i), 0))

    struct = jax.ShapeDtypeStruct
    dma = pltpu.SemaphoreType.DMA
    return pl.pallas_call(
        functools.partial(open_kernel, n, nb, attends, feeds, tile),
        grid=(attends + feeds,),
        in_specs=[pl.BlockSpec(memory_space=pltpu.SMEM), anywhere, anywhere, whole((m, tokens))]
        + [whole(v.shape) for v in given]
        + [wide(width, k * attends) for k in range(3)]
        + [whole((width, width))]
        + [chunk((width, 128), 1, b) for b in range(n)]
        + [chunk((128, width), 0, b) for b in range(n)],
        out_specs=[anywhere] * 4
        + [whole((m, width)), whole((m, 1)), wide(rows, 0), wide(m, 0), wide(m, 0)]
        + [pl.BlockSpec((1, rows, heads * m), lambda i: (early(i), 0, 0))]
        + [whole((rows, width))] * 3
        + [pl.BlockSpec((rows, block), lambda i: (0, late(i)))] * 2
        + [whole((n, tokens, width)), whole((VECTORS, width))],
        out_shape=[
            struct((n, tokens, width), BF16),
            struct((n, tokens, width), BF16),
            struct((n, m, tokens), BF16),
            struct((n, tokens, width), BF16),
            struct((m, width), BF16),
            struct((m, 1), F32),
            struct((rows, width), BF16),
            struct((m, width), BF16),
            struct((m, width), BF16),
            struct((attends, rows, heads * m), BF16),
            struct((rows, width), BF16),
            struct((rows, width), F32),
            struct((rows, width), BF16),
            struct((rows, hidden), BF16),
            struct((rows, hidden), BF16),
            struct((n, tokens, width), BF16),
            struct((VECTORS, width), F32),
        ],
        scratch_shapes=[
            pltpu.VMEM((n, tokens, width), BF16),
            pltpu.VMEM((n, tokens, width), BF16),
            pltpu.VMEM((n, m // nb, tokens), BF16),
            pltpu.VMEM((n, m, tokens), BF16),
            pltpu.VMEM((m, width), F32),
            pltpu.VMEM((m, 1), F32),
            pltpu.VMEM((rows, width), F32),
            pltpu.VMEM((m, width), BF16),
            dma((3,)),
            dma((n - 1,)),
            dma((n - 1,)),
            dma((nb - 1,)),
            dma((nb - 1,)),
            dma,
        ]
        + exchange_scratch(n)
        + exchange_scratch(n),
        compiler_params=pltpu.CompilerParams(
            collective_id=0, has_side_effects=True, vmem_limit_bytes=67043328, dimension_semantics=("arbitrary",)
        ),
        name="open",
    )(counts, inputs, cotangent, compress, *given, qkv_weight, qkv_weight, qkv_weight, ow, *[upw] * n, *[dnw] * n)


def back_kernel(n, units, counts, cot, result, active, slope, second, middle, mixed, *refs):
    upw, dnw, (ow, vectors), refs = refs[:n], refs[n : 2 * n], refs[2 * n : 2 * n + 2], refs[2 * n + 2 :]
    (home, up_part, down_part, up_last, down_last, up_bias_grad, middle_grad, mixed_grad, out_grad, sums) = refs[:10]
    (incoming, total, up_grad, down_grad, take, local, send, recv) = refs[10:18]
    outs = Exchange(result, home, *refs[18:21])
    refs = refs[21:]
    f = pl.program_id(0)
    batch, me = lax.axis_index("batch"), lax.axis_index("blk")
    feeds = len(units) // 2
    routes = []
    for k, unit in enumerate(units):
        count = len(unit.scratch())
        buffers, refs = refs[:count], refs[count:]
        source = (down_grad if k % 2 else up_grad).at[unit.lead]
        routes.append(Route(unit, source, None, buffers, local.at[k], send.at[k], recv.at[k]))
    pairs = [routes[2 * k : 2 * k + 2] for k in range(feeds)]

    def put(k):
        last = k == feeds - 1
        targets = (up_last, down_last) if last else (up_part.at[k], down_part.at[k])
        return [route.left_over(target) for route, target in zip(pairs[k], targets)]

    def advance(k, s):
        for route in pairs[k]:
            route.finish(s)
            if s + 1 < len(route.hops):
                route.start(s + 1)
        if s + 1 == len(pairs[k][0].hops):
            for copy in put(k):
                copy.start()

    @pl.when(f == 0)
    def _():
        fetch = pltpu.make_async_copy(cot, incoming, take)
        fetch.start()
        greet([at_batch(batch ^ 1), at_batch(batch ^ 2)] + [at_blk(me ^ d) for d in range(1, n)])
        outs.start()
        total[...] = jnp.zeros_like(total)
        fetch.wait()
        incoming[...] = jnp.where(alive_here(counts), incoming[...], jnp.zeros_like(incoming))

    low = incoming[...].reshape(total.shape)
    d = contract(low, side_by_side(dnw, 0), 1, 1)
    dh = (d * slope[...].astype(F32)).astype(BF16)
    up_bias_grad[...] = jnp.sum(dh.astype(F32), axis=0, keepdims=True)
    total[...] += contract(dh, side_by_side(upw, 1), 1, 1)

    for k in range(1, feeds):
        @pl.when(f == k)
        def _(k=k):
            if k > 1:
                advance(k - 2, 1)
            advance(k - 1, 0)

    grad = contract(active[...], low, 0, 0)
    for b in range(n):
        at = slice(b * 128, (b + 1) * 128)
        down_grad[f, b // 4, (b // 2) % 2, b % 2] = grad[at].astype(BF16)
    grad = contract(second[...], dh, 0, 0)
    tall = grad.shape[0] // n
    for b in range(n):
        at = slice(b * tall, (b + 1) * tall)
        up_grad[f, b // 4, (b // 2) % 2, b % 2] = grad[at].astype(BF16)

    for k in range(feeds):
        @pl.when(f == k)
        def _(k=k):
            for route in pairs[k]:
                route.start(0)

    @pl.when(f == feeds - 1)
    def _():
        hat, rate = norm_stats(middle[...])
        up = total[...]
        inc = low.astype(F32)
        grad = inc + norm_back(hat, rate, up, vectors[6:7, :])
        middle_grad[...] = grad
        branch = grad.astype(BF16)
        mixed_grad[...] = contract(branch, ow[...], 1, 1).astype(BF16)
        out_grad[...] = contract(mixed[...], branch, 0, 0).astype(BF16)
        sums[0:1, :] = jnp.sum(branch.astype(F32), axis=0, keepdims=True)
        sums[1:2, :] = jnp.sum(up * hat, axis=0, keepdims=True)
        sums[2:3, :] = jnp.sum(up, axis=0, keepdims=True)
        sums[3:4, :] = jnp.sum(inc, axis=0, keepdims=True)
        advance(feeds - 2, 1)
        advance(feeds - 1, 0)
        for k in range(feeds):
            for copy in put(k):
                copy.wait()
        for route in routes:
            route.close()
        outs.wait()


def back_all(counts, cot, result, active, slope, second, middle, mixed, upw, dnw, ow, vectors):
    n, tokens, width = cot.shape
    rows, hidden = active.shape
    feeds, block, tall = hidden // n // 128, n * 128, width // n
    anywhere = pl.BlockSpec(memory_space=pl.ANY)

    def chunk(shape, dim, b):
        if dim:
            return pl.BlockSpec(shape, lambda i: (0, b * feeds + i))
        return pl.BlockSpec(shape, lambda i: (b * feeds + i, 0))

    units = []
    for k in range(feeds):
        hops = 1 if k == feeds - 1 else 2
        units.append(Unit(tall, block, True, hops=hops, lead=k))
        units.append(Unit(128, width, k == feeds - 1, hops=hops, lead=k))
    struct = jax.ShapeDtypeStruct
    dma = pltpu.SemaphoreType.DMA
    scratch = [
        pltpu.VMEM((n, tokens, width), BF16),
        pltpu.VMEM((rows, width), F32),
        pltpu.VMEM((feeds, 2, 2, 2, tall, block), BF16),
        pltpu.VMEM((feeds, 2, 2, 2, 128, width), BF16),
        dma,
        dma((len(units),)),
        dma((len(units), 2)),
        dma((len(units), 2)),
    ] + exchange_scratch(n)
    for unit in units:
        scratch += unit.scratch()
    return pl.pallas_call(
        functools.partial(back_kernel, n, units),
        grid=(feeds,),
        in_specs=[
            pl.BlockSpec(memory_space=pltpu.SMEM),
            anywhere,
            anywhere,
            columns(rows, 0, block),
            columns(rows, 0, block),
            whole((rows, width)),
            whole((rows, width)),
            whole((rows, width)),
        ]
        + [chunk((width, 128), 1, b) for b in range(n)]
        + [chunk((128, width), 0, b) for b in range(n)]
        + [whole((width, width)), whole(vectors.shape)],
        out_specs=[
            anywhere,
            anywhere,
            anywhere,
            anywhere,
            anywhere,
            columns(1, 0, block),
            whole((rows, width)),
            whole((rows, width)),
            whole((width, width)),
            whole((4, width)),
        ],
        out_shape=[
            struct((n, tokens, width), BF16),
            struct((feeds - 1, 2, 2, 2, tall // 2, block // 2), BF16),
            struct((feeds - 1, 2, 2, 64, width), BF16),
            struct((2, 2, 2, tall // 2, block), BF16),
            struct((2, 2, 2, 64, width), BF16),
            struct((1, hidden), F32),
            struct((rows, width), F32),
            struct((rows, width), BF16),
            struct((width, width), BF16),
            struct((4, width), F32),
        ],
        scratch_shapes=scratch,
        compiler_params=pltpu.CompilerParams(
            collective_id=2, has_side_effects=True, vmem_limit_bytes=67043328, dimension_semantics=("arbitrary",)
        ),
        name="back",
    )(counts, cot, result, active, slope, second, middle, mixed, *[upw] * n, *[dnw] * n, ow, vectors)


def settle_kernel(n, *refs):
    sources, targets, refs = refs[:8], refs[8:23], refs[23:]
    held, wide, take, put = refs[:8], refs[8:13], refs[13], refs[14]
    blk = lax.axis_index("blk")
    takes = [pltpu.make_async_copy(a, b, take.at[k]) for k, (a, b) in enumerate(zip(sources, held))]
    ready = list(held[:2]) + list(wide)
    puts = [pltpu.make_async_copy(a, b, put.at[k]) for k, (a, b) in enumerate(zip(ready, targets[:7]))]
    order = (0, 1, 3, 2, 4, 5, 6)
    for k in (7,) + order:
        takes[k].start()
    takes[7].wait()
    sums = held[7]
    width = sums.shape[1]
    small = width // n

    def cut(rows, size):
        line = rows[0] if len(rows) == 1 else jnp.concatenate(rows, axis=1)
        return pltpu.roll(line, line.shape[1] - blk * size, 1)[:, :size]

    row = [sums[k : k + 1, :] for k in range(13)]
    feeds = 4 * width // n // 128
    hidden = jnp.concatenate(row[8:12], axis=1)
    ups = [cut([hidden[:, u * n * 128 : (u + 1) * n * 128]], 128) for u in range(feeds)]
    lines = [
        cut([row[0]], small),
        cut([row[1]], small),
        cut(row[2:5], 3 * small),
        cut([row[5]], small),
        cut([row[6]], small),
        cut([row[7]], small),
        jnp.concatenate(ups, axis=1),
        cut([row[12]], small),
    ]
    for target, line in zip(targets[7:], lines):
        target[...] = line.reshape(target.shape)
    for k in order:
        takes[k].wait()
        if k == 3:
            feeds = held[k].shape[1] // 128 // n
            for u in range(feeds):
                for b in range(n):
                    start, end = (u * n + b) * 128, (b * feeds + u) * 128
                    wide[1][:, end : end + 128] = held[k][:, start : start + 128].astype(F32)
        elif k == 4:
            steps = held[k].shape[1] // (3 * LANES)
            for i in range(steps):
                for j in range(3):
                    start, end = (i * 3 + j) * LANES, (j * steps + i) * LANES
                    wide[2][:, end : end + LANES] = held[k][:, start : start + LANES].astype(F32)
        elif k > 1:
            wide[k - 2][...] = held[k][...].astype(F32)
        puts[k].start()
    for copy in puts:
        copy.wait()


def settle(output, home, summed, sums):
    anywhere = pl.BlockSpec(memory_space=pl.ANY)
    vmem = pl.BlockSpec(memory_space=pltpu.VMEM)
    struct = jax.ShapeDtypeStruct
    dma = pltpu.SemaphoreType.DMA
    n, width = output.shape[0], output.shape[2]
    sizes = [width // n * k for k in (1, 1, 3, 1, 1, 1, 4, 1)]
    arrays = [output, home] + list(summed)
    return pl.pallas_call(
        functools.partial(settle_kernel, n),
        in_specs=[anywhere] * 8,
        out_specs=[anywhere] * 7 + [vmem] * 8,
        out_shape=[struct(output.shape, BF16), struct(home.shape, BF16)]
        + [struct(v.shape, F32) for v in summed]
        + [struct((size,), F32) for size in sizes],
        scratch_shapes=[pltpu.VMEM(v.shape, v.dtype) for v in arrays + [sums]]
        + [pltpu.VMEM(v.shape, F32) for v in summed]
        + [dma((8,)), dma((7,))],
        compiler_params=pltpu.CompilerParams(vmem_limit_bytes=60 << 20),
        name="settle",
    )(*arrays, sums)


def swap(values, axis, size, bit):
    return lax.ppermute(values, axis, [(i, i ^ bit) for i in range(size)])


def halve(values, dim, axis, size, bit):
    mine = (lax.axis_index(axis) // bit) % 2
    send = lax.dynamic_index_in_dim(values, 1 - mine, dim, keepdims=False).astype(BF16)
    keep = lax.dynamic_index_in_dim(values, mine, dim, keepdims=False)
    return keep.astype(F32) + swap(send, axis, size, bit).astype(F32)


def join(values, dim, axis, size, bit):
    mine = (lax.axis_index(axis) // bit) % 2
    other = swap(values, axis, size, bit)
    first = jnp.where(mine == 0, values, other)
    second = jnp.where(mine == 0, other, values)
    return jnp.concatenate([first, second], axis=dim)


def scatter_sum(terms, bits, order, nb, nk, early):
    _, rows, cols = terms.shape
    values = halve(terms.reshape(-1, 2, rows // 2, cols), 1, "batch", nb, 1)
    chips = [1 << i for i in range(1, nb.bit_length() - 1)]
    if early:
        for bit in chips:
            cols //= 2
            values = halve(values.reshape(-1, rows // 2, 2, cols), 2, "batch", nb, bit)
    left = list(bits)
    for bit in order:
        place = left.index(bit)
        values = values.reshape(1 << place, 2, -1, rows // 2, cols)
        values = halve(values, 1, "blk", nk, bit)
        left.remove(bit)
    values = values.reshape(rows // 2, cols).astype(BF16)
    for bit in reversed(chips) if early else chips:
        if early:
            values = join(values, 1, "batch", nb, bit)
        else:
            values = (values.astype(F32) + swap(values, "batch", nb, bit).astype(F32)).astype(BF16)
    return join(values, 0, "batch", nb, 1).astype(F32)


def body(
    inputs,
    cotangent,
    group_counts,
    first_gain,
    first_bias,
    qkv_weight,
    qkv_bias,
    out_weight,
    out_bias,
    second_gain,
    second_bias,
    up_weight,
    up_bias,
    down_weight,
    down_bias,
    compress,
    *,
    nb,
    nk,
):
    slots, tokens, width = inputs.shape
    splits = nk // slots
    teams = [[t * slots + i for i in range(slots)] for t in range(splits)]
    across = [[t * slots + i for t in range(splits)] for i in range(slots)]
    rows = slots * tokens
    low_first = [1 << i for i in range(nk.bit_length() - 1)]
    high_first = low_first[::-1]
    team_low = [1 << i for i in range(slots.bit_length() - 1)]

    def gather_rows(values):
        return lax.all_to_all(values, "blk", 0, 0, axis_index_groups=teams, tiled=True).reshape(
            rows, width
        )

    def spread_rows(values):
        return lax.all_to_all(
            values.reshape(slots, tokens, width), "blk", 0, 0, axis_index_groups=teams, tiled=True
        )

    def over_splits(values):
        if splits == 1:
            return values
        return lax.psum(values, "blk", axis_index_groups=across)

    def line(vector):
        return vector.reshape(1, -1)

    if nb == 4 and nk == slots == 8:
        lines = (
            first_gain,
            first_bias,
            qkv_bias,
            out_bias,
            second_gain,
            second_bias,
            up_bias,
            down_bias,
        )
        (
            low_x,
            normed,
            squeeze,
            low_cot,
            core,
            total,
            query,
            key,
            value,
            weights,
            mixed,
            middle,
            second,
            active,
            slope,
            result,
            vectors,
        ) = open_all(
            nb, group_counts, inputs, cotangent, compress, lines, qkv_weight, out_weight, up_weight, down_weight
        )
        (
            output,
            up_grad,
            down_grad,
            up_last,
            down_last,
            up_bias_grad,
            middle_grad,
            mixed_grad,
            out_grad,
            sums,
        ) = back_all(
            group_counts,
            low_cot,
            result,
            active,
            slope,
            second,
            middle,
            mixed,
            up_weight,
            down_weight,
            out_weight,
            vectors,
        )
        input_grad, *summed, flat = finish(
            mixed_grad,
            weights,
            query,
            key,
            value,
            normed.reshape(rows, width),
            core,
            total,
            squeeze,
            low_x,
            middle_grad,
            vectors,
            qkv_weight,
            up_bias_grad,
            sums,
            down_grad,
            up_grad,
            down_last,
            up_last,
            out_grad,
        )
        (
            output,
            input_grad,
            down_rows,
            up_rows,
            qkv_rows,
            out_rows,
            compress_rows,
            fg,
            fb,
            qb,
            ob,
            sg,
            sb,
            ub,
            db,
        ) = settle(output, input_grad, summed, flat)
    else:
        slot = lax.axis_index("blk") % slots
        alive = (slot < group_counts[lax.axis_index("batch")]).astype(jnp.int32).reshape(1)

        squeeze = compress[None]
        for bit in team_low[::-1]:
            squeeze = join(squeeze[:, None], 1, "blk", nk, bit)
            squeeze = squeeze.reshape((-1,) + compress.shape)
        low_x = gather_rows(inputs)
        hat_first, rate_first = norm_stats(low_x.astype(F32))
        normed = (hat_first * first_gain + first_bias).astype(BF16)
        core = jnp.einsum(
            "bjt,btc->jc",
            squeeze,
            normed.reshape(slots, tokens, width),
            preferred_element_type=F32,
        )
        total = jnp.sum(squeeze.astype(F32), axis=(0, 2))[:, None]
        low_cot = gather_rows(cotangent)
        core = over_splits(core).astype(BF16)
        total = over_splits(total)
        query, key, value, weights, mixed = attend(
            normed, core, total, qkv_weight, line(qkv_bias), tile=512
        )
        middle, second, active, slope, result = forward(
            alive,
            mixed,
            low_x,
            out_weight,
            line(out_bias),
            line(second_gain),
            line(second_bias),
            up_weight,
            line(up_bias),
            down_weight,
            line(down_bias),
        )
        output = spread_rows(result)
        up_grad, down_grad, up_bias_grad, middle_grad, mixed_grad, out_grad, sums = backward(
            alive,
            low_cot,
            active,
            slope,
            second,
            middle,
            mixed,
            up_weight,
            down_weight,
            out_weight,
            line(second_gain),
        )
        out_bias_grad, second_gain_grad, second_bias_grad, down_bias_grad = (sums[i] for i in range(4))
        (
            query_weight_grad,
            key_weight_grad,
            value_weight_grad,
            query_bias_grad,
            key_bias_grad,
            value_bias_grad,
            query_up,
            core_back,
            lift,
        ) = attend_back(
            mixed_grad, weights, query, key, value, normed, core, total, qkv_weight, line(qkv_bias)
        )
        core_back = over_splits(core_back).astype(BF16)
        lift = over_splits(lift)
        first_up = query_up + jnp.einsum(
            "bjt,jc->btc", squeeze, core_back, preferred_element_type=F32
        ).reshape(rows, width)
        first_gain_grad = jnp.sum(first_up * hat_first, axis=0)
        first_bias_grad = jnp.sum(first_up, axis=0)
        rows_grad = (
            middle_grad + norm_back(hat_first, rate_first, first_up, first_gain)
        ).astype(BF16)
        compress_terms = (
            jnp.einsum(
                "jc,btc->bjt",
                core_back,
                normed.reshape(slots, tokens, width),
                preferred_element_type=F32,
            )
            + lift[None]
        )

        vectors = (
            first_gain_grad,
            first_bias_grad,
            jnp.concatenate([query_bias_grad, key_bias_grad, value_bias_grad], axis=1),
            out_bias_grad,
            second_gain_grad,
            second_bias_grad,
            up_bias_grad,
            down_bias_grad,
        )
        sizes = [v.size // nk for v in vectors]
        packed = jnp.concatenate([v.reshape(nk, -1) for v in vectors], axis=1)
        tall = 32
        wide = -(-sum(sizes) // (tall * 128)) * 128
        packed = jnp.pad(packed, ((0, 0), (0, tall * wide - sum(sizes)))).reshape(nk, tall, wide)
        blocked = [
            grad.reshape(nk, grad.shape[0] // nk, grad.shape[1])
            for grad in (
                down_grad,
                up_grad,
                query_weight_grad,
                key_weight_grad,
                value_weight_grad,
                out_grad,
            )
        ]
        input_grad = spread_rows(rows_grad)
        blocked = blocked[:2] + [jnp.concatenate(blocked[2:], axis=2)]
        down_rows, up_rows, joined = (
            scatter_sum(grad, high_first, low_first, nb, nk, i > 0)
            for i, grad in enumerate(blocked)
        )
        qkv_rows, out_rows = joined[:, : 3 * width], joined[:, 3 * width :]
        compress_rows = scatter_sum(compress_terms, team_low[::-1], team_low, nb, nk, False)
        mine = scatter_sum(packed, high_first, low_first, nb, nk, False).reshape(-1)
        parts = []
        start = 0
        for size in sizes:
            parts.append(mine[start : start + size])
            start += size
        fg, fb, qb, ob, sg, sb, ub, db = parts
    return (
        output,
        input_grad,
        fg,
        fb,
        qkv_rows,
        qb,
        out_rows,
        ob,
        sg,
        sb,
        up_rows,
        ub,
        down_rows,
        db,
        compress_rows,
    )


def solution(mesh):
    rows = P("batch", "blk", None)
    placed = (rows, rows) + (P(),) * 13 + (P(None, "blk"),)
    vec, mat = P("blk"), P("blk", None)
    return jax.shard_map(
        functools.partial(body, nb=mesh.shape["batch"], nk=mesh.shape["blk"]),
        mesh=mesh,
        in_specs=placed,
        out_specs=(rows, rows, vec, vec, mat, vec, mat, vec, vec, vec, mat, vec, mat, vec)
        + (P(None, "blk"),),
        check_vma=False,
    )
```

```python
import functools
import math

import jax
import jax.numpy as jnp
from jax import lax
from jax.experimental import pallas as pl
from jax.experimental.pallas import tpu as pltpu
from jax.sharding import PartitionSpec as P

F32 = jnp.float32
BF16 = jnp.bfloat16
HD = 64
LANES = 256
GELU_A = math.sqrt(2.0 / math.pi)
GELU_B = 0.044715


def norm_stats(states):
    center = states - jnp.mean(states, axis=-1, keepdims=True)
    spread = jnp.mean(center * center, axis=-1, keepdims=True)
    rate = lax.rsqrt(spread + 1e-05)
    return center * rate, rate


def norm_back(hat, rate, upstream, gain):
    scaled = upstream * gain
    return rate * (
        scaled
        - jnp.mean(scaled, axis=-1, keepdims=True)
        - hat * jnp.mean(scaled * hat, axis=-1, keepdims=True)
    )


def contract(a, b, dim_a, dim_b):
    return lax.dot_general(a, b, (((dim_a,), (dim_b,)), ((), ())), preferred_element_type=F32)


def whole(shape):
    return pl.BlockSpec(shape, lambda *_: (0,) * len(shape), pipeline_mode=pl.Buffered(1))


def columns(height, start, width=LANES):
    return pl.BlockSpec((height, width), lambda i: (0, start + i))


def below(width, start, height=LANES):
    return pl.BlockSpec((height, width), lambda i: (start + i, 0))


PARAMS = dict(vmem_limit_bytes=62 << 20, dimension_semantics=("arbitrary",))


def by_head(values):
    lane = lax.broadcasted_iota(jnp.int32, values.shape, 1) // HD
    zero = jnp.zeros_like(values)
    return jnp.concatenate([jnp.where(lane == h, values, zero) for h in range(LANES // HD)], axis=0)


def own_head(values):
    n = values.shape[0] // (LANES // HD)
    lane = lax.broadcasted_iota(jnp.int32, (n, LANES), 1) // HD
    picked = values[:n]
    for h in range(1, LANES // HD):
        picked = jnp.where(lane == h, values[h * n : (h + 1) * n], picked)
    return picked


def attend_kernel(tile, normed, core, total, wq, wk, wv, bq, bk, bv, query, key, value, weights, mixed):
    rows, n = normed.shape[0], core.shape[0]
    key[...] = (contract(core[...], wk[...], 1, 0) + total[...] * bk[...]).astype(BF16)
    value[...] = (contract(core[...], wv[...], 1, 0) + total[...] * bv[...]).astype(BF16)
    keys = by_head(key[...] * jnp.asarray(1.0 / math.sqrt(HD), BF16))
    values = by_head(value[...])

    for r in range(rows // tile):
        at = slice(r * tile, (r + 1) * tile)
        q = (contract(normed[at, :], wq[...], 1, 0) + bq[...]).astype(BF16)
        query[at, :] = q
        scores = contract(q, keys, 1, 1)
        heads = []
        for h in range(LANES // HD):
            s = scores[:, h * n : (h + 1) * n]
            e = jnp.exp(s - jnp.max(s, axis=-1, keepdims=True))
            heads.append((e * (1.0 / jnp.sum(e, axis=-1, keepdims=True))).astype(BF16))
        low = jnp.concatenate(heads, axis=1)
        weights[0, at, :] = low
        mixed[at, :] = contract(low, values, 1, 0).astype(BF16)


def attend(normed, core, total, qkv_weight, qkv_bias, tile=1024):
    rows, width = normed.shape
    n = core.shape[0]
    steps = width // LANES
    heads = LANES // HD
    return pl.pallas_call(
        functools.partial(attend_kernel, tile),
        grid=(steps,),
        in_specs=[whole((rows, width)), whole((n, width)), whole((n, 1))]
        + [columns(width, k * steps) for k in range(3)]
        + [columns(1, k * steps) for k in range(3)],
        out_specs=[
            columns(rows, 0),
            columns(n, 0),
            columns(n, 0),
            pl.BlockSpec((1, rows, heads * n), lambda i: (i, 0, 0)),
            columns(rows, 0),
        ],
        out_shape=[
            jax.ShapeDtypeStruct((rows, width), BF16),
            jax.ShapeDtypeStruct((n, width), BF16),
            jax.ShapeDtypeStruct((n, width), BF16),
            jax.ShapeDtypeStruct((steps, rows, heads * n), BF16),
            jax.ShapeDtypeStruct((rows, width), BF16),
        ],
        compiler_params=pltpu.CompilerParams(**PARAMS),
        name="attend",
    )(normed, core, total, qkv_weight, qkv_weight, qkv_weight, qkv_bias, qkv_bias, qkv_bias)


def forward_kernel(tile, alive, mixed, states, ow, ob, gain, bias, upw, upb, dnw, dnb,
                   middle, second, active, slope, output, total):
    f = pl.program_id(0)
    rows = mixed.shape[0]

    @pl.when(f == 0)
    def _():
        mid = states[...].astype(F32) + contract(mixed[...], ow[...], 1, 0) + ob[...]
        middle[...] = mid
        second[...] = (norm_stats(mid)[0] * gain[...] + bias[...]).astype(BF16)
        total[...] = mid + dnb[...]

    for r in range(rows // tile):
        at = slice(r * tile, (r + 1) * tile)
        v = contract(second[at, :], upw[...], 1, 0) + upb[...]
        square = v * v
        t = jnp.tanh(v * (GELU_A + (GELU_A * GELU_B) * square))
        half = 0.5 + 0.5 * t
        act = (v * half).astype(BF16)
        active[at, :] = act
        slope[at, :] = (
            half + (0.5 * v) * (1.0 - t * t) * (GELU_A + (3 * GELU_A * GELU_B) * square)
        ).astype(BF16)
        total[at, :] += contract(act, dnw[...], 1, 0)

    @pl.when(f == pl.num_programs(0) - 1)
    def _():
        output[...] = jnp.where(alive[0] > 0, total[...], 0.0).astype(BF16)


def forward(alive, mixed, states, ow, ob, gain, bias, upw, upb, dnw, dnb, block=512, tile=1024):
    rows, width = mixed.shape
    hidden = upw.shape[1]
    vec = whole((1, width))
    return pl.pallas_call(
        functools.partial(forward_kernel, tile),
        grid=(hidden // block,),
        in_specs=[
            pl.BlockSpec(memory_space=pltpu.SMEM),
            whole((rows, width)),
            whole((rows, width)),
            whole((width, width)),
            vec,
            vec,
            vec,
            columns(width, 0, block),
            columns(1, 0, block),
            below(width, 0, block),
            vec,
        ],
        out_specs=[
            whole((rows, width)),
            whole((rows, width)),
            columns(rows, 0, block),
            columns(rows, 0, block),
            whole((rows, width)),
        ],
        out_shape=[
            jax.ShapeDtypeStruct((rows, width), F32),
            jax.ShapeDtypeStruct((rows, width), BF16),
            jax.ShapeDtypeStruct((rows, hidden), BF16),
            jax.ShapeDtypeStruct((rows, hidden), BF16),
            jax.ShapeDtypeStruct((rows, width), BF16),
        ],
        scratch_shapes=[pltpu.VMEM((rows, width), F32)],
        compiler_params=pltpu.CompilerParams(**PARAMS),
        name="forward",
    )(alive, mixed, states, ow, ob, gain, bias, upw, upb, dnw, dnb)


def backward_kernel(alive, cot, active, slope, second, middle, mixed, upw, dnw, ow, gain,
                    up_grad, down_grad, up_bias_grad, middle_grad, mixed_grad, out_grad, sums,
                    incoming, total):
    f = pl.program_id(0)

    @pl.when(f == 0)
    def _():
        incoming[...] = jnp.where(alive[0] > 0, cot[...], jnp.zeros_like(cot))
        total[...] = jnp.zeros_like(total)

    d = contract(incoming[...], dnw[...], 1, 1)
    dh = (d * slope[...].astype(F32)).astype(BF16)
    up_bias_grad[...] = jnp.sum(dh.astype(F32), axis=0, keepdims=True)
    total[...] += contract(dh, upw[...], 1, 1)
    down_grad[...] = contract(active[...], incoming[...], 0, 0).astype(BF16)
    up_grad[...] = contract(second[...], dh, 0, 0).astype(BF16)

    @pl.when(f == pl.num_programs(0) - 1)
    def _():
        hat, rate = norm_stats(middle[...])
        up = total[...]
        inc = incoming[...].astype(F32)
        grad = inc + norm_back(hat, rate, up, gain[...])
        middle_grad[...] = grad
        branch = grad.astype(BF16)
        mixed_grad[...] = contract(branch, ow[...], 1, 1).astype(BF16)
        out_grad[...] = contract(mixed[...], branch, 0, 0).astype(BF16)
        sums[0:1, :] = jnp.sum(branch.astype(F32), axis=0, keepdims=True)
        sums[1:2, :] = jnp.sum(up * hat, axis=0, keepdims=True)
        sums[2:3, :] = jnp.sum(up, axis=0, keepdims=True)
        sums[3:4, :] = jnp.sum(inc, axis=0, keepdims=True)


def backward(alive, cot, active, slope, second, middle, mixed, upw, dnw, ow, gain, block=512):
    rows, width = mixed.shape
    hidden = upw.shape[1]
    return pl.pallas_call(
        backward_kernel,
        grid=(hidden // block,),
        in_specs=[
            pl.BlockSpec(memory_space=pltpu.SMEM),
            whole((rows, width)),
            columns(rows, 0, block),
            columns(rows, 0, block),
            whole((rows, width)),
            whole((rows, width)),
            whole((rows, width)),
            columns(width, 0, block),
            below(width, 0, block),
            whole((width, width)),
            whole((1, width)),
        ],
        out_specs=[
            columns(width, 0, block),
            below(width, 0, block),
            columns(1, 0, block),
            whole((rows, width)),
            whole((rows, width)),
            whole((width, width)),
            whole((4, width)),
        ],
        out_shape=[
            jax.ShapeDtypeStruct((width, hidden), BF16),
            jax.ShapeDtypeStruct((hidden, width), BF16),
            jax.ShapeDtypeStruct((1, hidden), F32),
            jax.ShapeDtypeStruct((rows, width), F32),
            jax.ShapeDtypeStruct((rows, width), BF16),
            jax.ShapeDtypeStruct((width, width), BF16),
            jax.ShapeDtypeStruct((4, width), F32),
        ],
        scratch_shapes=[pltpu.VMEM((rows, width), BF16), pltpu.VMEM((rows, width), F32)],
        compiler_params=pltpu.CompilerParams(**PARAMS),
        name="backward",
    )(alive, cot, active, slope, second, middle, mixed, upw, dnw, ow, gain)


def attend_back_kernel(mixed_grad, weights, query, key, value, normed, core, total, wq, wk, wv, bk, bv,
                       query_grad, key_grad, value_grad, qb, kb, vb, up, core_grad, lift):
    i = pl.program_id(0)
    n = core.shape[0]

    @pl.when(i == 0)
    def _():
        up[...] = jnp.zeros_like(up)
        core_grad[...] = jnp.zeros_like(core_grad)
        lift[...] = jnp.zeros_like(lift)

    keys = by_head(key[...] * jnp.asarray(1.0 / math.sqrt(HD), BF16))
    values = by_head(value[...])
    grads = mixed_grad[...]
    back = contract(grads, values, 1, 1)
    heads = []
    for h in range(LANES // HD):
        p = weights[0, :, h * n : (h + 1) * n].astype(F32)
        g = back[:, h * n : (h + 1) * n]
        heads.append((p * (g - jnp.sum(p * g, axis=-1, keepdims=True))).astype(BF16))
    score = jnp.concatenate(heads, axis=1)
    dv = own_head(contract(weights[0], grads, 0, 0))
    dk = own_head(contract(score, query[...], 0, 0)) * (1.0 / math.sqrt(HD))
    dq = contract(score, keys, 1, 0).astype(BF16)
    dk_low, dv_low = dk.astype(BF16), dv.astype(BF16)
    up[...] += contract(dq, wq[...], 1, 1)
    core_grad[...] += contract(dk_low, wk[...], 1, 1) + contract(dv_low, wv[...], 1, 1)
    lift[...] += jnp.sum(dk * bk[...] + dv * bv[...], axis=1, keepdims=True)
    query_grad[...] = contract(normed[...], dq, 0, 0).astype(BF16)
    key_grad[...] = contract(core[...], dk_low, 0, 0).astype(BF16)
    value_grad[...] = contract(core[...], dv_low, 0, 0).astype(BF16)
    qb[...] = jnp.sum(dq.astype(F32), axis=0, keepdims=True)
    kb[...] = jnp.sum(total[...] * dk, axis=0, keepdims=True)
    vb[...] = jnp.sum(total[...] * dv, axis=0, keepdims=True)


def attend_back(mixed_grad, weights, query, key, value, normed, core, total, qkv_weight, qkv_bias):
    rows, width = normed.shape
    n = core.shape[0]
    steps = width // LANES
    heads = LANES // HD
    return pl.pallas_call(
        attend_back_kernel,
        grid=(steps,),
        in_specs=[
            columns(rows, 0),
            pl.BlockSpec((1, rows, heads * n), lambda i: (i, 0, 0)),
            columns(rows, 0),
            columns(n, 0),
            columns(n, 0),
            whole((rows, width)),
            whole((n, width)),
            whole((n, 1)),
        ]
        + [columns(width, k * steps) for k in range(3)]
        + [columns(1, k * steps) for k in range(1, 3)],
        out_specs=[columns(width, 0)] * 3
        + [columns(1, 0)] * 3
        + [whole((rows, width)), whole((n, width)), whole((n, 1))],
        out_shape=[jax.ShapeDtypeStruct((width, width), BF16)] * 3
        + [jax.ShapeDtypeStruct((1, width), F32)] * 3
        + [
            jax.ShapeDtypeStruct((rows, width), F32),
            jax.ShapeDtypeStruct((n, width), F32),
            jax.ShapeDtypeStruct((n, 1), F32),
        ],
        compiler_params=pltpu.CompilerParams(**PARAMS),
        name="attend_back",
    )(mixed_grad, weights, query, key, value, normed, core, total, qkv_weight, qkv_weight, qkv_weight, qkv_bias, qkv_bias)


MESH = pl.DeviceIdType.MESH


def at_batch(other):
    return {"batch": other}


def at_blk(other):
    return {"blk": other}


def remote(source, target, send, arrive, where):
    return pltpu.make_async_remote_copy(
        src_ref=source, dst_ref=target, send_sem=send, recv_sem=arrive, device_id=where, device_id_type=MESH
    )


def greet(places):
    barrier = pltpu.get_barrier_semaphore()
    for where in places:
        pl.semaphore_signal(barrier, inc=1, device_id=where, device_id_type=MESH)
    pl.semaphore_wait(barrier, len(places))


def spread_order(n, far_first=True):
    return sorted(range(1, n), key=lambda d: ((d & (n // 2)) * (-1 if far_first else 1), d))


class Unit:
    def __init__(self, rows, cols, early, result_top=0, result_left=0, kept="all", hops=None, lead=0):
        self.half, self.cols, self.early = rows // 2, cols, early
        self.result_top, self.result_left = result_top, result_left
        self.kept, self.lead = kept, lead
        every = ["core", "x", "y", "z1", "z2", "join", "pair"]
        if not early:
            every = ["core", "y", "z1", "z2", "late", "pair"]
        begin = {"all": 0, "core": 1, "first": 2}[kept]
        self.hops = every[begin : None if hops is None else begin + hops]

    def shape_after(self, hop):
        h, c = self.half, self.cols
        narrow = c // 2 if self.early else c
        return {
            "core": (2, 2, 2, h, c),
            "x": (2, 2, 2, h, narrow),
            "y": (2, 2, h, narrow),
            "z1": (2, h, narrow),
            "z2": (h, narrow),
            "late": (h, c),
        }.get(hop)

    def kept_shape(self):
        if self.kept == "core":
            return self.shape_after("core")
        return self.shape_after("x" if self.early else "y")

    def scratch(self):
        shapes = [] if self.kept == "all" else [self.kept_shape()]
        shapes += [self.shape_after(hop) for hop in self.hops if self.shape_after(hop)]
        return [pltpu.VMEM(shape, BF16) for shape in shapes]


HOPS = 7


class Route:
    def __init__(self, unit, source, result, buffers, local, send, recv):
        self.unit, self.source, self.result = unit, source, result
        self.hops = unit.hops
        self.moved = unit.kept != "all"
        self.acc, self.got = (buffers[0], buffers[1:]) if self.moved else (source, buffers)
        self.local, self.send, self.recv = local, send, recv
        self.batch, self.blk = lax.axis_index("batch"), lax.axis_index("blk")
        self.core, self.x = self.batch % 2, self.batch // 2
        self.z2, self.z1, self.y = self.blk // 4, (self.blk // 2) % 2, self.blk % 2

    def rows(self, top, core):
        return pl.ds(pl.multiple_of(top + core * self.unit.half, 16), self.unit.half)

    def lanes(self, left, x):
        u = self.unit
        if not u.early:
            return pl.ds(left, u.cols)
        return pl.ds(pl.multiple_of(left + x * (u.cols // 2), 128), u.cols // 2)

    def inside(self, x):
        rows = slice(None) if self.moved else self.rows(0, self.core)
        if self.unit.kept == "first":
            return rows, slice(None)
        return rows, self.lanes(0, x)

    def blocks(self, *place):
        if self.unit.kept == "first" and not self.unit.early:
            return place[:2]
        return place

    def copy(self, s):
        hop = self.hops[s]
        u, acc, mine = self.unit, self.acc, self.inside(self.x)
        y, z1, z2 = self.y, self.z1, self.z2
        every = slice(None)
        where = {
            "core": at_batch(self.batch ^ 1),
            "pair": at_batch(self.batch ^ 1),
            "x": at_batch(self.batch ^ 2),
            "late": at_batch(self.batch ^ 2),
            "join": at_batch(self.batch ^ 2),
            "y": at_blk(self.blk ^ 1),
            "z1": at_blk(self.blk ^ 2),
            "z2": at_blk(self.blk ^ 4),
        }[hop]
        if hop in ("join", "pair"):
            lanes = pl.ds(u.result_left, u.cols)
            if hop == "join":
                lanes = self.lanes(u.result_left, self.x)
            source = target = self.result.at[self.rows(u.result_top, self.core), lanes]
        else:
            target = self.got[s]
            if hop == "core":
                source = self.source.at[:, :, :, self.rows(0, 1 - self.core)]
            elif hop == "x":
                source = acc.at[(every, every, every) + self.inside(1 - self.x)]
            else:
                place = {
                    "y": (every, every, 1 - y),
                    "z1": (every, 1 - z1, y),
                    "z2": (1 - z2, z1, y),
                    "late": (z2, z1, y),
                }[hop]
                source = acc.at[self.blocks(*place) + mine]
        return remote(source, target, self.send.at[s], self.recv.at[s], where)

    def fetch(self):
        return pltpu.make_async_copy(self.source, self.acc, self.local)

    def left_over(self, target):
        every = slice(None)
        rows = self.rows(0, self.core)
        if len(self.hops) == 1:
            source = self.acc.at[:, :, :, rows]
        elif self.unit.early:
            source = self.acc.at[:, :, :, rows, self.lanes(0, self.x)]
        else:
            source = self.acc.at[:, :, self.y, rows]
        return pltpu.make_async_copy(source, target, self.local)

    def start(self, s):
        if s == 0 and self.moved:
            self.fetch().wait()
        self.copy(s).start()

    def finish(self, s):
        hop = self.hops[s]
        acc, mine, every = self.acc, self.inside(self.x), (slice(None), slice(None))
        self.copy(s).wait_recv()
        pairs = [(a, b) for a in range(2) for b in range(2)]

        def add(place, other):
            acc[place] = acc[place] + self.got[s][other]

        if hop in ("core", "x"):
            inside = (mine[0], slice(None)) if hop == "core" else mine
            for a, b in pairs:
                for c in range(2):
                    add((a, b, c) + inside, (a, b, c) + every)
        elif hop == "y":
            for a, b in pairs:
                add((a, b, self.y) + mine, (a, b) + every)
        elif hop == "z1":
            for a in range(2):
                add(self.blocks(a, self.z1, self.y) + mine, (a,) + every)
        elif hop == "z2" and not self.unit.early:
            add(self.blocks(self.z2, self.z1, self.y) + mine, every)
        elif hop in ("z2", "late"):
            place = self.blocks(self.z2, self.z1, self.y) + mine
            u = self.unit
            self.result[self.rows(u.result_top, self.core), self.lanes(u.result_left, self.x)] = (
                acc[place] + self.got[s][...]
            )

    def close(self):
        for s in range(len(self.hops)):
            self.copy(s).wait_send()


class Stream:
    def __init__(self, copies):
        self.hops = copies

    def start(self, s):
        self.hops[s].start()

    def finish(self, s):
        self.hops[s].wait_send()

    def close(self):
        pass


STREAMS = (((4, "z2"), (6, "z2")), ((5, "z2"), (7, "z2")), ((2, "z1"), (3, "z1")), ((1, "y"),))


class Wave:
    def __init__(self, steps, got, send, recv):
        self.steps, self.got, self.send, self.recv = steps, got, send, recv
        batch, blk = lax.axis_index("batch"), lax.axis_index("blk")
        self.hops = [at_batch(batch ^ 1), at_batch(batch ^ 2), at_blk(blk ^ 1), at_blk(blk ^ 2), at_blk(blk ^ 4)]

    def copy(self, s):
        return remote(self.steps.at[s], self.got.at[s], self.send.at[s], self.recv.at[s], self.hops[s])

    def start(self, s):
        self.copy(s).start()

    def finish(self, s):
        self.copy(s).wait_recv()
        self.steps[s + 1] = self.steps[s] + self.got[s]

    def close(self):
        for s in range(len(self.hops)):
            self.copy(s).wait_send()


DELAY = {"core": 1.8, "x": 2.6, "y": 2.6, "z1": 2.6, "z2": 3.6}
RATE = {"core": 210e3, "x": 36e3, "y": 36e3, "z1": 36e3, "z2": 22e3}
SAME = {"pair": "core", "late": "x", "join": "x"}
LINK = {"z1": "z", "z2": "z"}


def hop_bytes(unit, hop):
    shape = unit.shape_after(hop)
    if shape is None:
        shape = (unit.half, unit.cols // 2 if hop == "join" else unit.cols)
    return 2 * math.prod(shape)


def plan_hops(jobs, marks):
    free = {LINK.get(kind, kind): 0.0 for kind in RATE}
    due = {}
    result = []

    def begin(job, number, now):
        hop, size = jobs[job][1][number]
        kind = SAME.get(hop, hop)
        link = LINK.get(kind, kind)
        free[link] = max(now, free[link]) + size / RATE[kind]
        due[job] = (free[link] + DELAY[kind], number)

    for k, mark in enumerate(marks):
        now, last, events = mark, k == len(marks) - 1, []
        for job, (ready, _) in enumerate(jobs):
            if ready == k:
                events.append((job, 0, False))
                begin(job, 0, now)
        while due:
            job = min(due, key=lambda j: due[j][0])
            when, number = due[job]
            if when > now:
                if not last:
                    break
                now = when
            now += 0.2 if last else 0.0
            del due[job]
            events.append((job, number, True))
            if number + 1 < len(jobs[job][1]):
                begin(job, number + 1, now)
        result.append(events)
    return result


def follow(routes, events):
    for job, number, ends in events:
        route = routes[job]
        if ends:
            route.finish(number)
            number += 1
        if number < len(route.hops):
            route.start(number)


VECTORS = 16


def finish_kernel(n, tile, plan, *refs):
    (mixed_grad, weights, query, key, value, wq, wk, wv, normed, core, total, squeeze_in, low_x_in, middle_grad_in,
     params, up_bias, sums, down_in, up_in, down_last, up_last, out_in) = refs[:22]
    home, *summed, vec_out = refs[22:29]
    (down_out, up_out, qkv_out, out_out, small_out, put, out_here, out_sem, up, core_grad, lift, qkv_grad, small, ready, vectors, vec_got,
     own, send_d, recv_d, local, send, recv, vec_send, vec_recv, squeeze, low_x, middle_grad, late) = refs[29:57]
    refs = refs[57:]
    lates = [
        pltpu.make_async_copy(source, target, late.at[k])
        for k, (source, target) in enumerate(
            ((squeeze_in, squeeze), (low_x_in, low_x), (middle_grad_in, middle_grad))
        )
    ]
    units, plan = plan
    i = pl.program_id(0)
    m, tokens = core.shape[0], low_x.shape[1]
    batch, me = lax.axis_index("batch"), lax.axis_index("blk")
    places = {
        "up": (up_in, up_out),
        "up_last": (up_last, up_out),
        "down": (down_in, down_out),
        "down_last": (down_last, down_out),
        "out": (out_here, out_out),
        "qkv": (qkv_grad, qkv_out),
        "small": (small, small_out),
    }
    routes = []
    for k, (name, unit) in enumerate(units):
        count = len(unit.scratch())
        buffers, refs = refs[:count], refs[count:]
        source, result = places[name]
        if unit.kept == "first" or name == "qkv":
            source = source.at[unit.lead]
        routes.append(Route(unit, source, result, buffers, local.at[k], send.at[k], recv.at[k]))
    take_out = pltpu.make_async_copy(out_in, out_here, out_sem)
    wave = Wave(vectors, vec_got, vec_send, vec_recv)

    def ship(d):
        return remote(ready.at[me ^ d], home.at[me], send_d.at[d - 1], recv_d.at[d - 1], at_blk(me ^ d))

    streams = [Stream([ship(d) for d, _ in stream]) for stream in STREAMS]
    everyone = routes + [wave] + streams

    def look(step, mark):
        @pl.when(i == step)
        def _():
            follow(everyone, plan[mark])

    @pl.when(i == 0)
    def _():
        for route in routes:
            if route.moved:
                route.fetch().start()
        take_out.start()
        greet([at_batch(batch ^ 1), at_batch(batch ^ 2)] + [at_blk(me ^ d) for d in range(1, n)])
        take_out.wait()
        for copy in lates:
            copy.start()
        up[...] = jnp.zeros_like(up)
        core_grad[...] = jnp.zeros_like(core_grad)
        lift[...] = jnp.zeros_like(lift)
        vectors[0] = jnp.zeros(vectors.shape[1:], F32)

    look(0, 0)
    steps = qkv_grad.shape[0]
    scale = 1.0 / math.sqrt(HD)
    keys = by_head(key[...] * jnp.asarray(scale, BF16))
    values = by_head(value[...])
    rows = mixed_grad.shape[0]
    dv = dk = None
    grads_q = []
    for r in range(rows // tile):
        at = slice(r * tile, (r + 1) * tile)
        grads = mixed_grad[at, :]
        back = contract(grads, values, 1, 1)
        low = weights[0, at, :]
        heads = []
        for h in range(LANES // HD):
            p = low[:, h * m : (h + 1) * m].astype(F32)
            g = back[:, h * m : (h + 1) * m]
            heads.append((p * (g - jnp.sum(p * g, axis=-1, keepdims=True))).astype(BF16))
        score = jnp.concatenate(heads, axis=1)
        part_v = own_head(contract(low, grads, 0, 0))
        part_k = own_head(contract(score, query[at, :], 0, 0))
        dv = part_v if dv is None else dv + part_v
        dk = part_k if dk is None else dk + part_k
        grads_q.append(contract(score, keys, 1, 0).astype(BF16))
        if r < rows // tile - 1:
            for step in range(steps):
                look(step, step * (rows // tile) + r + 1)
    dq = jnp.concatenate(grads_q, axis=0)
    dk = dk * scale
    dk_low, dv_low = dk.astype(BF16), dv.astype(BF16)
    up[...] += contract(dq, wq[...], 1, 1)
    core_grad[...] += contract(dk_low, wk[...], 1, 1) + contract(dv_low, wv[...], 1, 1)
    lanes = pl.ds(pl.multiple_of(i * LANES, LANES), LANES)
    lift[...] += jnp.sum(dk * params[3:4, lanes] + dv * params[4:5, lanes], axis=1, keepdims=True)
    for k, grad in enumerate(
        (
            contract(normed[...], dq, 0, 0),
            contract(core[...], dk_low, 0, 0),
            contract(core[...], dv_low, 0, 0),
        )
    ):
        block = grad.shape[0] // n
        for b in range(n):
            qkv_grad[i, b // 4, (b // 2) % 2, b % 2, :, k * LANES : (k + 1) * LANES] = grad[
                b * block : (b + 1) * block
            ].astype(BF16)
    vectors[0, 2:3, lanes] = jnp.sum(dq.astype(F32), axis=0, keepdims=True)
    vectors[0, 3:4, lanes] = jnp.sum(total[...] * dk, axis=0, keepdims=True)
    vectors[0, 4:5, lanes] = jnp.sum(total[...] * dv, axis=0, keepdims=True)

    looks = rows // tile
    for step in range(steps):
        look(step, (step + 1) * looks)

    @pl.when(i == steps - 1)
    def _():
        width = low_x.shape[2]

        for copy in lates:
            copy.wait()
        low_core = core_grad[...].astype(BF16)
        gain_sum = bias_sum = jnp.zeros((1, width), F32)
        mine = pltpu.make_async_copy(ready.at[me], home.at[me], own)
        for turn, d in enumerate(spread_order(n) + [0]):
            b = me ^ d
            at = pl.ds(pl.multiple_of(b * tokens, tokens), tokens)
            rise = up[at, :] + contract(squeeze[b], low_core, 0, 0)
            hat, rate = norm_stats(low_x[b].astype(F32))
            gain_sum += jnp.sum(rise * hat, axis=0, keepdims=True)
            bias_sum += jnp.sum(rise, axis=0, keepdims=True)
            ready[b] = (middle_grad[at, :] + norm_back(hat, rate, rise, params[0:1, :])).astype(BF16)
            if d == 0:
                mine.start()
            if turn == TURN:
                follow(everyone, plan[steps * looks + 1])
        follow(everyone, plan[steps * looks + 2])
        for b in range(n):
            terms = contract(low_core, normed[b * tokens : (b + 1) * tokens, :], 1, 1) + lift[...]
            small[b // 4, (b // 2) % 2, b % 2] = terms.astype(BF16)
        vectors[0, 0:1, :] = gain_sum
        vectors[0, 1:2, :] = bias_sum
        vectors[0, 5:6, :] = sums[0:1, :]
        vectors[0, 6:7, :] = sums[1:2, :]
        vectors[0, 7:8, :] = sums[2:3, :]
        for k in range(up_bias.shape[1] // width):
            vectors[0, 8 + k : 9 + k, :] = up_bias[:, k * width : (k + 1) * width]
        vectors[0, 12:13, :] = sums[3:4, :]
        follow(everyone, plan[steps * looks + 3])
        puts = [
            pltpu.make_async_copy(source, target, put.at[k])
            for k, (source, target) in enumerate(
                zip((down_out, up_out, qkv_out, out_out, small_out), summed)
            )
        ]
        for copy in puts:
            copy.start()
        vec_out[...] = vectors[len(wave.hops)]
        for route in everyone:
            route.close()
        mine.wait()
        for d in range(1, n):
            ship(d).wait_recv()
        for copy in puts:
            copy.wait()


def finish(mixed_grad, weights, query, key, value, normed, core, total, squeeze, low_x, middle_grad, params,
           qkv_weight, up_bias, sums, down, up, down_last, up_last, out, tile=512):
    n, m, tokens = squeeze.shape
    rows, width = normed.shape
    steps, heads = width // LANES, LANES // HD
    tall = width // n
    feeds, block = up.shape[0] + 1, up.shape[-1] * 2
    hidden = feeds * block
    deep = down.shape[-2] * 2
    out = out.reshape(2, 2, 2, tall, width)
    units = []
    for k in range(feeds):
        kept = "core" if k == feeds - 1 else "first"
        tail = "_last" if k == feeds - 1 else ""
        units.append(("up" + tail, Unit(tall, block, True, 0, block * k, kept, None, k)))
        units.append(("down" + tail, Unit(deep, width, k == feeds - 1, deep * k, 0, kept, None, k)))
    units.append(("out", Unit(tall, width, True)))
    for k in range(steps):
        units.append(("qkv", Unit(tall, 3 * LANES, True, 0, 3 * LANES * k, lead=k)))
    units.append(("small", Unit(m, tokens, False)))
    looks = rows // tile
    end = steps * looks + 3
    begun = MARKS[0]
    marks = [begun] + [begun + MARKS[1] * (k + 1) / looks for k in range(steps * looks)]
    marks += [marks[-1] + late for late in MARKS[2:]]
    jobs = []
    for name, unit in units:
        begin = {"qkv": (unit.lead + 1) * looks, "small": end}.get(name, 0)
        jobs.append((begin, [(hop, hop_bytes(unit, hop)) for hop in unit.hops]))
    jobs.append((end, [(hop, 4 * VECTORS * width) for hop in ("core", "x", "y", "z1", "z2")]))
    for k, stream in enumerate(STREAMS):
        jobs.append((end - 2 + (k > 1), [(hop, 2 * tokens * width) for _, hop in stream]))
    plan = (units, plan_hops(jobs, marks))
    anywhere = pl.BlockSpec(memory_space=pl.ANY)
    vmem = pl.BlockSpec(memory_space=pltpu.VMEM)
    dma = pltpu.SemaphoreType.DMA
    blocks = (2, 2, 2, tall, width)
    results = [(hidden // n, width), (tall, hidden), (tall, 3 * width), (tall, width), (m, tokens)]
    scratch = [pltpu.VMEM(shape, BF16) for shape in results] + [
        dma((len(results),)),
        pltpu.VMEM(blocks, BF16),
        dma,
        pltpu.VMEM((rows, width), F32),
        pltpu.VMEM((m, width), F32),
        pltpu.VMEM((m, 1), F32),
        pltpu.VMEM((steps,) + blocks, BF16),
        pltpu.VMEM((2, 2, 2, m, tokens), BF16),
        pltpu.VMEM((n, tokens, width), BF16),
        pltpu.VMEM((6, VECTORS, width), F32),
        pltpu.VMEM((5, VECTORS, width), F32),
        dma,
        dma((n - 1,)),
        dma((n - 1,)),
        dma((len(units),)),
        dma((len(units), HOPS)),
        dma((len(units), HOPS)),
        dma((5,)),
        dma((5,)),
        pltpu.VMEM((n, m, tokens), BF16),
        pltpu.VMEM((n, tokens, width), BF16),
        pltpu.VMEM((rows, width), F32),
        dma((3,)),
    ]
    for _, unit in units:
        scratch += unit.scratch()
    return pl.pallas_call(
        functools.partial(finish_kernel, n, tile, plan),
        grid=(steps,),
        in_specs=[
            columns(rows, 0),
            pl.BlockSpec((1, rows, heads * m), lambda i: (i, 0, 0)),
            columns(rows, 0),
            columns(m, 0),
            columns(m, 0),
        ]
        + [columns(width, k * steps) for k in range(3)]
        + [
            whole((rows, width)),
            whole((m, width)),
            whole((m, 1)),
            anywhere,
            anywhere,
            anywhere,
            whole(params.shape),
            whole((1, hidden)),
            whole((4, width)),
            anywhere,
            anywhere,
            anywhere,
            anywhere,
            anywhere,
        ],
        out_specs=[anywhere] * (1 + len(results)) + [whole((VECTORS, width))],
        out_shape=[jax.ShapeDtypeStruct((n, tokens, width), BF16)]
        + [jax.ShapeDtypeStruct(shape, BF16) for shape in results]
        + [jax.ShapeDtypeStruct((VECTORS, width), F32)],
        scratch_shapes=scratch,
        compiler_params=pltpu.CompilerParams(
            collective_id=1, has_side_effects=True, vmem_limit_bytes=67043328, dimension_semantics=("arbitrary",)
        ),
        name="finish",
    )(mixed_grad, weights, query, key, value, qkv_weight, qkv_weight, qkv_weight, normed, core,
      total, squeeze, low_x, middle_grad, params, up_bias, sums, down, up, down_last, up_last, out)


MARKS = (1.0, 8.7, 3.0, 8.0, 11.0)
TURN = 3


class Exchange:
    def __init__(self, source, target, own, send, recv):
        self.source, self.target = source, target
        self.own, self.send, self.recv = own, send, recv
        self.n = source.shape[0]
        self.me = lax.axis_index("blk")

    def copy(self, d):
        return remote(
            self.source.at[self.me ^ d],
            self.target.at[self.me],
            self.send.at[d - 1],
            self.recv.at[d - 1],
            at_blk(self.me ^ d),
        )

    def mine(self):
        return pltpu.make_async_copy(self.source.at[self.me], self.target.at[self.me], self.own)

    def start(self, far_first=True):
        for d in spread_order(self.n, far_first):
            self.copy(d).start()
        self.mine().start()

    def wait(self):
        self.mine().wait()
        for d in range(1, self.n):
            self.copy(d).wait()


def exchange_scratch(n):
    dma = pltpu.SemaphoreType.DMA
    return [dma, dma((n - 1,)), dma((n - 1,))]


def alive_here(counts):
    return lax.axis_index("blk") < counts[lax.axis_index("batch")]


def side_by_side(refs, axis):
    return jnp.concatenate([ref[...] for ref in refs], axis=axis)


COTS_FIRST = False
COTS_AFTER = 6
ARRIVAL = (1, 2, 3, 4, 5, 6, 7)


def open_kernel(n, nb, attends, feeds, tile, counts, inputs, cotangent, compress, *refs):
    given, refs = refs[:8], refs[8:]
    (wq, wk, wv, ow), refs = refs[:4], refs[4:]
    upw, dnw, refs = refs[:n], refs[n : 2 * n], refs[2 * n :]
    (low_x, normed, squeeze, low_cot, core_out, total_out, query, key, value, weights, mixed,
     middle, second, active, slope, output, vectors) = refs[:17]
    (x_here, n_here, e_part, e_here, core_sum, total, acc, core) = refs[17:25]
    (keep, send_e, recv_e, send_q, recv_q, own_q) = refs[25:31]
    x_sems, cot_sems = refs[31:34], refs[34:37]
    i = pl.program_id(0)
    me, batch = lax.axis_index("blk"), lax.axis_index("batch")
    tokens = inputs.shape[1]
    rows, m, width = n * tokens, compress.shape[0], inputs.shape[2]
    share = m // nb

    def vector(k):
        return vectors[k : k + 1, :]

    def quarter(q):
        return pl.ds(pl.multiple_of(q * share, share), share)

    xs = Exchange(inputs, x_here, *x_sems)
    cots = Exchange(cotangent, low_cot, *cot_sems)

    def piece(d):
        return remote(
            compress.at[quarter(batch)], e_part.at[me], send_e.at[d - 1], recv_e.at[d - 1], at_blk(me ^ d)
        )

    def pass_on(c):
        return remote(
            e_part, e_here.at[:, quarter(batch)], send_q.at[c - 1], recv_q.at[c - 1], at_batch(batch ^ c)
        )

    keep_part = pltpu.make_async_copy(e_part, e_here.at[:, quarter(batch)], own_q)

    keeps = [
        pltpu.make_async_copy(source, target, keep.at[k])
        for k, (source, target) in enumerate(((x_here, low_x), (n_here, normed), (e_here, squeeze)))
    ]

    @pl.when(i == 0)
    def _():
        greet([at_blk(me ^ d) for d in range(1, n)] + [at_batch(batch ^ c) for c in range(1, nb)])
        for d in range(1, n):
            piece(d).start()
        for e in (7, 1, 6, 2, 5, 3, 4):
            xs.copy(e).start()
        xs.mine().start()
        if COTS_FIRST:
            cots.start()
        e_part[me] = compress[quarter(batch), :]
        row = 0
        for ref in given:
            for k in range(ref.shape[0] // width):
                vectors[row : row + 1, :] = ref[k * width : (k + 1) * width].reshape(1, width)
                row += 1
        core_sum[...] = jnp.zeros_like(core_sum)
        total[...] = jnp.zeros_like(total)
        for d in range(1, n):
            piece(d).wait_recv()
        for c in range(1, nb):
            pass_on(c).start()
        keep_part.start()

        def arrived(slot):
            low = (norm_stats(x_here[slot].astype(F32))[0] * vector(0) + vector(1)).astype(BF16)
            n_here[slot] = low

        def gather(slot):
            part = e_here[slot]
            core_sum[...] += contract(part, n_here[slot], 1, 0)
            total[...] += jnp.sum(part.astype(F32), axis=1, keepdims=True)

        xs.mine().wait()
        arrived(me)
        keep_part.wait()
        for c in range(1, nb):
            pass_on(c).wait_recv()
        gather(me)
        for d in ARRIVAL:
            xs.copy(d).wait_recv()
            if not COTS_FIRST and d == ARRIVAL[COTS_AFTER]:
                cots.start(False)
            arrived(me ^ d)
            gather(me ^ d)
        core[...] = core_sum[...].astype(BF16)
        core_out[...] = core[...]
        total_out[...] = total[...]
        for copy in keeps:
            copy.start()

    @pl.when(i < attends)
    def _():
        lanes = pl.ds(pl.multiple_of(i * LANES, LANES), LANES)
        bq, bk, bv = (vectors[k : k + 1, lanes] for k in (2, 3, 4))
        key[...] = (contract(core[...], wk[...], 1, 0) + total[...] * bk).astype(BF16)
        value[...] = (contract(core[...], wv[...], 1, 0) + total[...] * bv).astype(BF16)
        keys = by_head(key[...] * jnp.asarray(1.0 / math.sqrt(HD), BF16))
        values = by_head(value[...])
        for r in range(rows // tile):
            at = slice(r * tile, (r + 1) * tile)
            blocks = slice(r * tile // tokens, (r + 1) * tile // tokens)
            low_n = n_here[blocks].reshape(tile, -1)
            q = (contract(low_n, wq[...], 1, 0) + bq).astype(BF16)
            query[at, :] = q
            scores = contract(q, keys, 1, 1)
            heads = []
            for h in range(LANES // HD):
                s = scores[:, h * m : (h + 1) * m]
                e = jnp.exp(s - jnp.max(s, axis=-1, keepdims=True))
                heads.append((e * (1.0 / jnp.sum(e, axis=-1, keepdims=True))).astype(BF16))
            low = jnp.concatenate(heads, axis=1)
            weights[0, at, :] = low
            mixed[at, lanes] = contract(low, values, 1, 0).astype(BF16)

    @pl.when(i == attends)
    def _():
        mid = x_here[...].reshape(rows, -1).astype(F32) + contract(mixed[...], ow[...], 1, 0) + vector(5)
        middle[...] = mid
        second[...] = (norm_stats(mid)[0] * vector(6) + vector(7)).astype(BF16)
        acc[...] = mid + vector(12)

    @pl.when(i >= attends)
    def _():
        pieces = []
        for b in range(n):
            chosen = None
            for u in range(feeds):
                row, lane = divmod((b * feeds + u) * 128, width)
                here = vectors[8 + row : 9 + row, lane : lane + 128]
                chosen = here if u == 0 else jnp.where(i == attends + u, here, chosen)
            pieces.append(chosen)
        v = contract(second[...], side_by_side(upw, 1), 1, 0) + jnp.concatenate(pieces, axis=1)
        square = v * v
        t = jnp.tanh(v * (GELU_A + (GELU_A * GELU_B) * square))
        half = 0.5 + 0.5 * t
        act = (v * half).astype(BF16)
        active[...] = act
        slope[...] = (
            half + (0.5 * v) * (1.0 - t * t) * (GELU_A + (3 * GELU_A * GELU_B) * square)
        ).astype(BF16)
        acc[...] += contract(act, side_by_side(dnw, 0), 1, 0)

    @pl.when(i == pl.num_programs(0) - 1)
    def _():
        output[...] = jnp.where(alive_here(counts), acc[...], 0.0).astype(BF16).reshape(output.shape)
        for copy in keeps:
            copy.wait()
        for d in range(1, n):
            piece(d).wait_send()
            xs.copy(d).wait_send()
        for c in range(1, nb):
            pass_on(c).wait_send()
        cots.wait()


def open_all(nb, counts, inputs, cotangent, compress, given, qkv_weight, ow, upw, dnw, tile=512):
    n, tokens, width = inputs.shape
    rows, m, hidden = n * tokens, compress.shape[0], upw.shape[1]
    attends, heads = width // LANES, LANES // HD
    feeds = hidden // n // 128
    block = n * 128
    anywhere = pl.BlockSpec(memory_space=pl.ANY)

    def early(i):
        return jnp.minimum(i, attends - 1)

    def late(i):
        return jnp.maximum(i - attends, 0)

    def wide(height, start):
        return pl.BlockSpec((height, LANES), lambda i: (0, start + early(i)))

    def chunk(shape, dim, b):
        if dim:
            return pl.BlockSpec(shape, lambda i: (0, b * feeds + late(i)))
        return pl.BlockSpec(shape, lambda i: (b * feeds + late(i), 0))

    struct = jax.ShapeDtypeStruct
    dma = pltpu.SemaphoreType.DMA
    return pl.pallas_call(
        functools.partial(open_kernel, n, nb, attends, feeds, tile),
        grid=(attends + feeds,),
        in_specs=[pl.BlockSpec(memory_space=pltpu.SMEM), anywhere, anywhere, whole((m, tokens))]
        + [whole(v.shape) for v in given]
        + [wide(width, k * attends) for k in range(3)]
        + [whole((width, width))]
        + [chunk((width, 128), 1, b) for b in range(n)]
        + [chunk((128, width), 0, b) for b in range(n)],
        out_specs=[anywhere] * 4
        + [whole((m, width)), whole((m, 1)), wide(rows, 0), wide(m, 0), wide(m, 0)]
        + [pl.BlockSpec((1, rows, heads * m), lambda i: (early(i), 0, 0))]
        + [whole((rows, width))] * 3
        + [pl.BlockSpec((rows, block), lambda i: (0, late(i)))] * 2
        + [whole((n, tokens, width)), whole((VECTORS, width))],
        out_shape=[
            struct((n, tokens, width), BF16),
            struct((n, tokens, width), BF16),
            struct((n, m, tokens), BF16),
            struct((n, tokens, width), BF16),
            struct((m, width), BF16),
            struct((m, 1), F32),
            struct((rows, width), BF16),
            struct((m, width), BF16),
            struct((m, width), BF16),
            struct((attends, rows, heads * m), BF16),
            struct((rows, width), BF16),
            struct((rows, width), F32),
            struct((rows, width), BF16),
            struct((rows, hidden), BF16),
            struct((rows, hidden), BF16),
            struct((n, tokens, width), BF16),
            struct((VECTORS, width), F32),
        ],
        scratch_shapes=[
            pltpu.VMEM((n, tokens, width), BF16),
            pltpu.VMEM((n, tokens, width), BF16),
            pltpu.VMEM((n, m // nb, tokens), BF16),
            pltpu.VMEM((n, m, tokens), BF16),
            pltpu.VMEM((m, width), F32),
            pltpu.VMEM((m, 1), F32),
            pltpu.VMEM((rows, width), F32),
            pltpu.VMEM((m, width), BF16),
            dma((3,)),
            dma((n - 1,)),
            dma((n - 1,)),
            dma((nb - 1,)),
            dma((nb - 1,)),
            dma,
        ]
        + exchange_scratch(n)
        + exchange_scratch(n),
        compiler_params=pltpu.CompilerParams(
            collective_id=0, has_side_effects=True, vmem_limit_bytes=67043328, dimension_semantics=("arbitrary",)
        ),
        name="open",
    )(counts, inputs, cotangent, compress, *given, qkv_weight, qkv_weight, qkv_weight, ow, *[upw] * n, *[dnw] * n)


def back_kernel(n, units, counts, cot, result, active, slope, second, middle_in, mixed_in, *refs):
    upw, dnw, (ow_in, vectors), refs = refs[:n], refs[n : 2 * n], refs[2 * n : 2 * n + 2], refs[2 * n + 2 :]
    (home, up_part, down_part, up_last, down_last, up_bias_grad, middle_grad, mixed_grad, out_grad, sums) = refs[:10]
    (incoming, total, up_grad, down_grad, take, local, send, recv) = refs[10:18]
    outs = Exchange(result, home, *refs[18:21])
    middle, mixed, ow, late = refs[21:25]
    refs = refs[25:]
    lates = [
        pltpu.make_async_copy(source, target, late.at[k])
        for k, (source, target) in enumerate(((middle_in, middle), (mixed_in, mixed), (ow_in, ow)))
    ]
    f = pl.program_id(0)
    batch, me = lax.axis_index("batch"), lax.axis_index("blk")
    feeds = len(units) // 2
    routes = []
    for k, unit in enumerate(units):
        count = len(unit.scratch())
        buffers, refs = refs[:count], refs[count:]
        source = (down_grad if k % 2 else up_grad).at[unit.lead]
        routes.append(Route(unit, source, None, buffers, local.at[k], send.at[k], recv.at[k]))
    pairs = [routes[2 * k : 2 * k + 2] for k in range(feeds)]

    def put(k):
        last = k == feeds - 1
        targets = (up_last, down_last) if last else (up_part.at[k], down_part.at[k])
        return [route.left_over(target) for route, target in zip(pairs[k], targets)]

    def advance(k, s):
        for route in pairs[k]:
            route.finish(s)
            if s + 1 < len(route.hops):
                route.start(s + 1)
        if s + 1 == len(pairs[k][0].hops):
            for copy in put(k):
                copy.start()

    @pl.when(f == 0)
    def _():
        fetch = pltpu.make_async_copy(cot, incoming, take)
        fetch.start()
        greet([at_batch(batch ^ 1), at_batch(batch ^ 2)] + [at_blk(me ^ d) for d in range(1, n)])
        outs.start()
        for copy in lates:
            copy.start()
        total[...] = jnp.zeros_like(total)
        fetch.wait()
        incoming[...] = jnp.where(alive_here(counts), incoming[...], jnp.zeros_like(incoming))

    low = incoming[...].reshape(total.shape)
    d = contract(low, side_by_side(dnw, 0), 1, 1)
    dh = (d * slope[...].astype(F32)).astype(BF16)
    up_bias_grad[...] = jnp.sum(dh.astype(F32), axis=0, keepdims=True)
    total[...] += contract(dh, side_by_side(upw, 1), 1, 1)

    for k in range(1, feeds):
        @pl.when(f == k)
        def _(k=k):
            if k > 1:
                advance(k - 2, 1)
            advance(k - 1, 0)

    grad = contract(active[...], low, 0, 0)
    for b in range(n):
        at = slice(b * 128, (b + 1) * 128)
        down_grad[f, b // 4, (b // 2) % 2, b % 2] = grad[at].astype(BF16)
    grad = contract(second[...], dh, 0, 0)
    tall = grad.shape[0] // n
    for b in range(n):
        at = slice(b * tall, (b + 1) * tall)
        up_grad[f, b // 4, (b // 2) % 2, b % 2] = grad[at].astype(BF16)

    for k in range(feeds):
        @pl.when(f == k)
        def _(k=k):
            for route in pairs[k]:
                route.start(0)

    @pl.when(f == feeds - 1)
    def _():
        for copy in lates:
            copy.wait()
        hat, rate = norm_stats(middle[...])
        up = total[...]
        inc = low.astype(F32)
        grad = inc + norm_back(hat, rate, up, vectors[6:7, :])
        middle_grad[...] = grad
        branch = grad.astype(BF16)
        mixed_grad[...] = contract(branch, ow[...], 1, 1).astype(BF16)
        out_grad[...] = contract(mixed[...], branch, 0, 0).astype(BF16)
        sums[0:1, :] = jnp.sum(branch.astype(F32), axis=0, keepdims=True)
        sums[1:2, :] = jnp.sum(up * hat, axis=0, keepdims=True)
        sums[2:3, :] = jnp.sum(up, axis=0, keepdims=True)
        sums[3:4, :] = jnp.sum(inc, axis=0, keepdims=True)
        advance(feeds - 2, 1)
        advance(feeds - 1, 0)
        for k in range(feeds):
            for copy in put(k):
                copy.wait()
        for route in routes:
            route.close()
        outs.wait()


def back_all(counts, cot, result, active, slope, second, middle, mixed, upw, dnw, ow, vectors):
    n, tokens, width = cot.shape
    rows, hidden = active.shape
    feeds, block, tall = hidden // n // 128, n * 128, width // n
    anywhere = pl.BlockSpec(memory_space=pl.ANY)

    def chunk(shape, dim, b):
        if dim:
            return pl.BlockSpec(shape, lambda i: (0, b * feeds + i))
        return pl.BlockSpec(shape, lambda i: (b * feeds + i, 0))

    units = []
    for k in range(feeds):
        hops = 1 if k == feeds - 1 else 2
        units.append(Unit(tall, block, True, hops=hops, lead=k))
        units.append(Unit(128, width, k == feeds - 1, hops=hops, lead=k))
    struct = jax.ShapeDtypeStruct
    dma = pltpu.SemaphoreType.DMA
    scratch = [
        pltpu.VMEM((n, tokens, width), BF16),
        pltpu.VMEM((rows, width), F32),
        pltpu.VMEM((feeds, 2, 2, 2, tall, block), BF16),
        pltpu.VMEM((feeds, 2, 2, 2, 128, width), BF16),
        dma,
        dma((len(units),)),
        dma((len(units), 2)),
        dma((len(units), 2)),
    ] + exchange_scratch(n)
    scratch += [
        pltpu.VMEM((rows, width), F32),
        pltpu.VMEM((rows, width), BF16),
        pltpu.VMEM((width, width), BF16),
        dma((3,)),
    ]
    for unit in units:
        scratch += unit.scratch()
    return pl.pallas_call(
        functools.partial(back_kernel, n, units),
        grid=(feeds,),
        in_specs=[
            pl.BlockSpec(memory_space=pltpu.SMEM),
            anywhere,
            anywhere,
            columns(rows, 0, block),
            columns(rows, 0, block),
            whole((rows, width)),
            anywhere,
            anywhere,
        ]
        + [chunk((width, 128), 1, b) for b in range(n)]
        + [chunk((128, width), 0, b) for b in range(n)]
        + [anywhere, whole(vectors.shape)],
        out_specs=[
            anywhere,
            anywhere,
            anywhere,
            anywhere,
            anywhere,
            columns(1, 0, block),
            whole((rows, width)),
            whole((rows, width)),
            whole((width, width)),
            whole((4, width)),
        ],
        out_shape=[
            struct((n, tokens, width), BF16),
            struct((feeds - 1, 2, 2, 2, tall // 2, block // 2), BF16),
            struct((feeds - 1, 2, 2, 64, width), BF16),
            struct((2, 2, 2, tall // 2, block), BF16),
            struct((2, 2, 2, 64, width), BF16),
            struct((1, hidden), F32),
            struct((rows, width), F32),
            struct((rows, width), BF16),
            struct((width, width), BF16),
            struct((4, width), F32),
        ],
        scratch_shapes=scratch,
        compiler_params=pltpu.CompilerParams(
            collective_id=2, has_side_effects=True, vmem_limit_bytes=67043328, dimension_semantics=("arbitrary",)
        ),
        name="back",
    )(counts, cot, result, active, slope, second, middle, mixed, *[upw] * n, *[dnw] * n, ow, vectors)


def settle_kernel(n, *refs):
    sources, targets, refs = refs[:8], refs[8:23], refs[23:]
    held, wide, take, put = refs[:8], refs[8:13], refs[13], refs[14]
    blk = lax.axis_index("blk")
    takes = [pltpu.make_async_copy(a, b, take.at[k]) for k, (a, b) in enumerate(zip(sources, held))]
    ready = list(held[:2]) + list(wide)
    puts = [pltpu.make_async_copy(a, b, put.at[k]) for k, (a, b) in enumerate(zip(ready, targets[:7]))]
    order = (0, 1, 3, 2, 4, 5, 6)
    for k in (7,) + order:
        takes[k].start()
    takes[7].wait()
    sums = held[7]
    width = sums.shape[1]
    small = width // n

    def cut(rows, size):
        line = rows[0] if len(rows) == 1 else jnp.concatenate(rows, axis=1)
        return pltpu.roll(line, line.shape[1] - blk * size, 1)[:, :size]

    row = [sums[k : k + 1, :] for k in range(13)]
    feeds = 4 * width // n // 128
    hidden = jnp.concatenate(row[8:12], axis=1)
    ups = [cut([hidden[:, u * n * 128 : (u + 1) * n * 128]], 128) for u in range(feeds)]
    lines = [
        cut([row[0]], small),
        cut([row[1]], small),
        cut(row[2:5], 3 * small),
        cut([row[5]], small),
        cut([row[6]], small),
        cut([row[7]], small),
        jnp.concatenate(ups, axis=1),
        cut([row[12]], small),
    ]
    for target, line in zip(targets[7:], lines):
        target[...] = line.reshape(target.shape)
    for k in order:
        takes[k].wait()
        if k == 3:
            feeds = held[k].shape[1] // 128 // n
            for u in range(feeds):
                for b in range(n):
                    start, end = (u * n + b) * 128, (b * feeds + u) * 128
                    wide[1][:, end : end + 128] = held[k][:, start : start + 128].astype(F32)
        elif k == 4:
            steps = held[k].shape[1] // (3 * LANES)
            for i in range(steps):
                for j in range(3):
                    start, end = (i * 3 + j) * LANES, (j * steps + i) * LANES
                    wide[2][:, end : end + LANES] = held[k][:, start : start + LANES].astype(F32)
        elif k > 1:
            wide[k - 2][...] = held[k][...].astype(F32)
        puts[k].start()
    for copy in puts:
        copy.wait()


def settle(output, home, summed, sums):
    anywhere = pl.BlockSpec(memory_space=pl.ANY)
    vmem = pl.BlockSpec(memory_space=pltpu.VMEM)
    struct = jax.ShapeDtypeStruct
    dma = pltpu.SemaphoreType.DMA
    n, width = output.shape[0], output.shape[2]
    sizes = [width // n * k for k in (1, 1, 3, 1, 1, 1, 4, 1)]
    arrays = [output, home] + list(summed)
    return pl.pallas_call(
        functools.partial(settle_kernel, n),
        in_specs=[anywhere] * 8,
        out_specs=[anywhere] * 7 + [vmem] * 8,
        out_shape=[struct(output.shape, BF16), struct(home.shape, BF16)]
        + [struct(v.shape, F32) for v in summed]
        + [struct((size,), F32) for size in sizes],
        scratch_shapes=[pltpu.VMEM(v.shape, v.dtype) for v in arrays + [sums]]
        + [pltpu.VMEM(v.shape, F32) for v in summed]
        + [dma((8,)), dma((7,))],
        compiler_params=pltpu.CompilerParams(vmem_limit_bytes=60 << 20),
        name="settle",
    )(*arrays, sums)


def swap(values, axis, size, bit):
    return lax.ppermute(values, axis, [(i, i ^ bit) for i in range(size)])


def halve(values, dim, axis, size, bit):
    mine = (lax.axis_index(axis) // bit) % 2
    send = lax.dynamic_index_in_dim(values, 1 - mine, dim, keepdims=False).astype(BF16)
    keep = lax.dynamic_index_in_dim(values, mine, dim, keepdims=False)
    return keep.astype(F32) + swap(send, axis, size, bit).astype(F32)


def join(values, dim, axis, size, bit):
    mine = (lax.axis_index(axis) // bit) % 2
    other = swap(values, axis, size, bit)
    first = jnp.where(mine == 0, values, other)
    second = jnp.where(mine == 0, other, values)
    return jnp.concatenate([first, second], axis=dim)


def scatter_sum(terms, bits, order, nb, nk, early):
    _, rows, cols = terms.shape
    values = halve(terms.reshape(-1, 2, rows // 2, cols), 1, "batch", nb, 1)
    chips = [1 << i for i in range(1, nb.bit_length() - 1)]
    if early:
        for bit in chips:
            cols //= 2
            values = halve(values.reshape(-1, rows // 2, 2, cols), 2, "batch", nb, bit)
    left = list(bits)
    for bit in order:
        place = left.index(bit)
        values = values.reshape(1 << place, 2, -1, rows // 2, cols)
        values = halve(values, 1, "blk", nk, bit)
        left.remove(bit)
    values = values.reshape(rows // 2, cols).astype(BF16)
    for bit in reversed(chips) if early else chips:
        if early:
            values = join(values, 1, "batch", nb, bit)
        else:
            values = (values.astype(F32) + swap(values, "batch", nb, bit).astype(F32)).astype(BF16)
    return join(values, 0, "batch", nb, 1).astype(F32)


def body(
    inputs,
    cotangent,
    group_counts,
    first_gain,
    first_bias,
    qkv_weight,
    qkv_bias,
    out_weight,
    out_bias,
    second_gain,
    second_bias,
    up_weight,
    up_bias,
    down_weight,
    down_bias,
    compress,
    *,
    nb,
    nk,
):
    slots, tokens, width = inputs.shape
    splits = nk // slots
    teams = [[t * slots + i for i in range(slots)] for t in range(splits)]
    across = [[t * slots + i for t in range(splits)] for i in range(slots)]
    rows = slots * tokens
    low_first = [1 << i for i in range(nk.bit_length() - 1)]
    high_first = low_first[::-1]
    team_low = [1 << i for i in range(slots.bit_length() - 1)]

    def gather_rows(values):
        return lax.all_to_all(values, "blk", 0, 0, axis_index_groups=teams, tiled=True).reshape(
            rows, width
        )

    def spread_rows(values):
        return lax.all_to_all(
            values.reshape(slots, tokens, width), "blk", 0, 0, axis_index_groups=teams, tiled=True
        )

    def over_splits(values):
        if splits == 1:
            return values
        return lax.psum(values, "blk", axis_index_groups=across)

    def line(vector):
        return vector.reshape(1, -1)

    if nb == 4 and nk == slots == 8:
        lines = (
            first_gain,
            first_bias,
            qkv_bias,
            out_bias,
            second_gain,
            second_bias,
            up_bias,
            down_bias,
        )
        (
            low_x,
            normed,
            squeeze,
            low_cot,
            core,
            total,
            query,
            key,
            value,
            weights,
            mixed,
            middle,
            second,
            active,
            slope,
            result,
            vectors,
        ) = open_all(
            nb, group_counts, inputs, cotangent, compress, lines, qkv_weight, out_weight, up_weight, down_weight
        )
        (
            output,
            up_grad,
            down_grad,
            up_last,
            down_last,
            up_bias_grad,
            middle_grad,
            mixed_grad,
            out_grad,
            sums,
        ) = back_all(
            group_counts,
            low_cot,
            result,
            active,
            slope,
            second,
            middle,
            mixed,
            up_weight,
            down_weight,
            out_weight,
            vectors,
        )
        input_grad, *summed, flat = finish(
            mixed_grad,
            weights,
            query,
            key,
            value,
            normed.reshape(rows, width),
            core,
            total,
            squeeze,
            low_x,
            middle_grad,
            vectors,
            qkv_weight,
            up_bias_grad,
            sums,
            down_grad,
            up_grad,
            down_last,
            up_last,
            out_grad,
        )
        (
            output,
            input_grad,
            down_rows,
            up_rows,
            qkv_rows,
            out_rows,
            compress_rows,
            fg,
            fb,
            qb,
            ob,
            sg,
            sb,
            ub,
            db,
        ) = settle(output, input_grad, summed, flat)
    else:
        slot = lax.axis_index("blk") % slots
        alive = (slot < group_counts[lax.axis_index("batch")]).astype(jnp.int32).reshape(1)

        squeeze = compress[None]
        for bit in team_low[::-1]:
            squeeze = join(squeeze[:, None], 1, "blk", nk, bit)
            squeeze = squeeze.reshape((-1,) + compress.shape)
        low_x = gather_rows(inputs)
        hat_first, rate_first = norm_stats(low_x.astype(F32))
        normed = (hat_first * first_gain + first_bias).astype(BF16)
        core = jnp.einsum(
            "bjt,btc->jc",
            squeeze,
            normed.reshape(slots, tokens, width),
            preferred_element_type=F32,
        )
        total = jnp.sum(squeeze.astype(F32), axis=(0, 2))[:, None]
        low_cot = gather_rows(cotangent)
        core = over_splits(core).astype(BF16)
        total = over_splits(total)
        query, key, value, weights, mixed = attend(
            normed, core, total, qkv_weight, line(qkv_bias), tile=512
        )
        middle, second, active, slope, result = forward(
            alive,
            mixed,
            low_x,
            out_weight,
            line(out_bias),
            line(second_gain),
            line(second_bias),
            up_weight,
            line(up_bias),
            down_weight,
            line(down_bias),
        )
        output = spread_rows(result)
        up_grad, down_grad, up_bias_grad, middle_grad, mixed_grad, out_grad, sums = backward(
            alive,
            low_cot,
            active,
            slope,
            second,
            middle,
            mixed,
            up_weight,
            down_weight,
            out_weight,
            line(second_gain),
        )
        out_bias_grad, second_gain_grad, second_bias_grad, down_bias_grad = (sums[i] for i in range(4))
        (
            query_weight_grad,
            key_weight_grad,
            value_weight_grad,
            query_bias_grad,
            key_bias_grad,
            value_bias_grad,
            query_up,
            core_back,
            lift,
        ) = attend_back(
            mixed_grad, weights, query, key, value, normed, core, total, qkv_weight, line(qkv_bias)
        )
        core_back = over_splits(core_back).astype(BF16)
        lift = over_splits(lift)
        first_up = query_up + jnp.einsum(
            "bjt,jc->btc", squeeze, core_back, preferred_element_type=F32
        ).reshape(rows, width)
        first_gain_grad = jnp.sum(first_up * hat_first, axis=0)
        first_bias_grad = jnp.sum(first_up, axis=0)
        rows_grad = (
            middle_grad + norm_back(hat_first, rate_first, first_up, first_gain)
        ).astype(BF16)
        compress_terms = (
            jnp.einsum(
                "jc,btc->bjt",
                core_back,
                normed.reshape(slots, tokens, width),
                preferred_element_type=F32,
            )
            + lift[None]
        )

        vectors = (
            first_gain_grad,
            first_bias_grad,
            jnp.concatenate([query_bias_grad, key_bias_grad, value_bias_grad], axis=1),
            out_bias_grad,
            second_gain_grad,
            second_bias_grad,
            up_bias_grad,
            down_bias_grad,
        )
        sizes = [v.size // nk for v in vectors]
        packed = jnp.concatenate([v.reshape(nk, -1) for v in vectors], axis=1)
        tall = 32
        wide = -(-sum(sizes) // (tall * 128)) * 128
        packed = jnp.pad(packed, ((0, 0), (0, tall * wide - sum(sizes)))).reshape(nk, tall, wide)
        blocked = [
            grad.reshape(nk, grad.shape[0] // nk, grad.shape[1])
            for grad in (
                down_grad,
                up_grad,
                query_weight_grad,
                key_weight_grad,
                value_weight_grad,
                out_grad,
            )
        ]
        input_grad = spread_rows(rows_grad)
        blocked = blocked[:2] + [jnp.concatenate(blocked[2:], axis=2)]
        down_rows, up_rows, joined = (
            scatter_sum(grad, high_first, low_first, nb, nk, i > 0)
            for i, grad in enumerate(blocked)
        )
        qkv_rows, out_rows = joined[:, : 3 * width], joined[:, 3 * width :]
        compress_rows = scatter_sum(compress_terms, team_low[::-1], team_low, nb, nk, False)
        mine = scatter_sum(packed, high_first, low_first, nb, nk, False).reshape(-1)
        parts = []
        start = 0
        for size in sizes:
            parts.append(mine[start : start + size])
            start += size
        fg, fb, qb, ob, sg, sb, ub, db = parts
    return (
        output,
        input_grad,
        fg,
        fb,
        qkv_rows,
        qb,
        out_rows,
        ob,
        sg,
        sb,
        up_rows,
        ub,
        down_rows,
        db,
        compress_rows,
    )


def solution(mesh):
    rows = P("batch", "blk", None)
    placed = (rows, rows) + (P(),) * 13 + (P(None, "blk"),)
    vec, mat = P("blk"), P("blk", None)
    return jax.shard_map(
        functools.partial(body, nb=mesh.shape["batch"], nk=mesh.shape["blk"]),
        mesh=mesh,
        in_specs=placed,
        out_specs=(rows, rows, vec, vec, mat, vec, mat, vec, vec, vec, mat, vec, mat, vec)
        + (P(None, "blk"),),
        check_vma=False,
    )
```

```python
import functools
import math

import jax
import jax.numpy as jnp
from jax import lax
from jax.experimental import pallas as pl
from jax.experimental.pallas import tpu as pltpu
from jax.sharding import PartitionSpec as P

F32 = jnp.float32
BF16 = jnp.bfloat16
HD = 64
LANES = 256
GELU_A = math.sqrt(2.0 / math.pi)
GELU_B = 0.044715


def norm_stats(states):
    center = states - jnp.mean(states, axis=-1, keepdims=True)
    spread = jnp.mean(center * center, axis=-1, keepdims=True)
    rate = lax.rsqrt(spread + 1e-05)
    return center * rate, rate


def norm_back(hat, rate, upstream, gain):
    scaled = upstream * gain
    return rate * (
        scaled
        - jnp.mean(scaled, axis=-1, keepdims=True)
        - hat * jnp.mean(scaled * hat, axis=-1, keepdims=True)
    )


def contract(a, b, dim_a, dim_b):
    return lax.dot_general(a, b, (((dim_a,), (dim_b,)), ((), ())), preferred_element_type=F32)


def whole(shape):
    return pl.BlockSpec(shape, lambda *_: (0,) * len(shape), pipeline_mode=pl.Buffered(1))


def columns(height, start, width=LANES):
    return pl.BlockSpec((height, width), lambda i: (0, start + i))


def below(width, start, height=LANES):
    return pl.BlockSpec((height, width), lambda i: (start + i, 0))


PARAMS = dict(vmem_limit_bytes=62 << 20, dimension_semantics=("arbitrary",))


def by_head(values):
    lane = lax.broadcasted_iota(jnp.int32, values.shape, 1) // HD
    zero = jnp.zeros_like(values)
    return jnp.concatenate([jnp.where(lane == h, values, zero) for h in range(LANES // HD)], axis=0)


def own_head(values):
    n = values.shape[0] // (LANES // HD)
    lane = lax.broadcasted_iota(jnp.int32, (n, LANES), 1) // HD
    picked = values[:n]
    for h in range(1, LANES // HD):
        picked = jnp.where(lane == h, values[h * n : (h + 1) * n], picked)
    return picked


def attend_kernel(tile, normed, core, total, wq, wk, wv, bq, bk, bv, query, key, value, weights, mixed):
    rows, n = normed.shape[0], core.shape[0]
    key[...] = (contract(core[...], wk[...], 1, 0) + total[...] * bk[...]).astype(BF16)
    value[...] = (contract(core[...], wv[...], 1, 0) + total[...] * bv[...]).astype(BF16)
    keys = by_head(key[...] * jnp.asarray(1.0 / math.sqrt(HD), BF16))
    values = by_head(value[...])

    for r in range(rows // tile):
        at = slice(r * tile, (r + 1) * tile)
        q = (contract(normed[at, :], wq[...], 1, 0) + bq[...]).astype(BF16)
        query[at, :] = q
        scores = contract(q, keys, 1, 1)
        heads = []
        for h in range(LANES // HD):
            s = scores[:, h * n : (h + 1) * n]
            e = jnp.exp(s - jnp.max(s, axis=-1, keepdims=True))
            heads.append((e * (1.0 / jnp.sum(e, axis=-1, keepdims=True))).astype(BF16))
        low = jnp.concatenate(heads, axis=1)
        weights[0, at, :] = low
        mixed[at, :] = contract(low, values, 1, 0).astype(BF16)


def attend(normed, core, total, qkv_weight, qkv_bias, tile=1024):
    rows, width = normed.shape
    n = core.shape[0]
    steps = width // LANES
    heads = LANES // HD
    return pl.pallas_call(
        functools.partial(attend_kernel, tile),
        grid=(steps,),
        in_specs=[whole((rows, width)), whole((n, width)), whole((n, 1))]
        + [columns(width, k * steps) for k in range(3)]
        + [columns(1, k * steps) for k in range(3)],
        out_specs=[
            columns(rows, 0),
            columns(n, 0),
            columns(n, 0),
            pl.BlockSpec((1, rows, heads * n), lambda i: (i, 0, 0)),
            columns(rows, 0),
        ],
        out_shape=[
            jax.ShapeDtypeStruct((rows, width), BF16),
            jax.ShapeDtypeStruct((n, width), BF16),
            jax.ShapeDtypeStruct((n, width), BF16),
            jax.ShapeDtypeStruct((steps, rows, heads * n), BF16),
            jax.ShapeDtypeStruct((rows, width), BF16),
        ],
        compiler_params=pltpu.CompilerParams(**PARAMS),
        name="attend",
    )(normed, core, total, qkv_weight, qkv_weight, qkv_weight, qkv_bias, qkv_bias, qkv_bias)


def forward_kernel(tile, alive, mixed, states, ow, ob, gain, bias, upw, upb, dnw, dnb,
                   middle, second, active, slope, output, total):
    f = pl.program_id(0)
    rows = mixed.shape[0]

    @pl.when(f == 0)
    def _():
        mid = states[...].astype(F32) + contract(mixed[...], ow[...], 1, 0) + ob[...]
        middle[...] = mid
        second[...] = (norm_stats(mid)[0] * gain[...] + bias[...]).astype(BF16)
        total[...] = mid + dnb[...]

    for r in range(rows // tile):
        at = slice(r * tile, (r + 1) * tile)
        v = contract(second[at, :], upw[...], 1, 0) + upb[...]
        square = v * v
        t = jnp.tanh(v * (GELU_A + (GELU_A * GELU_B) * square))
        half = 0.5 + 0.5 * t
        act = (v * half).astype(BF16)
        active[at, :] = act
        slope[at, :] = (
            half + (0.5 * v) * (1.0 - t * t) * (GELU_A + (3 * GELU_A * GELU_B) * square)
        ).astype(BF16)
        total[at, :] += contract(act, dnw[...], 1, 0)

    @pl.when(f == pl.num_programs(0) - 1)
    def _():
        output[...] = jnp.where(alive[0] > 0, total[...], 0.0).astype(BF16)


def forward(alive, mixed, states, ow, ob, gain, bias, upw, upb, dnw, dnb, block=512, tile=1024):
    rows, width = mixed.shape
    hidden = upw.shape[1]
    vec = whole((1, width))
    return pl.pallas_call(
        functools.partial(forward_kernel, tile),
        grid=(hidden // block,),
        in_specs=[
            pl.BlockSpec(memory_space=pltpu.SMEM),
            whole((rows, width)),
            whole((rows, width)),
            whole((width, width)),
            vec,
            vec,
            vec,
            columns(width, 0, block),
            columns(1, 0, block),
            below(width, 0, block),
            vec,
        ],
        out_specs=[
            whole((rows, width)),
            whole((rows, width)),
            columns(rows, 0, block),
            columns(rows, 0, block),
            whole((rows, width)),
        ],
        out_shape=[
            jax.ShapeDtypeStruct((rows, width), F32),
            jax.ShapeDtypeStruct((rows, width), BF16),
            jax.ShapeDtypeStruct((rows, hidden), BF16),
            jax.ShapeDtypeStruct((rows, hidden), BF16),
            jax.ShapeDtypeStruct((rows, width), BF16),
        ],
        scratch_shapes=[pltpu.VMEM((rows, width), F32)],
        compiler_params=pltpu.CompilerParams(**PARAMS),
        name="forward",
    )(alive, mixed, states, ow, ob, gain, bias, upw, upb, dnw, dnb)


def backward_kernel(alive, cot, active, slope, second, middle, mixed, upw, dnw, ow, gain,
                    up_grad, down_grad, up_bias_grad, middle_grad, mixed_grad, out_grad, sums,
                    incoming, total):
    f = pl.program_id(0)

    @pl.when(f == 0)
    def _():
        incoming[...] = jnp.where(alive[0] > 0, cot[...], jnp.zeros_like(cot))
        total[...] = jnp.zeros_like(total)

    d = contract(incoming[...], dnw[...], 1, 1)
    dh = (d * slope[...].astype(F32)).astype(BF16)
    up_bias_grad[...] = jnp.sum(dh.astype(F32), axis=0, keepdims=True)
    total[...] += contract(dh, upw[...], 1, 1)
    down_grad[...] = contract(active[...], incoming[...], 0, 0).astype(BF16)
    up_grad[...] = contract(second[...], dh, 0, 0).astype(BF16)

    @pl.when(f == pl.num_programs(0) - 1)
    def _():
        hat, rate = norm_stats(middle[...])
        up = total[...]
        inc = incoming[...].astype(F32)
        grad = inc + norm_back(hat, rate, up, gain[...])
        middle_grad[...] = grad
        branch = grad.astype(BF16)
        mixed_grad[...] = contract(branch, ow[...], 1, 1).astype(BF16)
        out_grad[...] = contract(mixed[...], branch, 0, 0).astype(BF16)
        sums[0:1, :] = jnp.sum(branch.astype(F32), axis=0, keepdims=True)
        sums[1:2, :] = jnp.sum(up * hat, axis=0, keepdims=True)
        sums[2:3, :] = jnp.sum(up, axis=0, keepdims=True)
        sums[3:4, :] = jnp.sum(inc, axis=0, keepdims=True)


def backward(alive, cot, active, slope, second, middle, mixed, upw, dnw, ow, gain, block=512):
    rows, width = mixed.shape
    hidden = upw.shape[1]
    return pl.pallas_call(
        backward_kernel,
        grid=(hidden // block,),
        in_specs=[
            pl.BlockSpec(memory_space=pltpu.SMEM),
            whole((rows, width)),
            columns(rows, 0, block),
            columns(rows, 0, block),
            whole((rows, width)),
            whole((rows, width)),
            whole((rows, width)),
            columns(width, 0, block),
            below(width, 0, block),
            whole((width, width)),
            whole((1, width)),
        ],
        out_specs=[
            columns(width, 0, block),
            below(width, 0, block),
            columns(1, 0, block),
            whole((rows, width)),
            whole((rows, width)),
            whole((width, width)),
            whole((4, width)),
        ],
        out_shape=[
            jax.ShapeDtypeStruct((width, hidden), BF16),
            jax.ShapeDtypeStruct((hidden, width), BF16),
            jax.ShapeDtypeStruct((1, hidden), F32),
            jax.ShapeDtypeStruct((rows, width), F32),
            jax.ShapeDtypeStruct((rows, width), BF16),
            jax.ShapeDtypeStruct((width, width), BF16),
            jax.ShapeDtypeStruct((4, width), F32),
        ],
        scratch_shapes=[pltpu.VMEM((rows, width), BF16), pltpu.VMEM((rows, width), F32)],
        compiler_params=pltpu.CompilerParams(**PARAMS),
        name="backward",
    )(alive, cot, active, slope, second, middle, mixed, upw, dnw, ow, gain)


def attend_back_kernel(mixed_grad, weights, query, key, value, normed, core, total, wq, wk, wv, bk, bv,
                       query_grad, key_grad, value_grad, qb, kb, vb, up, core_grad, lift):
    i = pl.program_id(0)
    n = core.shape[0]

    @pl.when(i == 0)
    def _():
        up[...] = jnp.zeros_like(up)
        core_grad[...] = jnp.zeros_like(core_grad)
        lift[...] = jnp.zeros_like(lift)

    keys = by_head(key[...] * jnp.asarray(1.0 / math.sqrt(HD), BF16))
    values = by_head(value[...])
    grads = mixed_grad[...]
    back = contract(grads, values, 1, 1)
    heads = []
    for h in range(LANES // HD):
        p = weights[0, :, h * n : (h + 1) * n].astype(F32)
        g = back[:, h * n : (h + 1) * n]
        heads.append((p * (g - jnp.sum(p * g, axis=-1, keepdims=True))).astype(BF16))
    score = jnp.concatenate(heads, axis=1)
    dv = own_head(contract(weights[0], grads, 0, 0))
    dk = own_head(contract(score, query[...], 0, 0)) * (1.0 / math.sqrt(HD))
    dq = contract(score, keys, 1, 0).astype(BF16)
    dk_low, dv_low = dk.astype(BF16), dv.astype(BF16)
    up[...] += contract(dq, wq[...], 1, 1)
    core_grad[...] += contract(dk_low, wk[...], 1, 1) + contract(dv_low, wv[...], 1, 1)
    lift[...] += jnp.sum(dk * bk[...] + dv * bv[...], axis=1, keepdims=True)
    query_grad[...] = contract(normed[...], dq, 0, 0).astype(BF16)
    key_grad[...] = contract(core[...], dk_low, 0, 0).astype(BF16)
    value_grad[...] = contract(core[...], dv_low, 0, 0).astype(BF16)
    qb[...] = jnp.sum(dq.astype(F32), axis=0, keepdims=True)
    kb[...] = jnp.sum(total[...] * dk, axis=0, keepdims=True)
    vb[...] = jnp.sum(total[...] * dv, axis=0, keepdims=True)


def attend_back(mixed_grad, weights, query, key, value, normed, core, total, qkv_weight, qkv_bias):
    rows, width = normed.shape
    n = core.shape[0]
    steps = width // LANES
    heads = LANES // HD
    return pl.pallas_call(
        attend_back_kernel,
        grid=(steps,),
        in_specs=[
            columns(rows, 0),
            pl.BlockSpec((1, rows, heads * n), lambda i: (i, 0, 0)),
            columns(rows, 0),
            columns(n, 0),
            columns(n, 0),
            whole((rows, width)),
            whole((n, width)),
            whole((n, 1)),
        ]
        + [columns(width, k * steps) for k in range(3)]
        + [columns(1, k * steps) for k in range(1, 3)],
        out_specs=[columns(width, 0)] * 3
        + [columns(1, 0)] * 3
        + [whole((rows, width)), whole((n, width)), whole((n, 1))],
        out_shape=[jax.ShapeDtypeStruct((width, width), BF16)] * 3
        + [jax.ShapeDtypeStruct((1, width), F32)] * 3
        + [
            jax.ShapeDtypeStruct((rows, width), F32),
            jax.ShapeDtypeStruct((n, width), F32),
            jax.ShapeDtypeStruct((n, 1), F32),
        ],
        compiler_params=pltpu.CompilerParams(**PARAMS),
        name="attend_back",
    )(mixed_grad, weights, query, key, value, normed, core, total, qkv_weight, qkv_weight, qkv_weight, qkv_bias, qkv_bias)


MESH = pl.DeviceIdType.MESH


def at_batch(other):
    return {"batch": other}


def at_blk(other):
    return {"blk": other}


def remote(source, target, send, arrive, where):
    return pltpu.make_async_remote_copy(
        src_ref=source, dst_ref=target, send_sem=send, recv_sem=arrive, device_id=where, device_id_type=MESH
    )


def greet(places):
    barrier = pltpu.get_barrier_semaphore()
    for where in places:
        pl.semaphore_signal(barrier, inc=1, device_id=where, device_id_type=MESH)
    pl.semaphore_wait(barrier, len(places))


def spread_order(n, far_first=True):
    return sorted(range(1, n), key=lambda d: ((d & (n // 2)) * (-1 if far_first else 1), d))


class Unit:
    def __init__(self, rows, cols, early, result_top=0, result_left=0, kept="all", hops=None, lead=0):
        self.half, self.cols, self.early = rows // 2, cols, early
        self.result_top, self.result_left = result_top, result_left
        self.kept, self.lead = kept, lead
        every = ["core", "x", "y", "z1", "z2", "join", "pair"]
        if not early:
            every = ["core", "y", "z1", "z2", "late", "pair"]
        begin = {"all": 0, "core": 1, "first": 2}[kept]
        self.hops = every[begin : None if hops is None else begin + hops]

    def shape_after(self, hop):
        h, c = self.half, self.cols
        narrow = c // 2 if self.early else c
        return {
            "core": (2, 2, 2, h, c),
            "x": (2, 2, 2, h, narrow),
            "y": (2, 2, h, narrow),
            "z1": (2, h, narrow),
            "z2": (h, narrow),
            "late": (h, c),
        }.get(hop)

    def kept_shape(self):
        if self.kept == "core":
            return self.shape_after("core")
        return self.shape_after("x" if self.early else "y")

    def scratch(self):
        shapes = [] if self.kept == "all" else [self.kept_shape()]
        shapes += [self.shape_after(hop) for hop in self.hops if self.shape_after(hop)]
        return [pltpu.VMEM(shape, BF16) for shape in shapes]


HOPS = 7


class Route:
    def __init__(self, unit, source, result, buffers, local, send, recv):
        self.unit, self.source, self.result = unit, source, result
        self.hops = unit.hops
        self.moved = unit.kept != "all"
        self.acc, self.got = (buffers[0], buffers[1:]) if self.moved else (source, buffers)
        self.local, self.send, self.recv = local, send, recv
        self.batch, self.blk = lax.axis_index("batch"), lax.axis_index("blk")
        self.core, self.x = self.batch % 2, self.batch // 2
        self.z2, self.z1, self.y = self.blk // 4, (self.blk // 2) % 2, self.blk % 2

    def rows(self, top, core):
        return pl.ds(pl.multiple_of(top + core * self.unit.half, 16), self.unit.half)

    def lanes(self, left, x):
        u = self.unit
        if not u.early:
            return pl.ds(left, u.cols)
        return pl.ds(pl.multiple_of(left + x * (u.cols // 2), 128), u.cols // 2)

    def inside(self, x):
        rows = slice(None) if self.moved else self.rows(0, self.core)
        if self.unit.kept == "first":
            return rows, slice(None)
        return rows, self.lanes(0, x)

    def blocks(self, *place):
        if self.unit.kept == "first" and not self.unit.early:
            return place[:2]
        return place

    def copy(self, s):
        hop = self.hops[s]
        u, acc, mine = self.unit, self.acc, self.inside(self.x)
        y, z1, z2 = self.y, self.z1, self.z2
        every = slice(None)
        where = {
            "core": at_batch(self.batch ^ 1),
            "pair": at_batch(self.batch ^ 1),
            "x": at_batch(self.batch ^ 2),
            "late": at_batch(self.batch ^ 2),
            "join": at_batch(self.batch ^ 2),
            "y": at_blk(self.blk ^ 1),
            "z1": at_blk(self.blk ^ 2),
            "z2": at_blk(self.blk ^ 4),
        }[hop]
        if hop in ("join", "pair"):
            lanes = pl.ds(u.result_left, u.cols)
            if hop == "join":
                lanes = self.lanes(u.result_left, self.x)
            source = target = self.result.at[self.rows(u.result_top, self.core), lanes]
        else:
            target = self.got[s]
            if hop == "core":
                source = self.source.at[:, :, :, self.rows(0, 1 - self.core)]
            elif hop == "x":
                source = acc.at[(every, every, every) + self.inside(1 - self.x)]
            else:
                place = {
                    "y": (every, every, 1 - y),
                    "z1": (every, 1 - z1, y),
                    "z2": (1 - z2, z1, y),
                    "late": (z2, z1, y),
                }[hop]
                source = acc.at[self.blocks(*place) + mine]
        return remote(source, target, self.send.at[s], self.recv.at[s], where)

    def fetch(self):
        return pltpu.make_async_copy(self.source, self.acc, self.local)

    def left_over(self, target):
        every = slice(None)
        rows = self.rows(0, self.core)
        if len(self.hops) == 1:
            source = self.acc.at[:, :, :, rows]
        elif self.unit.early:
            source = self.acc.at[:, :, :, rows, self.lanes(0, self.x)]
        else:
            source = self.acc.at[:, :, self.y, rows]
        return pltpu.make_async_copy(source, target, self.local)

    def start(self, s):
        if s == 0 and self.moved:
            self.fetch().wait()
        self.copy(s).start()

    def finish(self, s):
        hop = self.hops[s]
        acc, mine, every = self.acc, self.inside(self.x), (slice(None), slice(None))
        self.copy(s).wait_recv()
        pairs = [(a, b) for a in range(2) for b in range(2)]

        def add(place, other):
            acc[place] = acc[place] + self.got[s][other]

        if hop in ("core", "x"):
            inside = (mine[0], slice(None)) if hop == "core" else mine
            for a, b in pairs:
                for c in range(2):
                    add((a, b, c) + inside, (a, b, c) + every)
        elif hop == "y":
            for a, b in pairs:
                add((a, b, self.y) + mine, (a, b) + every)
        elif hop == "z1":
            for a in range(2):
                add(self.blocks(a, self.z1, self.y) + mine, (a,) + every)
        elif hop == "z2" and not self.unit.early:
            add(self.blocks(self.z2, self.z1, self.y) + mine, every)
        elif hop in ("z2", "late"):
            place = self.blocks(self.z2, self.z1, self.y) + mine
            u = self.unit
            self.result[self.rows(u.result_top, self.core), self.lanes(u.result_left, self.x)] = (
                acc[place] + self.got[s][...]
            )

    def close(self):
        for s in range(len(self.hops)):
            self.copy(s).wait_send()


class Stream:
    def __init__(self, copies):
        self.hops = copies

    def start(self, s):
        self.hops[s].start()

    def finish(self, s):
        self.hops[s].wait_send()

    def close(self):
        pass


STREAMS = (((4, "z2"), (6, "z2")), ((5, "z2"), (7, "z2")), ((2, "z1"), (3, "z1")), ((1, "y"),))


class Wave:
    def __init__(self, steps, got, send, recv):
        self.steps, self.got, self.send, self.recv = steps, got, send, recv
        batch, blk = lax.axis_index("batch"), lax.axis_index("blk")
        self.hops = [at_batch(batch ^ 1), at_batch(batch ^ 2), at_blk(blk ^ 1), at_blk(blk ^ 2), at_blk(blk ^ 4)]

    def copy(self, s):
        return remote(self.steps.at[s], self.got.at[s], self.send.at[s], self.recv.at[s], self.hops[s])

    def start(self, s):
        self.copy(s).start()

    def finish(self, s):
        self.copy(s).wait_recv()
        self.steps[s + 1] = self.steps[s] + self.got[s]

    def close(self):
        for s in range(len(self.hops)):
            self.copy(s).wait_send()


DELAY = {"core": 1.8, "x": 2.6, "y": 2.6, "z1": 2.6, "z2": 3.6}
RATE = {"core": 210e3, "x": 36e3, "y": 36e3, "z1": 36e3, "z2": 22e3}
SAME = {"pair": "core", "late": "x", "join": "x"}
LINK = {"z1": "z", "z2": "z"}


def hop_bytes(unit, hop):
    shape = unit.shape_after(hop)
    if shape is None:
        shape = (unit.half, unit.cols // 2 if hop == "join" else unit.cols)
    return 2 * math.prod(shape)


def plan_hops(jobs, marks):
    free = {LINK.get(kind, kind): 0.0 for kind in RATE}
    due = {}
    result = []

    def begin(job, number, now):
        hop, size = jobs[job][1][number]
        kind = SAME.get(hop, hop)
        link = LINK.get(kind, kind)
        free[link] = max(now, free[link]) + size / RATE[kind]
        due[job] = (free[link] + DELAY[kind], number)

    for k, mark in enumerate(marks):
        now, last, events = mark, k == len(marks) - 1, []
        for job, (ready, _) in enumerate(jobs):
            if ready == k:
                events.append((job, 0, False))
                begin(job, 0, now)
        while due:
            job = min(due, key=lambda j: due[j][0])
            when, number = due[job]
            if when > now:
                if not last:
                    break
                now = when
            now += 0.2 if last else 0.0
            del due[job]
            events.append((job, number, True))
            if number + 1 < len(jobs[job][1]):
                begin(job, number + 1, now)
        result.append(events)
    return result


def follow(routes, events):
    for job, number, ends in events:
        route = routes[job]
        if ends:
            route.finish(number)
            number += 1
        if number < len(route.hops):
            route.start(number)


VECTORS = 16


def finish_kernel(n, tile, plan, *refs):
    (mixed_grad, weights, query, key, value, wq, wk, wv, normed, core, total, squeeze_in, low_x_in, middle_grad_in,
     params, up_bias, sums, down_in, up_in, down_last, up_last, out_in) = refs[:22]
    home, *summed, vec_out = refs[22:29]
    (down_out, up_out, qkv_out, out_out, small_out, put, out_here, out_sem, up, core_grad, lift, qkv_grad, small, ready, vectors, vec_got,
     own, send_d, recv_d, local, send, recv, vec_send, vec_recv, squeeze, low_x, middle_grad, late) = refs[29:57]
    refs = refs[57:]
    lates = [
        pltpu.make_async_copy(source, target, late.at[k])
        for k, (source, target) in enumerate(
            ((squeeze_in, squeeze), (low_x_in, low_x), (middle_grad_in, middle_grad))
        )
    ]
    units, plan = plan
    i = pl.program_id(0)
    m, tokens = core.shape[0], low_x.shape[1]
    batch, me = lax.axis_index("batch"), lax.axis_index("blk")
    places = {
        "up": (up_in, up_out),
        "up_last": (up_last, up_out),
        "down": (down_in, down_out),
        "down_last": (down_last, down_out),
        "out": (out_here, out_out),
        "qkv": (qkv_grad, qkv_out),
        "small": (small, small_out),
    }
    routes = []
    for k, (name, unit) in enumerate(units):
        count = len(unit.scratch())
        buffers, refs = refs[:count], refs[count:]
        source, result = places[name]
        if unit.kept == "first" or name == "qkv":
            source = source.at[unit.lead]
        routes.append(Route(unit, source, result, buffers, local.at[k], send.at[k], recv.at[k]))
    take_out = pltpu.make_async_copy(out_in, out_here, out_sem)
    wave = Wave(vectors, vec_got, vec_send, vec_recv)

    def ship(d):
        return remote(ready.at[me ^ d], home.at[me], send_d.at[d - 1], recv_d.at[d - 1], at_blk(me ^ d))

    streams = [Stream([ship(d) for d, _ in stream]) for stream in STREAMS]
    everyone = routes + [wave] + streams

    def look(step, mark):
        @pl.when(i == step)
        def _():
            follow(everyone, plan[mark])

    @pl.when(i == 0)
    def _():
        for route in routes:
            if route.moved:
                route.fetch().start()
        take_out.start()
        greet([at_batch(batch ^ 1), at_batch(batch ^ 2)] + [at_blk(me ^ d) for d in range(1, n)])
        take_out.wait()
        for copy in lates:
            copy.start()
        up[...] = jnp.zeros_like(up)
        core_grad[...] = jnp.zeros_like(core_grad)
        lift[...] = jnp.zeros_like(lift)
        vectors[0] = jnp.zeros(vectors.shape[1:], F32)

    look(0, 0)
    steps = qkv_grad.shape[0]
    scale = 1.0 / math.sqrt(HD)
    keys = by_head(key[...] * jnp.asarray(scale, BF16))
    values = by_head(value[...])
    rows = mixed_grad.shape[0]
    dv = dk = None
    grads_q = []
    for r in range(rows // tile):
        at = slice(r * tile, (r + 1) * tile)
        grads = mixed_grad[at, :]
        back = contract(grads, values, 1, 1)
        low = weights[0, at, :]
        heads = []
        for h in range(LANES // HD):
            p = low[:, h * m : (h + 1) * m].astype(F32)
            g = back[:, h * m : (h + 1) * m]
            heads.append((p * (g - jnp.sum(p * g, axis=-1, keepdims=True))).astype(BF16))
        score = jnp.concatenate(heads, axis=1)
        part_v = own_head(contract(low, grads, 0, 0))
        part_k = own_head(contract(score, query[at, :], 0, 0))
        dv = part_v if dv is None else dv + part_v
        dk = part_k if dk is None else dk + part_k
        grads_q.append(contract(score, keys, 1, 0).astype(BF16))
        if r < rows // tile - 1:
            for step in range(steps):
                look(step, step * (rows // tile) + r + 1)
    dq = jnp.concatenate(grads_q, axis=0)
    dk = dk * scale
    dk_low, dv_low = dk.astype(BF16), dv.astype(BF16)
    up[...] += contract(dq, wq[...], 1, 1)
    core_grad[...] += contract(dk_low, wk[...], 1, 1) + contract(dv_low, wv[...], 1, 1)
    lanes = pl.ds(pl.multiple_of(i * LANES, LANES), LANES)
    lift[...] += jnp.sum(dk * params[3:4, lanes] + dv * params[4:5, lanes], axis=1, keepdims=True)
    for k, grad in enumerate(
        (
            contract(normed[...], dq, 0, 0),
            contract(core[...], dk_low, 0, 0),
            contract(core[...], dv_low, 0, 0),
        )
    ):
        block = grad.shape[0] // n
        for b in range(n):
            qkv_grad[i, b // 4, (b // 2) % 2, b % 2, :, k * LANES : (k + 1) * LANES] = grad[
                b * block : (b + 1) * block
            ].astype(BF16)
    vectors[0, 2:3, lanes] = jnp.sum(dq.astype(F32), axis=0, keepdims=True)
    vectors[0, 3:4, lanes] = jnp.sum(total[...] * dk, axis=0, keepdims=True)
    vectors[0, 4:5, lanes] = jnp.sum(total[...] * dv, axis=0, keepdims=True)

    looks = rows // tile
    for step in range(steps):
        look(step, (step + 1) * looks)

    @pl.when(i == steps - 1)
    def _():
        width = low_x.shape[2]

        for copy in lates:
            copy.wait()
        low_core = core_grad[...].astype(BF16)
        gain_sum = bias_sum = jnp.zeros((1, width), F32)
        mine = pltpu.make_async_copy(ready.at[me], home.at[me], own)
        for turn, d in enumerate(spread_order(n) + [0]):
            b = me ^ d
            at = pl.ds(pl.multiple_of(b * tokens, tokens), tokens)
            rise = up[at, :] + contract(squeeze[b], low_core, 0, 0)
            hat, rate = norm_stats(low_x[b].astype(F32))
            gain_sum += jnp.sum(rise * hat, axis=0, keepdims=True)
            bias_sum += jnp.sum(rise, axis=0, keepdims=True)
            ready[b] = (middle_grad[at, :] + norm_back(hat, rate, rise, params[0:1, :])).astype(BF16)
            if d == 0:
                mine.start()
            if turn == TURN:
                follow(everyone, plan[steps * looks + 1])
        follow(everyone, plan[steps * looks + 2])
        for b in range(n):
            terms = contract(low_core, normed[b * tokens : (b + 1) * tokens, :], 1, 1) + lift[...]
            small[b // 4, (b // 2) % 2, b % 2] = terms.astype(BF16)
        vectors[0, 0:1, :] = gain_sum
        vectors[0, 1:2, :] = bias_sum
        vectors[0, 5:6, :] = sums[0:1, :]
        vectors[0, 6:7, :] = sums[1:2, :]
        vectors[0, 7:8, :] = sums[2:3, :]
        for k in range(up_bias.shape[1] // width):
            vectors[0, 8 + k : 9 + k, :] = up_bias[:, k * width : (k + 1) * width]
        vectors[0, 12:13, :] = sums[3:4, :]
        follow(everyone, plan[steps * looks + 3])
        puts = [
            pltpu.make_async_copy(source, target, put.at[k])
            for k, (source, target) in enumerate(
                zip((down_out, up_out, qkv_out, out_out, small_out), summed)
            )
        ]
        for copy in puts:
            copy.start()
        vec_out[...] = vectors[len(wave.hops)]
        for route in everyone:
            route.close()
        mine.wait()
        for d in range(1, n):
            ship(d).wait_recv()
        for copy in puts:
            copy.wait()


def finish(mixed_grad, weights, query, key, value, normed, core, total, squeeze, low_x, middle_grad, params,
           qkv_weight, up_bias, sums, down, up, down_last, up_last, out, tile=512):
    n, m, tokens = squeeze.shape
    rows, width = normed.shape
    steps, heads = width // LANES, LANES // HD
    tall = width // n
    feeds, block = up.shape[0] + 1, up.shape[-1] * 2
    hidden = feeds * block
    deep = down.shape[-2] * 2
    out = out.reshape(2, 2, 2, tall, width)
    units = []
    for k in range(feeds):
        kept = "core" if k == feeds - 1 else "first"
        tail = "_last" if k == feeds - 1 else ""
        units.append(("up" + tail, Unit(tall, block, True, 0, block * k, kept, None, k)))
        units.append(("down" + tail, Unit(deep, width, k == feeds - 1, deep * k, 0, kept, None, k)))
    units.append(("out", Unit(tall, width, True)))
    for k in range(steps):
        units.append(("qkv", Unit(tall, 3 * LANES, True, 0, 3 * LANES * k, lead=k)))
    units.append(("small", Unit(m, tokens, False)))
    looks = rows // tile
    end = steps * looks + 3
    begun = MARKS[0]
    marks = [begun] + [begun + MARKS[1] * (k + 1) / looks for k in range(steps * looks)]
    marks += [marks[-1] + late for late in MARKS[2:]]
    jobs = []
    for name, unit in units:
        begin = {"qkv": (unit.lead + 1) * looks, "small": end}.get(name, 0)
        jobs.append((begin, [(hop, hop_bytes(unit, hop)) for hop in unit.hops]))
    jobs.append((end, [(hop, 4 * VECTORS * width) for hop in ("core", "x", "y", "z1", "z2")]))
    for k, stream in enumerate(STREAMS):
        jobs.append((end - 2 + (k > 1), [(hop, 2 * tokens * width) for _, hop in stream]))
    plan = (units, plan_hops(jobs, marks))
    anywhere = pl.BlockSpec(memory_space=pl.ANY)
    vmem = pl.BlockSpec(memory_space=pltpu.VMEM)
    dma = pltpu.SemaphoreType.DMA
    blocks = (2, 2, 2, tall, width)
    results = [(hidden // n, width), (tall, hidden), (tall, 3 * width), (tall, width), (m, tokens)]
    scratch = [pltpu.VMEM(shape, BF16) for shape in results] + [
        dma((len(results),)),
        pltpu.VMEM(blocks, BF16),
        dma,
        pltpu.VMEM((rows, width), F32),
        pltpu.VMEM((m, width), F32),
        pltpu.VMEM((m, 1), F32),
        pltpu.VMEM((steps,) + blocks, BF16),
        pltpu.VMEM((2, 2, 2, m, tokens), BF16),
        pltpu.VMEM((n, tokens, width), BF16),
        pltpu.VMEM((6, VECTORS, width), F32),
        pltpu.VMEM((5, VECTORS, width), F32),
        dma,
        dma((n - 1,)),
        dma((n - 1,)),
        dma((len(units),)),
        dma((len(units), HOPS)),
        dma((len(units), HOPS)),
        dma((5,)),
        dma((5,)),
        pltpu.VMEM((n, m, tokens), BF16),
        pltpu.VMEM((n, tokens, width), BF16),
        pltpu.VMEM((rows, width), F32),
        dma((3,)),
    ]
    for _, unit in units:
        scratch += unit.scratch()
    return pl.pallas_call(
        functools.partial(finish_kernel, n, tile, plan),
        grid=(steps,),
        in_specs=[
            columns(rows, 0),
            pl.BlockSpec((1, rows, heads * m), lambda i: (i, 0, 0)),
            columns(rows, 0),
            columns(m, 0),
            columns(m, 0),
        ]
        + [columns(width, k * steps) for k in range(3)]
        + [
            whole((rows, width)),
            whole((m, width)),
            whole((m, 1)),
            anywhere,
            anywhere,
            anywhere,
            whole(params.shape),
            whole((1, hidden)),
            whole((4, width)),
            anywhere,
            anywhere,
            anywhere,
            anywhere,
            anywhere,
        ],
        out_specs=[anywhere] * (1 + len(results)) + [whole((VECTORS, width))],
        out_shape=[jax.ShapeDtypeStruct((n, tokens, width), BF16)]
        + [jax.ShapeDtypeStruct(shape, BF16) for shape in results]
        + [jax.ShapeDtypeStruct((VECTORS, width), F32)],
        scratch_shapes=scratch,
        compiler_params=pltpu.CompilerParams(
            collective_id=1, has_side_effects=True, vmem_limit_bytes=67043328, dimension_semantics=("arbitrary",)
        ),
        name="finish",
    )(mixed_grad, weights, query, key, value, qkv_weight, qkv_weight, qkv_weight, normed, core,
      total, squeeze, low_x, middle_grad, params, up_bias, sums, down, up, down_last, up_last, out)


MARKS = (1.0, 8.7, 3.0, 8.0, 11.0)
TURN = 3


class Exchange:
    def __init__(self, source, target, own, send, recv):
        self.source, self.target = source, target
        self.own, self.send, self.recv = own, send, recv
        self.n = source.shape[0]
        self.me = lax.axis_index("blk")

    def copy(self, d):
        return remote(
            self.source.at[self.me ^ d],
            self.target.at[self.me],
            self.send.at[d - 1],
            self.recv.at[d - 1],
            at_blk(self.me ^ d),
        )

    def mine(self):
        return pltpu.make_async_copy(self.source.at[self.me], self.target.at[self.me], self.own)

    def start(self, far_first=True):
        for d in spread_order(self.n, far_first):
            self.copy(d).start()
        self.mine().start()

    def wait(self):
        self.mine().wait()
        for d in range(1, self.n):
            self.copy(d).wait()


def exchange_scratch(n):
    dma = pltpu.SemaphoreType.DMA
    return [dma, dma((n - 1,)), dma((n - 1,))]


def alive_here(counts):
    return lax.axis_index("blk") < counts[lax.axis_index("batch")]


def side_by_side(refs, axis):
    return jnp.concatenate([ref[...] for ref in refs], axis=axis)


COTS_FIRST = False
COTS_AFTER = 6
ARRIVAL = (1, 2, 3, 4, 5, 6, 7)


def open_kernel(n, nb, attends, feeds, tile, counts, inputs, cotangent, compress, *refs):
    given, refs = refs[:8], refs[8:]
    (wq, wk, wv, ow_in), refs = refs[:4], refs[4:]
    upw, dnw, refs = refs[:n], refs[n : 2 * n], refs[2 * n :]
    (low_x, normed, squeeze, low_cot, core_out, total_out, query, key, value, weights, mixed,
     middle, second, active, slope, output, vectors) = refs[:17]
    (x_here, n_here, e_part, e_here, core_sum, total, acc, core) = refs[17:25]
    (keep, send_e, recv_e, send_q, recv_q, own_q) = refs[25:31]
    x_sems, cot_sems = refs[31:34], refs[34:37]
    ow, ow_sem = refs[37:39]
    take_ow = pltpu.make_async_copy(ow_in, ow, ow_sem)
    i = pl.program_id(0)
    me, batch = lax.axis_index("blk"), lax.axis_index("batch")
    tokens = inputs.shape[1]
    rows, m, width = n * tokens, compress.shape[0], inputs.shape[2]
    share = m // nb

    def vector(k):
        return vectors[k : k + 1, :]

    def quarter(q):
        return pl.ds(pl.multiple_of(q * share, share), share)

    xs = Exchange(inputs, x_here, *x_sems)
    cots = Exchange(cotangent, low_cot, *cot_sems)

    def piece(d):
        return remote(
            compress.at[quarter(batch)], e_part.at[me], send_e.at[d - 1], recv_e.at[d - 1], at_blk(me ^ d)
        )

    def pass_on(c):
        return remote(
            e_part, e_here.at[:, quarter(batch)], send_q.at[c - 1], recv_q.at[c - 1], at_batch(batch ^ c)
        )

    keep_part = pltpu.make_async_copy(e_part, e_here.at[:, quarter(batch)], own_q)

    keeps = [
        pltpu.make_async_copy(source, target, keep.at[k])
        for k, (source, target) in enumerate(((x_here, low_x), (n_here, normed), (e_here, squeeze)))
    ]

    @pl.when(i == 0)
    def _():
        greet([at_blk(me ^ d) for d in range(1, n)] + [at_batch(batch ^ c) for c in range(1, nb)])
        for d in range(1, n):
            piece(d).start()
        for e in (7, 1, 6, 2, 5, 3, 4):
            xs.copy(e).start()
        xs.mine().start()
        if COTS_FIRST:
            cots.start()
        take_ow.start()
        e_part[me] = compress[quarter(batch), :]
        row = 0
        for ref in given:
            for k in range(ref.shape[0] // width):
                vectors[row : row + 1, :] = ref[k * width : (k + 1) * width].reshape(1, width)
                row += 1
        core_sum[...] = jnp.zeros_like(core_sum)
        total[...] = jnp.zeros_like(total)
        for d in range(1, n):
            piece(d).wait_recv()
        for c in range(1, nb):
            pass_on(c).start()
        keep_part.start()

        def arrived(slot):
            low = (norm_stats(x_here[slot].astype(F32))[0] * vector(0) + vector(1)).astype(BF16)
            n_here[slot] = low

        def gather(slot):
            part = e_here[slot]
            core_sum[...] += contract(part, n_here[slot], 1, 0)
            total[...] += jnp.sum(part.astype(F32), axis=1, keepdims=True)

        xs.mine().wait()
        arrived(me)
        keep_part.wait()
        for c in range(1, nb):
            pass_on(c).wait_recv()
        gather(me)
        for d in ARRIVAL:
            xs.copy(d).wait_recv()
            if not COTS_FIRST and d == ARRIVAL[COTS_AFTER]:
                cots.start(False)
            arrived(me ^ d)
            gather(me ^ d)
        core[...] = core_sum[...].astype(BF16)
        core_out[...] = core[...]
        total_out[...] = total[...]
        for copy in keeps:
            copy.start()

    @pl.when(i < attends)
    def _():
        lanes = pl.ds(pl.multiple_of(i * LANES, LANES), LANES)
        bq, bk, bv = (vectors[k : k + 1, lanes] for k in (2, 3, 4))
        key[...] = (contract(core[...], wk[...], 1, 0) + total[...] * bk).astype(BF16)
        value[...] = (contract(core[...], wv[...], 1, 0) + total[...] * bv).astype(BF16)
        keys = by_head(key[...] * jnp.asarray(1.0 / math.sqrt(HD), BF16))
        values = by_head(value[...])
        for r in range(rows // tile):
            at = slice(r * tile, (r + 1) * tile)
            blocks = slice(r * tile // tokens, (r + 1) * tile // tokens)
            low_n = n_here[blocks].reshape(tile, -1)
            q = (contract(low_n, wq[...], 1, 0) + bq).astype(BF16)
            query[at, :] = q
            scores = contract(q, keys, 1, 1)
            heads = []
            for h in range(LANES // HD):
                s = scores[:, h * m : (h + 1) * m]
                e = jnp.exp(s - jnp.max(s, axis=-1, keepdims=True))
                heads.append((e * (1.0 / jnp.sum(e, axis=-1, keepdims=True))).astype(BF16))
            low = jnp.concatenate(heads, axis=1)
            weights[0, at, :] = low
            mixed[at, lanes] = contract(low, values, 1, 0).astype(BF16)

    @pl.when(i == attends)
    def _():
        take_ow.wait()
        mid = x_here[...].reshape(rows, -1).astype(F32) + contract(mixed[...], ow[...], 1, 0) + vector(5)
        middle[...] = mid
        second[...] = (norm_stats(mid)[0] * vector(6) + vector(7)).astype(BF16)
        acc[...] = mid + vector(12)

    @pl.when(i >= attends)
    def _():
        pieces = []
        for b in range(n):
            chosen = None
            for u in range(feeds):
                row, lane = divmod((b * feeds + u) * 128, width)
                here = vectors[8 + row : 9 + row, lane : lane + 128]
                chosen = here if u == 0 else jnp.where(i == attends + u, here, chosen)
            pieces.append(chosen)
        v = contract(second[...], side_by_side(upw, 1), 1, 0) + jnp.concatenate(pieces, axis=1)
        square = v * v
        t = jnp.tanh(v * (GELU_A + (GELU_A * GELU_B) * square))
        half = 0.5 + 0.5 * t
        act = (v * half).astype(BF16)
        active[...] = act
        slope[...] = (
            half + (0.5 * v) * (1.0 - t * t) * (GELU_A + (3 * GELU_A * GELU_B) * square)
        ).astype(BF16)
        acc[...] += contract(act, side_by_side(dnw, 0), 1, 0)

    @pl.when(i == pl.num_programs(0) - 1)
    def _():
        output[...] = jnp.where(alive_here(counts), acc[...], 0.0).astype(BF16).reshape(output.shape)
        for copy in keeps:
            copy.wait()
        for d in range(1, n):
            piece(d).wait_send()
            xs.copy(d).wait_send()
        for c in range(1, nb):
            pass_on(c).wait_send()
        cots.wait()


def open_all(nb, counts, inputs, cotangent, compress, given, qkv_weight, ow, upw, dnw, tile=512):
    n, tokens, width = inputs.shape
    rows, m, hidden = n * tokens, compress.shape[0], upw.shape[1]
    attends, heads = width // LANES, LANES // HD
    feeds = hidden // n // 128
    block = n * 128
    anywhere = pl.BlockSpec(memory_space=pl.ANY)

    def early(i):
        return jnp.minimum(i, attends - 1)

    def late(i):
        return jnp.maximum(i - attends, 0)

    def wide(height, start):
        return pl.BlockSpec((height, LANES), lambda i: (0, start + early(i)))

    def chunk(shape, dim, b):
        if dim:
            return pl.BlockSpec(shape, lambda i: (0, b * feeds + late(i)))
        return pl.BlockSpec(shape, lambda i: (b * feeds + late(i), 0))

    struct = jax.ShapeDtypeStruct
    dma = pltpu.SemaphoreType.DMA
    return pl.pallas_call(
        functools.partial(open_kernel, n, nb, attends, feeds, tile),
        grid=(attends + feeds,),
        in_specs=[pl.BlockSpec(memory_space=pltpu.SMEM), anywhere, anywhere, whole((m, tokens))]
        + [whole(v.shape) for v in given]
        + [wide(width, k * attends) for k in range(3)]
        + [anywhere]
        + [chunk((width, 128), 1, b) for b in range(n)]
        + [chunk((128, width), 0, b) for b in range(n)],
        out_specs=[anywhere] * 4
        + [whole((m, width)), whole((m, 1)), wide(rows, 0), wide(m, 0), wide(m, 0)]
        + [pl.BlockSpec((1, rows, heads * m), lambda i: (early(i), 0, 0))]
        + [whole((rows, width))] * 3
        + [pl.BlockSpec((rows, block), lambda i: (0, late(i)))] * 2
        + [whole((n, tokens, width)), whole((VECTORS, width))],
        out_shape=[
            struct((n, tokens, width), BF16),
            struct((n, tokens, width), BF16),
            struct((n, m, tokens), BF16),
            struct((n, tokens, width), BF16),
            struct((m, width), BF16),
            struct((m, 1), F32),
            struct((rows, width), BF16),
            struct((m, width), BF16),
            struct((m, width), BF16),
            struct((attends, rows, heads * m), BF16),
            struct((rows, width), BF16),
            struct((rows, width), F32),
            struct((rows, width), BF16),
            struct((rows, hidden), BF16),
            struct((rows, hidden), BF16),
            struct((n, tokens, width), BF16),
            struct((VECTORS, width), F32),
        ],
        scratch_shapes=[
            pltpu.VMEM((n, tokens, width), BF16),
            pltpu.VMEM((n, tokens, width), BF16),
            pltpu.VMEM((n, m // nb, tokens), BF16),
            pltpu.VMEM((n, m, tokens), BF16),
            pltpu.VMEM((m, width), F32),
            pltpu.VMEM((m, 1), F32),
            pltpu.VMEM((rows, width), F32),
            pltpu.VMEM((m, width), BF16),
            dma((3,)),
            dma((n - 1,)),
            dma((n - 1,)),
            dma((nb - 1,)),
            dma((nb - 1,)),
            dma,
        ]
        + exchange_scratch(n)
        + exchange_scratch(n)
        + [pltpu.VMEM((width, width), BF16), dma],
        compiler_params=pltpu.CompilerParams(
            collective_id=0, has_side_effects=True, vmem_limit_bytes=67043328, dimension_semantics=("arbitrary",)
        ),
        name="open",
    )(counts, inputs, cotangent, compress, *given, qkv_weight, qkv_weight, qkv_weight, ow, *[upw] * n, *[dnw] * n)


def back_kernel(n, units, counts, cot, result, active, slope, second_in, middle_in, mixed_in, *refs):
    upw, dnw, (ow_in, vectors), refs = refs[:n], refs[n : 2 * n], refs[2 * n : 2 * n + 2], refs[2 * n + 2 :]
    (home, up_part, down_part, up_last, down_last, up_bias_grad, middle_grad, mixed_grad, out_grad, sums) = refs[:10]
    (incoming, total, up_grad, down_grad, take, local, send, recv) = refs[10:18]
    outs = Exchange(result, home, *refs[18:21])
    middle, mixed, ow, late, second, soon = refs[21:27]
    refs = refs[27:]
    take_second = pltpu.make_async_copy(second_in, second, soon)
    lates = [
        pltpu.make_async_copy(source, target, late.at[k])
        for k, (source, target) in enumerate(((middle_in, middle), (mixed_in, mixed), (ow_in, ow)))
    ]
    f = pl.program_id(0)
    batch, me = lax.axis_index("batch"), lax.axis_index("blk")
    feeds = len(units) // 2
    routes = []
    for k, unit in enumerate(units):
        count = len(unit.scratch())
        buffers, refs = refs[:count], refs[count:]
        source = (down_grad if k % 2 else up_grad).at[unit.lead]
        routes.append(Route(unit, source, None, buffers, local.at[k], send.at[k], recv.at[k]))
    pairs = [routes[2 * k : 2 * k + 2] for k in range(feeds)]

    def put(k):
        last = k == feeds - 1
        targets = (up_last, down_last) if last else (up_part.at[k], down_part.at[k])
        return [route.left_over(target) for route, target in zip(pairs[k], targets)]

    def advance(k, s):
        for route in pairs[k]:
            route.finish(s)
            if s + 1 < len(route.hops):
                route.start(s + 1)
        if s + 1 == len(pairs[k][0].hops):
            for copy in put(k):
                copy.start()

    @pl.when(f == 0)
    def _():
        fetch = pltpu.make_async_copy(cot, incoming, take)
        fetch.start()
        greet([at_batch(batch ^ 1), at_batch(batch ^ 2)] + [at_blk(me ^ d) for d in range(1, n)])
        outs.start()
        take_second.start()
        for copy in lates:
            copy.start()
        total[...] = jnp.zeros_like(total)
        fetch.wait()
        incoming[...] = jnp.where(alive_here(counts), incoming[...], jnp.zeros_like(incoming))

    low = incoming[...].reshape(total.shape)
    d = contract(low, side_by_side(dnw, 0), 1, 1)
    dh = (d * slope[...].astype(F32)).astype(BF16)
    up_bias_grad[...] = jnp.sum(dh.astype(F32), axis=0, keepdims=True)
    total[...] += contract(dh, side_by_side(upw, 1), 1, 1)

    for k in range(1, feeds):
        @pl.when(f == k)
        def _(k=k):
            if k > 1:
                advance(k - 2, 1)
            advance(k - 1, 0)

    @pl.when(f == 0)
    def _():
        take_second.wait()

    grad = contract(active[...], low, 0, 0)
    for b in range(n):
        at = slice(b * 128, (b + 1) * 128)
        down_grad[f, b // 4, (b // 2) % 2, b % 2] = grad[at].astype(BF16)
    grad = contract(second[...], dh, 0, 0)
    tall = grad.shape[0] // n
    for b in range(n):
        at = slice(b * tall, (b + 1) * tall)
        up_grad[f, b // 4, (b // 2) % 2, b % 2] = grad[at].astype(BF16)

    for k in range(feeds):
        @pl.when(f == k)
        def _(k=k):
            for route in pairs[k]:
                route.start(0)

    @pl.when(f == feeds - 1)
    def _():
        for copy in lates:
            copy.wait()
        hat, rate = norm_stats(middle[...])
        up = total[...]
        inc = low.astype(F32)
        grad = inc + norm_back(hat, rate, up, vectors[6:7, :])
        middle_grad[...] = grad
        branch = grad.astype(BF16)
        mixed_grad[...] = contract(branch, ow[...], 1, 1).astype(BF16)
        out_grad[...] = contract(mixed[...], branch, 0, 0).astype(BF16)
        sums[0:1, :] = jnp.sum(branch.astype(F32), axis=0, keepdims=True)
        sums[1:2, :] = jnp.sum(up * hat, axis=0, keepdims=True)
        sums[2:3, :] = jnp.sum(up, axis=0, keepdims=True)
        sums[3:4, :] = jnp.sum(inc, axis=0, keepdims=True)
        advance(feeds - 2, 1)
        advance(feeds - 1, 0)
        for k in range(feeds):
            for copy in put(k):
                copy.wait()
        for route in routes:
            route.close()
        outs.wait()


def back_all(counts, cot, result, active, slope, second, middle, mixed, upw, dnw, ow, vectors):
    n, tokens, width = cot.shape
    rows, hidden = active.shape
    feeds, block, tall = hidden // n // 128, n * 128, width // n
    anywhere = pl.BlockSpec(memory_space=pl.ANY)

    def chunk(shape, dim, b):
        if dim:
            return pl.BlockSpec(shape, lambda i: (0, b * feeds + i))
        return pl.BlockSpec(shape, lambda i: (b * feeds + i, 0))

    units = []
    for k in range(feeds):
        hops = 1 if k == feeds - 1 else 2
        units.append(Unit(tall, block, True, hops=hops, lead=k))
        units.append(Unit(128, width, k == feeds - 1, hops=hops, lead=k))
    struct = jax.ShapeDtypeStruct
    dma = pltpu.SemaphoreType.DMA
    scratch = [
        pltpu.VMEM((n, tokens, width), BF16),
        pltpu.VMEM((rows, width), F32),
        pltpu.VMEM((feeds, 2, 2, 2, tall, block), BF16),
        pltpu.VMEM((feeds, 2, 2, 2, 128, width), BF16),
        dma,
        dma((len(units),)),
        dma((len(units), 2)),
        dma((len(units), 2)),
    ] + exchange_scratch(n)
    scratch += [
        pltpu.VMEM((rows, width), F32),
        pltpu.VMEM((rows, width), BF16),
        pltpu.VMEM((width, width), BF16),
        dma((3,)),
        pltpu.VMEM((rows, width), BF16),
        dma,
    ]
    for unit in units:
        scratch += unit.scratch()
    return pl.pallas_call(
        functools.partial(back_kernel, n, units),
        grid=(feeds,),
        in_specs=[
            pl.BlockSpec(memory_space=pltpu.SMEM),
            anywhere,
            anywhere,
            columns(rows, 0, block),
            columns(rows, 0, block),
            anywhere,
            anywhere,
            anywhere,
        ]
        + [chunk((width, 128), 1, b) for b in range(n)]
        + [chunk((128, width), 0, b) for b in range(n)]
        + [anywhere, whole(vectors.shape)],
        out_specs=[
            anywhere,
            anywhere,
            anywhere,
            anywhere,
            anywhere,
            columns(1, 0, block),
            whole((rows, width)),
            whole((rows, width)),
            whole((width, width)),
            whole((4, width)),
        ],
        out_shape=[
            struct((n, tokens, width), BF16),
            struct((feeds - 1, 2, 2, 2, tall // 2, block // 2), BF16),
            struct((feeds - 1, 2, 2, 64, width), BF16),
            struct((2, 2, 2, tall // 2, block), BF16),
            struct((2, 2, 2, 64, width), BF16),
            struct((1, hidden), F32),
            struct((rows, width), F32),
            struct((rows, width), BF16),
            struct((width, width), BF16),
            struct((4, width), F32),
        ],
        scratch_shapes=scratch,
        compiler_params=pltpu.CompilerParams(
            collective_id=2, has_side_effects=True, vmem_limit_bytes=67043328, dimension_semantics=("arbitrary",)
        ),
        name="back",
    )(counts, cot, result, active, slope, second, middle, mixed, *[upw] * n, *[dnw] * n, ow, vectors)


def settle_kernel(n, *refs):
    sources, targets, refs = refs[:8], refs[8:23], refs[23:]
    held, wide, take, put = refs[:8], refs[8:13], refs[13], refs[14]
    blk = lax.axis_index("blk")
    takes = [pltpu.make_async_copy(a, b, take.at[k]) for k, (a, b) in enumerate(zip(sources, held))]
    ready = list(held[:2]) + list(wide)
    puts = [pltpu.make_async_copy(a, b, put.at[k]) for k, (a, b) in enumerate(zip(ready, targets[:7]))]
    order = (0, 1, 3, 2, 4, 5, 6)
    for k in (7,) + order:
        takes[k].start()
    takes[7].wait()
    sums = held[7]
    width = sums.shape[1]
    small = width // n

    def cut(rows, size):
        line = rows[0] if len(rows) == 1 else jnp.concatenate(rows, axis=1)
        return pltpu.roll(line, line.shape[1] - blk * size, 1)[:, :size]

    row = [sums[k : k + 1, :] for k in range(13)]
    feeds = 4 * width // n // 128
    hidden = jnp.concatenate(row[8:12], axis=1)
    ups = [cut([hidden[:, u * n * 128 : (u + 1) * n * 128]], 128) for u in range(feeds)]
    lines = [
        cut([row[0]], small),
        cut([row[1]], small),
        cut(row[2:5], 3 * small),
        cut([row[5]], small),
        cut([row[6]], small),
        cut([row[7]], small),
        jnp.concatenate(ups, axis=1),
        cut([row[12]], small),
    ]
    for target, line in zip(targets[7:], lines):
        target[...] = line.reshape(target.shape)
    for k in order:
        takes[k].wait()
        if k == 3:
            feeds = held[k].shape[1] // 128 // n
            for u in range(feeds):
                for b in range(n):
                    start, end = (u * n + b) * 128, (b * feeds + u) * 128
                    wide[1][:, end : end + 128] = held[k][:, start : start + 128].astype(F32)
        elif k == 4:
            steps = held[k].shape[1] // (3 * LANES)
            for i in range(steps):
                for j in range(3):
                    start, end = (i * 3 + j) * LANES, (j * steps + i) * LANES
                    wide[2][:, end : end + LANES] = held[k][:, start : start + LANES].astype(F32)
        elif k > 1:
            wide[k - 2][...] = held[k][...].astype(F32)
        puts[k].start()
    for copy in puts:
        copy.wait()


def settle(output, home, summed, sums):
    anywhere = pl.BlockSpec(memory_space=pl.ANY)
    vmem = pl.BlockSpec(memory_space=pltpu.VMEM)
    struct = jax.ShapeDtypeStruct
    dma = pltpu.SemaphoreType.DMA
    n, width = output.shape[0], output.shape[2]
    sizes = [width // n * k for k in (1, 1, 3, 1, 1, 1, 4, 1)]
    arrays = [output, home] + list(summed)
    return pl.pallas_call(
        functools.partial(settle_kernel, n),
        in_specs=[anywhere] * 8,
        out_specs=[anywhere] * 7 + [vmem] * 8,
        out_shape=[struct(output.shape, BF16), struct(home.shape, BF16)]
        + [struct(v.shape, F32) for v in summed]
        + [struct((size,), F32) for size in sizes],
        scratch_shapes=[pltpu.VMEM(v.shape, v.dtype) for v in arrays + [sums]]
        + [pltpu.VMEM(v.shape, F32) for v in summed]
        + [dma((8,)), dma((7,))],
        compiler_params=pltpu.CompilerParams(vmem_limit_bytes=60 << 20),
        name="settle",
    )(*arrays, sums)


def swap(values, axis, size, bit):
    return lax.ppermute(values, axis, [(i, i ^ bit) for i in range(size)])


def halve(values, dim, axis, size, bit):
    mine = (lax.axis_index(axis) // bit) % 2
    send = lax.dynamic_index_in_dim(values, 1 - mine, dim, keepdims=False).astype(BF16)
    keep = lax.dynamic_index_in_dim(values, mine, dim, keepdims=False)
    return keep.astype(F32) + swap(send, axis, size, bit).astype(F32)


def join(values, dim, axis, size, bit):
    mine = (lax.axis_index(axis) // bit) % 2
    other = swap(values, axis, size, bit)
    first = jnp.where(mine == 0, values, other)
    second = jnp.where(mine == 0, other, values)
    return jnp.concatenate([first, second], axis=dim)


def scatter_sum(terms, bits, order, nb, nk, early):
    _, rows, cols = terms.shape
    values = halve(terms.reshape(-1, 2, rows // 2, cols), 1, "batch", nb, 1)
    chips = [1 << i for i in range(1, nb.bit_length() - 1)]
    if early:
        for bit in chips:
            cols //= 2
            values = halve(values.reshape(-1, rows // 2, 2, cols), 2, "batch", nb, bit)
    left = list(bits)
    for bit in order:
        place = left.index(bit)
        values = values.reshape(1 << place, 2, -1, rows // 2, cols)
        values = halve(values, 1, "blk", nk, bit)
        left.remove(bit)
    values = values.reshape(rows // 2, cols).astype(BF16)
    for bit in reversed(chips) if early else chips:
        if early:
            values = join(values, 1, "batch", nb, bit)
        else:
            values = (values.astype(F32) + swap(values, "batch", nb, bit).astype(F32)).astype(BF16)
    return join(values, 0, "batch", nb, 1).astype(F32)


def body(
    inputs,
    cotangent,
    group_counts,
    first_gain,
    first_bias,
    qkv_weight,
    qkv_bias,
    out_weight,
    out_bias,
    second_gain,
    second_bias,
    up_weight,
    up_bias,
    down_weight,
    down_bias,
    compress,
    *,
    nb,
    nk,
):
    slots, tokens, width = inputs.shape
    splits = nk // slots
    teams = [[t * slots + i for i in range(slots)] for t in range(splits)]
    across = [[t * slots + i for t in range(splits)] for i in range(slots)]
    rows = slots * tokens
    low_first = [1 << i for i in range(nk.bit_length() - 1)]
    high_first = low_first[::-1]
    team_low = [1 << i for i in range(slots.bit_length() - 1)]

    def gather_rows(values):
        return lax.all_to_all(values, "blk", 0, 0, axis_index_groups=teams, tiled=True).reshape(
            rows, width
        )

    def spread_rows(values):
        return lax.all_to_all(
            values.reshape(slots, tokens, width), "blk", 0, 0, axis_index_groups=teams, tiled=True
        )

    def over_splits(values):
        if splits == 1:
            return values
        return lax.psum(values, "blk", axis_index_groups=across)

    def line(vector):
        return vector.reshape(1, -1)

    if nb == 4 and nk == slots == 8:
        lines = (
            first_gain,
            first_bias,
            qkv_bias,
            out_bias,
            second_gain,
            second_bias,
            up_bias,
            down_bias,
        )
        (
            low_x,
            normed,
            squeeze,
            low_cot,
            core,
            total,
            query,
            key,
            value,
            weights,
            mixed,
            middle,
            second,
            active,
            slope,
            result,
            vectors,
        ) = open_all(
            nb, group_counts, inputs, cotangent, compress, lines, qkv_weight, out_weight, up_weight, down_weight
        )
        (
            output,
            up_grad,
            down_grad,
            up_last,
            down_last,
            up_bias_grad,
            middle_grad,
            mixed_grad,
            out_grad,
            sums,
        ) = back_all(
            group_counts,
            low_cot,
            result,
            active,
            slope,
            second,
            middle,
            mixed,
            up_weight,
            down_weight,
            out_weight,
            vectors,
        )
        input_grad, *summed, flat = finish(
            mixed_grad,
            weights,
            query,
            key,
            value,
            normed.reshape(rows, width),
            core,
            total,
            squeeze,
            low_x,
            middle_grad,
            vectors,
            qkv_weight,
            up_bias_grad,
            sums,
            down_grad,
            up_grad,
            down_last,
            up_last,
            out_grad,
        )
        (
            output,
            input_grad,
            down_rows,
            up_rows,
            qkv_rows,
            out_rows,
            compress_rows,
            fg,
            fb,
            qb,
            ob,
            sg,
            sb,
            ub,
            db,
        ) = settle(output, input_grad, summed, flat)
    else:
        slot = lax.axis_index("blk") % slots
        alive = (slot < group_counts[lax.axis_index("batch")]).astype(jnp.int32).reshape(1)

        squeeze = compress[None]
        for bit in team_low[::-1]:
            squeeze = join(squeeze[:, None], 1, "blk", nk, bit)
            squeeze = squeeze.reshape((-1,) + compress.shape)
        low_x = gather_rows(inputs)
        hat_first, rate_first = norm_stats(low_x.astype(F32))
        normed = (hat_first * first_gain + first_bias).astype(BF16)
        core = jnp.einsum(
            "bjt,btc->jc",
            squeeze,
            normed.reshape(slots, tokens, width),
            preferred_element_type=F32,
        )
        total = jnp.sum(squeeze.astype(F32), axis=(0, 2))[:, None]
        low_cot = gather_rows(cotangent)
        core = over_splits(core).astype(BF16)
        total = over_splits(total)
        query, key, value, weights, mixed = attend(
            normed, core, total, qkv_weight, line(qkv_bias), tile=512
        )
        middle, second, active, slope, result = forward(
            alive,
            mixed,
            low_x,
            out_weight,
            line(out_bias),
            line(second_gain),
            line(second_bias),
            up_weight,
            line(up_bias),
            down_weight,
            line(down_bias),
        )
        output = spread_rows(result)
        up_grad, down_grad, up_bias_grad, middle_grad, mixed_grad, out_grad, sums = backward(
            alive,
            low_cot,
            active,
            slope,
            second,
            middle,
            mixed,
            up_weight,
            down_weight,
            out_weight,
            line(second_gain),
        )
        out_bias_grad, second_gain_grad, second_bias_grad, down_bias_grad = (sums[i] for i in range(4))
        (
            query_weight_grad,
            key_weight_grad,
            value_weight_grad,
            query_bias_grad,
            key_bias_grad,
            value_bias_grad,
            query_up,
            core_back,
            lift,
        ) = attend_back(
            mixed_grad, weights, query, key, value, normed, core, total, qkv_weight, line(qkv_bias)
        )
        core_back = over_splits(core_back).astype(BF16)
        lift = over_splits(lift)
        first_up = query_up + jnp.einsum(
            "bjt,jc->btc", squeeze, core_back, preferred_element_type=F32
        ).reshape(rows, width)
        first_gain_grad = jnp.sum(first_up * hat_first, axis=0)
        first_bias_grad = jnp.sum(first_up, axis=0)
        rows_grad = (
            middle_grad + norm_back(hat_first, rate_first, first_up, first_gain)
        ).astype(BF16)
        compress_terms = (
            jnp.einsum(
                "jc,btc->bjt",
                core_back,
                normed.reshape(slots, tokens, width),
                preferred_element_type=F32,
            )
            + lift[None]
        )

        vectors = (
            first_gain_grad,
            first_bias_grad,
            jnp.concatenate([query_bias_grad, key_bias_grad, value_bias_grad], axis=1),
            out_bias_grad,
            second_gain_grad,
            second_bias_grad,
            up_bias_grad,
            down_bias_grad,
        )
        sizes = [v.size // nk for v in vectors]
        packed = jnp.concatenate([v.reshape(nk, -1) for v in vectors], axis=1)
        tall = 32
        wide = -(-sum(sizes) // (tall * 128)) * 128
        packed = jnp.pad(packed, ((0, 0), (0, tall * wide - sum(sizes)))).reshape(nk, tall, wide)
        blocked = [
            grad.reshape(nk, grad.shape[0] // nk, grad.shape[1])
            for grad in (
                down_grad,
                up_grad,
                query_weight_grad,
                key_weight_grad,
                value_weight_grad,
                out_grad,
            )
        ]
        input_grad = spread_rows(rows_grad)
        blocked = blocked[:2] + [jnp.concatenate(blocked[2:], axis=2)]
        down_rows, up_rows, joined = (
            scatter_sum(grad, high_first, low_first, nb, nk, i > 0)
            for i, grad in enumerate(blocked)
        )
        qkv_rows, out_rows = joined[:, : 3 * width], joined[:, 3 * width :]
        compress_rows = scatter_sum(compress_terms, team_low[::-1], team_low, nb, nk, False)
        mine = scatter_sum(packed, high_first, low_first, nb, nk, False).reshape(-1)
        parts = []
        start = 0
        for size in sizes:
            parts.append(mine[start : start + size])
            start += size
        fg, fb, qb, ob, sg, sb, ub, db = parts
    return (
        output,
        input_grad,
        fg,
        fb,
        qkv_rows,
        qb,
        out_rows,
        ob,
        sg,
        sb,
        up_rows,
        ub,
        down_rows,
        db,
        compress_rows,
    )


def solution(mesh):
    rows = P("batch", "blk", None)
    placed = (rows, rows) + (P(),) * 13 + (P(None, "blk"),)
    vec, mat = P("blk"), P("blk", None)
    return jax.shard_map(
        functools.partial(body, nb=mesh.shape["batch"], nk=mesh.shape["blk"]),
        mesh=mesh,
        in_specs=placed,
        out_specs=(rows, rows, vec, vec, mat, vec, mat, vec, vec, vec, mat, vec, mat, vec)
        + (P(None, "blk"),),
        check_vma=False,
    )
```
